32 devices in a mesh: rep: 16 (over z, y, x), shard: 2 (over core).
Axes of the slice: x: 2, y: 2, z: 4, core: 2. Of those that a mesh axis runs over, the one named last changes fastest.
Arguments:
- layer_input: bfloat16 [4096, 1024], P(('rep', 'shard')), may hold values from -6 to 6
- cotangent: bfloat16 [4096, 1024], P(('rep', 'shard')), may hold values from -6 to 6
- w_qkv: float32 [1024, 3072], P('shard'), may hold values from -0.1875 to 0.1875
- qv_bias: float32 [2, 1024], P(None, 'shard'), may hold values from -2 to 2
- w_out: float32 [1024, 1024], P('shard'), may hold values from -0.1875 to 0.1875
- out_bias: float32 [1024], P('shard'), may hold values from -2 to 2
- head_scale: float32 [16], P('shard'), may hold values from 0.5 to 2
- ln1_gain: float32 [1024], P('shard'), may hold values from 0.5 to 1.5
- ln1_bias: float32 [1024], P('shard'), may hold values from -2 to 2
- ln2_gain: float32 [1024], P('shard'), may hold values from 0.5 to 1.5
- ln2_bias: float32 [1024], P('shard'), may hold values from -2 to 2
- ln3_gain: float32 [1024], P('shard'), may hold values from 0.5 to 1.5
- ln3_bias: float32 [1024], P('shard'), may hold values from -2 to 2
- w_fc1: float32 [1024, 4096], P('shard'), may hold values from -0.1875 to 0.1875
- fc1_bias: float32 [4096], P('shard'), may hold values from -2 to 2
- ln4_gain: float32 [4096], P('shard'), may hold values from 0.5 to 1.5
- ln4_bias: float32 [4096], P('shard'), may hold values from -2 to 2
- w_fc2: float32 [4096, 1024], P('shard'), may hold values from -0.09375 to 0.09375
- fc2_bias: float32 [1024], P('shard'), may hold values from -2 to 2
Outputs:
- output: bfloat16 [4096, 1024], P(('rep', 'shard'))
- grad_input: float32 [4096, 1024], P(('rep', 'shard'))
- grad_w_qkv: float32 [1024, 3072], P('shard')
- grad_qv_bias: float32 [2, 1024], P(None, 'shard')
- grad_w_out: float32 [1024, 1024], P('shard')
- grad_out_bias: float32 [1024], P('shard')
- grad_head_scale: float32 [16], P('shard')
- grad_ln1_gain: float32 [1024], P('shard')
- grad_ln1_bias: float32 [1024], P('shard')
- grad_ln2_gain: float32 [1024], P('shard')
- grad_ln2_bias: float32 [1024], P('shard')
- grad_ln3_gain: float32 [1024], P('shard')
- grad_ln3_bias: float32 [1024], P('shard')
- grad_w_fc1: float32 [1024, 4096], P('shard')
- grad_fc1_bias: float32 [4096], P('shard')
- grad_ln4_gain: float32 [4096], P('shard')
- grad_ln4_bias: float32 [4096], P('shard')
- grad_w_fc2: float32 [4096, 1024], P('shard')
- grad_fc2_bias: float32 [1024], P('shard')
The draws below stay inside these ranges and needn't reach their ends.
All inputs are finite; a program needn't handle non-finite values.
Results may differ from the reference program's by a relative error of at most 0.012.
The reference program's roundings to bfloat16 on the way count: a program that leaves them out, or rounds other values in their place, can miss the bound.
Values may be sent and summed in bfloat16 or wider, within the bound.
A program may use at most 320 MiB of HBM per device.

```python
import math
import jax
import jax.numpy as jnp
from jax import lax

D = 1024
FF = 4096
HEADS = 16
HEAD_DIM = 64
LEN = 128
TOKENS = 4096


def steps_of(own_key, dims, split, low, high):
    def one(dim, parts):
        heights = jax.random.uniform(jax.random.fold_in(jax.random.fold_in(own_key, 6), dim), (parts,), jnp.float32, low / len(split), high / len(split))
        return jnp.repeat(jnp.exp(heights), dims[dim] // parts).reshape((-1,) + (1,) * (len(dims) - dim - 1))

    loudness = one(*split[0])
    for cut in split[1:]:
        loudness = loudness * one(*cut)
    return loudness


def bell_draw(key, shape, scale, limit, cuts=(), held_as=jnp.bfloat16):
    values = jax.random.normal(key, shape, jnp.float32) * scale
    if len(cuts) > 0:
        values = steps_of(key, shape, cuts, -0.22, 0.18) * values
    return jnp.clip(values, min=-limit, max=limit).astype(held_as)


def setup_inputs(seed: int = 0) -> dict:
    key_of = jax.random.split(jax.random.key(seed), 20)
    layer_input = bell_draw(key_of[0], (TOKENS, D), 1.0, 6.0, ((0, 32),))
    cotangent = bell_draw(key_of[1], (TOKENS, D), 1.0, 6.0, ((0, 32),))
    w_qkv = bell_draw(key_of[2], (D, 3 * D), D ** -0.5, 0.1875, ((0, 2),), jnp.float32)
    qv_bias = bell_draw(key_of[3], (2, D), 0.3, 2.0, ((1, 2),), jnp.float32)
    w_out = bell_draw(key_of[4], (D, D), D ** -0.5, 0.1875, ((0, 2),), jnp.float32)
    out_bias = bell_draw(key_of[5], (D,), 0.3, 2.0, ((0, 2),), jnp.float32)
    head_scale = jnp.clip(jnp.exp(math.log(2.0) - 1.3862944 * jax.random.uniform(key_of[6], (HEADS,), jnp.float32) ** steps_of(key_of[6], (HEADS,), ((0, 2),), -0.2, 0.2)), 0.5, 2.0)
    ln1_gain = jnp.clip(1.0 + 0.1 * jax.random.normal(key_of[7], (D,), jnp.float32), 0.5, 1.5)
    ln1_bias = bell_draw(key_of[8], (D,), 0.3, 2.0, ((0, 2),), jnp.float32)
    ln2_gain = jnp.clip(1.0 + 0.1 * jax.random.normal(key_of[9], (D,), jnp.float32), 0.5, 1.5)
    ln2_bias = bell_draw(key_of[10], (D,), 0.3, 2.0, ((0, 2),), jnp.float32)
    ln3_gain = jnp.clip(1.0 + 0.1 * jax.random.normal(key_of[11], (D,), jnp.float32), 0.5, 1.5)
    ln3_bias = bell_draw(key_of[12], (D,), 0.3, 2.0, ((0, 2),), jnp.float32)
    w_fc1 = bell_draw(key_of[13], (D, FF), D ** -0.5, 0.1875, ((0, 2),), jnp.float32)
    fc1_bias = bell_draw(key_of[14], (FF,), 0.3, 2.0, ((0, 2),), jnp.float32)
    ln4_gain = jnp.clip(1.0 + 0.1 * jax.random.normal(key_of[15], (FF,), jnp.float32), 0.5, 1.5)
    ln4_bias = bell_draw(key_of[16], (FF,), 0.3, 2.0, ((0, 2),), jnp.float32)
    w_fc2 = bell_draw(key_of[17], (FF, D), FF ** -0.5, 0.09375, ((0, 2),), jnp.float32)
    fc2_bias = bell_draw(key_of[18], (D,), 0.3, 2.0, ((0, 2),), jnp.float32)
    return dict(layer_input=layer_input, cotangent=cotangent, w_qkv=w_qkv, qv_bias=qv_bias, w_out=w_out, out_bias=out_bias, head_scale=head_scale, ln1_gain=ln1_gain, ln1_bias=ln1_bias, ln2_gain=ln2_gain, ln2_bias=ln2_bias, ln3_gain=ln3_gain, ln3_bias=ln3_bias, w_fc1=w_fc1, fc1_bias=fc1_bias, ln4_gain=ln4_gain, ln4_bias=ln4_bias, w_fc2=w_fc2, fc2_bias=fc2_bias)


@jax.custom_vjp
def low(v):
    return lax.optimization_barrier(v.astype(jnp.bfloat16)).astype(jnp.float32)

@jax.custom_vjp
def low_back(v):
    return v

def low_keep(v):
    return (low(v), None)

def low_pass(kept, grad):
    return (grad,)

def back_keep(v):
    return (v, None)

def back_low(kept, grad):
    return (low(grad),)
low.defvjp(low_keep, low_pass)
low_back.defvjp(back_keep, back_low)
EPS = 1e-05
NEG = -1e+30
HIGH = lax.Precision.HIGHEST

def norm_rows(v, gain, bias):
    centre = lax.optimization_barrier(jnp.mean(v, axis=-1, keepdims=True))
    centred = v - centre
    spread = lax.optimization_barrier(jnp.mean(centred * centred, axis=-1, keepdims=True))
    return centred * lax.rsqrt(spread + EPS) * gain + bias

def forward(inputs, params):
    weight_qkv, bias_qv, weight_out, bias_out, head_gain, gain_one, shift_one, gain_two, shift_two, gain_three, shift_three, weight_up, bias_up, gain_four, shift_four, weight_down, bias_down = tuple((low(p) for p in params))
    groups, length, width = inputs.shape
    act_one = low(norm_rows(inputs, gain_one, shift_one))
    bias_full = jnp.concatenate([bias_qv[0], jnp.zeros_like(bias_qv[0]), bias_qv[1]])
    qkv = low(low_back(jnp.dot(act_one, weight_qkv, precision=HIGH) + bias_full))
    qkv = qkv.reshape(groups, length, 3, HEADS, HEAD_DIM)
    queries = qkv[:, :, 0]
    keys_all = qkv[:, :, 1]
    values_all = qkv[:, :, 2]
    qblock = min(512, length)
    blocks = length // qblock
    scale = HEAD_DIM ** (-0.5)

    def one_block(index):
        rows_q = lax.dynamic_slice_in_dim(queries, index * qblock, qblock, 1)
        scores = low_back(jnp.einsum('gqhd,gkhd->ghqk', rows_q, keys_all, precision=HIGH) * scale)
        rows = index * qblock + lax.iota(jnp.int32, qblock)
        cols = lax.iota(jnp.int32, length)
        allowed = cols[None, :] <= rows[:, None]
        scores = jnp.where(allowed[None, None], scores, NEG)
        total = jax.nn.logsumexp(scores, axis=-1, keepdims=True)
        probs = low(jnp.exp(scores - total))
        return low_back(jnp.einsum('ghqk,gkhd->gqhd', probs, values_all, precision=HIGH))
    pieces = lax.map(jax.checkpoint(one_block), jnp.arange(blocks, dtype=jnp.int32))
    attended = jnp.moveaxis(pieces, 0, 1).reshape(groups, length, HEADS, HEAD_DIM)
    mixed = low((attended * head_gain[:, None]).reshape(groups, length, width))
    branch = low_back(jnp.dot(mixed, weight_out, precision=HIGH) + bias_out)
    middle = inputs + norm_rows(branch, gain_two, shift_two)
    act_three = low(norm_rows(middle, gain_three, shift_three))
    hidden = low_back(jnp.dot(act_three, weight_up, precision=HIGH) + bias_up)
    act_four = low(norm_rows(jax.nn.gelu(hidden, approximate=False), gain_four, shift_four))
    down = low_back(jnp.dot(act_four, weight_down, precision=HIGH) + bias_down)
    return middle + down

def reference(layer_input, cotangent, w_qkv, qv_bias, w_out, out_bias, head_scale, ln1_gain, ln1_bias, ln2_gain, ln2_bias, ln3_gain, ln3_bias, w_fc1, fc1_bias, ln4_gain, ln4_bias, w_fc2, fc2_bias):
    params = (w_qkv, qv_bias, w_out, out_bias, head_scale, ln1_gain, ln1_bias, ln2_gain, ln2_bias, ln3_gain, ln3_bias, w_fc1, fc1_bias, ln4_gain, ln4_bias, w_fc2, fc2_bias)
    params = tuple((p.astype(jnp.float32) for p in params))
    count = layer_input.shape[0] // LEN
    group = math.gcd(count, max(1, 4096 // LEN))
    turns = count // group
    inputs = layer_input.astype(jnp.float32).reshape(turns, group, LEN, D)
    cotans = cotangent.astype(jnp.float32).reshape(turns, group, LEN, D)
    zeros = tuple((jnp.zeros_like(p) for p in params))

    def one_group(totals, pair):
        batch_in, batch_cot = pair
        result, pull = jax.vjp(forward, batch_in, params)
        grad_in, grad_params = pull(batch_cot)
        totals = tuple((a + b for a, b in zip(totals, grad_params)))
        return (totals, (result.astype(jnp.bfloat16), grad_in))
    totals, (results, grads_in) = lax.scan(one_group, zeros, (inputs, cotans))
    output = results.reshape(-1, D)
    grad_input = grads_in.reshape(-1, D)
    return (output, grad_input, totals[0], totals[1], totals[2], totals[3], totals[4], totals[5], totals[6], totals[7], totals[8], totals[9], totals[10], totals[11], totals[12], totals[13], totals[14], totals[15], totals[16])
```

```python
import functools

import jax
import jax.numpy as jnp
from jax import lax
from jax.experimental import pallas as pl
from jax.experimental.pallas import tpu as pltpu
from jax.sharding import PartitionSpec as P

D = 1024
HEADS = 16
HEAD_DIM = 64


EPS = 1e-05
NEG = -1e30


def norm_rows(v, gain, bias):
    centre = jnp.mean(v, axis=-1, keepdims=True)
    centred = v - centre
    spread = jnp.mean(centred * centred, axis=-1, keepdims=True)
    return centred * lax.rsqrt(spread + EPS) * gain + bias


def ffn_middle(hidden, gain, bias):
    return norm_rows(jax.nn.gelu(hidden, approximate=False), gain, bias)


def causal_mask(index, qblock, length):
    rows = index * qblock + lax.iota(jnp.int32, qblock)
    cols = lax.iota(jnp.int32, length)
    return (cols[None, :] <= rows[:, None])[None]


def block_scores(queries, keys_all, index, qblock, scale):
    length = keys_all.shape[0]
    scores = (
        jnp.einsum("qhd,khd->hqk", queries, keys_all, preferred_element_type=jnp.float32) * scale
    )
    return (queries, jnp.where(causal_mask(index, qblock, length), scores, NEG))


def attend_forward(queries, keys_all, values_all, scale):
    length, heads, width = queries.shape
    qblock = min(512, length)
    blocks = length // qblock

    def one_block(index):
        rows_q, scores = block_scores(queries, keys_all, index, qblock, scale)
        total = jax.nn.logsumexp(scores, axis=-1, keepdims=True)
        probs = jnp.exp(scores - total).astype(jnp.bfloat16)
        outcome = jnp.einsum("hqk,khd->qhd", probs, values_all, preferred_element_type=jnp.float32)
        return (outcome, total)

    outcome, totals = lax.map(one_block, jnp.arange(blocks, dtype=jnp.int32))
    return (outcome.reshape(length, heads, width), totals)


def attend_backward(queries, keys_all, values_all, totals, grad_out, scale):
    length, heads, width = queries.shape
    qblock = min(512, length)
    blocks = length // qblock

    def one_block(carry, index):
        grad_keys, grad_values = carry
        rows_q, scores = block_scores(queries, keys_all, index, qblock, scale)
        probs = jnp.exp(scores - totals[index])
        probs_low = probs.astype(jnp.bfloat16)
        grad_values = grad_values + jnp.einsum(
            "hqk,qhd->khd", probs_low, grad_out, preferred_element_type=jnp.float32
        )
        grad_probs = jnp.einsum(
            "qhd,khd->hqk", grad_out, values_all, preferred_element_type=jnp.float32
        )
        row_dot = jnp.sum(probs * grad_probs, axis=-1, keepdims=True)
        grad_scores = (probs * (grad_probs - row_dot)).astype(jnp.bfloat16)
        grad_rows = (
            jnp.einsum("hqk,khd->qhd", grad_scores, keys_all, preferred_element_type=jnp.float32)
            * scale
        )
        grad_keys = (
            grad_keys
            + jnp.einsum("hqk,qhd->khd", grad_scores, rows_q, preferred_element_type=jnp.float32)
            * scale
        )
        return ((grad_keys, grad_values), grad_rows)

    empty = jnp.zeros((length, heads, width), jnp.float32)
    (grad_keys, grad_values), grad_queries = lax.scan(
        one_block, (empty, empty), jnp.arange(blocks, dtype=jnp.int32)
    )
    return (grad_queries.reshape(length, heads, width), grad_keys, grad_values)


def on_any_mesh(
    layer_input,
    cotangent,
    w_qkv,
    qv_bias,
    w_out,
    out_bias,
    head_scale,
    ln1_gain,
    ln1_bias,
    ln2_gain,
    ln2_bias,
    ln3_gain,
    ln3_bias,
    w_fc1,
    fc1_bias,
    ln4_gain,
    ln4_bias,
    w_fc2,
    fc2_bias,
):
    low_qkv = w_qkv.astype(jnp.bfloat16)
    low_out = w_out.astype(jnp.bfloat16)
    low_heads = head_scale.astype(jnp.bfloat16)
    low_up = w_fc1.astype(jnp.bfloat16)
    low_down = w_fc2.astype(jnp.bfloat16)
    whole = (
        lax.all_gather(low_qkv, "shard", axis=0, tiled=True),
        lax.all_gather(qv_bias.astype(jnp.bfloat16), "shard", axis=1, tiled=True),
        lax.all_gather(low_out, "shard", axis=0, tiled=True),
        lax.all_gather(out_bias.astype(jnp.bfloat16), "shard", axis=0, tiled=True),
        lax.all_gather(low_heads, "shard", axis=0, tiled=True),
        lax.all_gather(ln1_gain.astype(jnp.bfloat16), "shard", axis=0, tiled=True),
        lax.all_gather(ln1_bias.astype(jnp.bfloat16), "shard", axis=0, tiled=True),
        lax.all_gather(ln2_gain.astype(jnp.bfloat16), "shard", axis=0, tiled=True),
        lax.all_gather(ln2_bias.astype(jnp.bfloat16), "shard", axis=0, tiled=True),
        lax.all_gather(ln3_gain.astype(jnp.bfloat16), "shard", axis=0, tiled=True),
        lax.all_gather(ln3_bias.astype(jnp.bfloat16), "shard", axis=0, tiled=True),
        lax.all_gather(low_up, "shard", axis=0, tiled=True),
        lax.all_gather(fc1_bias.astype(jnp.bfloat16), "shard", axis=0, tiled=True),
        lax.all_gather(ln4_gain.astype(jnp.bfloat16), "shard", axis=0, tiled=True),
        lax.all_gather(ln4_bias.astype(jnp.bfloat16), "shard", axis=0, tiled=True),
        lax.all_gather(low_down, "shard", axis=0, tiled=True),
        lax.all_gather(fc2_bias.astype(jnp.bfloat16), "shard", axis=0, tiled=True),
    )
    weight_qkv, weight_out, weight_up, weight_down = (whole[0], whole[2], whole[11], whole[15])
    (
        bias_qv,
        bias_out,
        head_gain,
        gain_one,
        shift_one,
        gain_two,
        shift_two,
        gain_three,
        shift_three,
        bias_up,
        gain_four,
        shift_four,
        bias_down,
    ) = tuple(
        (whole[index].astype(jnp.float32) for index in (1, 3, 4, 5, 6, 7, 8, 9, 10, 12, 13, 14, 16))
    )
    length = layer_input.shape[0]
    scale = HEAD_DIM ** (-0.5)
    inputs = layer_input.astype(jnp.float32)
    normed_one, pull_one = jax.vjp(norm_rows, inputs, gain_one, shift_one)
    act_one = normed_one.astype(jnp.bfloat16)
    bias_full = jnp.concatenate([bias_qv[0], jnp.zeros((D,), jnp.float32), bias_qv[1]])
    qkv = (jnp.dot(act_one, weight_qkv, preferred_element_type=jnp.float32) + bias_full).astype(
        jnp.bfloat16
    )
    triple = qkv.reshape(length, 3, HEADS, HEAD_DIM)
    queries = triple[:, 0]
    keys_all = triple[:, 1]
    values_all = triple[:, 2]
    attended, totals = attend_forward(queries, keys_all, values_all, scale)
    mixed = (attended * head_gain[:, None]).reshape(length, D).astype(jnp.bfloat16)
    branch = jnp.dot(mixed, weight_out, preferred_element_type=jnp.float32) + bias_out
    normed_two, pull_two = jax.vjp(norm_rows, branch, gain_two, shift_two)
    middle = inputs + normed_two
    normed_three, pull_three = jax.vjp(norm_rows, middle, gain_three, shift_three)
    act_three = normed_three.astype(jnp.bfloat16)
    hidden = jnp.dot(act_three, weight_up, preferred_element_type=jnp.float32) + bias_up
    normed_four, pull_four = jax.vjp(ffn_middle, hidden, gain_four, shift_four)
    act_four = normed_four.astype(jnp.bfloat16)
    result = middle + (
        jnp.dot(act_four, weight_down, preferred_element_type=jnp.float32) + bias_down
    )
    output = result.astype(jnp.bfloat16)
    again = (
        lax.all_gather(low_qkv, "shard", axis=0, tiled=True),
        lax.all_gather(low_out, "shard", axis=0, tiled=True),
        lax.all_gather(low_heads, "shard", axis=0, tiled=True),
        lax.all_gather(low_up, "shard", axis=0, tiled=True),
        lax.all_gather(low_down, "shard", axis=0, tiled=True),
    )
    back_qkv, back_out, back_up, back_down = (again[0], again[1], again[3], again[4])
    back_heads = again[2].astype(jnp.float32)
    cot_full = cotangent.astype(jnp.float32)
    grad_down_bias = jnp.sum(cot_full, axis=0)
    grad_down = jnp.einsum("tf,td->fd", act_four, cotangent, preferred_element_type=jnp.float32)
    grad_four = jnp.einsum("td,fd->tf", cotangent, back_down, preferred_element_type=jnp.float32)
    grad_hidden, grad_gain_four, grad_shift_four = pull_four(grad_four)
    hidden_low = grad_hidden.astype(jnp.bfloat16)
    grad_up_bias = jnp.sum(hidden_low, axis=0, dtype=jnp.float32)
    grad_up = jnp.einsum("td,tf->df", act_three, hidden_low, preferred_element_type=jnp.float32)
    grad_three = jnp.einsum("tf,df->td", hidden_low, back_up, preferred_element_type=jnp.float32)
    grad_mid_part, grad_gain_three, grad_shift_three = pull_three(grad_three)
    grad_middle = cot_full + grad_mid_part
    grad_branch, grad_gain_two, grad_shift_two = pull_two(grad_middle)
    branch_low = grad_branch.astype(jnp.bfloat16)
    grad_out_b = jnp.sum(branch_low, axis=0, dtype=jnp.float32)
    grad_out_w = jnp.einsum("td,te->de", mixed, branch_low, preferred_element_type=jnp.float32)
    grad_mixed = jnp.einsum("te,de->td", branch_low, back_out, preferred_element_type=jnp.float32)
    grad_mixed = grad_mixed.reshape(length, HEADS, HEAD_DIM)
    grad_heads = jnp.sum(grad_mixed * attended, axis=(0, 2))
    grad_attended = (grad_mixed * back_heads[:, None]).astype(jnp.bfloat16)
    grad_queries, grad_keys, grad_values = attend_backward(
        queries, keys_all, values_all, totals, grad_attended, scale
    )
    grad_qkv = (
        jnp.stack([grad_queries, grad_keys, grad_values], axis=1)
        .reshape(length, 3 * D)
        .astype(jnp.bfloat16)
    )
    grad_qv = jnp.stack(
        [
            jnp.sum(grad_qkv[:, :D], axis=0, dtype=jnp.float32),
            jnp.sum(grad_qkv[:, 2 * D :], axis=0, dtype=jnp.float32),
        ]
    )
    grad_qkv_w = jnp.einsum("td,te->de", act_one, grad_qkv, preferred_element_type=jnp.float32)
    grad_one = jnp.einsum("te,de->td", grad_qkv, back_qkv, preferred_element_type=jnp.float32)
    grad_in_part, grad_gain_one, grad_shift_one = pull_one(grad_one)
    grad_input = grad_middle + grad_in_part
    shares = (
        lax.psum_scatter(grad_qkv_w, "shard", scatter_dimension=0, tiled=True),
        lax.psum_scatter(grad_qv, "shard", scatter_dimension=1, tiled=True),
        lax.psum_scatter(grad_out_w, "shard", scatter_dimension=0, tiled=True),
        lax.psum_scatter(grad_out_b, "shard", scatter_dimension=0, tiled=True),
        lax.psum_scatter(grad_heads, "shard", scatter_dimension=0, tiled=True),
        lax.psum_scatter(grad_gain_one, "shard", scatter_dimension=0, tiled=True),
        lax.psum_scatter(grad_shift_one, "shard", scatter_dimension=0, tiled=True),
        lax.psum_scatter(grad_gain_two, "shard", scatter_dimension=0, tiled=True),
        lax.psum_scatter(grad_shift_two, "shard", scatter_dimension=0, tiled=True),
        lax.psum_scatter(grad_gain_three, "shard", scatter_dimension=0, tiled=True),
        lax.psum_scatter(grad_shift_three, "shard", scatter_dimension=0, tiled=True),
        lax.psum_scatter(grad_up, "shard", scatter_dimension=0, tiled=True),
        lax.psum_scatter(grad_up_bias, "shard", scatter_dimension=0, tiled=True),
        lax.psum_scatter(grad_gain_four, "shard", scatter_dimension=0, tiled=True),
        lax.psum_scatter(grad_shift_four, "shard", scatter_dimension=0, tiled=True),
        lax.psum_scatter(grad_down, "shard", scatter_dimension=0, tiled=True),
        lax.psum_scatter(grad_down_bias, "shard", scatter_dimension=0, tiled=True),
    )
    summed = lax.psum(
        (
            shares[0],
            shares[1],
            shares[2],
            shares[3],
            shares[4],
            shares[5],
            shares[6],
            shares[7],
            shares[8],
            shares[9],
            shares[10],
            shares[11],
            shares[12],
            shares[13],
            shares[14],
            shares[15],
            shares[16],
        ),
        "rep",
    )
    return (output, grad_input) + tuple(summed)


MESH = pl.DeviceIdType.MESH
BF16 = jnp.bfloat16
F32 = jnp.float32
UNIT_ROWS = 256
UNIT_COLS = 1024
MIB = 1 << 20
COMMS = ("d1", "d2", "z1", "z2", "z3", "u1", "w1", "u2", "w2", "u3", "w3", "g1", "g2")
SLOT = {name: index for index, name in enumerate(COMMS)}


def unit_table(dims):
    table = []
    for matrix in (3, 2, 1, 0):
        rows, cols = dims[matrix]
        for col in range(0, cols, UNIT_COLS):
            for row in range(0, rows, UNIT_ROWS):
                table.append((matrix, row, col))
    return table


def kinds_of(count):
    kinds, lines = [], 0
    for index in range(count):
        kind = "XYXYZ"[index % 5]
        if kind == "Z":
            kind = ("ZX", "ZY")[lines % 2]
            lines += 1
        kinds.append(kind)
    return kinds


def task_order(kinds):
    keys = []
    for unit, kind in enumerate(kinds):
        offsets = Z_OFFSETS if kind[0] == "Z" else XY_OFFSETS
        for step, offset in enumerate(offsets):
            keys.append((unit + offset, unit, step))
    keys.sort()
    return [(unit, step) for _, unit, step in keys]


XY_OFFSETS = (0, 3.5, 7.0, 11.5, 14.5, 17.5, 21.0, 23.0, 25.0, 27.5, 30.5)
Z_OFFSETS = (0.0, 4.5, 7.0, 10.0, 13.0, 16.5, 19.0, 23.0, 25.0, 28.0, 32.5)


def sum_kernel(dims, at_base, g_base, *refs):
    at_in, g_in, vec_in = refs[0:4], refs[4:8], refs[8]
    outs, vec_out = refs[9:13], refs[13]
    (at, g, res, give, pair, line_xy, line_z, vec_own, vec_got, send, recv, v_send, v_recv, p_send, p_recv, l_sem, o_sem) = refs[14:]
    r = lax.axis_index("rep")
    c = lax.axis_index("shard")
    x, y, z = r % 2, (r // 2) % 2, r // 4
    core = {"shard": 1 - c}
    to = {
        "X": {"rep": r + 1 - 2 * x},
        "Y": {"rep": r + 2 - 4 * y},
        "U": {"rep": r + 4},
        "D": {"rep": r - 4},
    }
    line_end = (z == 0) | (z == 3)
    line_mid = (z == 1) | (z == 2)
    outward = {"rep": r + 4 * (2 * (z // 2) - 1)}
    inward = {"rep": r + 4 * (1 - 2 * (z // 2))}
    across = {"rep": r + 4 * (3 - 2 * z)}
    upper = z // 2

    barrier = pltpu.get_barrier_semaphore()
    for peer in (core, to["X"], to["Y"]):
        pl.semaphore_signal(barrier, inc=1, device_id=peer, device_id_type=MESH)

    @pl.when(z < 3)
    def _():
        pl.semaphore_signal(barrier, inc=1, device_id=to["U"], device_id_type=MESH)

    @pl.when(z > 0)
    def _():
        pl.semaphore_signal(barrier, inc=1, device_id=to["D"], device_id_type=MESH)

    @pl.when(line_end)
    def _():
        pl.semaphore_signal(barrier, inc=1, device_id=across, device_id_type=MESH)

    pl.semaphore_wait(barrier, 5)

    own_copies, pair_copies = [], []
    for m in (3, 2, 1, 0):
        rows, cols = dims[m]
        mine = pltpu.make_async_copy(
            at_in[m].at[pl.ds(pl.multiple_of(c * rows, rows), rows), :],
            at.at[pl.ds(at_base[m], rows), pl.ds(0, 128)],
            l_sem.at[m, 0],
        )
        mine.start()
        grads = pltpu.make_async_copy(
            g_in[m], g.at[pl.ds(0, 128), pl.ds(g_base[m], cols)], l_sem.at[m, 1]
        )
        grads.start()
        far = pltpu.make_async_remote_copy(
            src_ref=at_in[m].at[pl.ds(pl.multiple_of((1 - c) * rows, rows), rows), :],
            dst_ref=at.at[pl.ds(at_base[m], rows), pl.ds(128, 128)],
            send_sem=p_send.at[m, 0], recv_sem=p_recv.at[m, 0], device_id=core, device_id_type=MESH,
        )
        far.start()
        far_g = pltpu.make_async_remote_copy(
            src_ref=g_in[m],
            dst_ref=g.at[pl.ds(128, 128), pl.ds(g_base[m], cols)],
            send_sem=p_send.at[m, 1], recv_sem=p_recv.at[m, 1], device_id=core, device_id_type=MESH,
        )
        far_g.start()
        own_copies.append((m, (mine, grads)))
        pair_copies.append((m, (far, far_g)))
    own_copies, pair_copies = dict(own_copies), dict(pair_copies)

    vec_steps = (core, to["X"], to["Y"], {"rep": r + 4 * (1 - 2 * (z % 2))}, across)

    def vec_copy(step):
        source = vec_in.at[1 - c] if step == 0 else vec_own.at[step]
        return pltpu.make_async_remote_copy(
            src_ref=source, dst_ref=vec_got.at[step], send_sem=v_send.at[step], recv_sem=v_recv.at[step],
            device_id=vec_steps[step], device_id_type=MESH,
        )

    units = unit_table(dims)
    kinds = kinds_of(len(units))
    xy_at, z_at = {}, {}
    for unit, kind in enumerate(kinds):
        (z_at if kind[0] == "Z" else xy_at)[unit] = len(z_at) if kind[0] == "Z" else len(xy_at)
    ready = set()

    def copy(unit, name, source, dest, device):
        return functools.partial(
            pltpu.make_async_remote_copy,
            src_ref=source, dst_ref=dest, send_sem=send.at[unit, SLOT[name]], recv_sem=recv.at[unit, SLOT[name]],
            device_id=device, device_id_type=MESH,
        )

    def rows_of(unit, start, count):
        if not isinstance(start, int):
            start = pl.multiple_of(start, 16)
        return res.at[unit, pl.ds(start, count), :]

    def product(unit, start, count, dest, dest_start, got=None, got_start=0):
        m, row, col = units[unit]
        step = 128 if count % 128 == 0 else min(count, 64)

        def block(index, _):
            part, strip = index // (UNIT_COLS // 256), index % (UNIT_COLS // 256)
            cols = pl.ds(pl.multiple_of(strip * 256, 256), 256)
            value = jnp.dot(
                at[pl.ds(pl.multiple_of(at_base[m] + row + start + part * step, 16), step), :],
                g[:, pl.ds(pl.multiple_of(g_base[m] + col + strip * 256, 256), 256)],
                preferred_element_type=F32,
            )
            if got is not None:
                value = value + got[pl.ds(pl.multiple_of(got_start + part * step, 16), step), cols].astype(F32)
            dest[pl.ds(pl.multiple_of(dest_start + part * step, 16), step), cols] = value.astype(BF16)
            return 0

        lax.fori_loop(0, (count // step) * (UNIT_COLS // 256), block, 0)

    def accumulate(unit, start, count, got, got_start, dest, dest_start):
        def block(strip, _):
            cols = pl.ds(pl.multiple_of(strip * 256, 256), 256)
            value = res[unit, pl.ds(pl.multiple_of(start, 16), count), cols].astype(F32)
            value = value + got[pl.ds(pl.multiple_of(got_start, 16), count), cols].astype(F32)
            dest[pl.ds(pl.multiple_of(dest_start, 16), count), cols] = value.astype(BF16)
            return 0

        lax.fori_loop(0, UNIT_COLS // 256, block, 0)

    def gather_line(unit, base, size, level):
        up, down = "u%d" % level, "w%d" % level
        low, high = z - (level - 1), z + (level - 1)

        @pl.when((low >= 0) & (z < 3))
        def _():
            part = rows_of(unit, base + low * size, size)
            copy(unit, up, part, part, to["U"])().start()

        @pl.when((high <= 3) & (z > 0))
        def _():
            part = rows_of(unit, base + high * size, size)
            copy(unit, down, part, part, to["D"])().start()

    def gather_arrived(unit, base, size, level):
        up, down = "u%d" % level, "w%d" % level
        low, high = z - level, z + level

        @pl.when(low >= 0)
        def _():
            part = rows_of(unit, base + low * size, size)
            copy(unit, up, part, part, to["U"])().wait_recv()

        @pl.when(high <= 3)
        def _():
            part = rows_of(unit, base + high * size, size)
            copy(unit, down, part, part, to["D"])().wait_recv()

    def gather_sent(unit, base, size):
        for level in (1, 2, 3):
            up, down = "u%d" % level, "w%d" % level
            low, high = z - (level - 1), z + (level - 1)

            @pl.when((low >= 0) & (z < 3))
            def _():
                part = rows_of(unit, base + low * size, size)
                copy(unit, up, part, part, to["U"])().wait_send()

            @pl.when((high <= 3) & (z > 0))
            def _():
                part = rows_of(unit, base + high * size, size)
                copy(unit, down, part, part, to["D"])().wait_send()

    def write_out(unit):
        m, row, col = units[unit]
        return pltpu.make_async_copy(
            res.at[unit],
            outs[m].at[pl.ds(row, UNIT_ROWS), pl.ds(col, UNIT_COLS)],
            o_sem.at[unit],
        )

    def finish(unit, base, size, sent):
        write_out(unit).start()
        for name in sent[:4]:
            name().wait_send()
        pl.when(line_end)(lambda: sent[4]().wait_send())

        @pl.when(line_mid)
        def _():
            sent[5]().wait_send()
            sent[6]().wait_send()

        gather_sent(unit, base, size)

    def task_xy(unit, step):
        half, quarter, size = UNIT_ROWS // 2, UNIT_ROWS // 4, UNIT_ROWS // 16
        first, second = ("X", "Y") if kinds[unit] == "X" else ("Y", "X")
        p, q = (x, y) if kinds[unit] == "X" else (y, x)
        line, block, out, other = line_xy.at[xy_at[unit]], res.at[unit], give.at[unit], pair.at[unit]
        keep, away_half = p * half, (1 - p) * half
        base = keep + q * quarter
        away = keep + (1 - q) * quarter
        at_z = half + quarter
        d1 = copy(unit, "d1", out.at[pl.ds(0, half), :], rows_of(unit, away_half, half), to[first])
        d2 = copy(unit, "d2", out.at[pl.ds(half, quarter), :], other.at[pl.ds(0, quarter), :], to[second])
        z1 = copy(unit, "z1", out.at[pl.ds(at_z, 3 * size), :], line.at[pl.ds(0, 3 * size), :], inward)
        z2 = copy(unit, "z2", out.at[pl.ds(at_z, 2 * size), :], line.at[pl.ds(3 * size, 2 * size), :], across)
        z3 = copy(unit, "z3", out.at[pl.ds(at_z + 2 * size, size), :], line.at[pl.ds(0, size), :], outward)
        own_quarter = rows_of(unit, base, quarter)
        g2 = copy(unit, "g2", own_quarter, own_quarter, to[second])
        own_half = rows_of(unit, keep, half)
        g1 = copy(unit, "g1", own_half, own_half, to[first])
        own = base + z * size
        if step == 0:
            product(unit, away_half, half, out, 0)
            d1().start()
        elif step == 1:
            d1().wait_recv()
            product(unit, away, quarter, out, half, block, away)
            d2().start()
            product(unit, base, quarter, block, base, block, base)
        elif step == 2:
            d2().wait_recv()

            @pl.when(line_end)
            def _():
                skip = (1 - upper) * size
                accumulate(unit, base + skip, 3 * size, other, skip, out, at_z)
                z1().start()
                accumulate(unit, own, size, other, z * size, block, own)

            @pl.when(line_mid)
            def _():
                accumulate(unit, base, quarter, other, 0, block, base)

        elif step == 3:

            @pl.when(line_mid)
            def _():
                z1().wait_recv()
                accumulate(unit, base + (1 - upper) * 2 * size, 2 * size, line, (1 - upper) * size, out, at_z)
                z2().start()
                accumulate(unit, own, size, line, upper * 2 * size, block, own)

        elif step == 4:

            @pl.when(line_mid)
            def _():
                z2().wait_recv()
                accumulate(unit, base + upper * 3 * size, size, line, (3 + upper) * size, out, at_z + 2 * size)
                z3().start()
                accumulate(unit, own, size, line, (4 - upper) * size, block, own)
                gather_line(unit, base, size, 1)

        elif step == 5:

            @pl.when(line_end)
            def _():
                z3().wait_recv()
                accumulate(unit, own, size, line, 0, block, own)
                gather_line(unit, base, size, 1)

        elif step in (6, 7):
            gather_arrived(unit, base, size, step - 5)
            gather_line(unit, base, size, step - 4)
        elif step == 8:
            gather_arrived(unit, base, size, 3)
            g2().start()
        elif step == 9:
            g2().wait_recv()
            g1().start()
        else:
            g1().wait_recv()
            finish(unit, base, size, (d1, d2, g2, g1, z1, z2, z3))

    def task_z(unit, step):
        size, half, quarter = UNIT_ROWS // 4, UNIT_ROWS // 8, UNIT_ROWS // 16
        first, second = ("X", "Y") if kinds[unit] == "ZX" else ("Y", "X")
        p, q = (x, y) if kinds[unit] == "ZX" else (y, x)
        line, block, out, other = line_z.at[z_at[unit]], res.at[unit], give.at[unit], pair.at[unit]
        own = z * size
        keep, away_half = own + p * half, own + (1 - p) * half
        base, away = keep + q * quarter, keep + (1 - q) * quarter
        at_d = 3 * size
        z1 = copy(unit, "z1", out.at[pl.ds(0, 3 * size), :], line.at[pl.ds(0, 3 * size), :], inward)
        z2 = copy(unit, "z2", out.at[pl.ds(0, 2 * size), :], line.at[pl.ds(3 * size, 2 * size), :], across)
        z3 = copy(unit, "z3", out.at[pl.ds(2 * size, size), :], line.at[pl.ds(0, size), :], outward)
        d1 = copy(unit, "d1", out.at[pl.ds(at_d, half), :], other.at[pl.ds(0, half), :], to[first])
        d2 = copy(unit, "d2", out.at[pl.ds(at_d + half, quarter), :], other.at[pl.ds(half, quarter), :], to[second])
        own_quarter = rows_of(unit, base, quarter)
        g2 = copy(unit, "g2", own_quarter, own_quarter, to[second])
        own_half = rows_of(unit, keep, half)
        g1 = copy(unit, "g1", own_half, own_half, to[first])
        if step == 0:

            @pl.when(line_end)
            def _():
                product(unit, (1 - upper) * size, 3 * size, out, 0)
                z1().start()

        elif step == 1:

            @pl.when(line_mid)
            def _():
                z1().wait_recv()
                product(unit, (1 - upper) * 2 * size, 2 * size, out, 0, line, (1 - upper) * size)
                z2().start()
                product(unit, own, size, block, own, line, upper * 2 * size)

        elif step == 2:

            @pl.when(line_mid)
            def _():
                z2().wait_recv()
                product(unit, upper * 3 * size, size, out, 2 * size, line, (3 + upper) * size)
                z3().start()
                got = (4 - upper) * size
                accumulate(unit, away_half, half, line, got + (1 - p) * half, out, at_d)
                d1().start()
                accumulate(unit, keep, half, line, got + p * half, block, keep)

        elif step == 3:

            @pl.when(line_end)
            def _():
                z3().wait_recv()
                product(unit, away_half, half, out, at_d, line, (1 - p) * half)
                d1().start()
                product(unit, keep, half, block, keep, line, p * half)

        elif step == 4:
            d1().wait_recv()
            accumulate(unit, away, quarter, other, (1 - q) * quarter, out, at_d + half)
            d2().start()
            accumulate(unit, base, quarter, other, q * quarter, block, base)
        elif step == 5:
            d2().wait_recv()
            accumulate(unit, base, quarter, other, half, block, base)
            g2().start()
        elif step == 6:
            g2().wait_recv()
            g1().start()
        elif step == 7:
            g1().wait_recv()
            gather_line(unit, 0, size, 1)
        elif step in (8, 9):
            gather_arrived(unit, 0, size, step - 7)
            gather_line(unit, 0, size, step - 6)
        else:
            gather_arrived(unit, 0, size, 3)
            finish(unit, 0, size, (d1, d2, g2, g1, z1, z2, z3))

    vec_copy(0).start()
    order = task_order(kinds)
    vec_at = {12 + 8 * step: step for step in range(5)}
    for index, (unit, step) in enumerate(order):
        m = units[unit][0]
        if m not in ready:
            ready.add(m)
            for piece in own_copies[m] + pair_copies[m]:
                piece.wait()
        if kinds[unit][0] == "Z":
            task_z(unit, step)
        else:
            task_xy(unit, step)
        if index in vec_at:
            k = vec_at[index]
            vec_copy(k).wait_recv()
            total = (vec_in[c] if k == 0 else vec_own[k]) + vec_got[k]
            if k < 4:
                vec_own[k + 1] = total
                vec_copy(k + 1).start()
            else:
                vec_out[...] = total
    for step in range(5):
        vec_copy(step).wait_send()
    for unit in range(len(units)):
        write_out(unit).wait()


def sum_over_replicas(ats, gs, vec, dims):
    at_rows = sum(rows for rows, _ in dims)
    g_cols = sum(cols for _, cols in dims)
    at_base = [sum(rows for rows, _ in dims[:m]) for m in range(4)]
    g_base = [sum(cols for _, cols in dims[:m]) for m in range(4)]
    units = unit_table(dims)
    kinds = kinds_of(len(units))
    n, n_z = len(units), sum(kind[0] == "Z" for kind in kinds)
    hbm = pl.BlockSpec(memory_space=pl.ANY)
    vmem = pl.BlockSpec(memory_space=pltpu.VMEM)
    dma = pltpu.SemaphoreType.DMA
    return pl.pallas_call(
        functools.partial(sum_kernel, dims, at_base, g_base),
        out_shape=[jax.ShapeDtypeStruct(d, BF16) for d in dims] + [jax.ShapeDtypeStruct(vec.shape[1:], F32)],
        in_specs=[hbm] * 8 + [vmem],
        out_specs=[hbm] * 4 + [vmem],
        scratch_shapes=[
            pltpu.VMEM((at_rows, 256), BF16),
            pltpu.VMEM((256, g_cols), BF16),
            pltpu.VMEM((n, UNIT_ROWS, UNIT_COLS), BF16),
            pltpu.VMEM((n, 15 * UNIT_ROWS // 16, UNIT_COLS), BF16),
            pltpu.VMEM((n, UNIT_ROWS // 4, UNIT_COLS), BF16),
            pltpu.VMEM((n - n_z, 5 * UNIT_ROWS // 16, UNIT_COLS), BF16),
            pltpu.VMEM((n_z, 5 * UNIT_ROWS // 4, UNIT_COLS), BF16),
            pltpu.VMEM((5,) + vec.shape[1:], F32),
            pltpu.VMEM((5,) + vec.shape[1:], F32),
            dma((n, len(COMMS))),
            dma((n, len(COMMS))),
            dma((5,)),
            dma((5,)),
            dma((4, 2)),
            dma((4, 2)),
            dma((4, 2)),
            dma((n,)),
        ],
        compiler_params=pltpu.CompilerParams(
            collective_id=1, has_side_effects=True, vmem_limit_bytes=56 * MIB
        ),
        name="sum_over_replicas",
    )(*ats, *gs, vec)


def piece_rows(rows, cols):
    while 4 * rows * cols > MIB and rows % 32 == 0:
        rows //= 2
    return rows


def spread_kernel(dims, steps, *refs):
    weights, small, wholes, small_out = refs[0:4], refs[4], refs[5:9], refs[9]
    wide, low, in_sem, out_sem, send, recv, s_sem = refs[10:14], refs[14:18], refs[18], refs[19], refs[20], refs[21], refs[22]
    c = lax.axis_index("shard")
    core = {"shard": 1 - c}
    barrier = pltpu.get_barrier_semaphore()
    pl.semaphore_signal(barrier, inc=1, device_id=core, device_id_type=MESH)
    pieces = []
    for m, (rows, _) in enumerate(dims):
        for row in range(0, rows, steps[m]):
            pieces.append((m, row))

    def read(index):
        m, row = pieces[index]
        part = pl.ds(row, steps[m])
        return pltpu.make_async_copy(weights[m].at[part, :], wide[m].at[part, :], in_sem.at[index])

    def keep(index):
        m, row = pieces[index]
        own = pl.ds(pl.multiple_of(c * dims[m][0] + row, steps[m]), steps[m])
        return pltpu.make_async_copy(low[m].at[pl.ds(row, steps[m]), :], wholes[m].at[own, :], out_sem.at[index])

    def give(index):
        m, row = pieces[index]
        own = pl.ds(pl.multiple_of(c * dims[m][0] + row, steps[m]), steps[m])
        return pltpu.make_async_remote_copy(
            src_ref=low[m].at[pl.ds(row, steps[m]), :], dst_ref=wholes[m].at[own, :],
            send_sem=send.at[index], recv_sem=recv.at[index], device_id=core, device_id_type=MESH,
        )

    for index in range(len(pieces)):
        read(index).start()
    small_out[c] = small[...]
    pl.semaphore_wait(barrier, 1)
    small_copy = pltpu.make_async_remote_copy(
        src_ref=small, dst_ref=small_out.at[c], send_sem=s_sem.at[0], recv_sem=s_sem.at[1],
        device_id=core, device_id_type=MESH,
    )
    small_copy.start()
    for index, (m, row) in enumerate(pieces):
        read(index).wait()

        def convert(block, _):
            part = pl.ds(pl.multiple_of(row + block * 16, 16), 16)
            low[m][part, :] = wide[m][part, :].astype(BF16)
            return 0

        lax.fori_loop(0, steps[m] // 16, convert, 0)
        keep(index).start()
        give(index).start()
    for index in range(len(pieces)):
        keep(index).wait()
        give(index).wait()
    small_copy.wait()


def spread_weights(weights, small):
    dims = [w.shape for w in weights]
    steps = [piece_rows(rows, cols) for rows, cols in dims]
    count = sum(rows // step for (rows, _), step in zip(dims, steps))
    hbm = pl.BlockSpec(memory_space=pl.ANY)
    vmem = pl.BlockSpec(memory_space=pltpu.VMEM)
    dma = pltpu.SemaphoreType.DMA
    return pl.pallas_call(
        functools.partial(spread_kernel, dims, steps),
        out_shape=[jax.ShapeDtypeStruct((2 * rows, cols), BF16) for rows, cols in dims]
        + [jax.ShapeDtypeStruct((2,) + small.shape, BF16)],
        in_specs=[hbm] * 4 + [vmem],
        out_specs=[hbm] * 4 + [vmem],
        scratch_shapes=[pltpu.VMEM(d, F32) for d in dims]
        + [pltpu.VMEM(d, BF16) for d in dims]
        + [dma((count,)), dma((count,)), dma((count,)), dma((count,)), dma((2,))],
        compiler_params=pltpu.CompilerParams(collective_id=0, has_side_effects=True, vmem_limit_bytes=56 * MIB),
        name="spread_weights",
    )(*weights, small)


def pack_halves(parts, dtype):
    flat = []
    for part in parts:
        if part.ndim == 2:
            halves = part.reshape(part.shape[0], 2, -1).swapaxes(0, 1).reshape(2, -1)
        else:
            halves = part.reshape(2, -1)
        flat.append(jnp.pad(halves.astype(dtype), ((0, 0), (0, -halves.shape[1] % 128))))
    rows = jnp.concatenate(flat, axis=1)
    rows = jnp.pad(rows, ((0, 0), (0, -rows.shape[1] % 4096)))
    return rows.reshape(2, -1, 128)


def unpack_half(rows, shapes):
    flat, at, parts = rows.reshape(-1), 0, []
    for shape in shapes:
        size = 1
        for n in shape:
            size *= n
        parts.append(flat[at : at + size].reshape(shape))
        at += size + -size % 128
    return parts


def pack_own(parts, dtype):
    flat = [jnp.pad(p.reshape(-1).astype(dtype), (0, -p.size % 128)) for p in parts]
    rows = jnp.concatenate(flat)
    return jnp.pad(rows, (0, -rows.shape[0] % 4096)).reshape(-1, 128)


def on_pair_of_cores(
    layer_input, cotangent, w_qkv, qv_bias, w_out, out_bias, head_scale, ln1_gain, ln1_bias, ln2_gain, ln2_bias,
    ln3_gain, ln3_bias, w_fc1, fc1_bias, ln4_gain, ln4_bias, w_fc2, fc2_bias,
):
    smalls = (
        qv_bias, out_bias, head_scale, ln1_gain, ln1_bias, ln2_gain, ln2_bias, ln3_gain, ln3_bias, fc1_bias,
        ln4_gain, ln4_bias, fc2_bias,
    )
    shapes = [s.shape for s in smalls]
    weights = (w_qkv, w_out, w_fc1, w_fc2)
    dims = tuple(w.shape for w in weights)
    *wholes, both = spread_weights(weights, pack_own(smalls, jnp.bfloat16))
    weight_qkv, weight_out, weight_up, weight_down = wholes
    halves = [unpack_half(both[k], shapes) for k in range(2)]
    (
        bias_qv, bias_out, head_gain, gain_one, shift_one, gain_two, shift_two, gain_three, shift_three, bias_up,
        gain_four, shift_four, bias_down,
    ) = [jnp.concatenate([a, b], axis=-1).astype(jnp.float32) for a, b in zip(*halves)]
    length = layer_input.shape[0]
    scale = HEAD_DIM ** (-0.5)
    inputs = layer_input.astype(jnp.float32)
    normed_one, pull_one = jax.vjp(norm_rows, inputs, gain_one, shift_one)
    act_one = normed_one.astype(jnp.bfloat16)
    bias_full = jnp.concatenate([bias_qv[0], jnp.zeros((D,), jnp.float32), bias_qv[1]])
    qkv = (jnp.dot(act_one, weight_qkv, preferred_element_type=jnp.float32) + bias_full).astype(
        jnp.bfloat16
    )
    triple = qkv.reshape(length, 3, HEADS, HEAD_DIM)
    queries = triple[:, 0]
    keys_all = triple[:, 1]
    values_all = triple[:, 2]
    attended, totals = attend_forward(queries, keys_all, values_all, scale)
    mixed = (attended * head_gain[:, None]).reshape(length, D).astype(jnp.bfloat16)
    branch = jnp.dot(mixed, weight_out, preferred_element_type=jnp.float32) + bias_out
    normed_two, pull_two = jax.vjp(norm_rows, branch, gain_two, shift_two)
    middle = inputs + normed_two
    normed_three, pull_three = jax.vjp(norm_rows, middle, gain_three, shift_three)
    act_three = normed_three.astype(jnp.bfloat16)
    hidden = jnp.dot(act_three, weight_up, preferred_element_type=jnp.float32) + bias_up
    normed_four, pull_four = jax.vjp(ffn_middle, hidden, gain_four, shift_four)
    act_four = normed_four.astype(jnp.bfloat16)
    result = middle + (
        jnp.dot(act_four, weight_down, preferred_element_type=jnp.float32) + bias_down
    )
    output = result.astype(jnp.bfloat16)
    cot_full = cotangent.astype(jnp.float32)
    grad_down_bias = jnp.sum(cot_full, axis=0)
    grad_four = jnp.einsum("td,fd->tf", cotangent, weight_down, preferred_element_type=jnp.float32)
    grad_hidden, grad_gain_four, grad_shift_four = pull_four(grad_four)
    hidden_low = grad_hidden.astype(jnp.bfloat16)
    grad_up_bias = jnp.sum(hidden_low, axis=0, dtype=jnp.float32)
    grad_three = jnp.einsum("tf,df->td", hidden_low, weight_up, preferred_element_type=jnp.float32)
    grad_mid_part, grad_gain_three, grad_shift_three = pull_three(grad_three)
    grad_middle = cot_full + grad_mid_part
    grad_branch, grad_gain_two, grad_shift_two = pull_two(grad_middle)
    branch_low = grad_branch.astype(jnp.bfloat16)
    grad_out_b = jnp.sum(branch_low, axis=0, dtype=jnp.float32)
    grad_mixed = jnp.einsum("te,de->td", branch_low, weight_out, preferred_element_type=jnp.float32)
    grad_mixed = grad_mixed.reshape(length, HEADS, HEAD_DIM)
    grad_heads = jnp.sum(grad_mixed * attended, axis=(0, 2))
    grad_attended = (grad_mixed * head_gain[:, None]).astype(jnp.bfloat16)
    grad_queries, grad_keys, grad_values = attend_backward(
        queries, keys_all, values_all, totals, grad_attended, scale
    )
    grad_qkv = (
        jnp.stack([grad_queries, grad_keys, grad_values], axis=1)
        .reshape(length, 3 * D)
        .astype(jnp.bfloat16)
    )
    grad_qv = jnp.stack(
        [
            jnp.sum(grad_qkv[:, :D], axis=0, dtype=jnp.float32),
            jnp.sum(grad_qkv[:, 2 * D :], axis=0, dtype=jnp.float32),
        ]
    )
    grad_one = jnp.einsum("te,de->td", grad_qkv, weight_qkv, preferred_element_type=jnp.float32)
    grad_in_part, grad_gain_one, grad_shift_one = pull_one(grad_one)
    grad_input = grad_middle + grad_in_part
    vec = pack_halves(
        (
            grad_qv, grad_out_b, grad_heads, grad_gain_one, grad_shift_one, grad_gain_two, grad_shift_two,
            grad_gain_three, grad_shift_three, grad_up_bias, grad_gain_four, grad_shift_four, grad_down_bias,
        ),
        jnp.float32,
    )
    lefts = (act_one.T, mixed.T, act_three.T, act_four.T)
    rights = (grad_qkv, branch_low, hidden_low, cotangent)
    *sums, vec_sum = sum_over_replicas(lefts, rights, vec, dims)
    sums = [s.astype(jnp.float32) for s in sums]
    (
        sum_qv, sum_out_b, sum_heads, sum_g1, sum_b1, sum_g2, sum_b2, sum_g3, sum_b3, sum_up, sum_g4, sum_b4, sum_down,
    ) = unpack_half(vec_sum, shapes)
    return (
        output, grad_input, sums[0], sum_qv, sums[1], sum_out_b, sum_heads, sum_g1, sum_b1, sum_g2, sum_b2, sum_g3,
        sum_b3, sums[2], sum_up, sum_g4, sum_b4, sums[3], sum_down,
    )


def fits_pair(mesh):
    return mesh.shape["shard"] == 2 and mesh.shape["rep"] == 16


def solution(mesh):
    return jax.shard_map(
        on_pair_of_cores if fits_pair(mesh) else on_any_mesh,
        mesh=mesh,
        in_specs=(
            P(("rep", "shard"), None),
            P(("rep", "shard"), None),
            P("shard", None),
            P(None, "shard"),
            P("shard", None),
            P("shard"),
            P("shard"),
            P("shard"),
            P("shard"),
            P("shard"),
            P("shard"),
            P("shard"),
            P("shard"),
            P("shard", None),
            P("shard"),
            P("shard"),
            P("shard"),
            P("shard", None),
            P("shard"),
        ),
        out_specs=(
            P(("rep", "shard"), None),
            P(("rep", "shard"), None),
            P("shard", None),
            P(None, "shard"),
            P("shard", None),
            P("shard"),
            P("shard"),
            P("shard"),
            P("shard"),
            P("shard"),
            P("shard"),
            P("shard"),
            P("shard"),
            P("shard", None),
            P("shard"),
            P("shard"),
            P("shard"),
            P("shard", None),
            P("shard"),
        ),
        check_vma=False,
    )
```

```python
import functools

import jax
import jax.numpy as jnp
from jax import lax
from jax.experimental import pallas as pl
from jax.experimental.pallas import tpu as pltpu
from jax.sharding import PartitionSpec as P

D = 1024
HEADS = 16
HEAD_DIM = 64


EPS = 1e-05
NEG = -1e30


def norm_rows(v, gain, bias):
    centre = jnp.mean(v, axis=-1, keepdims=True)
    centred = v - centre
    spread = jnp.mean(centred * centred, axis=-1, keepdims=True)
    return centred * lax.rsqrt(spread + EPS) * gain + bias


def ffn_middle(hidden, gain, bias):
    return norm_rows(jax.nn.gelu(hidden, approximate=False), gain, bias)


def causal_mask(index, qblock, length):
    rows = index * qblock + lax.iota(jnp.int32, qblock)
    cols = lax.iota(jnp.int32, length)
    return (cols[None, :] <= rows[:, None])[None]


def block_scores(queries, keys_all, index, qblock, scale):
    length = keys_all.shape[0]
    scores = (
        jnp.einsum("qhd,khd->hqk", queries, keys_all, preferred_element_type=jnp.float32) * scale
    )
    return (queries, jnp.where(causal_mask(index, qblock, length), scores, NEG))


def attend_forward(queries, keys_all, values_all, scale):
    length, heads, width = queries.shape
    qblock = min(512, length)
    blocks = length // qblock

    def one_block(index):
        rows_q, scores = block_scores(queries, keys_all, index, qblock, scale)
        total = jax.nn.logsumexp(scores, axis=-1, keepdims=True)
        probs = jnp.exp(scores - total).astype(jnp.bfloat16)
        outcome = jnp.einsum("hqk,khd->qhd", probs, values_all, preferred_element_type=jnp.float32)
        return (outcome, total)

    outcome, totals = lax.map(one_block, jnp.arange(blocks, dtype=jnp.int32))
    return (outcome.reshape(length, heads, width), totals)


def attend_backward(queries, keys_all, values_all, totals, grad_out, scale):
    length, heads, width = queries.shape
    qblock = min(512, length)
    blocks = length // qblock

    def one_block(carry, index):
        grad_keys, grad_values = carry
        rows_q, scores = block_scores(queries, keys_all, index, qblock, scale)
        probs = jnp.exp(scores - totals[index])
        probs_low = probs.astype(jnp.bfloat16)
        grad_values = grad_values + jnp.einsum(
            "hqk,qhd->khd", probs_low, grad_out, preferred_element_type=jnp.float32
        )
        grad_probs = jnp.einsum(
            "qhd,khd->hqk", grad_out, values_all, preferred_element_type=jnp.float32
        )
        row_dot = jnp.sum(probs * grad_probs, axis=-1, keepdims=True)
        grad_scores = (probs * (grad_probs - row_dot)).astype(jnp.bfloat16)
        grad_rows = (
            jnp.einsum("hqk,khd->qhd", grad_scores, keys_all, preferred_element_type=jnp.float32)
            * scale
        )
        grad_keys = (
            grad_keys
            + jnp.einsum("hqk,qhd->khd", grad_scores, rows_q, preferred_element_type=jnp.float32)
            * scale
        )
        return ((grad_keys, grad_values), grad_rows)

    empty = jnp.zeros((length, heads, width), jnp.float32)
    (grad_keys, grad_values), grad_queries = lax.scan(
        one_block, (empty, empty), jnp.arange(blocks, dtype=jnp.int32)
    )
    return (grad_queries.reshape(length, heads, width), grad_keys, grad_values)


def on_any_mesh(
    layer_input,
    cotangent,
    w_qkv,
    qv_bias,
    w_out,
    out_bias,
    head_scale,
    ln1_gain,
    ln1_bias,
    ln2_gain,
    ln2_bias,
    ln3_gain,
    ln3_bias,
    w_fc1,
    fc1_bias,
    ln4_gain,
    ln4_bias,
    w_fc2,
    fc2_bias,
):
    low_qkv = w_qkv.astype(jnp.bfloat16)
    low_out = w_out.astype(jnp.bfloat16)
    low_heads = head_scale.astype(jnp.bfloat16)
    low_up = w_fc1.astype(jnp.bfloat16)
    low_down = w_fc2.astype(jnp.bfloat16)
    whole = (
        lax.all_gather(low_qkv, "shard", axis=0, tiled=True),
        lax.all_gather(qv_bias.astype(jnp.bfloat16), "shard", axis=1, tiled=True),
        lax.all_gather(low_out, "shard", axis=0, tiled=True),
        lax.all_gather(out_bias.astype(jnp.bfloat16), "shard", axis=0, tiled=True),
        lax.all_gather(low_heads, "shard", axis=0, tiled=True),
        lax.all_gather(ln1_gain.astype(jnp.bfloat16), "shard", axis=0, tiled=True),
        lax.all_gather(ln1_bias.astype(jnp.bfloat16), "shard", axis=0, tiled=True),
        lax.all_gather(ln2_gain.astype(jnp.bfloat16), "shard", axis=0, tiled=True),
        lax.all_gather(ln2_bias.astype(jnp.bfloat16), "shard", axis=0, tiled=True),
        lax.all_gather(ln3_gain.astype(jnp.bfloat16), "shard", axis=0, tiled=True),
        lax.all_gather(ln3_bias.astype(jnp.bfloat16), "shard", axis=0, tiled=True),
        lax.all_gather(low_up, "shard", axis=0, tiled=True),
        lax.all_gather(fc1_bias.astype(jnp.bfloat16), "shard", axis=0, tiled=True),
        lax.all_gather(ln4_gain.astype(jnp.bfloat16), "shard", axis=0, tiled=True),
        lax.all_gather(ln4_bias.astype(jnp.bfloat16), "shard", axis=0, tiled=True),
        lax.all_gather(low_down, "shard", axis=0, tiled=True),
        lax.all_gather(fc2_bias.astype(jnp.bfloat16), "shard", axis=0, tiled=True),
    )
    weight_qkv, weight_out, weight_up, weight_down = (whole[0], whole[2], whole[11], whole[15])
    (
        bias_qv,
        bias_out,
        head_gain,
        gain_one,
        shift_one,
        gain_two,
        shift_two,
        gain_three,
        shift_three,
        bias_up,
        gain_four,
        shift_four,
        bias_down,
    ) = tuple(
        (whole[index].astype(jnp.float32) for index in (1, 3, 4, 5, 6, 7, 8, 9, 10, 12, 13, 14, 16))
    )
    length = layer_input.shape[0]
    scale = HEAD_DIM ** (-0.5)
    inputs = layer_input.astype(jnp.float32)
    normed_one, pull_one = jax.vjp(norm_rows, inputs, gain_one, shift_one)
    act_one = normed_one.astype(jnp.bfloat16)
    bias_full = jnp.concatenate([bias_qv[0], jnp.zeros((D,), jnp.float32), bias_qv[1]])
    qkv = (jnp.dot(act_one, weight_qkv, preferred_element_type=jnp.float32) + bias_full).astype(
        jnp.bfloat16
    )
    triple = qkv.reshape(length, 3, HEADS, HEAD_DIM)
    queries = triple[:, 0]
    keys_all = triple[:, 1]
    values_all = triple[:, 2]
    attended, totals = attend_forward(queries, keys_all, values_all, scale)
    mixed = (attended * head_gain[:, None]).reshape(length, D).astype(jnp.bfloat16)
    branch = jnp.dot(mixed, weight_out, preferred_element_type=jnp.float32) + bias_out
    normed_two, pull_two = jax.vjp(norm_rows, branch, gain_two, shift_two)
    middle = inputs + normed_two
    normed_three, pull_three = jax.vjp(norm_rows, middle, gain_three, shift_three)
    act_three = normed_three.astype(jnp.bfloat16)
    hidden = jnp.dot(act_three, weight_up, preferred_element_type=jnp.float32) + bias_up
    normed_four, pull_four = jax.vjp(ffn_middle, hidden, gain_four, shift_four)
    act_four = normed_four.astype(jnp.bfloat16)
    result = middle + (
        jnp.dot(act_four, weight_down, preferred_element_type=jnp.float32) + bias_down
    )
    output = result.astype(jnp.bfloat16)
    again = (
        lax.all_gather(low_qkv, "shard", axis=0, tiled=True),
        lax.all_gather(low_out, "shard", axis=0, tiled=True),
        lax.all_gather(low_heads, "shard", axis=0, tiled=True),
        lax.all_gather(low_up, "shard", axis=0, tiled=True),
        lax.all_gather(low_down, "shard", axis=0, tiled=True),
    )
    back_qkv, back_out, back_up, back_down = (again[0], again[1], again[3], again[4])
    back_heads = again[2].astype(jnp.float32)
    cot_full = cotangent.astype(jnp.float32)
    grad_down_bias = jnp.sum(cot_full, axis=0)
    grad_down = jnp.einsum("tf,td->fd", act_four, cotangent, preferred_element_type=jnp.float32)
    grad_four = jnp.einsum("td,fd->tf", cotangent, back_down, preferred_element_type=jnp.float32)
    grad_hidden, grad_gain_four, grad_shift_four = pull_four(grad_four)
    hidden_low = grad_hidden.astype(jnp.bfloat16)
    grad_up_bias = jnp.sum(hidden_low, axis=0, dtype=jnp.float32)
    grad_up = jnp.einsum("td,tf->df", act_three, hidden_low, preferred_element_type=jnp.float32)
    grad_three = jnp.einsum("tf,df->td", hidden_low, back_up, preferred_element_type=jnp.float32)
    grad_mid_part, grad_gain_three, grad_shift_three = pull_three(grad_three)
    grad_middle = cot_full + grad_mid_part
    grad_branch, grad_gain_two, grad_shift_two = pull_two(grad_middle)
    branch_low = grad_branch.astype(jnp.bfloat16)
    grad_out_b = jnp.sum(branch_low, axis=0, dtype=jnp.float32)
    grad_out_w = jnp.einsum("td,te->de", mixed, branch_low, preferred_element_type=jnp.float32)
    grad_mixed = jnp.einsum("te,de->td", branch_low, back_out, preferred_element_type=jnp.float32)
    grad_mixed = grad_mixed.reshape(length, HEADS, HEAD_DIM)
    grad_heads = jnp.sum(grad_mixed * attended, axis=(0, 2))
    grad_attended = (grad_mixed * back_heads[:, None]).astype(jnp.bfloat16)
    grad_queries, grad_keys, grad_values = attend_backward(
        queries, keys_all, values_all, totals, grad_attended, scale
    )
    grad_qkv = (
        jnp.stack([grad_queries, grad_keys, grad_values], axis=1)
        .reshape(length, 3 * D)
        .astype(jnp.bfloat16)
    )
    grad_qv = jnp.stack(
        [
            jnp.sum(grad_qkv[:, :D], axis=0, dtype=jnp.float32),
            jnp.sum(grad_qkv[:, 2 * D :], axis=0, dtype=jnp.float32),
        ]
    )
    grad_qkv_w = jnp.einsum("td,te->de", act_one, grad_qkv, preferred_element_type=jnp.float32)
    grad_one = jnp.einsum("te,de->td", grad_qkv, back_qkv, preferred_element_type=jnp.float32)
    grad_in_part, grad_gain_one, grad_shift_one = pull_one(grad_one)
    grad_input = grad_middle + grad_in_part
    shares = (
        lax.psum_scatter(grad_qkv_w, "shard", scatter_dimension=0, tiled=True),
        lax.psum_scatter(grad_qv, "shard", scatter_dimension=1, tiled=True),
        lax.psum_scatter(grad_out_w, "shard", scatter_dimension=0, tiled=True),
        lax.psum_scatter(grad_out_b, "shard", scatter_dimension=0, tiled=True),
        lax.psum_scatter(grad_heads, "shard", scatter_dimension=0, tiled=True),
        lax.psum_scatter(grad_gain_one, "shard", scatter_dimension=0, tiled=True),
        lax.psum_scatter(grad_shift_one, "shard", scatter_dimension=0, tiled=True),
        lax.psum_scatter(grad_gain_two, "shard", scatter_dimension=0, tiled=True),
        lax.psum_scatter(grad_shift_two, "shard", scatter_dimension=0, tiled=True),
        lax.psum_scatter(grad_gain_three, "shard", scatter_dimension=0, tiled=True),
        lax.psum_scatter(grad_shift_three, "shard", scatter_dimension=0, tiled=True),
        lax.psum_scatter(grad_up, "shard", scatter_dimension=0, tiled=True),
        lax.psum_scatter(grad_up_bias, "shard", scatter_dimension=0, tiled=True),
        lax.psum_scatter(grad_gain_four, "shard", scatter_dimension=0, tiled=True),
        lax.psum_scatter(grad_shift_four, "shard", scatter_dimension=0, tiled=True),
        lax.psum_scatter(grad_down, "shard", scatter_dimension=0, tiled=True),
        lax.psum_scatter(grad_down_bias, "shard", scatter_dimension=0, tiled=True),
    )
    summed = lax.psum(
        (
            shares[0],
            shares[1],
            shares[2],
            shares[3],
            shares[4],
            shares[5],
            shares[6],
            shares[7],
            shares[8],
            shares[9],
            shares[10],
            shares[11],
            shares[12],
            shares[13],
            shares[14],
            shares[15],
            shares[16],
        ),
        "rep",
    )
    return (output, grad_input) + tuple(summed)


MESH = pl.DeviceIdType.MESH
BF16 = jnp.bfloat16
F32 = jnp.float32
UNIT_ROWS = 256
UNIT_COLS = 1024
MIB = 1 << 20
COMMS = ("d1", "d2", "z1", "z2", "z3", "u1", "w1", "u2", "w2", "u3", "w3", "g1", "g2")
SLOT = {name: index for index, name in enumerate(COMMS)}


def unit_table(dims):
    table = []
    for matrix in (3, 2, 1, 0):
        rows, cols = dims[matrix]
        for col in range(0, cols, UNIT_COLS):
            for row in range(0, rows, UNIT_ROWS):
                table.append((matrix, row, col))
    return table


def kinds_of(count):
    kinds, lines = [], 0
    for index in range(count):
        kind = "XYXYZ"[index % 5]
        if kind == "Z":
            kind = ("ZX", "ZY")[lines % 2]
            lines += 1
        kinds.append(kind)
    return kinds


def task_order(kinds):
    keys = []
    for unit, kind in enumerate(kinds):
        offsets = Z_OFFSETS if kind[0] == "Z" else XY_OFFSETS
        for step, offset in enumerate(offsets):
            keys.append((unit + offset, unit, step))
    keys.sort()
    return [(unit, step) for _, unit, step in keys]


XY_OFFSETS = (0, 3.5, 7.0, 11.5, 14.5, 17.5, 21.0, 23.0, 25.0, 27.5, 30.5)
Z_OFFSETS = (0.0, 4.5, 7.0, 10.0, 13.0, 16.5, 19.0, 23.0, 25.0, 28.0, 32.5)


GIVE_ROWS = 240


def program_order(units, kinds, costs, ends):
    steps = task_order(kinds)
    order, task, waited, left = [], 0, {3}, len(costs)
    order.append(("wait", 3, 0))
    vec_at = None
    for index, (unit, step) in enumerate(steps):
        m = units[unit][0]
        if m not in waited:
            while task < ends[m]:
                order.append(("task", task, 0))
                task += 1
            order.append(("wait", m, 0))
            waited.add(m)
        order.append(("sum", unit, step))
        if index >= 6 and task < len(costs):
            order.append(("task", task, 0))
            task += 1
            if task == len(costs):
                vec_at = {index + 6 + 8 * k: k for k in range(5)}
        if vec_at and index in vec_at:
            order.append(("vec", vec_at[index], 0))
    return order


EPS_TILE = 32


def fold(v):
    total = v[0:8]
    for k in range(1, v.shape[0] // 8):
        total = total + v[8 * k : 8 * k + 8]
    return total


def layer_kernel(dims, at_base, g_base, *refs):
    x_in, cot_in, weights, params = refs[0], refs[1], refs[2:6], refs[6:19]
    y_out, dx_out, outs, vec_out, tiles_hbm = refs[19], refs[20], refs[21:25], refs[25], refs[26]
    (
        at, g, res, give, pair, line_xy, line_z, ring, big, left, act, hid, qkv, probs, attended, branch, middle, dmid,
        vec_w, vec_h, rstd4, sums4, vec_in, vec_own, vec_got,
        send, recv, v_send, v_recv, p_send, p_recv, l_sem, o_sem, w_in, w_keep, w_send, w_recv, t_sem, s_sem, e_sem,
    ) = refs[27:]
    r = lax.axis_index("rep")
    c = lax.axis_index("shard")
    x, y, z = r % 2, (r // 2) % 2, r // 4
    core = {"shard": 1 - c}
    to = {
        "X": {"rep": r + 1 - 2 * x},
        "Y": {"rep": r + 2 - 4 * y},
        "U": {"rep": r + 4},
        "D": {"rep": r - 4},
    }
    line_end = (z == 0) | (z == 3)
    line_mid = (z == 1) | (z == 2)
    outward = {"rep": r + 4 * (2 * (z // 2) - 1)}
    inward = {"rep": r + 4 * (1 - 2 * (z // 2))}
    across = {"rep": r + 4 * (3 - 2 * z)}
    upper = z // 2
    length = x_in.shape[0]
    width = x_in.shape[1]
    half_w = width // 2
    hidden = dims[2][1]
    half_h = hidden // 2
    blocks = hidden // width
    TILE = 512

    tile_of = []
    for m, (rows, cols) in enumerate(dims):
        for row in range(0, rows, TILE):
            for col in range(0, cols, UNIT_COLS):
                tile_of.append((m, row, col))
    first_tile = [min(t for t, v in enumerate(tile_of) if v[0] == m) for m in range(4)]
    parts = 2 * len(tile_of)
    slots_f, slots_b = 6, 16

    def part_read(i):
        m, row, col = tile_of[i // 2]
        return pltpu.make_async_copy(
            weights[m].at[pl.ds(row + (i % 2) * 256, 256), pl.ds(col, UNIT_COLS)],
            big.at[pl.ds((i % slots_f) * 256, 256), :],
            w_in.at[i],
        )

    def part_low(i):
        return low_buf.at[pl.ds((i % slots_b) * 256, 256), :]

    low_buf = give

    def part_place(i):
        return tiles_hbm.at[c, i // 2, pl.ds((i % 2) * 256, 256), :]

    def part_keep(i):
        return pltpu.make_async_copy(part_low(i), part_place(i), w_keep.at[i])

    def part_give(i):
        return pltpu.make_async_remote_copy(
            src_ref=part_low(i), dst_ref=part_place(i), send_sem=w_send.at[i], recv_sem=w_recv.at[i],
            device_id=core, device_id_type=MESH,
        )

    def part_got(i):
        return pltpu.make_async_remote_copy(
            src_ref=part_low(i), dst_ref=tiles_hbm.at[1 - c, i // 2, pl.ds((i % 2) * 256, 256), :],
            send_sem=w_send.at[i], recv_sem=w_recv.at[i], device_id=core, device_id_type=MESH,
        )

    for i in range(slots_f):
        part_read(i).start()

    barrier = pltpu.get_barrier_semaphore()
    for peer in (core, to["X"], to["Y"]):
        pl.semaphore_signal(barrier, inc=1, device_id=peer, device_id_type=MESH)

    @pl.when(z < 3)
    def _():
        pl.semaphore_signal(barrier, inc=1, device_id=to["U"], device_id_type=MESH)

    @pl.when(z > 0)
    def _():
        pl.semaphore_signal(barrier, inc=1, device_id=to["D"], device_id_type=MESH)

    @pl.when(line_end)
    def _():
        pl.semaphore_signal(barrier, inc=1, device_id=across, device_id_type=MESH)

    narrow = (0, 0, 2, 3, 4, 5, 6, 7, 8, 9, 10)

    def rounded(v):
        return v.astype(BF16).astype(F32)

    lane_w = pl.ds(pl.multiple_of(c * half_w, half_w), half_w)
    lane_h = pl.ds(pl.multiple_of(c * half_h, half_h), half_h)
    (qv_ref, ob_ref, hs_ref, g1_ref, b1_ref, g2_ref, b2_ref, g3_ref, b3_ref, ub_ref, g4_ref, b4_ref, db_ref) = params
    vec_w[0:2, lane_w] = rounded(qv_ref[...])
    for row, ref in zip(range(2, 11), (ob_ref, hs_ref, g1_ref, b1_ref, g2_ref, b2_ref, g3_ref, b3_ref, db_ref)):
        vec_w[row : row + 1, lane_w] = rounded(ref[...])
    for row, ref in enumerate((ub_ref, g4_ref, b4_ref)):
        vec_h[row : row + 1, lane_h] = rounded(ref[...])
    QB, VB, OB, HS, G1, B1, G2, B2, G3, B3, DB = range(11)
    UB, G4, B4 = range(3)

    def small_copy(k, give_it):
        ref, lane, far = ((vec_w, lane_w, 1 - c), (vec_h, lane_h, 1 - c))[k]
        size = half_w if k == 0 else half_h
        other = pl.ds(pl.multiple_of((1 - c) * size, size), size)
        here = ref.at[:, lane]
        return pltpu.make_async_remote_copy(
            src_ref=here, dst_ref=here if give_it else ref.at[:, other], send_sem=s_sem.at[k, 0], recv_sem=s_sem.at[k, 1],
            device_id=core, device_id_type=MESH,
        )

    e_copy = pltpu.make_async_copy(cot_in, g.at[pl.ds(0, length), pl.ds(g_base[3], width)], e_sem.at[0])
    e_copy.start()
    e_copy.wait()
    pl.semaphore_wait(barrier, 5)
    small_copy(0, True).start()
    small_copy(1, True).start()

    def left_own(m):
        rows = dims[m][0]
        return pltpu.make_async_copy(
            left.at[pl.ds(pl.multiple_of(2 * at_base[m] + c * rows, 512), rows), :],
            at.at[pl.ds(at_base[m], rows), pl.ds(0, length)],
            l_sem.at[m],
        )

    def left_far(m):
        rows = dims[m][0]
        return pltpu.make_async_remote_copy(
            src_ref=left.at[pl.ds(pl.multiple_of(2 * at_base[m] + (1 - c) * rows, 512), rows), :],
            dst_ref=at.at[pl.ds(at_base[m], rows), pl.ds(length, length)],
            send_sem=p_send.at[m, 0], recv_sem=p_recv.at[m, 0], device_id=core, device_id_type=MESH,
        )

    def right_far(m):
        cols = pl.ds(g_base[m], dims[m][1])
        return pltpu.make_async_remote_copy(
            src_ref=g.at[pl.ds(0, length), cols], dst_ref=g.at[pl.ds(length, length), cols],
            send_sem=p_send.at[m, 1], recv_sem=p_recv.at[m, 1], device_id=core, device_id_type=MESH,
        )

    right_far(3).start()

    def start_left(m):
        left_own(m).start()
        left_far(m).start()

    def wait_pair(m):
        left_own(m).wait()
        left_far(m).wait()
        right_far(m).wait()

    for i in range(parts):
        part_read(i).wait()
        if i >= slots_b:
            part_keep(i - slots_b).wait()
            part_give(i - slots_b).wait_send()

        def convert(b, _, i=i):
            rows = pl.multiple_of((i % slots_f) * 256 + b * 32, 32)
            low = pl.multiple_of((i % slots_b) * 256 + b * 32, 32)
            low_buf[pl.ds(low, 32), :] = big[pl.ds(rows, 32), :].astype(BF16)
            return 0

        lax.fori_loop(0, 8, convert, 0)
        part_keep(i).start()
        part_give(i).start()
        if i + slots_f < parts:
            part_read(i + slots_f).start()

    def tile(m, half, index):
        return (half, first_tile[m] + index)

    stream = []
    for m in (0, 1, 2):
        for index in range(dims[m][1] // UNIT_COLS):
            stream += [tile(m, 0, index), tile(m, 1, index)]
    per_half = dims[3][0] // TILE
    stream += [tile(3, h, k) for h in range(2) for k in range(per_half)]
    for m in (2, 1, 0):
        for index in range(dims[m][1] // UNIT_COLS):
            stream += [tile(m, 0, index), tile(m, 1, index)]
    slots_t = 4
    here = set()

    def tile_load(i):
        half, t = stream[i]
        return pltpu.make_async_copy(
            tiles_hbm.at[half, t], ring.at[i % slots_t], t_sem.at[i % slots_t]
        )

    def tile_start(i):
        half, t = stream[i]
        if (1, t) not in here:
            here.add((1, t))
            for k in (2 * t, 2 * t + 1):
                if k + slots_b >= parts:
                    part_keep(k).wait()
                    part_give(k).wait_send()
                part_got(k).wait_recv()
        tile_load(i).start()

    at_tile = [0]

    def next_tile():
        i = at_tile[0]
        tile_load(i).wait()
        return ring.at[i % slots_t]

    def done_tile():
        i = at_tile[0]
        if i + slots_t < len(stream):
            tile_start(i + slots_t)
        at_tile[0] = i + 1

    def mean(v):
        return jnp.sum(v, axis=-1, keepdims=True) / v.shape[-1]

    def normal(v):
        centred = v - mean(v)
        scale = lax.rsqrt(mean(centred * centred) + 1e-05)
        return centred * scale, scale

    def each(fn, step=32, init=0):
        def body(i, carry):
            return fn(pl.ds(pl.multiple_of(i * step, step), step), carry)

        return lax.fori_loop(0, length // step, body, init)

    def w_row(i):
        return vec_w[i : i + 1, :]

    def turn(source, m, block=0):
        def body(k, _):
            cols = pl.ds(pl.multiple_of(k * 256, 256), 256)
            rows = pl.ds(pl.multiple_of(2 * at_base[m] + block * width + k * 256, 256), 256)
            left[rows, :] = jnp.transpose(source[:, cols])
            return 0

        lax.fori_loop(0, width // 256, body, 0)

    NT = (((1,), (1,)), ((), ()))
    TN = (((0,), (0,)), ((), ()))

    def nt(a, b):
        return lax.dot_general(a, b, NT, preferred_element_type=F32)

    def tn(a, b):
        return lax.dot_general(a, b, TN, preferred_element_type=F32)

    def product_pair(source, write):
        first = next_tile()
        i = at_tile[0]
        at_tile[0] = i + 1
        second = next_tile()
        at_tile[0] = i

        def body(k, _):
            cols = pl.ds(pl.multiple_of(k * 256, 256), 256)
            value = jnp.dot(source[:, 0:half_w], first[:, cols], preferred_element_type=F32)
            value = value + jnp.dot(source[:, half_w:width], second[:, cols], preferred_element_type=F32)
            write(cols, value)
            return 0

        lax.fori_loop(0, UNIT_COLS // 256, body, 0)
        done_tile()
        done_tile()

    for i in range(slots_t):
        tile_start(i)
    small_copy(0, True).wait_send()
    small_copy(1, True).wait_send()
    small_copy(0, False).wait_recv()
    small_copy(1, False).wait_recv()

    def first_norm(rows, _):
        hat, _s = normal(x_in[rows, :].astype(F32))
        act[rows, :] = (hat * w_row(G1) + w_row(B1)).astype(BF16)
        return 0

    each(first_norm)
    for index in range(3):

        def put_qkv(cols, value, index=index):
            start = pl.multiple_of(index * width + cols.start, 256)
            if index == 0:
                value = value + vec_w[QB : QB + 1, cols]
            if index == 2:
                value = value + vec_w[VB : VB + 1, cols]
            qkv[:, pl.ds(start, 256)] = value.astype(BF16)

        product_pair(act, put_qkv)
    turn(act, 0)
    start_left(0)

    low_lane = lax.broadcasted_iota(jnp.int32, (length, 128), 1) < 64
    allowed = lax.broadcasted_iota(jnp.int32, (length, length), 1) <= lax.broadcasted_iota(
        jnp.int32, (length, length), 0
    )
    scale = 64 ** (-0.5)
    keep_lane = (low_lane.astype(F32).astype(BF16), jnp.logical_not(low_lane).astype(F32).astype(BF16))

    def attend(p, _):
        q = qkv[:, pl.ds(pl.multiple_of(p * 128, 128), 128)]
        k = qkv[:, pl.ds(pl.multiple_of(width + p * 128, 128), 128)]
        v = qkv[:, pl.ds(pl.multiple_of(2 * width + p * 128, 128), 128)]
        got = []
        for h in range(2):
            own = q * keep_lane[h]
            scores = jnp.where(allowed, nt(own, k) * scale, -1e30)
            top = jnp.max(scores, axis=-1, keepdims=True)
            lse = top + jnp.log(jnp.sum(jnp.exp(scores - top), axis=-1, keepdims=True))
            prob = jnp.exp(scores - lse)
            probs[2 * p + h] = prob
            got.append(jnp.dot(prob.astype(BF16), v, preferred_element_type=F32))
        cols = pl.ds(pl.multiple_of(p * 128, 128), 128)
        value = jnp.where(low_lane, got[0], got[1])
        attended[:, cols] = value
        act[:, cols] = (value * vec_w[HS : HS + 1, cols]).astype(BF16)
        return 0

    lax.fori_loop(0, width // 128, attend, 0)

    def put_branch(cols, value):
        branch[:, cols] = value + vec_w[OB : OB + 1, cols]

    product_pair(act, put_branch)
    turn(act, 1)
    start_left(1)

    def second_norm(rows, _):
        hat, _s = normal(branch[rows, :])
        mid = x_in[rows, :].astype(F32) + (hat * w_row(G2) + w_row(B2))
        middle[rows, :] = mid
        hat, _s = normal(mid)
        act[rows, :] = (hat * w_row(G3) + w_row(B3)).astype(BF16)
        return 0

    each(second_norm)
    U0, H0, D0 = 0, blocks * length, 2 * blocks * length
    for j in range(blocks):

        def put_hidden(cols, value, j=j):
            start = pl.multiple_of(j * width + cols.start, 256)
            big[U0 + j * length : U0 + (j + 1) * length, cols] = value + vec_h[UB : UB + 1, pl.ds(start, 256)]

        product_pair(act, put_hidden)
    turn(act, 2)
    start_left(2)
    root_half = 0.7071067811865476

    def near(base, start):
        return pl.ds(pl.multiple_of(base + start, 16), 16)

    def hidden_norm(rows, _):
        total = jnp.zeros((16, 1), F32)
        for j in range(blocks):
            u = big[near(U0 + j * length, rows.start), :]
            h = u * (1.0 + lax.erf(u * root_half)) * 0.5
            big[near(H0 + j * length, rows.start), :] = h
            total = total + jnp.sum(h, axis=-1, keepdims=True)
        centre = total / hidden
        total = jnp.zeros((16, 1), F32)
        for j in range(blocks):
            h = big[near(H0 + j * length, rows.start), :] - centre
            total = total + jnp.sum(h * h, axis=-1, keepdims=True)
        s = lax.rsqrt(total / hidden + 1e-05)
        rstd4[rows, :] = jnp.broadcast_to(s, (16, 128))
        for j in range(blocks):
            at_h = near(H0 + j * length, rows.start)
            hat = (big[at_h, :] - centre) * s
            big[at_h, :] = hat
            cols = slice(j * width, (j + 1) * width)
            hid[near(j * length, rows.start), :] = (
                hat * vec_h[G4 : G4 + 1, cols] + vec_h[B4 : B4 + 1, cols]
            ).astype(BF16)
        return 0

    each(hidden_norm, 16)
    for j in range(blocks):
        turn(hid.at[pl.ds(j * length, length), :], 3, j)
    start_left(3)

    tasks = []
    zeros8 = jnp.zeros((8, width), F32)
    dirs = g.at[pl.ds(0, length), :]

    def put_sum(row, value):
        line = jnp.sum(value, axis=0, keepdims=True)
        vec_in[0, row : row + 1, :] = line[:, 0:half_w]
        vec_in[1, row : row + 1, :] = line[:, half_w:width]

    def task_down(h, k):
        def run():
            w = next_tile()
            row = h * dims[3][0] + k * TILE
            j, lane = row // width, row % width
            if h == 0 and k == 0:
                y_acc[...] = middle[...] + w_row(DB)
            for n in range(TILE // 256):
                big[D0 + j * length : D0 + (j + 1) * length, lane + n * 256 : lane + (n + 1) * 256] = nt(
                    dirs[:, g_base[3] : g_base[3] + width], w[n * 256 : (n + 1) * 256, :]
                )

            def body(n, _):
                cols = pl.ds(pl.multiple_of(n * 256, 256), 256)
                y_acc[:, cols] += jnp.dot(
                    hid[j * length : (j + 1) * length, lane : lane + TILE], w[:, cols], preferred_element_type=F32
                )
                return 0

            lax.fori_loop(0, width // 256, body, 0)
            done_tile()
            if h == 1 and k == per_half - 1:
                y_out[...] = y_acc[...].astype(BF16)

        return run

    y_acc = dmid
    for h in range(2):
        for k in range(per_half):
            tasks.append((1.2, task_down(h, k)))

    def task_hidden(first, count):
        def run():
            if first == 0:
                sums4[...] = jnp.zeros_like(sums4)

                def e_sum(rows, carry):
                    return carry + fold(dirs[rows, g_base[3] : g_base[3] + width].astype(F32))

                put_sum(DB, each(e_sum, 32, zeros8))

            def body(i, _):
                at_r = pl.multiple_of(first + i * 16, 16)
                one = jnp.zeros((16, 1), F32)
                two = jnp.zeros((16, 1), F32)
                for j in range(blocks):
                    gain = vec_h[G4 : G4 + 1, j * width : (j + 1) * width]
                    d = big[near(D0 + j * length, at_r), :] * gain
                    hat = big[near(H0 + j * length, at_r), :]
                    one = one + jnp.sum(d, axis=-1, keepdims=True)
                    two = two + jnp.sum(d * hat, axis=-1, keepdims=True)
                one, two = one / hidden, two / hidden
                s = rstd4[pl.ds(at_r, 16), 0:1]
                for j in range(blocks):
                    cols = slice(j * width, (j + 1) * width)
                    da = big[near(D0 + j * length, at_r), :]
                    hat = big[near(H0 + j * length, at_r), :]
                    u = big[near(U0 + j * length, at_r), :]
                    dh = s * (da * vec_h[G4 : G4 + 1, cols] - one - hat * two)
                    slope = 0.5 * (1.0 + lax.erf(u * root_half)) + u * (jnp.exp(u * u * -0.5) * 0.3989422804014327)
                    du = (dh * slope).astype(BF16)
                    g[pl.ds(at_r, 16), g_base[2] + j * width : g_base[2] + (j + 1) * width] = du
                    sums4[0:8, cols] += fold(du.astype(F32))
                    sums4[8:16, cols] += fold(da * hat)
                    sums4[16:24, cols] += fold(da)
                return 0

            lax.fori_loop(0, count // 16, body, 0)
            if first + count == length:
                for i in range(3):
                    line = jnp.sum(sums4[8 * i : 8 * i + 8, :], axis=0, keepdims=True)
                    for n in range(hidden // half_w):
                        hh, k = divmod(n, half_h // half_w)
                        vec_in[hh, 11 + 4 * i + k : 12 + 4 * i + k, :] = line[:, n * half_w : (n + 1) * half_w]
                right_far(2).start()

        return run

    for first in range(0, length, 32):
        tasks.append((3.0, task_hidden(first, 32)))

    def add_pair(acc, index_of, cols_of, count, width_to):
        def make(index):
            def run():
                for h in range(2):
                    w = next_tile()
                    for n in range(TILE // 256):
                        cols = slice(h * half_w + n * 256, h * half_w + (n + 1) * 256)
                        value = nt(dirs[:, cols_of(index)], w[n * 256 : (n + 1) * 256, :])
                        if index == 0:
                            acc[:, cols] = value
                        else:
                            acc[:, cols] += value
                    done_tile()

            return run

        return [(1.2, make(index)) for index in range(count)]

    ends = {2: len(tasks)}
    acc = big.at[pl.ds(U0, length), :]
    tasks += add_pair(acc, None, lambda j: slice(g_base[2] + j * width, g_base[2] + (j + 1) * width), blocks, width)

    def task_norms():
        def body(rows, carry):
            s3g, s3b, s2g, s2b, sob = carry
            da = acc[rows, :]
            hat, s = normal(middle[rows, :])
            d = da * w_row(G3)
            d_mid = dirs[rows, g_base[3] : g_base[3] + width].astype(F32) + s * (d - mean(d) - hat * mean(d * hat))
            dmid[rows, :] = d_mid
            s3g, s3b = s3g + fold(da * hat), s3b + fold(da)
            hat, s = normal(branch[rows, :])
            d = d_mid * w_row(G2)
            dy = (s * (d - mean(d) - hat * mean(d * hat))).astype(BF16)
            s2g, s2b = s2g + fold(d_mid * hat), s2b + fold(d_mid)
            g[rows, g_base[1] : g_base[1] + width] = dy
            return (s3g, s3b, s2g, s2b, sob + fold(dy.astype(F32)))

        got = each(body, 16, (zeros8,) * 5)
        for row, value in zip((G3, B3, G2, B2, OB), got):
            put_sum(row, value)
        right_far(1).start()

    tasks.append((2.5, task_norms))
    ends[1] = len(tasks)
    d_mixed = big.at[pl.ds(U0 + length, length), :]
    tasks += add_pair(d_mixed, None, lambda j: slice(g_base[1], g_base[1] + width), 1, width)

    def task_heads():
        def body(rows, carry):
            d = d_mixed[rows, :]
            act[rows, :] = (d * w_row(HS)).astype(BF16)
            return carry + fold(d * attended[rows, :])

        put_sum(HS, each(body, 32, zeros8))

    tasks.append((0.6, task_heads))

    def task_attend(first, count):
        def run():
            def body(i, _):
                p = first + i
                q_cols = pl.ds(pl.multiple_of(p * 128, 128), 128)
                k_cols = pl.ds(pl.multiple_of(width + p * 128, 128), 128)
                v_cols = pl.ds(pl.multiple_of(2 * width + p * 128, 128), 128)
                q, k, v, do = qkv[:, q_cols], qkv[:, k_cols], qkv[:, v_cols], act[:, q_cols]
                dq, dk, dv = [], [], []
                for h in range(2):
                    prob = probs[2 * p + h]
                    own = do * keep_lane[h]
                    dv.append(tn(prob.astype(BF16), do))
                    dp = nt(own, v)
                    ds = prob * (dp - jnp.sum(prob * dp, axis=-1, keepdims=True))
                    ds = ds.astype(BF16)
                    dq.append(jnp.dot(ds, k, preferred_element_type=F32) * scale)
                    dk.append(tn(ds, q) * scale)
                for cols, value in ((q_cols, dq), (k_cols, dk), (v_cols, dv)):
                    low = jnp.where(low_lane, value[0], value[1]).astype(BF16)
                    g[0:length, cols] = low
                return 0

            lax.fori_loop(0, count, body, 0)
            if first + count == width // 128:

                def sums(rows, carry):
                    a, b = carry
                    return (
                        a + fold(g[rows, 0:width].astype(F32)),
                        b + fold(g[rows, 2 * width : 3 * width].astype(F32)),
                    )

                a, b = each(sums, 32, (zeros8, zeros8))
                put_sum(QB, a)
                put_sum(VB, b)
                right_far(0).start()

        return run

    for first in range(0, width // 128, 2):
        tasks.append((3.0, task_attend(first, 2)))
    ends[0] = len(tasks)
    d_first = big.at[pl.ds(U0 + 2 * length, length), :]
    tasks += add_pair(d_first, None, lambda j: slice(j * width, (j + 1) * width), 3, width)

    def task_last():
        def body(rows, carry):
            sg, sb = carry
            da = d_first[rows, :]
            hat, s = normal(x_in[rows, :].astype(F32))
            d = da * w_row(G1)
            dx_out[rows, :] = dmid[rows, :] + s * (d - mean(d) - hat * mean(d * hat))
            return (sg + fold(da * hat), sb + fold(da))

        sg, sb = each(body, 16, (zeros8, zeros8))
        put_sum(G1, sg)
        put_sum(B1, sb)
        vec_in[0, 23:24, :] = jnp.zeros((1, half_w), F32)
        vec_in[1, 23:24, :] = jnp.zeros((1, half_w), F32)
        vec_copy(0).start()

    tasks.append((1.5, task_last))

    vec_steps = (core, to["X"], to["Y"], {"rep": r + 4 * (1 - 2 * (z % 2))}, across)

    def vec_copy(step):
        source = vec_in.at[1 - c] if step == 0 else vec_own.at[step]
        return pltpu.make_async_remote_copy(
            src_ref=source, dst_ref=vec_got.at[step], send_sem=v_send.at[step], recv_sem=v_recv.at[step],
            device_id=vec_steps[step], device_id_type=MESH,
        )

    def vec_task(k):
        vec_copy(k).wait_recv()
        total = (vec_in[c] if k == 0 else vec_own[k]) + vec_got[k]
        if k < 4:
            vec_own[k + 1] = total
            vec_copy(k + 1).start()
        else:
            vec_out[...] = total

    units = unit_table(dims)
    kinds = kinds_of(len(units))
    xy_at, z_at = {}, {}
    for unit, kind in enumerate(kinds):
        (z_at if kind[0] == "Z" else xy_at)[unit] = len(z_at) if kind[0] == "Z" else len(xy_at)

    def copy(unit, name, source, dest, device):
        return functools.partial(
            pltpu.make_async_remote_copy,
            src_ref=source, dst_ref=dest, send_sem=send.at[unit, SLOT[name]], recv_sem=recv.at[unit, SLOT[name]],
            device_id=device, device_id_type=MESH,
        )

    def rows_of(unit, start, count):
        if not isinstance(start, int):
            start = pl.multiple_of(start, 16)
        return res.at[unit, pl.ds(start, count), :]

    def product(unit, start, count, dest, dest_start, got=None, got_start=0):
        m, row, col = units[unit]
        step = 128 if count % 128 == 0 else min(count, 64)

        def block(index, _):
            part, strip = index // (UNIT_COLS // 256), index % (UNIT_COLS // 256)
            cols = pl.ds(pl.multiple_of(strip * 256, 256), 256)
            value = jnp.dot(
                at[pl.ds(pl.multiple_of(at_base[m] + row + start + part * step, 16), step), :],
                g[:, pl.ds(pl.multiple_of(g_base[m] + col + strip * 256, 256), 256)],
                preferred_element_type=F32,
            )
            if got is not None:
                value = value + got[pl.ds(pl.multiple_of(got_start + part * step, 16), step), cols].astype(F32)
            dest[pl.ds(pl.multiple_of(dest_start + part * step, 16), step), cols] = value.astype(BF16)
            return 0

        lax.fori_loop(0, (count // step) * (UNIT_COLS // 256), block, 0)

    def accumulate(unit, start, count, got, got_start, dest, dest_start):
        def block(strip, _):
            cols = pl.ds(pl.multiple_of(strip * 256, 256), 256)
            value = res[unit, pl.ds(pl.multiple_of(start, 16), count), cols].astype(F32)
            value = value + got[pl.ds(pl.multiple_of(got_start, 16), count), cols].astype(F32)
            dest[pl.ds(pl.multiple_of(dest_start, 16), count), cols] = value.astype(BF16)
            return 0

        lax.fori_loop(0, UNIT_COLS // 256, block, 0)

    def gather_line(unit, base, size, level):
        up, down = "u%d" % level, "w%d" % level
        low, high = z - (level - 1), z + (level - 1)

        @pl.when((low >= 0) & (z < 3))
        def _():
            part = rows_of(unit, base + low * size, size)
            copy(unit, up, part, part, to["U"])().start()

        @pl.when((high <= 3) & (z > 0))
        def _():
            part = rows_of(unit, base + high * size, size)
            copy(unit, down, part, part, to["D"])().start()

    def gather_arrived(unit, base, size, level):
        up, down = "u%d" % level, "w%d" % level
        low, high = z - level, z + level

        @pl.when(low >= 0)
        def _():
            part = rows_of(unit, base + low * size, size)
            copy(unit, up, part, part, to["U"])().wait_recv()

        @pl.when(high <= 3)
        def _():
            part = rows_of(unit, base + high * size, size)
            copy(unit, down, part, part, to["D"])().wait_recv()

    def gather_sent(unit, base, size):
        for level in (1, 2, 3):
            up, down = "u%d" % level, "w%d" % level
            low, high = z - (level - 1), z + (level - 1)

            @pl.when((low >= 0) & (z < 3))
            def _():
                part = rows_of(unit, base + low * size, size)
                copy(unit, up, part, part, to["U"])().wait_send()

            @pl.when((high <= 3) & (z > 0))
            def _():
                part = rows_of(unit, base + high * size, size)
                copy(unit, down, part, part, to["D"])().wait_send()

    def write_out(unit):
        m, row, col = units[unit]
        return pltpu.make_async_copy(
            res.at[unit],
            outs[m].at[pl.ds(row, UNIT_ROWS), pl.ds(col, UNIT_COLS)],
            o_sem.at[unit],
        )

    def finish(unit, base, size, sent):
        write_out(unit).start()
        for name in sent[:4]:
            name().wait_send()
        pl.when(line_end)(lambda: sent[4]().wait_send())

        @pl.when(line_mid)
        def _():
            sent[5]().wait_send()
            sent[6]().wait_send()

        gather_sent(unit, base, size)

    def task_xy(unit, step):
        half, quarter, size = UNIT_ROWS // 2, UNIT_ROWS // 4, UNIT_ROWS // 16
        first, second = ("X", "Y") if kinds[unit] == "X" else ("Y", "X")
        p, q = (x, y) if kinds[unit] == "X" else (y, x)
        line, block, out, other = line_xy.at[xy_at[unit]], res.at[unit], give.at[pl.ds(unit * GIVE_ROWS, GIVE_ROWS), :], pair.at[unit]
        keep, away_half = p * half, (1 - p) * half
        base = keep + q * quarter
        away = keep + (1 - q) * quarter
        at_z = half + quarter
        d1 = copy(unit, "d1", out.at[pl.ds(0, half), :], rows_of(unit, away_half, half), to[first])
        d2 = copy(unit, "d2", out.at[pl.ds(half, quarter), :], other.at[pl.ds(0, quarter), :], to[second])
        z1 = copy(unit, "z1", out.at[pl.ds(at_z, 3 * size), :], line.at[pl.ds(0, 3 * size), :], inward)
        z2 = copy(unit, "z2", out.at[pl.ds(at_z, 2 * size), :], line.at[pl.ds(3 * size, 2 * size), :], across)
        z3 = copy(unit, "z3", out.at[pl.ds(at_z + 2 * size, size), :], line.at[pl.ds(0, size), :], outward)
        own_quarter = rows_of(unit, base, quarter)
        g2 = copy(unit, "g2", own_quarter, own_quarter, to[second])
        own_half = rows_of(unit, keep, half)
        g1 = copy(unit, "g1", own_half, own_half, to[first])
        own = base + z * size
        if step == 0:
            product(unit, away_half, half, out, 0)
            d1().start()
        elif step == 1:
            d1().wait_recv()
            product(unit, away, quarter, out, half, block, away)
            d2().start()
            product(unit, base, quarter, block, base, block, base)
        elif step == 2:
            d2().wait_recv()

            @pl.when(line_end)
            def _():
                skip = (1 - upper) * size
                accumulate(unit, base + skip, 3 * size, other, skip, out, at_z)
                z1().start()
                accumulate(unit, own, size, other, z * size, block, own)

            @pl.when(line_mid)
            def _():
                accumulate(unit, base, quarter, other, 0, block, base)

        elif step == 3:

            @pl.when(line_mid)
            def _():
                z1().wait_recv()
                accumulate(unit, base + (1 - upper) * 2 * size, 2 * size, line, (1 - upper) * size, out, at_z)
                z2().start()
                accumulate(unit, own, size, line, upper * 2 * size, block, own)

        elif step == 4:

            @pl.when(line_mid)
            def _():
                z2().wait_recv()
                accumulate(unit, base + upper * 3 * size, size, line, (3 + upper) * size, out, at_z + 2 * size)
                z3().start()
                accumulate(unit, own, size, line, (4 - upper) * size, block, own)
                gather_line(unit, base, size, 1)

        elif step == 5:

            @pl.when(line_end)
            def _():
                z3().wait_recv()
                accumulate(unit, own, size, line, 0, block, own)
                gather_line(unit, base, size, 1)

        elif step in (6, 7):
            gather_arrived(unit, base, size, step - 5)
            gather_line(unit, base, size, step - 4)
        elif step == 8:
            gather_arrived(unit, base, size, 3)
            g2().start()
        elif step == 9:
            g2().wait_recv()
            g1().start()
        else:
            g1().wait_recv()
            finish(unit, base, size, (d1, d2, g2, g1, z1, z2, z3))

    def task_z(unit, step):
        size, half, quarter = UNIT_ROWS // 4, UNIT_ROWS // 8, UNIT_ROWS // 16
        first, second = ("X", "Y") if kinds[unit] == "ZX" else ("Y", "X")
        p, q = (x, y) if kinds[unit] == "ZX" else (y, x)
        line, block, out, other = line_z.at[z_at[unit]], res.at[unit], give.at[pl.ds(unit * GIVE_ROWS, GIVE_ROWS), :], pair.at[unit]
        own = z * size
        keep, away_half = own + p * half, own + (1 - p) * half
        base, away = keep + q * quarter, keep + (1 - q) * quarter
        at_d = 3 * size
        z1 = copy(unit, "z1", out.at[pl.ds(0, 3 * size), :], line.at[pl.ds(0, 3 * size), :], inward)
        z2 = copy(unit, "z2", out.at[pl.ds(0, 2 * size), :], line.at[pl.ds(3 * size, 2 * size), :], across)
        z3 = copy(unit, "z3", out.at[pl.ds(2 * size, size), :], line.at[pl.ds(0, size), :], outward)
        d1 = copy(unit, "d1", out.at[pl.ds(at_d, half), :], other.at[pl.ds(0, half), :], to[first])
        d2 = copy(unit, "d2", out.at[pl.ds(at_d + half, quarter), :], other.at[pl.ds(half, quarter), :], to[second])
        own_quarter = rows_of(unit, base, quarter)
        g2 = copy(unit, "g2", own_quarter, own_quarter, to[second])
        own_half = rows_of(unit, keep, half)
        g1 = copy(unit, "g1", own_half, own_half, to[first])
        if step == 0:

            @pl.when(line_end)
            def _():
                product(unit, (1 - upper) * size, 3 * size, out, 0)
                z1().start()

        elif step == 1:

            @pl.when(line_mid)
            def _():
                z1().wait_recv()
                product(unit, (1 - upper) * 2 * size, 2 * size, out, 0, line, (1 - upper) * size)
                z2().start()
                product(unit, own, size, block, own, line, upper * 2 * size)

        elif step == 2:

            @pl.when(line_mid)
            def _():
                z2().wait_recv()
                product(unit, upper * 3 * size, size, out, 2 * size, line, (3 + upper) * size)
                z3().start()
                got = (4 - upper) * size
                accumulate(unit, away_half, half, line, got + (1 - p) * half, out, at_d)
                d1().start()
                accumulate(unit, keep, half, line, got + p * half, block, keep)

        elif step == 3:

            @pl.when(line_end)
            def _():
                z3().wait_recv()
                product(unit, away_half, half, out, at_d, line, (1 - p) * half)
                d1().start()
                product(unit, keep, half, block, keep, line, p * half)

        elif step == 4:
            d1().wait_recv()
            accumulate(unit, away, quarter, other, (1 - q) * quarter, out, at_d + half)
            d2().start()
            accumulate(unit, base, quarter, other, q * quarter, block, base)
        elif step == 5:
            d2().wait_recv()
            accumulate(unit, base, quarter, other, half, block, base)
            g2().start()
        elif step == 6:
            g2().wait_recv()
            g1().start()
        elif step == 7:
            g1().wait_recv()
            gather_line(unit, 0, size, 1)
        elif step in (8, 9):
            gather_arrived(unit, 0, size, step - 7)
            gather_line(unit, 0, size, step - 6)
        else:
            gather_arrived(unit, 0, size, 3)
            finish(unit, 0, size, (d1, d2, g2, g1, z1, z2, z3))


    for kind, a, b in program_order(units, kinds, [cost for cost, _ in tasks], ends):
        if kind == "task":
            tasks[a][1]()
        elif kind == "wait":
            wait_pair(a)
        elif kind == "vec":
            vec_task(a)
        elif kinds[a][0] == "Z":
            task_z(a, b)
        else:
            task_xy(a, b)
    for step in range(5):
        vec_copy(step).wait_send()
    for unit in range(len(units)):
        write_out(unit).wait()


def whole_layer(layer_input, cotangent, weights, params):
    dims = tuple(w.shape for w in weights)
    at_rows = sum(rows for rows, _ in dims)
    g_cols = sum(cols for _, cols in dims)
    at_base = [sum(rows for rows, _ in dims[:m]) for m in range(4)]
    g_base = [sum(cols for _, cols in dims[:m]) for m in range(4)]
    length, width = layer_input.shape
    hidden = dims[2][1]
    blocks = hidden // width
    units = unit_table(dims)
    kinds = kinds_of(len(units))
    n, n_z = len(units), sum(kind[0] == "Z" for kind in kinds)
    tiles = n // 2
    hbm = pl.BlockSpec(memory_space=pl.ANY)
    vmem = pl.BlockSpec(memory_space=pltpu.VMEM)
    dma = pltpu.SemaphoreType.DMA
    small = (24, width // 2)
    got = pl.pallas_call(
        functools.partial(layer_kernel, dims, at_base, g_base),
        out_shape=[jax.ShapeDtypeStruct((length, width), BF16), jax.ShapeDtypeStruct((length, width), F32)]
        + [jax.ShapeDtypeStruct(d, BF16) for d in dims]
        + [jax.ShapeDtypeStruct(small, F32), jax.ShapeDtypeStruct((2, tiles, 512, UNIT_COLS), BF16)],
        in_specs=[vmem, hbm] + [hbm] * 4 + [vmem] * 13,
        out_specs=[vmem, vmem] + [hbm] * 4 + [vmem, hbm],
        scratch_shapes=[
            pltpu.VMEM((at_rows, 2 * length), BF16),
            pltpu.VMEM((2 * length, g_cols), BF16),
            pltpu.VMEM((n, UNIT_ROWS, UNIT_COLS), BF16),
            pltpu.VMEM((n * GIVE_ROWS, UNIT_COLS), BF16),
            pltpu.VMEM((n, UNIT_ROWS // 4, UNIT_COLS), BF16),
            pltpu.VMEM((n - n_z, 5 * UNIT_ROWS // 16, UNIT_COLS), BF16),
            pltpu.VMEM((n_z, 5 * UNIT_ROWS // 4, UNIT_COLS), BF16),
            pltpu.VMEM((4, 512, UNIT_COLS), BF16),
            pltpu.VMEM((3 * blocks * length, width), F32),
            pltpu.VMEM((2 * at_rows, length), BF16),
            pltpu.VMEM((length, width), BF16),
            pltpu.VMEM((blocks * length, width), BF16),
            pltpu.VMEM((length, 3 * width), BF16),
            pltpu.VMEM((width // 64, length, length), F32),
            pltpu.VMEM((length, width), F32),
            pltpu.VMEM((length, width), F32),
            pltpu.VMEM((length, width), F32),
            pltpu.VMEM((length, width), F32),
            pltpu.VMEM((16, width), F32),
            pltpu.VMEM((8, hidden), F32),
            pltpu.VMEM((length, 128), F32),
            pltpu.VMEM((24, hidden), F32),
            pltpu.VMEM((2,) + small, F32),
            pltpu.VMEM((5,) + small, F32),
            pltpu.VMEM((5,) + small, F32),
            dma((n, len(COMMS))),
            dma((n, len(COMMS))),
            dma((5,)),
            dma((5,)),
            dma((4, 2)),
            dma((4, 2)),
            dma((4,)),
            dma((n,)),
            dma((2 * tiles,)),
            dma((2 * tiles,)),
            dma((2 * tiles,)),
            dma((2 * tiles,)),
            dma((4,)),
            dma((2, 2)),
            dma((1,)),
        ],
        compiler_params=pltpu.CompilerParams(
            collective_id=0, has_side_effects=True, vmem_limit_bytes=67043328
        ),
        name="whole_layer",
    )(layer_input, cotangent, *weights, *params)
    return got[0], got[1], got[2:6], got[6]


def on_pair_of_cores(
    layer_input, cotangent, w_qkv, qv_bias, w_out, out_bias, head_scale, ln1_gain, ln1_bias, ln2_gain, ln2_bias,
    ln3_gain, ln3_bias, w_fc1, fc1_bias, ln4_gain, ln4_bias, w_fc2, fc2_bias,
):
    params = (
        qv_bias, out_bias, jnp.repeat(head_scale, HEAD_DIM), ln1_gain, ln1_bias, ln2_gain, ln2_bias, ln3_gain, ln3_bias,
        fc1_bias, ln4_gain, ln4_bias, fc2_bias,
    )
    params = [p.reshape(-1, p.shape[-1]) for p in params]
    output, grad_input, sums, vec = whole_layer(layer_input, cotangent, (w_qkv, w_out, w_fc1, w_fc2), params)
    sums = [s.astype(jnp.float32) for s in sums]
    rows = [vec[k] for k in range(2, 11)]
    wide = [vec[11 + 4 * k : 15 + 4 * k].reshape(-1) for k in range(3)]
    heads = rows[1].reshape(-1, HEAD_DIM).sum(axis=-1)
    return (
        output, grad_input, sums[0], vec[0:2], sums[1], rows[0], heads, rows[2], rows[3], rows[4], rows[5], rows[6],
        rows[7], sums[2], wide[0], wide[1], wide[2], sums[3], rows[8],
    )


def fits_pair(mesh):
    return mesh.shape["shard"] == 2 and mesh.shape["rep"] == 16


def solution(mesh):
    return jax.shard_map(
        on_pair_of_cores if fits_pair(mesh) else on_any_mesh,
        mesh=mesh,
        in_specs=(
            P(("rep", "shard"), None),
            P(("rep", "shard"), None),
            P("shard", None),
            P(None, "shard"),
            P("shard", None),
            P("shard"),
            P("shard"),
            P("shard"),
            P("shard"),
            P("shard"),
            P("shard"),
            P("shard"),
            P("shard"),
            P("shard", None),
            P("shard"),
            P("shard"),
            P("shard"),
            P("shard", None),
            P("shard"),
        ),
        out_specs=(
            P(("rep", "shard"), None),
            P(("rep", "shard"), None),
            P("shard", None),
            P(None, "shard"),
            P("shard", None),
            P("shard"),
            P("shard"),
            P("shard"),
            P("shard"),
            P("shard"),
            P("shard"),
            P("shard"),
            P("shard"),
            P("shard", None),
            P("shard"),
            P("shard"),
            P("shard"),
            P("shard", None),
            P("shard"),
        ),
        check_vma=False,
    )
```

```python
import functools

import jax
import jax.numpy as jnp
from jax import lax
from jax.experimental import pallas as pl
from jax.experimental.pallas import tpu as pltpu
from jax.sharding import PartitionSpec as P

D = 1024
HEADS = 16
HEAD_DIM = 64


EPS = 1e-05
NEG = -1e30


def norm_rows(v, gain, bias):
    centre = jnp.mean(v, axis=-1, keepdims=True)
    centred = v - centre
    spread = jnp.mean(centred * centred, axis=-1, keepdims=True)
    return centred * lax.rsqrt(spread + EPS) * gain + bias


def ffn_middle(hidden, gain, bias):
    return norm_rows(jax.nn.gelu(hidden, approximate=False), gain, bias)


def causal_mask(index, qblock, length):
    rows = index * qblock + lax.iota(jnp.int32, qblock)
    cols = lax.iota(jnp.int32, length)
    return (cols[None, :] <= rows[:, None])[None]


def block_scores(queries, keys_all, index, qblock, scale):
    length = keys_all.shape[0]
    scores = (
        jnp.einsum("qhd,khd->hqk", queries, keys_all, preferred_element_type=jnp.float32) * scale
    )
    return (queries, jnp.where(causal_mask(index, qblock, length), scores, NEG))


def attend_forward(queries, keys_all, values_all, scale):
    length, heads, width = queries.shape
    qblock = min(512, length)
    blocks = length // qblock

    def one_block(index):
        rows_q, scores = block_scores(queries, keys_all, index, qblock, scale)
        total = jax.nn.logsumexp(scores, axis=-1, keepdims=True)
        probs = jnp.exp(scores - total).astype(jnp.bfloat16)
        outcome = jnp.einsum("hqk,khd->qhd", probs, values_all, preferred_element_type=jnp.float32)
        return (outcome, total)

    outcome, totals = lax.map(one_block, jnp.arange(blocks, dtype=jnp.int32))
    return (outcome.reshape(length, heads, width), totals)


def attend_backward(queries, keys_all, values_all, totals, grad_out, scale):
    length, heads, width = queries.shape
    qblock = min(512, length)
    blocks = length // qblock

    def one_block(carry, index):
        grad_keys, grad_values = carry
        rows_q, scores = block_scores(queries, keys_all, index, qblock, scale)
        probs = jnp.exp(scores - totals[index])
        probs_low = probs.astype(jnp.bfloat16)
        grad_values = grad_values + jnp.einsum(
            "hqk,qhd->khd", probs_low, grad_out, preferred_element_type=jnp.float32
        )
        grad_probs = jnp.einsum(
            "qhd,khd->hqk", grad_out, values_all, preferred_element_type=jnp.float32
        )
        row_dot = jnp.sum(probs * grad_probs, axis=-1, keepdims=True)
        grad_scores = (probs * (grad_probs - row_dot)).astype(jnp.bfloat16)
        grad_rows = (
            jnp.einsum("hqk,khd->qhd", grad_scores, keys_all, preferred_element_type=jnp.float32)
            * scale
        )
        grad_keys = (
            grad_keys
            + jnp.einsum("hqk,qhd->khd", grad_scores, rows_q, preferred_element_type=jnp.float32)
            * scale
        )
        return ((grad_keys, grad_values), grad_rows)

    empty = jnp.zeros((length, heads, width), jnp.float32)
    (grad_keys, grad_values), grad_queries = lax.scan(
        one_block, (empty, empty), jnp.arange(blocks, dtype=jnp.int32)
    )
    return (grad_queries.reshape(length, heads, width), grad_keys, grad_values)


def on_any_mesh(
    layer_input,
    cotangent,
    w_qkv,
    qv_bias,
    w_out,
    out_bias,
    head_scale,
    ln1_gain,
    ln1_bias,
    ln2_gain,
    ln2_bias,
    ln3_gain,
    ln3_bias,
    w_fc1,
    fc1_bias,
    ln4_gain,
    ln4_bias,
    w_fc2,
    fc2_bias,
):
    low_qkv = w_qkv.astype(jnp.bfloat16)
    low_out = w_out.astype(jnp.bfloat16)
    low_heads = head_scale.astype(jnp.bfloat16)
    low_up = w_fc1.astype(jnp.bfloat16)
    low_down = w_fc2.astype(jnp.bfloat16)
    whole = (
        lax.all_gather(low_qkv, "shard", axis=0, tiled=True),
        lax.all_gather(qv_bias.astype(jnp.bfloat16), "shard", axis=1, tiled=True),
        lax.all_gather(low_out, "shard", axis=0, tiled=True),
        lax.all_gather(out_bias.astype(jnp.bfloat16), "shard", axis=0, tiled=True),
        lax.all_gather(low_heads, "shard", axis=0, tiled=True),
        lax.all_gather(ln1_gain.astype(jnp.bfloat16), "shard", axis=0, tiled=True),
        lax.all_gather(ln1_bias.astype(jnp.bfloat16), "shard", axis=0, tiled=True),
        lax.all_gather(ln2_gain.astype(jnp.bfloat16), "shard", axis=0, tiled=True),
        lax.all_gather(ln2_bias.astype(jnp.bfloat16), "shard", axis=0, tiled=True),
        lax.all_gather(ln3_gain.astype(jnp.bfloat16), "shard", axis=0, tiled=True),
        lax.all_gather(ln3_bias.astype(jnp.bfloat16), "shard", axis=0, tiled=True),
        lax.all_gather(low_up, "shard", axis=0, tiled=True),
        lax.all_gather(fc1_bias.astype(jnp.bfloat16), "shard", axis=0, tiled=True),
        lax.all_gather(ln4_gain.astype(jnp.bfloat16), "shard", axis=0, tiled=True),
        lax.all_gather(ln4_bias.astype(jnp.bfloat16), "shard", axis=0, tiled=True),
        lax.all_gather(low_down, "shard", axis=0, tiled=True),
        lax.all_gather(fc2_bias.astype(jnp.bfloat16), "shard", axis=0, tiled=True),
    )
    weight_qkv, weight_out, weight_up, weight_down = (whole[0], whole[2], whole[11], whole[15])
    (
        bias_qv,
        bias_out,
        head_gain,
        gain_one,
        shift_one,
        gain_two,
        shift_two,
        gain_three,
        shift_three,
        bias_up,
        gain_four,
        shift_four,
        bias_down,
    ) = tuple(
        (whole[index].astype(jnp.float32) for index in (1, 3, 4, 5, 6, 7, 8, 9, 10, 12, 13, 14, 16))
    )
    length = layer_input.shape[0]
    scale = HEAD_DIM ** (-0.5)
    inputs = layer_input.astype(jnp.float32)
    normed_one, pull_one = jax.vjp(norm_rows, inputs, gain_one, shift_one)
    act_one = normed_one.astype(jnp.bfloat16)
    bias_full = jnp.concatenate([bias_qv[0], jnp.zeros((D,), jnp.float32), bias_qv[1]])
    qkv = (jnp.dot(act_one, weight_qkv, preferred_element_type=jnp.float32) + bias_full).astype(
        jnp.bfloat16
    )
    triple = qkv.reshape(length, 3, HEADS, HEAD_DIM)
    queries = triple[:, 0]
    keys_all = triple[:, 1]
    values_all = triple[:, 2]
    attended, totals = attend_forward(queries, keys_all, values_all, scale)
    mixed = (attended * head_gain[:, None]).reshape(length, D).astype(jnp.bfloat16)
    branch = jnp.dot(mixed, weight_out, preferred_element_type=jnp.float32) + bias_out
    normed_two, pull_two = jax.vjp(norm_rows, branch, gain_two, shift_two)
    middle = inputs + normed_two
    normed_three, pull_three = jax.vjp(norm_rows, middle, gain_three, shift_three)
    act_three = normed_three.astype(jnp.bfloat16)
    hidden = jnp.dot(act_three, weight_up, preferred_element_type=jnp.float32) + bias_up
    normed_four, pull_four = jax.vjp(ffn_middle, hidden, gain_four, shift_four)
    act_four = normed_four.astype(jnp.bfloat16)
    result = middle + (
        jnp.dot(act_four, weight_down, preferred_element_type=jnp.float32) + bias_down
    )
    output = result.astype(jnp.bfloat16)
    again = (
        lax.all_gather(low_qkv, "shard", axis=0, tiled=True),
        lax.all_gather(low_out, "shard", axis=0, tiled=True),
        lax.all_gather(low_heads, "shard", axis=0, tiled=True),
        lax.all_gather(low_up, "shard", axis=0, tiled=True),
        lax.all_gather(low_down, "shard", axis=0, tiled=True),
    )
    back_qkv, back_out, back_up, back_down = (again[0], again[1], again[3], again[4])
    back_heads = again[2].astype(jnp.float32)
    cot_full = cotangent.astype(jnp.float32)
    grad_down_bias = jnp.sum(cot_full, axis=0)
    grad_down = jnp.einsum("tf,td->fd", act_four, cotangent, preferred_element_type=jnp.float32)
    grad_four = jnp.einsum("td,fd->tf", cotangent, back_down, preferred_element_type=jnp.float32)
    grad_hidden, grad_gain_four, grad_shift_four = pull_four(grad_four)
    hidden_low = grad_hidden.astype(jnp.bfloat16)
    grad_up_bias = jnp.sum(hidden_low, axis=0, dtype=jnp.float32)
    grad_up = jnp.einsum("td,tf->df", act_three, hidden_low, preferred_element_type=jnp.float32)
    grad_three = jnp.einsum("tf,df->td", hidden_low, back_up, preferred_element_type=jnp.float32)
    grad_mid_part, grad_gain_three, grad_shift_three = pull_three(grad_three)
    grad_middle = cot_full + grad_mid_part
    grad_branch, grad_gain_two, grad_shift_two = pull_two(grad_middle)
    branch_low = grad_branch.astype(jnp.bfloat16)
    grad_out_b = jnp.sum(branch_low, axis=0, dtype=jnp.float32)
    grad_out_w = jnp.einsum("td,te->de", mixed, branch_low, preferred_element_type=jnp.float32)
    grad_mixed = jnp.einsum("te,de->td", branch_low, back_out, preferred_element_type=jnp.float32)
    grad_mixed = grad_mixed.reshape(length, HEADS, HEAD_DIM)
    grad_heads = jnp.sum(grad_mixed * attended, axis=(0, 2))
    grad_attended = (grad_mixed * back_heads[:, None]).astype(jnp.bfloat16)
    grad_queries, grad_keys, grad_values = attend_backward(
        queries, keys_all, values_all, totals, grad_attended, scale
    )
    grad_qkv = (
        jnp.stack([grad_queries, grad_keys, grad_values], axis=1)
        .reshape(length, 3 * D)
        .astype(jnp.bfloat16)
    )
    grad_qv = jnp.stack(
        [
            jnp.sum(grad_qkv[:, :D], axis=0, dtype=jnp.float32),
            jnp.sum(grad_qkv[:, 2 * D :], axis=0, dtype=jnp.float32),
        ]
    )
    grad_qkv_w = jnp.einsum("td,te->de", act_one, grad_qkv, preferred_element_type=jnp.float32)
    grad_one = jnp.einsum("te,de->td", grad_qkv, back_qkv, preferred_element_type=jnp.float32)
    grad_in_part, grad_gain_one, grad_shift_one = pull_one(grad_one)
    grad_input = grad_middle + grad_in_part
    shares = (
        lax.psum_scatter(grad_qkv_w, "shard", scatter_dimension=0, tiled=True),
        lax.psum_scatter(grad_qv, "shard", scatter_dimension=1, tiled=True),
        lax.psum_scatter(grad_out_w, "shard", scatter_dimension=0, tiled=True),
        lax.psum_scatter(grad_out_b, "shard", scatter_dimension=0, tiled=True),
        lax.psum_scatter(grad_heads, "shard", scatter_dimension=0, tiled=True),
        lax.psum_scatter(grad_gain_one, "shard", scatter_dimension=0, tiled=True),
        lax.psum_scatter(grad_shift_one, "shard", scatter_dimension=0, tiled=True),
        lax.psum_scatter(grad_gain_two, "shard", scatter_dimension=0, tiled=True),
        lax.psum_scatter(grad_shift_two, "shard", scatter_dimension=0, tiled=True),
        lax.psum_scatter(grad_gain_three, "shard", scatter_dimension=0, tiled=True),
        lax.psum_scatter(grad_shift_three, "shard", scatter_dimension=0, tiled=True),
        lax.psum_scatter(grad_up, "shard", scatter_dimension=0, tiled=True),
        lax.psum_scatter(grad_up_bias, "shard", scatter_dimension=0, tiled=True),
        lax.psum_scatter(grad_gain_four, "shard", scatter_dimension=0, tiled=True),
        lax.psum_scatter(grad_shift_four, "shard", scatter_dimension=0, tiled=True),
        lax.psum_scatter(grad_down, "shard", scatter_dimension=0, tiled=True),
        lax.psum_scatter(grad_down_bias, "shard", scatter_dimension=0, tiled=True),
    )
    summed = lax.psum(
        (
            shares[0],
            shares[1],
            shares[2],
            shares[3],
            shares[4],
            shares[5],
            shares[6],
            shares[7],
            shares[8],
            shares[9],
            shares[10],
            shares[11],
            shares[12],
            shares[13],
            shares[14],
            shares[15],
            shares[16],
        ),
        "rep",
    )
    return (output, grad_input) + tuple(summed)


MESH = pl.DeviceIdType.MESH
BF16 = jnp.bfloat16
F32 = jnp.float32
UNIT_ROWS = 256
UNIT_COLS = 1024
MIB = 1 << 20
SLOT = {
    "d1": 0, "d2": 1, "z1": 2, "z3": 2, "z2": 3, "u1": 4, "w1": 4, "u2": 5, "w2": 5, "u3": 6, "w3": 6, "g1": 7, "g2": 8,
}


def unit_table(dims):
    table = []
    for matrix in (3, 2, 1, 0):
        rows, cols = dims[matrix]
        for col in range(0, cols, UNIT_COLS):
            for row in range(0, rows, UNIT_ROWS):
                table.append((matrix, row, col))
    return table


KINDS = (
    "X", "ZY", "ZY", "Y", "Y", "X", "X", "ZY", "Y", "Y", "Y", "X", "X", "ZX", "X", "ZY", "X", "ZX", "Y", "Y",
    "X", "X", "Y", "ZY",
)
TASK = 24
ORDER = (
    5, 2, 0, 6, 7, 3, 24, 24, 24, 4, 24, 5, 24, 3, 1, 24, 2, 0, 24, 4, 24, 24, 5, 0, 2, 6, 3, 7, 24, 2, 4, 24,
    6, 5, 2, 24, 0, 7, 2, 3, 5, 24, 24, 14, 2, 12, 4, 13, 9, 6, 11, 7, 5, 3, 8, 15, 0, 24, 2, 3, 4, 10, 24, 0,
    6, 24, 14, 9, 4, 7, 24, 5, 13, 16, 17, 12, 6, 1, 5, 24, 8, 24, 5, 11, 24, 9, 13, 7, 10, 2, 15, 3, 0, 24, 14,
    4, 1, 24, 12, 16, 13, 24, 24, 8, 5, 7, 2, 24, 20, 11, 21, 3, 22, 0, 10, 9, 23, 1, 16, 6, 15, 4, 17, 14, 19,
    18, 7, 9, 13, 24, 3, 0, 2, 12, 8, 6, 5, 11, 17, 10, 14, 22, 15, 4, 1, 20, 9, 6, 19, 17, 14, 12, 21, 8, 11,
    23, 10, 16, 3, 12, 18, 13, 8, 22, 11, 7, 0, 9, 10, 14, 15, 12, 4, 8, 1, 20, 23, 22, 11, 19, 10, 16, 17, 6,
    20, 7, 9, 19, 14, 12, 8, 18, 18, 21, 22, 21, 23, 11, 10, 16, 16, 0, 3, 15, 13, 1, 20, 7, 9, 14, 12, 8, 22,
    19, 4, 18, 11, 6, 10, 15, 22, 17, 21, 23, 16, 13, 20, 1, 19, 18, 21, 16, 22, 9, 14, 20, 8, 12, 19, 18, 21,
    10, 23, 13, 11, 15, 17, 1, 22, 20, 19, 18, 21, 16, 14, 13, 15, 9, 12, 23, 1, 20, 19, 18, 21, 13, 15, 8, 11,
    17, 10, 22, 23, 1, 20, 16, 15, 21, 19, 17, 18, 23, 22, 17, 23, 20, 19, 17, 23, 21, 18,
)


GIVE_ROWS = 240


def program_order(units, ends):
    order, task, waited, step = [], 0, {3}, [0] * len(units)
    order.append(("wait", 3, 0))
    for entry in ORDER:
        if entry == TASK:
            order.append(("task", task, 0))
            task += 1
            continue
        m = units[entry][0]
        if m not in waited:
            assert task >= ends[m]
            order.append(("wait", m, 0))
            waited.add(m)
        order.append(("sum", entry, step[entry]))
        step[entry] += 1
    last = max(k for k, (kind, _, _) in enumerate(order) if kind == "task")
    for k in range(5):
        order.insert(min(last + 7 + 9 * k, len(order)), ("vec", k, 0))
    return order


EPS_TILE = 32


def fold(v):
    total = v[0:8]
    for k in range(1, v.shape[0] // 8):
        total = total + v[8 * k : 8 * k + 8]
    return total


def layer_kernel(dims, at_base, g_base, *refs):
    x_in, cot_in, weights, params = refs[0], refs[1], refs[2:6], refs[6:19]
    y_out, dx_out, res, vec_out, tiles_hbm = refs[19:24]
    (
        at, g, give, pair, line_xy, line_z, ring, big, left, act, hid, qkv, probs, attended, branch, middle, dmid,
        vec_w, vec_h, rstd4, sums4, vec_in, vec_own, vec_got,
        send, recv, v_send, v_recv, p_send, p_recv, l_sem, w_in, w_keep, w_send, w_recv, t_sem, s_sem, e_sem,
    ) = refs[24:]
    r = lax.axis_index("rep")
    c = lax.axis_index("shard")
    x, y, z = r % 2, (r // 2) % 2, r // 4
    core = {"shard": 1 - c}
    to = {
        "X": {"rep": r + 1 - 2 * x},
        "Y": {"rep": r + 2 - 4 * y},
        "U": {"rep": r + 4},
        "D": {"rep": r - 4},
    }
    line_end = (z == 0) | (z == 3)
    line_mid = (z == 1) | (z == 2)
    outward = {"rep": r + 4 * (2 * (z // 2) - 1)}
    inward = {"rep": r + 4 * (1 - 2 * (z // 2))}
    across = {"rep": r + 4 * (3 - 2 * z)}
    upper = z // 2
    length = x_in.shape[0]
    width = x_in.shape[1]
    half_w = width // 2
    hidden = dims[2][1]
    half_h = hidden // 2
    blocks = hidden // width
    TILE = 512

    tile_of = []
    for m, (rows, cols) in enumerate(dims):
        for row in range(0, rows, TILE):
            for col in range(0, cols, UNIT_COLS):
                tile_of.append((m, row, col))
    first_tile = [min(t for t, v in enumerate(tile_of) if v[0] == m) for m in range(4)]
    parts = 2 * len(tile_of)
    slots_f, slots_b = 6, 16

    def part_read(i):
        m, row, col = tile_of[i // 2]
        return pltpu.make_async_copy(
            weights[m].at[pl.ds(row + (i % 2) * 256, 256), pl.ds(col, UNIT_COLS)],
            big.at[pl.ds((i % slots_f) * 256, 256), :],
            w_in.at[i % slots_f],
        )

    def part_low(i):
        return low_buf.at[pl.ds((i % slots_b) * 256, 256), :]

    low_buf = give

    def part_place(i):
        return tiles_hbm.at[c, i // 2, pl.ds((i % 2) * 256, 256), :]

    def part_keep(i):
        return pltpu.make_async_copy(part_low(i), part_place(i), w_keep.at[i % slots_b])

    def part_give(i):
        return pltpu.make_async_remote_copy(
            src_ref=part_low(i), dst_ref=part_place(i), send_sem=w_send.at[i % slots_b], recv_sem=w_recv.at[i],
            device_id=core, device_id_type=MESH,
        )

    def part_got(i):
        return pltpu.make_async_remote_copy(
            src_ref=part_low(i), dst_ref=tiles_hbm.at[1 - c, i // 2, pl.ds((i % 2) * 256, 256), :],
            send_sem=w_send.at[i % slots_b], recv_sem=w_recv.at[i], device_id=core, device_id_type=MESH,
        )

    for i in range(slots_f):
        part_read(i).start()

    barrier = pltpu.get_barrier_semaphore()
    for peer in (core, to["X"], to["Y"]):
        pl.semaphore_signal(barrier, inc=1, device_id=peer, device_id_type=MESH)

    @pl.when(z < 3)
    def _():
        pl.semaphore_signal(barrier, inc=1, device_id=to["U"], device_id_type=MESH)

    @pl.when(z > 0)
    def _():
        pl.semaphore_signal(barrier, inc=1, device_id=to["D"], device_id_type=MESH)

    @pl.when(line_end)
    def _():
        pl.semaphore_signal(barrier, inc=1, device_id=across, device_id_type=MESH)

    narrow = (0, 0, 2, 3, 4, 5, 6, 7, 8, 9, 10)

    def rounded(v):
        return v.astype(BF16).astype(F32)

    lane_w = pl.ds(pl.multiple_of(c * half_w, half_w), half_w)
    lane_h = pl.ds(pl.multiple_of(c * half_h, half_h), half_h)
    (qv_ref, ob_ref, hs_ref, g1_ref, b1_ref, g2_ref, b2_ref, g3_ref, b3_ref, ub_ref, g4_ref, b4_ref, db_ref) = params
    vec_w[0:2, lane_w] = rounded(qv_ref[...])
    for row, ref in zip(range(2, 11), (ob_ref, hs_ref, g1_ref, b1_ref, g2_ref, b2_ref, g3_ref, b3_ref, db_ref)):
        vec_w[row : row + 1, lane_w] = rounded(ref[...])
    for row, ref in enumerate((ub_ref, g4_ref, b4_ref)):
        vec_h[row : row + 1, lane_h] = rounded(ref[...])
    QB, VB, OB, HS, G1, B1, G2, B2, G3, B3, DB = range(11)
    UB, G4, B4 = range(3)

    def small_copy(k, give_it):
        ref, lane, far = ((vec_w, lane_w, 1 - c), (vec_h, lane_h, 1 - c))[k]
        size = half_w if k == 0 else half_h
        other = pl.ds(pl.multiple_of((1 - c) * size, size), size)
        here = ref.at[:, lane]
        return pltpu.make_async_remote_copy(
            src_ref=here, dst_ref=here if give_it else ref.at[:, other], send_sem=s_sem.at[k, 0], recv_sem=s_sem.at[k, 1],
            device_id=core, device_id_type=MESH,
        )

    e_copy = pltpu.make_async_copy(cot_in, g.at[pl.ds(0, length), pl.ds(g_base[3], width)], e_sem.at[0])
    e_copy.start()
    e_copy.wait()
    pl.semaphore_wait(barrier, 5)
    small_copy(0, True).start()
    small_copy(1, True).start()

    def left_own(m):
        rows = dims[m][0]
        return pltpu.make_async_copy(
            left.at[pl.ds(pl.multiple_of(2 * at_base[m] + c * rows, 512), rows), :],
            at.at[pl.ds(at_base[m], rows), pl.ds(0, length)],
            l_sem.at[m],
        )

    def left_far(m):
        rows = dims[m][0]
        return pltpu.make_async_remote_copy(
            src_ref=left.at[pl.ds(pl.multiple_of(2 * at_base[m] + (1 - c) * rows, 512), rows), :],
            dst_ref=at.at[pl.ds(at_base[m], rows), pl.ds(length, length)],
            send_sem=p_send.at[m, 0], recv_sem=p_recv.at[m, 0], device_id=core, device_id_type=MESH,
        )

    def right_far(m):
        cols = pl.ds(g_base[m], dims[m][1])
        return pltpu.make_async_remote_copy(
            src_ref=g.at[pl.ds(0, length), cols], dst_ref=g.at[pl.ds(length, length), cols],
            send_sem=p_send.at[m, 1], recv_sem=p_recv.at[m, 1], device_id=core, device_id_type=MESH,
        )

    right_far(3).start()

    def start_left(m):
        left_own(m).start()
        left_far(m).start()

    def wait_pair(m):
        left_own(m).wait()
        left_far(m).wait()
        right_far(m).wait()

    for i in range(parts):
        part_read(i).wait()
        if i >= slots_b:
            part_keep(i - slots_b).wait()
            part_give(i - slots_b).wait_send()

        def convert(b, _, i=i):
            rows = pl.multiple_of((i % slots_f) * 256 + b * 32, 32)
            low = pl.multiple_of((i % slots_b) * 256 + b * 32, 32)
            low_buf[pl.ds(low, 32), :] = big[pl.ds(rows, 32), :].astype(BF16)
            return 0

        lax.fori_loop(0, 8, convert, 0)
        part_keep(i).start()
        part_give(i).start()
        if i + slots_f < parts:
            part_read(i + slots_f).start()

    def tile(m, half, index):
        return (half, first_tile[m] + index)

    stream = []
    for m in (0, 1, 2):
        for index in range(dims[m][1] // UNIT_COLS):
            stream += [tile(m, 0, index), tile(m, 1, index)]
    per_half = dims[3][0] // TILE
    stream += [tile(3, h, k) for h in range(2) for k in range(per_half)]
    for m in (2, 1, 0):
        for index in range(dims[m][1] // UNIT_COLS):
            stream += [tile(m, 0, index), tile(m, 1, index)]
    slots_t = 4
    here = set()

    def tile_load(i):
        half, t = stream[i]
        return pltpu.make_async_copy(
            tiles_hbm.at[half, t], ring.at[i % slots_t], t_sem.at[i % slots_t]
        )

    def tile_start(i):
        half, t = stream[i]
        if (1, t) not in here:
            here.add((1, t))
            for k in (2 * t, 2 * t + 1):
                if k + slots_b >= parts:
                    part_keep(k).wait()
                    part_give(k).wait_send()
                part_got(k).wait_recv()
        tile_load(i).start()

    at_tile = [0]

    def next_tile():
        i = at_tile[0]
        tile_load(i).wait()
        return ring.at[i % slots_t]

    def done_tile():
        i = at_tile[0]
        if i + slots_t < len(stream):
            tile_start(i + slots_t)
        at_tile[0] = i + 1

    def mean(v):
        return jnp.sum(v, axis=-1, keepdims=True) / v.shape[-1]

    def normal(v):
        centred = v - mean(v)
        scale = lax.rsqrt(mean(centred * centred) + 1e-05)
        return centred * scale, scale

    def each(fn, step=32, init=0):
        def body(i, carry):
            return fn(pl.ds(pl.multiple_of(i * step, step), step), carry)

        return lax.fori_loop(0, length // step, body, init)

    def w_row(i):
        return vec_w[i : i + 1, :]

    def turn(source, m, block=0):
        def body(k, _):
            cols = pl.ds(pl.multiple_of(k * 256, 256), 256)
            rows = pl.ds(pl.multiple_of(2 * at_base[m] + block * width + k * 256, 256), 256)
            left[rows, :] = jnp.transpose(source[:, cols])
            return 0

        lax.fori_loop(0, width // 256, body, 0)

    NT = (((1,), (1,)), ((), ()))
    TN = (((0,), (0,)), ((), ()))

    def nt(a, b):
        return lax.dot_general(a, b, NT, preferred_element_type=F32)

    def tn(a, b):
        return lax.dot_general(a, b, TN, preferred_element_type=F32)

    def product_pair(source, write):
        first = next_tile()
        i = at_tile[0]
        at_tile[0] = i + 1
        second = next_tile()
        at_tile[0] = i

        def body(k, _):
            cols = pl.ds(pl.multiple_of(k * 256, 256), 256)
            value = jnp.dot(source[:, 0:half_w], first[:, cols], preferred_element_type=F32)
            value = value + jnp.dot(source[:, half_w:width], second[:, cols], preferred_element_type=F32)
            write(cols, value)
            return 0

        lax.fori_loop(0, UNIT_COLS // 256, body, 0)
        done_tile()
        done_tile()

    for i in range(slots_t):
        tile_start(i)
    small_copy(0, True).wait_send()
    small_copy(1, True).wait_send()
    small_copy(0, False).wait_recv()
    small_copy(1, False).wait_recv()

    def first_norm(rows, _):
        hat, _s = normal(x_in[rows, :].astype(F32))
        act[rows, :] = (hat * w_row(G1) + w_row(B1)).astype(BF16)
        return 0

    each(first_norm)
    for index in range(3):

        def put_qkv(cols, value, index=index):
            start = pl.multiple_of(index * width + cols.start, 256)
            if index == 0:
                value = value + vec_w[QB : QB + 1, cols]
            if index == 2:
                value = value + vec_w[VB : VB + 1, cols]
            qkv[:, pl.ds(start, 256)] = value.astype(BF16)

        product_pair(act, put_qkv)
    turn(act, 0)
    start_left(0)

    low_lane = lax.broadcasted_iota(jnp.int32, (length, 128), 1) < 64
    allowed = lax.broadcasted_iota(jnp.int32, (length, length), 1) <= lax.broadcasted_iota(
        jnp.int32, (length, length), 0
    )
    scale = 64 ** (-0.5)
    keep_lane = (low_lane.astype(F32).astype(BF16), jnp.logical_not(low_lane).astype(F32).astype(BF16))

    def attend(p, _):
        q = qkv[:, pl.ds(pl.multiple_of(p * 128, 128), 128)]
        k = qkv[:, pl.ds(pl.multiple_of(width + p * 128, 128), 128)]
        v = qkv[:, pl.ds(pl.multiple_of(2 * width + p * 128, 128), 128)]
        got = []
        for h in range(2):
            own = q * keep_lane[h]
            scores = jnp.where(allowed, nt(own, k) * scale, -1e30)
            top = jnp.max(scores, axis=-1, keepdims=True)
            lse = top + jnp.log(jnp.sum(jnp.exp(scores - top), axis=-1, keepdims=True))
            prob = jnp.exp(scores - lse)
            probs[2 * p + h] = prob
            got.append(jnp.dot(prob.astype(BF16), v, preferred_element_type=F32))
        cols = pl.ds(pl.multiple_of(p * 128, 128), 128)
        value = jnp.where(low_lane, got[0], got[1])
        attended[:, cols] = value
        act[:, cols] = (value * vec_w[HS : HS + 1, cols]).astype(BF16)
        return 0

    lax.fori_loop(0, width // 128, attend, 0)

    def put_branch(cols, value):
        branch[:, cols] = value + vec_w[OB : OB + 1, cols]

    product_pair(act, put_branch)
    turn(act, 1)
    start_left(1)

    def second_norm(rows, _):
        hat, _s = normal(branch[rows, :])
        mid = x_in[rows, :].astype(F32) + (hat * w_row(G2) + w_row(B2))
        middle[rows, :] = mid
        hat, _s = normal(mid)
        act[rows, :] = (hat * w_row(G3) + w_row(B3)).astype(BF16)
        return 0

    each(second_norm)
    U0, H0, D0 = 0, blocks * length, 2 * blocks * length
    for j in range(blocks):

        def put_hidden(cols, value, j=j):
            start = pl.multiple_of(j * width + cols.start, 256)
            big[U0 + j * length : U0 + (j + 1) * length, cols] = value + vec_h[UB : UB + 1, pl.ds(start, 256)]

        product_pair(act, put_hidden)
    turn(act, 2)
    start_left(2)
    root_half = 0.7071067811865476

    def near(base, start):
        return pl.ds(pl.multiple_of(base + start, 16), 16)

    def hidden_norm(rows, _):
        total = jnp.zeros((16, 1), F32)
        for j in range(blocks):
            u = big[near(U0 + j * length, rows.start), :]
            h = u * (1.0 + lax.erf(u * root_half)) * 0.5
            big[near(H0 + j * length, rows.start), :] = h
            total = total + jnp.sum(h, axis=-1, keepdims=True)
        centre = total / hidden
        total = jnp.zeros((16, 1), F32)
        for j in range(blocks):
            h = big[near(H0 + j * length, rows.start), :] - centre
            total = total + jnp.sum(h * h, axis=-1, keepdims=True)
        s = lax.rsqrt(total / hidden + 1e-05)
        rstd4[rows, :] = jnp.broadcast_to(s, (16, 128))
        for j in range(blocks):
            at_h = near(H0 + j * length, rows.start)
            hat = (big[at_h, :] - centre) * s
            big[at_h, :] = hat
            cols = slice(j * width, (j + 1) * width)
            hid[near(j * length, rows.start), :] = (
                hat * vec_h[G4 : G4 + 1, cols] + vec_h[B4 : B4 + 1, cols]
            ).astype(BF16)
        return 0

    each(hidden_norm, 16)
    for j in range(blocks):
        turn(hid.at[pl.ds(j * length, length), :], 3, j)
    start_left(3)

    tasks = []
    zeros8 = jnp.zeros((8, width), F32)
    dirs = g.at[pl.ds(0, length), :]

    def put_sum(row, value):
        line = jnp.sum(value, axis=0, keepdims=True)
        vec_in[0, row : row + 1, :] = line[:, 0:half_w]
        vec_in[1, row : row + 1, :] = line[:, half_w:width]

    def task_down(h, k):
        def run():
            w = next_tile()
            row = h * dims[3][0] + k * TILE
            j, lane = row // width, row % width
            if h == 0 and k == 0:
                y_acc[...] = middle[...] + w_row(DB)
            for n in range(TILE // 256):
                big[D0 + j * length : D0 + (j + 1) * length, lane + n * 256 : lane + (n + 1) * 256] = nt(
                    dirs[:, g_base[3] : g_base[3] + width], w[n * 256 : (n + 1) * 256, :]
                )

            def body(n, _):
                cols = pl.ds(pl.multiple_of(n * 256, 256), 256)
                y_acc[:, cols] += jnp.dot(
                    hid[j * length : (j + 1) * length, lane : lane + TILE], w[:, cols], preferred_element_type=F32
                )
                return 0

            lax.fori_loop(0, width // 256, body, 0)
            done_tile()
            if h == 1 and k == per_half - 1:
                y_out[...] = y_acc[...].astype(BF16)

        return run

    y_acc = dmid
    for h in range(2):
        for k in range(per_half):
            tasks.append((1.2, task_down(h, k)))

    def task_hidden(first, count):
        def run():
            if first == 0:
                sums4[...] = jnp.zeros_like(sums4)

                def e_sum(rows, carry):
                    return carry + fold(dirs[rows, g_base[3] : g_base[3] + width].astype(F32))

                put_sum(DB, each(e_sum, 32, zeros8))

            def body(i, _):
                at_r = pl.multiple_of(first + i * 16, 16)
                one = jnp.zeros((16, 1), F32)
                two = jnp.zeros((16, 1), F32)
                for j in range(blocks):
                    gain = vec_h[G4 : G4 + 1, j * width : (j + 1) * width]
                    d = big[near(D0 + j * length, at_r), :] * gain
                    hat = big[near(H0 + j * length, at_r), :]
                    one = one + jnp.sum(d, axis=-1, keepdims=True)
                    two = two + jnp.sum(d * hat, axis=-1, keepdims=True)
                one, two = one / hidden, two / hidden
                s = rstd4[pl.ds(at_r, 16), 0:1]
                for j in range(blocks):
                    cols = slice(j * width, (j + 1) * width)
                    da = big[near(D0 + j * length, at_r), :]
                    hat = big[near(H0 + j * length, at_r), :]
                    u = big[near(U0 + j * length, at_r), :]
                    dh = s * (da * vec_h[G4 : G4 + 1, cols] - one - hat * two)
                    slope = 0.5 * (1.0 + lax.erf(u * root_half)) + u * (jnp.exp(u * u * -0.5) * 0.3989422804014327)
                    du = (dh * slope).astype(BF16)
                    g[pl.ds(at_r, 16), g_base[2] + j * width : g_base[2] + (j + 1) * width] = du
                    sums4[0:8, cols] += fold(du.astype(F32))
                    sums4[8:16, cols] += fold(da * hat)
                    sums4[16:24, cols] += fold(da)
                return 0

            lax.fori_loop(0, count // 16, body, 0)
            if first + count == length:
                for i in range(3):
                    line = jnp.sum(sums4[8 * i : 8 * i + 8, :], axis=0, keepdims=True)
                    for n in range(hidden // half_w):
                        hh, k = divmod(n, half_h // half_w)
                        vec_in[hh, 11 + 4 * i + k : 12 + 4 * i + k, :] = line[:, n * half_w : (n + 1) * half_w]
                right_far(2).start()

        return run

    for first in range(0, length, 32):
        tasks.append((3.0, task_hidden(first, 32)))

    def add_pair(acc, index_of, cols_of, count, width_to):
        def make(index):
            def run():
                for h in range(2):
                    w = next_tile()
                    for n in range(TILE // 256):
                        cols = slice(h * half_w + n * 256, h * half_w + (n + 1) * 256)
                        value = nt(dirs[:, cols_of(index)], w[n * 256 : (n + 1) * 256, :])
                        if index == 0:
                            acc[:, cols] = value
                        else:
                            acc[:, cols] += value
                    done_tile()

            return run

        return [(1.2, make(index)) for index in range(count)]

    ends = {2: len(tasks)}
    acc = big.at[pl.ds(U0, length), :]
    tasks += add_pair(acc, None, lambda j: slice(g_base[2] + j * width, g_base[2] + (j + 1) * width), blocks, width)

    def task_norms():
        def body(rows, carry):
            s3g, s3b, s2g, s2b, sob = carry
            da = acc[rows, :]
            hat, s = normal(middle[rows, :])
            d = da * w_row(G3)
            d_mid = dirs[rows, g_base[3] : g_base[3] + width].astype(F32) + s * (d - mean(d) - hat * mean(d * hat))
            dmid[rows, :] = d_mid
            s3g, s3b = s3g + fold(da * hat), s3b + fold(da)
            hat, s = normal(branch[rows, :])
            d = d_mid * w_row(G2)
            dy = (s * (d - mean(d) - hat * mean(d * hat))).astype(BF16)
            s2g, s2b = s2g + fold(d_mid * hat), s2b + fold(d_mid)
            g[rows, g_base[1] : g_base[1] + width] = dy
            return (s3g, s3b, s2g, s2b, sob + fold(dy.astype(F32)))

        got = each(body, 16, (zeros8,) * 5)
        for row, value in zip((G3, B3, G2, B2, OB), got):
            put_sum(row, value)
        right_far(1).start()

    tasks.append((2.5, task_norms))
    ends[1] = len(tasks)
    d_mixed = big.at[pl.ds(U0 + length, length), :]
    tasks += add_pair(d_mixed, None, lambda j: slice(g_base[1], g_base[1] + width), 1, width)

    def task_heads():
        def body(rows, carry):
            d = d_mixed[rows, :]
            act[rows, :] = (d * w_row(HS)).astype(BF16)
            return carry + fold(d * attended[rows, :])

        put_sum(HS, each(body, 32, zeros8))

    tasks.append((0.6, task_heads))

    def task_attend(first, count):
        def run():
            def body(i, _):
                p = first + i
                q_cols = pl.ds(pl.multiple_of(p * 128, 128), 128)
                k_cols = pl.ds(pl.multiple_of(width + p * 128, 128), 128)
                v_cols = pl.ds(pl.multiple_of(2 * width + p * 128, 128), 128)
                q, k, v, do = qkv[:, q_cols], qkv[:, k_cols], qkv[:, v_cols], act[:, q_cols]
                dq, dk, dv = [], [], []
                for h in range(2):
                    prob = probs[2 * p + h]
                    own = do * keep_lane[h]
                    dv.append(tn(prob.astype(BF16), do))
                    dp = nt(own, v)
                    ds = prob * (dp - jnp.sum(prob * dp, axis=-1, keepdims=True))
                    ds = ds.astype(BF16)
                    dq.append(jnp.dot(ds, k, preferred_element_type=F32) * scale)
                    dk.append(tn(ds, q) * scale)
                for cols, value in ((q_cols, dq), (k_cols, dk), (v_cols, dv)):
                    low = jnp.where(low_lane, value[0], value[1]).astype(BF16)
                    g[0:length, cols] = low
                return 0

            lax.fori_loop(0, count, body, 0)
            if first + count == width // 128:

                def sums(rows, carry):
                    a, b = carry
                    return (
                        a + fold(g[rows, 0:width].astype(F32)),
                        b + fold(g[rows, 2 * width : 3 * width].astype(F32)),
                    )

                a, b = each(sums, 32, (zeros8, zeros8))
                put_sum(QB, a)
                put_sum(VB, b)
                right_far(0).start()

        return run

    for first in range(0, width // 128, 2):
        tasks.append((3.0, task_attend(first, 2)))
    ends[0] = len(tasks)
    d_first = big.at[pl.ds(U0 + 2 * length, length), :]
    tasks += add_pair(d_first, None, lambda j: slice(j * width, (j + 1) * width), 3, width)

    def task_last():
        def body(rows, carry):
            sg, sb = carry
            da = d_first[rows, :]
            hat, s = normal(x_in[rows, :].astype(F32))
            d = da * w_row(G1)
            dx_out[rows, :] = dmid[rows, :] + s * (d - mean(d) - hat * mean(d * hat))
            return (sg + fold(da * hat), sb + fold(da))

        sg, sb = each(body, 16, (zeros8, zeros8))
        put_sum(G1, sg)
        put_sum(B1, sb)
        vec_in[0, 23:24, :] = jnp.zeros((1, half_w), F32)
        vec_in[1, 23:24, :] = jnp.zeros((1, half_w), F32)
        vec_copy(0).start()

    tasks.append((1.5, task_last))

    vec_steps = (core, to["X"], to["Y"], {"rep": r + 4 * (1 - 2 * (z % 2))}, across)

    def vec_copy(step):
        source = vec_in.at[1 - c] if step == 0 else vec_own.at[step]
        return pltpu.make_async_remote_copy(
            src_ref=source, dst_ref=vec_got.at[step], send_sem=v_send.at[step], recv_sem=v_recv.at[step],
            device_id=vec_steps[step], device_id_type=MESH,
        )

    def vec_task(k):
        vec_copy(k).wait_recv()
        total = (vec_in[c] if k == 0 else vec_own[k]) + vec_got[k]
        if k < 4:
            vec_own[k + 1] = total
            vec_copy(k + 1).start()
        else:
            vec_out[...] = total

    units = unit_table(dims)
    kinds = KINDS
    xy_at, z_at = {}, {}
    for unit, kind in enumerate(kinds):
        (z_at if kind[0] == "Z" else xy_at)[unit] = len(z_at) if kind[0] == "Z" else len(xy_at)

    def copy(unit, name, source, dest, device):
        return functools.partial(
            pltpu.make_async_remote_copy,
            src_ref=source, dst_ref=dest, send_sem=send.at[unit], recv_sem=recv.at[unit, SLOT[name]],
            device_id=device, device_id_type=MESH,
        )

    def rows_of(unit, start, count):
        if not isinstance(start, int):
            start = pl.multiple_of(start, 16)
        return res.at[unit, pl.ds(start, count), :]

    def product(unit, start, count, dest, dest_start, got=None, got_start=0):
        m, row, col = units[unit]
        step = 128 if count % 128 == 0 else min(count, 64)

        def block(index, _):
            part, strip = index // (UNIT_COLS // 256), index % (UNIT_COLS // 256)
            cols = pl.ds(pl.multiple_of(strip * 256, 256), 256)
            value = jnp.dot(
                at[pl.ds(pl.multiple_of(at_base[m] + row + start + part * step, 16), step), :],
                g[:, pl.ds(pl.multiple_of(g_base[m] + col + strip * 256, 256), 256)],
                preferred_element_type=F32,
            )
            if got is not None:
                value = value + got[pl.ds(pl.multiple_of(got_start + part * step, 16), step), cols].astype(F32)
            dest[pl.ds(pl.multiple_of(dest_start + part * step, 16), step), cols] = value.astype(BF16)
            return 0

        lax.fori_loop(0, (count // step) * (UNIT_COLS // 256), block, 0)

    def accumulate(unit, start, count, got, got_start, dest, dest_start):
        def block(strip, _):
            cols = pl.ds(pl.multiple_of(strip * 256, 256), 256)
            value = res[unit, pl.ds(pl.multiple_of(start, 16), count), cols].astype(F32)
            value = value + got[pl.ds(pl.multiple_of(got_start, 16), count), cols].astype(F32)
            dest[pl.ds(pl.multiple_of(dest_start, 16), count), cols] = value.astype(BF16)
            return 0

        lax.fori_loop(0, UNIT_COLS // 256, block, 0)

    def gather_line(unit, base, size, level):
        up, down = "u%d" % level, "w%d" % level
        low, high = z - (level - 1), z + (level - 1)

        @pl.when((low >= 0) & (z < 3))
        def _():
            part = rows_of(unit, base + low * size, size)
            copy(unit, up, part, part, to["U"])().start()

        @pl.when((high <= 3) & (z > 0))
        def _():
            part = rows_of(unit, base + high * size, size)
            copy(unit, down, part, part, to["D"])().start()

    def gather_arrived(unit, base, size, level):
        def wait(chunks):
            part = give.at[pl.ds(0, chunks * size), :]
            copy(unit, "u%d" % level, part, part, to["U"])().wait_recv()

        if level == 1:
            pl.when(line_mid)(lambda: wait(2))
        if level == 2:
            wait(1)
        else:
            pl.when(line_end)(lambda: wait(1))

    def finish(unit, ends, mids):
        def wait(rows):
            part = give.at[pl.ds(0, rows), :]
            copy(unit, "d1", part, part, to["X"])().wait_send()

        pl.when(line_end)(lambda: wait(ends))
        pl.when(line_mid)(lambda: wait(mids))

    def task_xy(unit, step):
        half, quarter, size = UNIT_ROWS // 2, UNIT_ROWS // 4, UNIT_ROWS // 16
        first, second = ("X", "Y") if kinds[unit] == "X" else ("Y", "X")
        p, q = (x, y) if kinds[unit] == "X" else (y, x)
        line, block, out, other = line_xy.at[xy_at[unit]], res.at[unit], give.at[pl.ds(unit * GIVE_ROWS, GIVE_ROWS), :], pair.at[unit]
        keep, away_half = p * half, (1 - p) * half
        base = keep + q * quarter
        away = keep + (1 - q) * quarter
        at_z = half + quarter
        d1 = copy(unit, "d1", out.at[pl.ds(0, half), :], rows_of(unit, away_half, half), to[first])
        d2 = copy(unit, "d2", out.at[pl.ds(half, quarter), :], other.at[pl.ds(0, quarter), :], to[second])
        z1 = copy(unit, "z1", out.at[pl.ds(at_z, 3 * size), :], line.at[pl.ds(0, 3 * size), :], inward)
        z2 = copy(unit, "z2", out.at[pl.ds(at_z, 2 * size), :], line.at[pl.ds(3 * size, 2 * size), :], across)
        z3 = copy(unit, "z3", out.at[pl.ds(at_z + 2 * size, size), :], line.at[pl.ds(0, size), :], outward)
        own_quarter = rows_of(unit, base, quarter)
        g2 = copy(unit, "g2", own_quarter, own_quarter, to[second])
        own_half = rows_of(unit, keep, half)
        g1 = copy(unit, "g1", own_half, own_half, to[first])
        own = base + z * size
        if step == 0:
            product(unit, away_half, half, out, 0)
            d1().start()
        elif step == 1:
            d1().wait_recv()
            product(unit, away, quarter, out, half, block, away)
            d2().start()
            product(unit, base, quarter, block, base, block, base)
        elif step == 2:
            d2().wait_recv()

            @pl.when(line_end)
            def _():
                skip = (1 - upper) * size
                accumulate(unit, base + skip, 3 * size, other, skip, out, at_z)
                z1().start()
                accumulate(unit, own, size, other, z * size, block, own)

            @pl.when(line_mid)
            def _():
                accumulate(unit, base, quarter, other, 0, block, base)

        elif step == 3:

            @pl.when(line_mid)
            def _():
                z1().wait_recv()
                accumulate(unit, base + (1 - upper) * 2 * size, 2 * size, line, (1 - upper) * size, out, at_z)
                z2().start()
                accumulate(unit, own, size, line, upper * 2 * size, block, own)

        elif step == 4:

            @pl.when(line_mid)
            def _():
                z2().wait_recv()
                accumulate(unit, base + upper * 3 * size, size, line, (3 + upper) * size, out, at_z + 2 * size)
                z3().start()
                accumulate(unit, own, size, line, (4 - upper) * size, block, own)
                gather_line(unit, base, size, 1)

        elif step == 5:

            @pl.when(line_end)
            def _():
                z3().wait_recv()
                accumulate(unit, own, size, line, 0, block, own)
                gather_line(unit, base, size, 1)

        elif step in (6, 7):
            gather_arrived(unit, base, size, step - 5)
            gather_line(unit, base, size, step - 4)
        elif step == 8:
            gather_arrived(unit, base, size, 3)
            g2().start()
        elif step == 9:
            g2().wait_recv()
            g1().start()
        else:
            g1().wait_recv()
            finish(unit, 2 * half + 2 * quarter + 4 * size, 2 * half + 2 * quarter + 8 * size)

    def task_z(unit, step):
        size, half, quarter = UNIT_ROWS // 4, UNIT_ROWS // 8, UNIT_ROWS // 16
        first, second = ("X", "Y") if kinds[unit] == "ZX" else ("Y", "X")
        p, q = (x, y) if kinds[unit] == "ZX" else (y, x)
        line, block, out, other = line_z.at[z_at[unit]], res.at[unit], give.at[pl.ds(unit * GIVE_ROWS, GIVE_ROWS), :], pair.at[unit]
        own = z * size
        keep, away_half = own + p * half, own + (1 - p) * half
        base, away = keep + q * quarter, keep + (1 - q) * quarter
        at_d = 3 * size
        z1 = copy(unit, "z1", out.at[pl.ds(0, 3 * size), :], line.at[pl.ds(0, 3 * size), :], inward)
        z2 = copy(unit, "z2", out.at[pl.ds(0, 2 * size), :], line.at[pl.ds(3 * size, 2 * size), :], across)
        z3 = copy(unit, "z3", out.at[pl.ds(2 * size, size), :], line.at[pl.ds(0, size), :], outward)
        d1 = copy(unit, "d1", out.at[pl.ds(at_d, half), :], other.at[pl.ds(0, half), :], to[first])
        d2 = copy(unit, "d2", out.at[pl.ds(at_d + half, quarter), :], other.at[pl.ds(half, quarter), :], to[second])
        own_quarter = rows_of(unit, base, quarter)
        g2 = copy(unit, "g2", own_quarter, own_quarter, to[second])
        own_half = rows_of(unit, keep, half)
        g1 = copy(unit, "g1", own_half, own_half, to[first])
        if step == 0:

            @pl.when(line_end)
            def _():
                product(unit, (1 - upper) * size, 3 * size, out, 0)
                z1().start()

        elif step == 1:

            @pl.when(line_mid)
            def _():
                z1().wait_recv()
                product(unit, (1 - upper) * 2 * size, 2 * size, out, 0, line, (1 - upper) * size)
                z2().start()
                product(unit, own, size, block, own, line, upper * 2 * size)

        elif step == 2:

            @pl.when(line_mid)
            def _():
                z2().wait_recv()
                product(unit, upper * 3 * size, size, out, 2 * size, line, (3 + upper) * size)
                z3().start()
                got = (4 - upper) * size
                accumulate(unit, away_half, half, line, got + (1 - p) * half, out, at_d)
                d1().start()
                accumulate(unit, keep, half, line, got + p * half, block, keep)

        elif step == 3:

            @pl.when(line_end)
            def _():
                z3().wait_recv()
                product(unit, away_half, half, out, at_d, line, (1 - p) * half)
                d1().start()
                product(unit, keep, half, block, keep, line, p * half)

        elif step == 4:
            d1().wait_recv()
            accumulate(unit, away, quarter, other, (1 - q) * quarter, out, at_d + half)
            d2().start()
            accumulate(unit, base, quarter, other, q * quarter, block, base)
        elif step == 5:
            d2().wait_recv()
            accumulate(unit, base, quarter, other, half, block, base)
            g2().start()
        elif step == 6:
            g2().wait_recv()
            g1().start()
        elif step == 7:
            g1().wait_recv()
            gather_line(unit, 0, size, 1)
        elif step in (8, 9):
            gather_arrived(unit, 0, size, step - 7)
            gather_line(unit, 0, size, step - 6)
        else:
            gather_arrived(unit, 0, size, 3)
            finish(unit, 2 * half + 2 * quarter + 4 * size, 2 * half + 2 * quarter + 8 * size)


    for kind, a, b in program_order(units, ends):
        if kind == "task":
            tasks[a][1]()
        elif kind == "wait":
            wait_pair(a)
        elif kind == "vec":
            vec_task(a)
        elif kinds[a][0] == "Z":
            task_z(a, b)
        else:
            task_xy(a, b)
    for step in range(5):
        vec_copy(step).wait_send()


def whole_layer(layer_input, cotangent, weights, params):
    dims = tuple(w.shape for w in weights)
    at_rows = sum(rows for rows, _ in dims)
    g_cols = sum(cols for _, cols in dims)
    at_base = [sum(rows for rows, _ in dims[:m]) for m in range(4)]
    g_base = [sum(cols for _, cols in dims[:m]) for m in range(4)]
    length, width = layer_input.shape
    hidden = dims[2][1]
    blocks = hidden // width
    units = unit_table(dims)
    kinds = KINDS
    n, n_z = len(units), sum(kind[0] == "Z" for kind in kinds)
    tiles = n // 2
    hbm = pl.BlockSpec(memory_space=pl.ANY)
    vmem = pl.BlockSpec(memory_space=pltpu.VMEM)
    dma = pltpu.SemaphoreType.DMA
    small = (24, width // 2)
    got = pl.pallas_call(
        functools.partial(layer_kernel, dims, at_base, g_base),
        out_shape=[
            pltpu.VMEM((length, width), BF16),
            pltpu.VMEM((length, width), F32),
            pltpu.VMEM((n, UNIT_ROWS, UNIT_COLS), BF16),
            pltpu.VMEM(small, F32),
            jax.ShapeDtypeStruct((2, tiles, 512, UNIT_COLS), BF16),
        ],
        in_specs=[vmem, hbm] + [hbm] * 4 + [vmem] * 13,
        out_specs=[vmem] * 4 + [hbm],
        scratch_shapes=[
            pltpu.VMEM((at_rows, 2 * length), BF16),
            pltpu.VMEM((2 * length, g_cols), BF16),
            pltpu.VMEM((n * GIVE_ROWS, UNIT_COLS), BF16),
            pltpu.VMEM((n, UNIT_ROWS // 4, UNIT_COLS), BF16),
            pltpu.VMEM((n - n_z, 5 * UNIT_ROWS // 16, UNIT_COLS), BF16),
            pltpu.VMEM((n_z, 5 * UNIT_ROWS // 4, UNIT_COLS), BF16),
            pltpu.VMEM((4, 512, UNIT_COLS), BF16),
            pltpu.VMEM((3 * blocks * length, width), F32),
            pltpu.VMEM((2 * at_rows, length), BF16),
            pltpu.VMEM((length, width), BF16),
            pltpu.VMEM((blocks * length, width), BF16),
            pltpu.VMEM((length, 3 * width), BF16),
            pltpu.VMEM((width // 64, length, length), F32),
            pltpu.VMEM((length, width), F32),
            pltpu.VMEM((length, width), F32),
            pltpu.VMEM((length, width), F32),
            pltpu.VMEM((length, width), F32),
            pltpu.VMEM((16, width), F32),
            pltpu.VMEM((8, hidden), F32),
            pltpu.VMEM((length, 128), F32),
            pltpu.VMEM((24, hidden), F32),
            pltpu.VMEM((2,) + small, F32),
            pltpu.VMEM((5,) + small, F32),
            pltpu.VMEM((5,) + small, F32),
            dma((n,)),
            dma((n, 9)),
            dma((5,)),
            dma((5,)),
            dma((4, 2)),
            dma((4, 2)),
            dma((4,)),
            dma((6,)),
            dma((16,)),
            dma((16,)),
            dma((2 * tiles,)),
            dma((4,)),
            dma((2, 2)),
            dma((1,)),
        ],
        compiler_params=pltpu.CompilerParams(
            collective_id=0, has_side_effects=True, vmem_limit_bytes=50 * MIB
        ),
        name="whole_layer",
    )(layer_input, cotangent, *weights, *params)
    return got[:4]


def finish_kernel(dims, *refs):
    y_in, dx_in, res, vec = refs[0:4]
    y_out, dx_out, outs, smalls = refs[4], refs[5], refs[6:10], refs[10:23]
    wide, lines, o_sem, s_sem = refs[23], refs[24:37], refs[37], refs[38]
    slots = wide.shape[0]
    copies = [pltpu.make_async_copy(y_in, y_out, s_sem.at[13]), pltpu.make_async_copy(dx_in, dx_out, s_sem.at[14])]
    rows_of = [range(0, 2)] + [range(k, k + 1) for k in range(2, 11)] + [range(11 + 4 * k, 15 + 4 * k) for k in range(3)]
    for k, rows in enumerate(rows_of):
        if len(rows) == 4:
            for j, row in enumerate(rows):
                lines[k][:, j * vec.shape[1] : (j + 1) * vec.shape[1]] = vec[row : row + 1, :]
        else:
            lines[k][...] = vec[rows.start : rows.stop, :]
        copies.append(pltpu.make_async_copy(lines[k], smalls[k], s_sem.at[k]))
    for piece in copies:
        piece.start()
    units = unit_table(dims)

    def put(unit):
        m, row, col = units[unit]
        return pltpu.make_async_copy(
            wide.at[unit % slots], outs[m].at[pl.ds(row, UNIT_ROWS), pl.ds(col, UNIT_COLS)], o_sem.at[unit % slots]
        )

    for unit in range(len(units)):
        if unit >= slots:
            put(unit - slots).wait()

        def widen(b, _, unit=unit):
            rows = pl.ds(pl.multiple_of(b * 32, 32), 32)
            wide[unit % slots, rows, :] = res[unit, rows, :].astype(F32)
            return 0

        lax.fori_loop(0, UNIT_ROWS // 32, widen, 0)
        put(unit).start()
    for unit in range(len(units) - slots, len(units)):
        put(unit).wait()
    for piece in copies:
        piece.wait()


def write_results(got, dims):
    y, dx, _, vec = got
    half = vec.shape[1]
    small = [(2, half)] + [(1, half)] * 9 + [(1, 4 * half)] * 3
    hbm = pl.BlockSpec(memory_space=pl.ANY)
    vmem = pl.BlockSpec(memory_space=pltpu.VMEM)
    dma = pltpu.SemaphoreType.DMA
    return pl.pallas_call(
        functools.partial(finish_kernel, dims),
        out_shape=[jax.ShapeDtypeStruct(y.shape, BF16), jax.ShapeDtypeStruct(dx.shape, F32)]
        + [jax.ShapeDtypeStruct(d, F32) for d in dims]
        + [jax.ShapeDtypeStruct(s, F32) for s in small],
        in_specs=[vmem] * 4,
        out_specs=[hbm] * 19,
        scratch_shapes=[pltpu.VMEM((6, UNIT_ROWS, UNIT_COLS), F32)]
        + [pltpu.VMEM(s, F32) for s in small]
        + [dma((6,)), dma((15,))],
        compiler_params=pltpu.CompilerParams(vmem_limit_bytes=30 * MIB),
        name="write_results",
    )(*got)


def on_pair_of_cores(
    layer_input, cotangent, w_qkv, qv_bias, w_out, out_bias, head_scale, ln1_gain, ln1_bias, ln2_gain, ln2_bias,
    ln3_gain, ln3_bias, w_fc1, fc1_bias, ln4_gain, ln4_bias, w_fc2, fc2_bias,
):
    params = (
        qv_bias, out_bias, jnp.repeat(head_scale, HEAD_DIM), ln1_gain, ln1_bias, ln2_gain, ln2_bias, ln3_gain, ln3_bias,
        fc1_bias, ln4_gain, ln4_bias, fc2_bias,
    )
    params = [p.reshape(-1, p.shape[-1]) for p in params]
    weights = (w_qkv, w_out, w_fc1, w_fc2)
    got = whole_layer(layer_input, cotangent, weights, params)
    output, grad_input, qkv, out, up, down, *smalls = write_results(got, tuple(w.shape for w in weights))
    heads = smalls[2].reshape(-1, HEAD_DIM).sum(axis=-1)
    rows = [s.reshape(-1) for s in smalls]
    return (
        output, grad_input, qkv, smalls[0], out, rows[1], heads, rows[3], rows[4], rows[5], rows[6], rows[7], rows[8], up,
        rows[10], rows[11], rows[12], down, rows[9],
    )


def fits_pair(mesh):
    return mesh.shape["shard"] == 2 and mesh.shape["rep"] == 16


def solution(mesh):
    return jax.shard_map(
        on_pair_of_cores if fits_pair(mesh) else on_any_mesh,
        mesh=mesh,
        in_specs=(
            P(("rep", "shard"), None),
            P(("rep", "shard"), None),
            P("shard", None),
            P(None, "shard"),
            P("shard", None),
            P("shard"),
            P("shard"),
            P("shard"),
            P("shard"),
            P("shard"),
            P("shard"),
            P("shard"),
            P("shard"),
            P("shard", None),
            P("shard"),
            P("shard"),
            P("shard"),
            P("shard", None),
            P("shard"),
        ),
        out_specs=(
            P(("rep", "shard"), None),
            P(("rep", "shard"), None),
            P("shard", None),
            P(None, "shard"),
            P("shard", None),
            P("shard"),
            P("shard"),
            P("shard"),
            P("shard"),
            P("shard"),
            P("shard"),
            P("shard"),
            P("shard"),
            P("shard", None),
            P("shard"),
            P("shard"),
            P("shard"),
            P("shard", None),
            P("shard"),
        ),
        check_vma=False,
    )
```

```python
import functools

import jax
import jax.numpy as jnp
from jax import lax
from jax.experimental import pallas as pl
from jax.experimental.pallas import tpu as pltpu
from jax.sharding import PartitionSpec as P

D = 1024
HEADS = 16
HEAD_DIM = 64


EPS = 1e-05
NEG = -1e30


def norm_rows(v, gain, bias):
    centre = jnp.mean(v, axis=-1, keepdims=True)
    centred = v - centre
    spread = jnp.mean(centred * centred, axis=-1, keepdims=True)
    return centred * lax.rsqrt(spread + EPS) * gain + bias


def ffn_middle(hidden, gain, bias):
    return norm_rows(jax.nn.gelu(hidden, approximate=False), gain, bias)


def causal_mask(index, qblock, length):
    rows = index * qblock + lax.iota(jnp.int32, qblock)
    cols = lax.iota(jnp.int32, length)
    return (cols[None, :] <= rows[:, None])[None]


def block_scores(queries, keys_all, index, qblock, scale):
    length = keys_all.shape[0]
    scores = (
        jnp.einsum("qhd,khd->hqk", queries, keys_all, preferred_element_type=jnp.float32) * scale
    )
    return (queries, jnp.where(causal_mask(index, qblock, length), scores, NEG))


def attend_forward(queries, keys_all, values_all, scale):
    length, heads, width = queries.shape
    qblock = min(512, length)
    blocks = length // qblock

    def one_block(index):
        rows_q, scores = block_scores(queries, keys_all, index, qblock, scale)
        total = jax.nn.logsumexp(scores, axis=-1, keepdims=True)
        probs = jnp.exp(scores - total).astype(jnp.bfloat16)
        outcome = jnp.einsum("hqk,khd->qhd", probs, values_all, preferred_element_type=jnp.float32)
        return (outcome, total)

    outcome, totals = lax.map(one_block, jnp.arange(blocks, dtype=jnp.int32))
    return (outcome.reshape(length, heads, width), totals)


def attend_backward(queries, keys_all, values_all, totals, grad_out, scale):
    length, heads, width = queries.shape
    qblock = min(512, length)
    blocks = length // qblock

    def one_block(carry, index):
        grad_keys, grad_values = carry
        rows_q, scores = block_scores(queries, keys_all, index, qblock, scale)
        probs = jnp.exp(scores - totals[index])
        probs_low = probs.astype(jnp.bfloat16)
        grad_values = grad_values + jnp.einsum(
            "hqk,qhd->khd", probs_low, grad_out, preferred_element_type=jnp.float32
        )
        grad_probs = jnp.einsum(
            "qhd,khd->hqk", grad_out, values_all, preferred_element_type=jnp.float32
        )
        row_dot = jnp.sum(probs * grad_probs, axis=-1, keepdims=True)
        grad_scores = (probs * (grad_probs - row_dot)).astype(jnp.bfloat16)
        grad_rows = (
            jnp.einsum("hqk,khd->qhd", grad_scores, keys_all, preferred_element_type=jnp.float32)
            * scale
        )
        grad_keys = (
            grad_keys
            + jnp.einsum("hqk,qhd->khd", grad_scores, rows_q, preferred_element_type=jnp.float32)
            * scale
        )
        return ((grad_keys, grad_values), grad_rows)

    empty = jnp.zeros((length, heads, width), jnp.float32)
    (grad_keys, grad_values), grad_queries = lax.scan(
        one_block, (empty, empty), jnp.arange(blocks, dtype=jnp.int32)
    )
    return (grad_queries.reshape(length, heads, width), grad_keys, grad_values)


def on_any_mesh(
    layer_input,
    cotangent,
    w_qkv,
    qv_bias,
    w_out,
    out_bias,
    head_scale,
    ln1_gain,
    ln1_bias,
    ln2_gain,
    ln2_bias,
    ln3_gain,
    ln3_bias,
    w_fc1,
    fc1_bias,
    ln4_gain,
    ln4_bias,
    w_fc2,
    fc2_bias,
):
    low_qkv = w_qkv.astype(jnp.bfloat16)
    low_out = w_out.astype(jnp.bfloat16)
    low_heads = head_scale.astype(jnp.bfloat16)
    low_up = w_fc1.astype(jnp.bfloat16)
    low_down = w_fc2.astype(jnp.bfloat16)
    whole = (
        lax.all_gather(low_qkv, "shard", axis=0, tiled=True),
        lax.all_gather(qv_bias.astype(jnp.bfloat16), "shard", axis=1, tiled=True),
        lax.all_gather(low_out, "shard", axis=0, tiled=True),
        lax.all_gather(out_bias.astype(jnp.bfloat16), "shard", axis=0, tiled=True),
        lax.all_gather(low_heads, "shard", axis=0, tiled=True),
        lax.all_gather(ln1_gain.astype(jnp.bfloat16), "shard", axis=0, tiled=True),
        lax.all_gather(ln1_bias.astype(jnp.bfloat16), "shard", axis=0, tiled=True),
        lax.all_gather(ln2_gain.astype(jnp.bfloat16), "shard", axis=0, tiled=True),
        lax.all_gather(ln2_bias.astype(jnp.bfloat16), "shard", axis=0, tiled=True),
        lax.all_gather(ln3_gain.astype(jnp.bfloat16), "shard", axis=0, tiled=True),
        lax.all_gather(ln3_bias.astype(jnp.bfloat16), "shard", axis=0, tiled=True),
        lax.all_gather(low_up, "shard", axis=0, tiled=True),
        lax.all_gather(fc1_bias.astype(jnp.bfloat16), "shard", axis=0, tiled=True),
        lax.all_gather(ln4_gain.astype(jnp.bfloat16), "shard", axis=0, tiled=True),
        lax.all_gather(ln4_bias.astype(jnp.bfloat16), "shard", axis=0, tiled=True),
        lax.all_gather(low_down, "shard", axis=0, tiled=True),
        lax.all_gather(fc2_bias.astype(jnp.bfloat16), "shard", axis=0, tiled=True),
    )
    weight_qkv, weight_out, weight_up, weight_down = (whole[0], whole[2], whole[11], whole[15])
    (
        bias_qv,
        bias_out,
        head_gain,
        gain_one,
        shift_one,
        gain_two,
        shift_two,
        gain_three,
        shift_three,
        bias_up,
        gain_four,
        shift_four,
        bias_down,
    ) = tuple(
        (whole[index].astype(jnp.float32) for index in (1, 3, 4, 5, 6, 7, 8, 9, 10, 12, 13, 14, 16))
    )
    length = layer_input.shape[0]
    scale = HEAD_DIM ** (-0.5)
    inputs = layer_input.astype(jnp.float32)
    normed_one, pull_one = jax.vjp(norm_rows, inputs, gain_one, shift_one)
    act_one = normed_one.astype(jnp.bfloat16)
    bias_full = jnp.concatenate([bias_qv[0], jnp.zeros((D,), jnp.float32), bias_qv[1]])
    qkv = (jnp.dot(act_one, weight_qkv, preferred_element_type=jnp.float32) + bias_full).astype(
        jnp.bfloat16
    )
    triple = qkv.reshape(length, 3, HEADS, HEAD_DIM)
    queries = triple[:, 0]
    keys_all = triple[:, 1]
    values_all = triple[:, 2]
    attended, totals = attend_forward(queries, keys_all, values_all, scale)
    mixed = (attended * head_gain[:, None]).reshape(length, D).astype(jnp.bfloat16)
    branch = jnp.dot(mixed, weight_out, preferred_element_type=jnp.float32) + bias_out
    normed_two, pull_two = jax.vjp(norm_rows, branch, gain_two, shift_two)
    middle = inputs + normed_two
    normed_three, pull_three = jax.vjp(norm_rows, middle, gain_three, shift_three)
    act_three = normed_three.astype(jnp.bfloat16)
    hidden = jnp.dot(act_three, weight_up, preferred_element_type=jnp.float32) + bias_up
    normed_four, pull_four = jax.vjp(ffn_middle, hidden, gain_four, shift_four)
    act_four = normed_four.astype(jnp.bfloat16)
    result = middle + (
        jnp.dot(act_four, weight_down, preferred_element_type=jnp.float32) + bias_down
    )
    output = result.astype(jnp.bfloat16)
    again = (
        lax.all_gather(low_qkv, "shard", axis=0, tiled=True),
        lax.all_gather(low_out, "shard", axis=0, tiled=True),
        lax.all_gather(low_heads, "shard", axis=0, tiled=True),
        lax.all_gather(low_up, "shard", axis=0, tiled=True),
        lax.all_gather(low_down, "shard", axis=0, tiled=True),
    )
    back_qkv, back_out, back_up, back_down = (again[0], again[1], again[3], again[4])
    back_heads = again[2].astype(jnp.float32)
    cot_full = cotangent.astype(jnp.float32)
    grad_down_bias = jnp.sum(cot_full, axis=0)
    grad_down = jnp.einsum("tf,td->fd", act_four, cotangent, preferred_element_type=jnp.float32)
    grad_four = jnp.einsum("td,fd->tf", cotangent, back_down, preferred_element_type=jnp.float32)
    grad_hidden, grad_gain_four, grad_shift_four = pull_four(grad_four)
    hidden_low = grad_hidden.astype(jnp.bfloat16)
    grad_up_bias = jnp.sum(hidden_low, axis=0, dtype=jnp.float32)
    grad_up = jnp.einsum("td,tf->df", act_three, hidden_low, preferred_element_type=jnp.float32)
    grad_three = jnp.einsum("tf,df->td", hidden_low, back_up, preferred_element_type=jnp.float32)
    grad_mid_part, grad_gain_three, grad_shift_three = pull_three(grad_three)
    grad_middle = cot_full + grad_mid_part
    grad_branch, grad_gain_two, grad_shift_two = pull_two(grad_middle)
    branch_low = grad_branch.astype(jnp.bfloat16)
    grad_out_b = jnp.sum(branch_low, axis=0, dtype=jnp.float32)
    grad_out_w = jnp.einsum("td,te->de", mixed, branch_low, preferred_element_type=jnp.float32)
    grad_mixed = jnp.einsum("te,de->td", branch_low, back_out, preferred_element_type=jnp.float32)
    grad_mixed = grad_mixed.reshape(length, HEADS, HEAD_DIM)
    grad_heads = jnp.sum(grad_mixed * attended, axis=(0, 2))
    grad_attended = (grad_mixed * back_heads[:, None]).astype(jnp.bfloat16)
    grad_queries, grad_keys, grad_values = attend_backward(
        queries, keys_all, values_all, totals, grad_attended, scale
    )
    grad_qkv = (
        jnp.stack([grad_queries, grad_keys, grad_values], axis=1)
        .reshape(length, 3 * D)
        .astype(jnp.bfloat16)
    )
    grad_qv = jnp.stack(
        [
            jnp.sum(grad_qkv[:, :D], axis=0, dtype=jnp.float32),
            jnp.sum(grad_qkv[:, 2 * D :], axis=0, dtype=jnp.float32),
        ]
    )
    grad_qkv_w = jnp.einsum("td,te->de", act_one, grad_qkv, preferred_element_type=jnp.float32)
    grad_one = jnp.einsum("te,de->td", grad_qkv, back_qkv, preferred_element_type=jnp.float32)
    grad_in_part, grad_gain_one, grad_shift_one = pull_one(grad_one)
    grad_input = grad_middle + grad_in_part
    shares = (
        lax.psum_scatter(grad_qkv_w, "shard", scatter_dimension=0, tiled=True),
        lax.psum_scatter(grad_qv, "shard", scatter_dimension=1, tiled=True),
        lax.psum_scatter(grad_out_w, "shard", scatter_dimension=0, tiled=True),
        lax.psum_scatter(grad_out_b, "shard", scatter_dimension=0, tiled=True),
        lax.psum_scatter(grad_heads, "shard", scatter_dimension=0, tiled=True),
        lax.psum_scatter(grad_gain_one, "shard", scatter_dimension=0, tiled=True),
        lax.psum_scatter(grad_shift_one, "shard", scatter_dimension=0, tiled=True),
        lax.psum_scatter(grad_gain_two, "shard", scatter_dimension=0, tiled=True),
        lax.psum_scatter(grad_shift_two, "shard", scatter_dimension=0, tiled=True),
        lax.psum_scatter(grad_gain_three, "shard", scatter_dimension=0, tiled=True),
        lax.psum_scatter(grad_shift_three, "shard", scatter_dimension=0, tiled=True),
        lax.psum_scatter(grad_up, "shard", scatter_dimension=0, tiled=True),
        lax.psum_scatter(grad_up_bias, "shard", scatter_dimension=0, tiled=True),
        lax.psum_scatter(grad_gain_four, "shard", scatter_dimension=0, tiled=True),
        lax.psum_scatter(grad_shift_four, "shard", scatter_dimension=0, tiled=True),
        lax.psum_scatter(grad_down, "shard", scatter_dimension=0, tiled=True),
        lax.psum_scatter(grad_down_bias, "shard", scatter_dimension=0, tiled=True),
    )
    summed = lax.psum(
        (
            shares[0],
            shares[1],
            shares[2],
            shares[3],
            shares[4],
            shares[5],
            shares[6],
            shares[7],
            shares[8],
            shares[9],
            shares[10],
            shares[11],
            shares[12],
            shares[13],
            shares[14],
            shares[15],
            shares[16],
        ),
        "rep",
    )
    return (output, grad_input) + tuple(summed)


MESH = pl.DeviceIdType.MESH
BF16 = jnp.bfloat16
F32 = jnp.float32
UNIT_ROWS = 256
UNIT_COLS = 1024
MIB = 1 << 20
SLOT = {
    "d1": 0, "d2": 1, "z1": 2, "z3": 2, "z2": 3, "u1": 4, "w1": 4, "u2": 5, "w2": 5, "u3": 6, "w3": 6, "g1": 7, "g2": 8,
}


def unit_table(dims):
    table = []
    for matrix in (3, 2, 1, 0):
        rows, cols = dims[matrix]
        for col in range(0, cols, UNIT_COLS):
            for row in range(0, rows, UNIT_ROWS):
                table.append((matrix, row, col))
    return table


KINDS = (
    "X", "ZY", "ZY", "Y", "X", "Y", "X", "Y", "ZY", "X", "Y", "Y", "X", "Y", "ZY", "X", "ZY", "X", "X", "Y",
    "X", "Y", "X", "ZY",
)
TASK, VECTORS = 24, 25
ORDER = (
    0, 7, 1, 6, 24, 24, 24, 24, 5, 24, 24, 24, 24, 24, 2, 3, 4, 24, 24, 24, 24, 7, 1, 24, 0, 9, 14, 24, 6, 5, 4,
    10, 24, 24, 2, 0, 24, 7, 24, 3, 17, 4, 11, 24, 14, 24, 15, 3, 5, 8, 9, 1, 10, 24, 4, 6, 24, 7, 3, 17, 0, 11,
    1, 21, 2, 4, 12, 14, 5, 0, 7, 15, 8, 1, 10, 11, 24, 9, 17, 3, 2, 13, 18, 5, 11, 0, 4, 14, 21, 24, 20, 7, 8,
    5, 24, 15, 3, 6, 11, 17, 9, 7, 16, 1, 6, 4, 19, 2, 15, 3, 17, 14, 13, 12, 5, 6, 17, 9, 4, 7, 11, 0, 18, 22,
    15, 14, 5, 1, 7, 4, 10, 0, 9, 8, 17, 15, 6, 23, 16, 0, 3, 11, 2, 6, 24, 10, 15, 1, 22, 19, 9, 21, 12, 3, 18,
    16, 20, 6, 23, 11, 4, 1, 15, 8, 13, 17, 25, 9, 14, 7, 10, 19, 2, 20, 21, 11, 23, 18, 17, 10, 25, 8, 1, 6,
    22, 21, 19, 9, 13, 23, 2, 3, 22, 10, 0, 5, 15, 12, 20, 19, 21, 13, 23, 21, 10, 16, 18, 12, 22, 12, 13, 2,
    11, 9, 21, 18, 19, 21, 23, 16, 20, 22, 18, 19, 15, 20, 3, 5, 7, 2, 14, 13, 18, 20, 23, 22, 12, 8, 16, 19,
    18, 19, 20, 25, 5, 13, 1, 10, 14, 17, 13, 12, 8, 22, 16, 0, 20, 25, 2, 23, 22, 8, 9, 18, 16, 12, 23, 11, 20,
    21, 6, 14, 18, 22, 12, 19, 14, 16, 21, 16, 13, 4, 23, 20, 16, 8, 23, 15, 22, 19, 10, 25, 17, 8, 13, 12,
)


GIVE_ROWS = 240


def program_order(units, ends):
    order, task, vector, waited, step = [], 0, 0, {3}, [0] * len(units)
    order.append(("wait", 3, 0))
    for entry in ORDER:
        if entry == TASK:
            order.append(("task", task, 0))
            task += 1
            continue
        if entry == VECTORS:
            order.append(("vec", vector, 0))
            vector += 1
            continue
        m = units[entry][0]
        if m not in waited:
            assert task >= ends[m]
            order.append(("wait", m, 0))
            waited.add(m)
        order.append(("sum", entry, step[entry]))
        step[entry] += 1
    return order


PAIRS = 2


def fold(v):
    total = v[0:8]
    for k in range(1, v.shape[0] // 8):
        total = total + v[8 * k : 8 * k + 8]
    return total


def layer_kernel(dims, at_base, g_base, *refs):
    x_in, cot_in, weights, params = refs[0], refs[1], refs[2:6], refs[6:19]
    y_out, dx_out, res, vec_out, tiles_hbm = refs[19:24]
    (
        at, g, give, pair, line_xy, line_z, ring, big, left, act, hid, qkv, probs, attended, branch, middle, dmid,
        vec_w, vec_h, rstd4, sums4, vec_in, vec_own, vec_got,
        send, recv, v_send, v_recv, p_send, p_recv, l_sem, w_in, w_keep, w_send, w_recv, t_sem, s_sem, e_sem,
    ) = refs[24:]
    r = lax.axis_index("rep")
    c = lax.axis_index("shard")
    x, y, z = r % 2, (r // 2) % 2, r // 4
    core = {"shard": 1 - c}
    to = {
        "X": {"rep": r + 1 - 2 * x},
        "Y": {"rep": r + 2 - 4 * y},
        "U": {"rep": r + 4},
        "D": {"rep": r - 4},
    }
    line_end = (z == 0) | (z == 3)
    line_mid = (z == 1) | (z == 2)
    outward = {"rep": r + 4 * (2 * (z // 2) - 1)}
    inward = {"rep": r + 4 * (1 - 2 * (z // 2))}
    across = {"rep": r + 4 * (3 - 2 * z)}
    upper = z // 2
    length = x_in.shape[0]
    width = x_in.shape[1]
    half_w = width // 2
    hidden = dims[2][1]
    half_h = hidden // 2
    blocks = hidden // width
    TILE = 512

    tile_of = []
    for m, (rows, cols) in enumerate(dims):
        for row in range(0, rows, TILE):
            for col in range(0, cols, UNIT_COLS):
                tile_of.append((m, row, col))
    first_tile = [min(t for t, v in enumerate(tile_of) if v[0] == m) for m in range(4)]
    parts = 2 * len(tile_of)
    slots_f, slots_b = 6, 16

    def part_read(i):
        m, row, col = tile_of[i // 2]
        return pltpu.make_async_copy(
            weights[m].at[pl.ds(row + (i % 2) * 256, 256), pl.ds(col, UNIT_COLS)],
            big.at[pl.ds((i % slots_f) * 256, 256), :],
            w_in.at[i % slots_f],
        )

    def part_low(i):
        return low_buf.at[pl.ds((i % slots_b) * 256, 256), :]

    low_buf = give

    def part_place(i):
        return tiles_hbm.at[c, i // 2, pl.ds((i % 2) * 256, 256), :]

    def part_keep(i):
        return pltpu.make_async_copy(part_low(i), part_place(i), w_keep.at[i % slots_b])

    def part_give(i):
        return pltpu.make_async_remote_copy(
            src_ref=part_low(i), dst_ref=part_place(i), send_sem=w_send.at[i % slots_b], recv_sem=w_recv.at[i],
            device_id=core, device_id_type=MESH,
        )

    def part_got(i):
        return pltpu.make_async_remote_copy(
            src_ref=part_low(i), dst_ref=tiles_hbm.at[1 - c, i // 2, pl.ds((i % 2) * 256, 256), :],
            send_sem=w_send.at[i % slots_b], recv_sem=w_recv.at[i], device_id=core, device_id_type=MESH,
        )

    for i in range(slots_f):
        part_read(i).start()

    barrier = pltpu.get_barrier_semaphore()
    for peer in (core, to["X"], to["Y"]):
        pl.semaphore_signal(barrier, inc=1, device_id=peer, device_id_type=MESH)

    @pl.when(z < 3)
    def _():
        pl.semaphore_signal(barrier, inc=1, device_id=to["U"], device_id_type=MESH)

    @pl.when(z > 0)
    def _():
        pl.semaphore_signal(barrier, inc=1, device_id=to["D"], device_id_type=MESH)

    @pl.when(line_end)
    def _():
        pl.semaphore_signal(barrier, inc=1, device_id=across, device_id_type=MESH)

    narrow = (0, 0, 2, 3, 4, 5, 6, 7, 8, 9, 10)

    def rounded(v):
        return v.astype(BF16).astype(F32)

    lane_w = pl.ds(pl.multiple_of(c * half_w, half_w), half_w)
    lane_h = pl.ds(pl.multiple_of(c * half_h, half_h), half_h)
    (qv_ref, ob_ref, hs_ref, g1_ref, b1_ref, g2_ref, b2_ref, g3_ref, b3_ref, ub_ref, g4_ref, b4_ref, db_ref) = params
    vec_w[0:2, lane_w] = rounded(qv_ref[...])
    for row, ref in zip(range(2, 11), (ob_ref, hs_ref, g1_ref, b1_ref, g2_ref, b2_ref, g3_ref, b3_ref, db_ref)):
        vec_w[row : row + 1, lane_w] = rounded(ref[...])
    for row, ref in enumerate((ub_ref, g4_ref, b4_ref)):
        vec_h[row : row + 1, lane_h] = rounded(ref[...])
    QB, VB, OB, HS, G1, B1, G2, B2, G3, B3, DB = range(11)
    UB, G4, B4 = range(3)

    def small_copy(k, give_it):
        ref, lane, far = ((vec_w, lane_w, 1 - c), (vec_h, lane_h, 1 - c))[k]
        size = half_w if k == 0 else half_h
        other = pl.ds(pl.multiple_of((1 - c) * size, size), size)
        here = ref.at[:, lane]
        return pltpu.make_async_remote_copy(
            src_ref=here, dst_ref=here if give_it else ref.at[:, other], send_sem=s_sem.at[k, 0], recv_sem=s_sem.at[k, 1],
            device_id=core, device_id_type=MESH,
        )

    e_copy = pltpu.make_async_copy(cot_in, g.at[pl.ds(0, length), pl.ds(g_base[3], width)], e_sem.at[0])
    e_copy.start()

    def left_own(m):
        rows = dims[m][0]
        return pltpu.make_async_copy(
            left.at[pl.ds(pl.multiple_of(2 * at_base[m] + c * rows, 512), rows), :],
            at.at[pl.ds(at_base[m], rows), pl.ds(0, length)],
            l_sem.at[m],
        )

    def left_far(m):
        rows = dims[m][0]
        return pltpu.make_async_remote_copy(
            src_ref=left.at[pl.ds(pl.multiple_of(2 * at_base[m] + (1 - c) * rows, 512), rows), :],
            dst_ref=at.at[pl.ds(at_base[m], rows), pl.ds(length, length)],
            send_sem=p_send.at[m, 0], recv_sem=p_recv.at[m, 0], device_id=core, device_id_type=MESH,
        )

    def right_far(m):
        cols = pl.ds(g_base[m], dims[m][1])
        return pltpu.make_async_remote_copy(
            src_ref=g.at[pl.ds(0, length), cols], dst_ref=g.at[pl.ds(length, length), cols],
            send_sem=p_send.at[m, 1], recv_sem=p_recv.at[m, 1], device_id=core, device_id_type=MESH,
        )

    def start_left(m):
        left_own(m).start()
        left_far(m).start()

    def wait_pair(m):
        left_own(m).wait()
        left_far(m).wait()
        right_far(m).wait()

    converted, kept_parts, given_parts = [0], set(), set()

    def kept(i):
        if i not in kept_parts:
            kept_parts.add(i)
            part_keep(i).wait()

    def given(i):
        if i not in given_parts:
            given_parts.add(i)
            part_give(i).wait_send()

    def convert_parts(upto):
        for i in range(converted[0], upto):
            part_read(i).wait()
            if i >= slots_b:
                kept(i - slots_b)
                given(i - slots_b)

            def convert(b, _, i=i):
                rows = pl.multiple_of((i % slots_f) * 256 + b * 32, 32)
                low = pl.multiple_of((i % slots_b) * 256 + b * 32, 32)
                low_buf[pl.ds(low, 32), :] = big[pl.ds(rows, 32), :].astype(BF16)
                return 0

            lax.fori_loop(0, 8, convert, 0)
            part_keep(i).start()
            if i == 0:
                pl.semaphore_wait(barrier, 5)
                small_copy(0, True).start()
                small_copy(1, True).start()
            part_give(i).start()
            if i + slots_f < parts:
                part_read(i + slots_f).start()
        converted[0] = max(converted[0], upto)

    convert_parts(2)
    e_copy.wait()
    right_far(3).start()
    convert_parts(4)

    def tile(m, half, index):
        return (half, first_tile[m] + index)

    stream = []
    for m in (0, 1, 2):
        for index in range(dims[m][1] // UNIT_COLS):
            stream += [tile(m, 0, index), tile(m, 1, index)]
    per_half = dims[3][0] // TILE
    stream += [tile(3, h, k) for h in range(2) for k in range(per_half)]
    for m in (2, 1, 0):
        for index in range(dims[m][1] // UNIT_COLS):
            stream += [tile(m, 0, index), tile(m, 1, index)]
    slots_t = 4
    here = set()

    def tile_load(i):
        half, t = stream[i]
        return pltpu.make_async_copy(
            tiles_hbm.at[half, t], ring.at[i % slots_t], t_sem.at[i % slots_t]
        )

    def tile_start(i):
        half, t = stream[i]
        if (1, t) not in here:
            here.add((1, t))
            convert_parts(2 * t + 2)
            for k in (2 * t, 2 * t + 1):
                kept(k)
                part_got(k).wait_recv()
        tile_load(i).start()

    at_tile, started, allowed_to = [0], [0], [0]

    def fill(limit=None):
        if limit is not None:
            allowed_to[0] = limit
        while started[0] < min(at_tile[0] + slots_t, allowed_to[0], len(stream)):
            tile_start(started[0])
            started[0] += 1

    def next_tile(ahead=0):
        i = at_tile[0] + ahead
        assert i < started[0]
        tile_load(i).wait()
        return ring.at[i % slots_t]

    def done_tile(count=1):
        at_tile[0] += count
        fill()

    def mean(v):
        return jnp.sum(v, axis=-1, keepdims=True) / v.shape[-1]

    def normal(v):
        centred = v - mean(v)
        scale = lax.rsqrt(mean(centred * centred) + 1e-05)
        return centred * scale, scale

    def each(fn, step=32, init=0):
        def body(i, carry):
            return fn(pl.ds(pl.multiple_of(i * step, step), step), carry)

        return lax.fori_loop(0, length // step, body, init)

    def w_row(i):
        return vec_w[i : i + 1, :]

    def turn(source, m, block=0):
        for k in range(width // 256):
            row = 2 * at_base[m] + block * width + k * 256
            left[row : row + 256, :] = jnp.transpose(source[:, k * 256 : (k + 1) * 256])

    NT = (((1,), (1,)), ((), ()))
    TN = (((0,), (0,)), ((), ()))

    def nt(a, b):
        return lax.dot_general(a, b, NT, preferred_element_type=F32)

    def tn(a, b):
        return lax.dot_general(a, b, TN, preferred_element_type=F32)

    def product_pair(source, write):
        first, second = next_tile(), next_tile(1)
        for k in range(UNIT_COLS // 256):
            cols = slice(k * 256, (k + 1) * 256)
            value = jnp.dot(source[:, 0:half_w], first[:, cols], preferred_element_type=F32)
            value = value + jnp.dot(source[:, half_w:width], second[:, cols], preferred_element_type=F32)
            write(cols, value)
        done_tile(2)

    small_copy(0, True).wait_send()
    small_copy(1, True).wait_send()
    small_copy(0, False).wait_recv()
    small_copy(1, False).wait_recv()

    def first_norm(rows, _):
        hat, _s = normal(x_in[rows, :].astype(F32))
        act[rows, :] = (hat * w_row(G1) + w_row(B1)).astype(BF16)
        return 0

    each(first_norm)
    fill(8)
    for index in range(3):

        def put_qkv(cols, value, index=index):
            if index == 0:
                value = value + vec_w[QB : QB + 1, cols]
            if index == 2:
                value = value + vec_w[VB : VB + 1, cols]
            qkv[:, index * width + cols.start : index * width + cols.stop] = value.astype(BF16)

        product_pair(act, put_qkv)
        convert_parts(10 + 2 * index)
    turn(act, 0)
    start_left(0)
    convert_parts(16)

    low_lane = lax.broadcasted_iota(jnp.int32, (length, 128), 1) < 64
    allowed = lax.broadcasted_iota(jnp.int32, (length, length), 1) <= lax.broadcasted_iota(
        jnp.int32, (length, length), 0
    )
    scale = 64 ** (-0.5)
    keep_lane = (low_lane.astype(F32).astype(BF16), jnp.logical_not(low_lane).astype(F32).astype(BF16))

    def attend(p):
        q = qkv[:, pl.ds(pl.multiple_of(p * 128, 128), 128)]
        k = qkv[:, pl.ds(pl.multiple_of(width + p * 128, 128), 128)]
        v = qkv[:, pl.ds(pl.multiple_of(2 * width + p * 128, 128), 128)]
        got = []
        for h in range(2):
            own = q * keep_lane[h]
            scores = jnp.where(allowed, nt(own, k) * scale, -1e30)
            top = jnp.max(scores, axis=-1, keepdims=True)
            lse = top + jnp.log(jnp.sum(jnp.exp(scores - top), axis=-1, keepdims=True))
            prob = jnp.exp(scores - lse)
            probs[2 * p + h] = prob
            got.append(jnp.dot(prob.astype(BF16), v, preferred_element_type=F32))
        cols = pl.ds(pl.multiple_of(p * 128, 128), 128)
        value = jnp.where(low_lane, got[0], got[1])
        attended[:, cols] = value
        act[:, cols] = (value * vec_w[HS : HS + 1, cols]).astype(BF16)

    def attend_some(i, _):
        for n in range(PAIRS):
            attend(i * PAIRS + n)
        return 0

    lax.fori_loop(0, width // 128 // PAIRS, attend_some, 0)
    fill(10)
    convert_parts(20)

    def put_branch(cols, value):
        branch[:, cols] = value + vec_w[OB : OB + 1, cols]

    product_pair(act, put_branch)
    fill(16)
    turn(act, 1)
    start_left(1)
    convert_parts(24)

    def second_norm(rows, _):
        hat, _s = normal(branch[rows, :])
        mid = x_in[rows, :].astype(F32) + (hat * w_row(G2) + w_row(B2))
        middle[rows, :] = mid
        hat, _s = normal(mid)
        act[rows, :] = (hat * w_row(G3) + w_row(B3)).astype(BF16)
        return 0

    each(second_norm)
    U0, H0, D0 = 0, blocks * length, 2 * blocks * length
    for j in range(blocks):

        def put_hidden(cols, value, j=j):
            wide = slice(j * width + cols.start, j * width + cols.stop)
            big[U0 + j * length : U0 + (j + 1) * length, cols] = value + vec_h[UB : UB + 1, wide]

        product_pair(act, put_hidden)
    turn(act, 2)
    start_left(2)
    root_half = 0.7071067811865476

    def near(base, start):
        return pl.ds(pl.multiple_of(base + start, 16), 16)

    def hidden_norm(rows, _):
        total = jnp.zeros((16, 1), F32)
        for j in range(blocks):
            u = big[near(U0 + j * length, rows.start), :]
            h = u * (1.0 + lax.erf(u * root_half)) * 0.5
            big[near(H0 + j * length, rows.start), :] = h
            total = total + jnp.sum(h, axis=-1, keepdims=True)
        centre = total / hidden
        total = jnp.zeros((16, 1), F32)
        for j in range(blocks):
            h = big[near(H0 + j * length, rows.start), :] - centre
            total = total + jnp.sum(h * h, axis=-1, keepdims=True)
        s = lax.rsqrt(total / hidden + 1e-05)
        rstd4[rows, :] = jnp.broadcast_to(s, (16, 128))
        for j in range(blocks):
            at_h = near(H0 + j * length, rows.start)
            hat = (big[at_h, :] - centre) * s
            big[at_h, :] = hat
            cols = slice(j * width, (j + 1) * width)
            hid[near(j * length, rows.start), :] = (
                hat * vec_h[G4 : G4 + 1, cols] + vec_h[B4 : B4 + 1, cols]
            ).astype(BF16)
        return 0

    each(hidden_norm, 16)
    fill(len(stream))
    for j in range(blocks):
        turn(hid.at[pl.ds(j * length, length), :], 3, j)
    start_left(3)
    for i in range(parts):
        given(i)

    tasks = []
    zeros8 = jnp.zeros((8, width), F32)
    dirs = g.at[pl.ds(0, length), :]

    def put_sum(row, value):
        line = jnp.sum(value, axis=0, keepdims=True)
        vec_in[0, row : row + 1, :] = line[:, 0:half_w]
        vec_in[1, row : row + 1, :] = line[:, half_w:width]

    def task_down(h, k):
        def run():
            w = next_tile()
            row = h * dims[3][0] + k * TILE
            j, lane = row // width, row % width
            if h == 0 and k == 0:
                y_acc[...] = middle[...] + w_row(DB)
            for n in range(TILE // 256):
                big[D0 + j * length : D0 + (j + 1) * length, lane + n * 256 : lane + (n + 1) * 256] = nt(
                    dirs[:, g_base[3] : g_base[3] + width], w[n * 256 : (n + 1) * 256, :]
                )

            for n in range(width // 256):
                cols = slice(n * 256, (n + 1) * 256)
                y_acc[:, cols] += jnp.dot(
                    hid[j * length : (j + 1) * length, lane : lane + TILE], w[:, cols], preferred_element_type=F32
                )
            done_tile()
            if h == 1 and k == per_half - 1:
                y_out[...] = y_acc[...].astype(BF16)

        return run

    y_acc = dmid
    for h in range(2):
        for k in range(per_half):
            tasks.append((1.2, task_down(h, k)))

    def task_hidden(first, count):
        def run():
            if first == 0:
                sums4[...] = jnp.zeros_like(sums4)

                def e_sum(rows, carry):
                    return carry + fold(dirs[rows, g_base[3] : g_base[3] + width].astype(F32))

                put_sum(DB, each(e_sum, 32, zeros8))

            def body(i, _):
                at_r = pl.multiple_of(first + i * 16, 16)
                one = jnp.zeros((16, 1), F32)
                two = jnp.zeros((16, 1), F32)
                for j in range(blocks):
                    gain = vec_h[G4 : G4 + 1, j * width : (j + 1) * width]
                    d = big[near(D0 + j * length, at_r), :] * gain
                    hat = big[near(H0 + j * length, at_r), :]
                    one = one + jnp.sum(d, axis=-1, keepdims=True)
                    two = two + jnp.sum(d * hat, axis=-1, keepdims=True)
                one, two = one / hidden, two / hidden
                s = rstd4[pl.ds(at_r, 16), 0:1]
                for j in range(blocks):
                    cols = slice(j * width, (j + 1) * width)
                    da = big[near(D0 + j * length, at_r), :]
                    hat = big[near(H0 + j * length, at_r), :]
                    u = big[near(U0 + j * length, at_r), :]
                    dh = s * (da * vec_h[G4 : G4 + 1, cols] - one - hat * two)
                    slope = 0.5 * (1.0 + lax.erf(u * root_half)) + u * (jnp.exp(u * u * -0.5) * 0.3989422804014327)
                    du = (dh * slope).astype(BF16)
                    g[pl.ds(at_r, 16), g_base[2] + j * width : g_base[2] + (j + 1) * width] = du
                    sums4[0:8, cols] += fold(du.astype(F32))
                    sums4[8:16, cols] += fold(da * hat)
                    sums4[16:24, cols] += fold(da)
                return 0

            lax.fori_loop(0, count // 16, body, 0)
            if first + count == length:
                for i in range(3):
                    line = jnp.sum(sums4[8 * i : 8 * i + 8, :], axis=0, keepdims=True)
                    for n in range(hidden // half_w):
                        hh, k = divmod(n, half_h // half_w)
                        vec_in[hh, 11 + 4 * i + k : 12 + 4 * i + k, :] = line[:, n * half_w : (n + 1) * half_w]
                right_far(2).start()

        return run

    for first in range(0, length, 32):
        tasks.append((3.0, task_hidden(first, 32)))

    def add_pair(acc, index_of, cols_of, count, width_to):
        def make(index):
            def run():
                for h in range(2):
                    w = next_tile()
                    for n in range(TILE // 256):
                        cols = slice(h * half_w + n * 256, h * half_w + (n + 1) * 256)
                        value = nt(dirs[:, cols_of(index)], w[n * 256 : (n + 1) * 256, :])
                        if index == 0:
                            acc[:, cols] = value
                        else:
                            acc[:, cols] += value
                    done_tile()

            return run

        return [(1.2, make(index)) for index in range(count)]

    ends = {2: len(tasks)}
    acc = big.at[pl.ds(U0, length), :]
    tasks += add_pair(acc, None, lambda j: slice(g_base[2] + j * width, g_base[2] + (j + 1) * width), blocks, width)

    def task_norms():
        def body(rows, carry):
            s3g, s3b, s2g, s2b, sob = carry
            da = acc[rows, :]
            hat, s = normal(middle[rows, :])
            d = da * w_row(G3)
            d_mid = dirs[rows, g_base[3] : g_base[3] + width].astype(F32) + s * (d - mean(d) - hat * mean(d * hat))
            dmid[rows, :] = d_mid
            s3g, s3b = s3g + fold(da * hat), s3b + fold(da)
            hat, s = normal(branch[rows, :])
            d = d_mid * w_row(G2)
            dy = (s * (d - mean(d) - hat * mean(d * hat))).astype(BF16)
            s2g, s2b = s2g + fold(d_mid * hat), s2b + fold(d_mid)
            g[rows, g_base[1] : g_base[1] + width] = dy
            return (s3g, s3b, s2g, s2b, sob + fold(dy.astype(F32)))

        got = each(body, 16, (zeros8,) * 5)
        for row, value in zip((G3, B3, G2, B2, OB), got):
            put_sum(row, value)
        right_far(1).start()

    tasks.append((2.5, task_norms))
    ends[1] = len(tasks)
    d_mixed = big.at[pl.ds(U0 + length, length), :]
    tasks += add_pair(d_mixed, None, lambda j: slice(g_base[1], g_base[1] + width), 1, width)

    def task_heads():
        def body(rows, carry):
            d = d_mixed[rows, :]
            act[rows, :] = (d * w_row(HS)).astype(BF16)
            return carry + fold(d * attended[rows, :])

        put_sum(HS, each(body, 32, zeros8))

    tasks.append((0.6, task_heads))

    def task_attend(first, count):
        def run():
            def pair_of_heads(p):
                q_cols = pl.ds(pl.multiple_of(p * 128, 128), 128)
                k_cols = pl.ds(pl.multiple_of(width + p * 128, 128), 128)
                v_cols = pl.ds(pl.multiple_of(2 * width + p * 128, 128), 128)
                q, k, v, do = qkv[:, q_cols], qkv[:, k_cols], qkv[:, v_cols], act[:, q_cols]
                dq, dk, dv = [], [], []
                for h in range(2):
                    prob = probs[2 * p + h]
                    own = do * keep_lane[h]
                    dv.append(tn(prob.astype(BF16), do))
                    dp = nt(own, v)
                    ds = prob * (dp - jnp.sum(prob * dp, axis=-1, keepdims=True))
                    ds = ds.astype(BF16)
                    dq.append(jnp.dot(ds, k, preferred_element_type=F32) * scale)
                    dk.append(tn(ds, q) * scale)
                for cols, value in ((q_cols, dq), (k_cols, dk), (v_cols, dv)):
                    low = jnp.where(low_lane, value[0], value[1]).astype(BF16)
                    g[0:length, cols] = low

            for n in range(count):
                pair_of_heads(first + n)
            if first + count == width // 128:

                def sums(rows, carry):
                    a, b = carry
                    return (
                        a + fold(g[rows, 0:width].astype(F32)),
                        b + fold(g[rows, 2 * width : 3 * width].astype(F32)),
                    )

                a, b = each(sums, 32, (zeros8, zeros8))
                put_sum(QB, a)
                put_sum(VB, b)
                right_far(0).start()

        return run

    for first in range(0, width // 128, 2):
        tasks.append((3.0, task_attend(first, 2)))
    ends[0] = len(tasks)
    d_first = big.at[pl.ds(U0 + 2 * length, length), :]
    tasks += add_pair(d_first, None, lambda j: slice(j * width, (j + 1) * width), 3, width)

    def task_last():
        def body(rows, carry):
            sg, sb = carry
            da = d_first[rows, :]
            hat, s = normal(x_in[rows, :].astype(F32))
            d = da * w_row(G1)
            dx_out[rows, :] = dmid[rows, :] + s * (d - mean(d) - hat * mean(d * hat))
            return (sg + fold(da * hat), sb + fold(da))

        sg, sb = each(body, 16, (zeros8, zeros8))
        put_sum(G1, sg)
        put_sum(B1, sb)
        vec_in[0, 23:24, :] = jnp.zeros((1, half_w), F32)
        vec_in[1, 23:24, :] = jnp.zeros((1, half_w), F32)
        vec_copy(0).start()

    tasks.append((1.5, task_last))

    vec_steps = (core, to["X"], to["Y"], {"rep": r + 4 * (1 - 2 * (z % 2))}, across)

    def vec_copy(step):
        source = vec_in.at[1 - c] if step == 0 else vec_own.at[step]
        return pltpu.make_async_remote_copy(
            src_ref=source, dst_ref=vec_got.at[step], send_sem=v_send.at[step], recv_sem=v_recv.at[step],
            device_id=vec_steps[step], device_id_type=MESH,
        )

    def vec_task(k):
        vec_copy(k).wait_recv()
        total = (vec_in[c] if k == 0 else vec_own[k]) + vec_got[k]
        if k < 4:
            vec_own[k + 1] = total
            vec_copy(k + 1).start()
        else:
            vec_out[...] = total

    units = unit_table(dims)
    kinds = KINDS
    xy_at, z_at = {}, {}
    for unit, kind in enumerate(kinds):
        (z_at if kind[0] == "Z" else xy_at)[unit] = len(z_at) if kind[0] == "Z" else len(xy_at)

    def copy(unit, name, source, dest, device):
        return functools.partial(
            pltpu.make_async_remote_copy,
            src_ref=source, dst_ref=dest, send_sem=send.at[unit], recv_sem=recv.at[unit, SLOT[name]],
            device_id=device, device_id_type=MESH,
        )

    def rows_of(unit, start, count):
        if not isinstance(start, int):
            start = pl.multiple_of(start, 16)
        return res.at[unit, pl.ds(start, count), :]

    def product(unit, start, count, dest, dest_start, got=None, got_start=0):
        m, row, col = units[unit]
        step = 128 if count % 128 == 0 else min(count, 64)

        def block(index, _):
            part, strip = index // (UNIT_COLS // 256), index % (UNIT_COLS // 256)
            cols = pl.ds(pl.multiple_of(strip * 256, 256), 256)
            value = jnp.dot(
                at[pl.ds(pl.multiple_of(at_base[m] + row + start + part * step, 16), step), :],
                g[:, pl.ds(pl.multiple_of(g_base[m] + col + strip * 256, 256), 256)],
                preferred_element_type=F32,
            )
            if got is not None:
                value = value + got[pl.ds(pl.multiple_of(got_start + part * step, 16), step), cols].astype(F32)
            dest[pl.ds(pl.multiple_of(dest_start + part * step, 16), step), cols] = value.astype(BF16)
            return 0

        lax.fori_loop(0, (count // step) * (UNIT_COLS // 256), block, 0)

    def accumulate(unit, start, count, got, got_start, dest, dest_start):
        def block(strip, _):
            cols = pl.ds(pl.multiple_of(strip * 256, 256), 256)
            value = res[unit, pl.ds(pl.multiple_of(start, 16), count), cols].astype(F32)
            value = value + got[pl.ds(pl.multiple_of(got_start, 16), count), cols].astype(F32)
            dest[pl.ds(pl.multiple_of(dest_start, 16), count), cols] = value.astype(BF16)
            return 0

        lax.fori_loop(0, UNIT_COLS // 256, block, 0)

    def gather_line(unit, base, size, level):
        up, down = "u%d" % level, "w%d" % level
        low, high = z - (level - 1), z + (level - 1)

        @pl.when((low >= 0) & (z < 3))
        def _():
            part = rows_of(unit, base + low * size, size)
            copy(unit, up, part, part, to["U"])().start()

        @pl.when((high <= 3) & (z > 0))
        def _():
            part = rows_of(unit, base + high * size, size)
            copy(unit, down, part, part, to["D"])().start()

    def gather_arrived(unit, base, size, level):
        def wait(chunks):
            part = give.at[pl.ds(0, chunks * size), :]
            copy(unit, "u%d" % level, part, part, to["U"])().wait_recv()

        if level == 1:
            pl.when(line_mid)(lambda: wait(2))
        if level == 2:
            wait(1)
        else:
            pl.when(line_end)(lambda: wait(1))

    def finish(unit, ends, mids):
        def wait(rows):
            part = give.at[pl.ds(0, rows), :]
            copy(unit, "d1", part, part, to["X"])().wait_send()

        pl.when(line_end)(lambda: wait(ends))
        pl.when(line_mid)(lambda: wait(mids))

    def task_xy(unit, step):
        half, quarter, size = UNIT_ROWS // 2, UNIT_ROWS // 4, UNIT_ROWS // 16
        first, second = ("X", "Y") if kinds[unit] == "X" else ("Y", "X")
        p, q = (x, y) if kinds[unit] == "X" else (y, x)
        line, block, out, other = line_xy.at[xy_at[unit]], res.at[unit], give.at[pl.ds(unit * GIVE_ROWS, GIVE_ROWS), :], pair.at[unit]
        keep, away_half = p * half, (1 - p) * half
        base = keep + q * quarter
        away = keep + (1 - q) * quarter
        at_z = half + quarter
        d1 = copy(unit, "d1", out.at[pl.ds(0, half), :], rows_of(unit, away_half, half), to[first])
        d2 = copy(unit, "d2", out.at[pl.ds(half, quarter), :], other.at[pl.ds(0, quarter), :], to[second])
        z1 = copy(unit, "z1", out.at[pl.ds(at_z, 3 * size), :], line.at[pl.ds(0, 3 * size), :], inward)
        z2 = copy(unit, "z2", out.at[pl.ds(at_z, 2 * size), :], line.at[pl.ds(3 * size, 2 * size), :], across)
        z3 = copy(unit, "z3", out.at[pl.ds(at_z + 2 * size, size), :], line.at[pl.ds(0, size), :], outward)
        own_quarter = rows_of(unit, base, quarter)
        g2 = copy(unit, "g2", own_quarter, own_quarter, to[second])
        own_half = rows_of(unit, keep, half)
        g1 = copy(unit, "g1", own_half, own_half, to[first])
        own = base + z * size
        if step == 0:
            product(unit, away_half, half, out, 0)
            d1().start()
        elif step == 1:
            d1().wait_recv()
            product(unit, away, quarter, out, half, block, away)
            d2().start()
            product(unit, base, quarter, block, base, block, base)
        elif step == 2:
            d2().wait_recv()

            @pl.when(line_end)
            def _():
                skip = (1 - upper) * size
                accumulate(unit, base + skip, 3 * size, other, skip, out, at_z)
                z1().start()
                accumulate(unit, own, size, other, z * size, block, own)

            @pl.when(line_mid)
            def _():
                accumulate(unit, base, quarter, other, 0, block, base)

        elif step == 3:

            @pl.when(line_mid)
            def _():
                z1().wait_recv()
                accumulate(unit, base + (1 - upper) * 2 * size, 2 * size, line, (1 - upper) * size, out, at_z)
                z2().start()
                accumulate(unit, own, size, line, upper * 2 * size, block, own)

        elif step == 4:

            @pl.when(line_mid)
            def _():
                z2().wait_recv()
                accumulate(unit, base + upper * 3 * size, size, line, (3 + upper) * size, out, at_z + 2 * size)
                z3().start()
                accumulate(unit, own, size, line, (4 - upper) * size, block, own)
                gather_line(unit, base, size, 1)

        elif step == 5:

            @pl.when(line_end)
            def _():
                z3().wait_recv()
                accumulate(unit, own, size, line, 0, block, own)
                gather_line(unit, base, size, 1)

        elif step in (6, 7):
            gather_arrived(unit, base, size, step - 5)
            gather_line(unit, base, size, step - 4)
        elif step == 8:
            gather_arrived(unit, base, size, 3)
            g2().start()
        elif step == 9:
            g2().wait_recv()
            g1().start()
        else:
            g1().wait_recv()
            finish(unit, 2 * half + 2 * quarter + 4 * size, 2 * half + 2 * quarter + 8 * size)

    def task_z(unit, step):
        size, half, quarter = UNIT_ROWS // 4, UNIT_ROWS // 8, UNIT_ROWS // 16
        first, second = ("X", "Y") if kinds[unit] == "ZX" else ("Y", "X")
        p, q = (x, y) if kinds[unit] == "ZX" else (y, x)
        line, block, out, other = line_z.at[z_at[unit]], res.at[unit], give.at[pl.ds(unit * GIVE_ROWS, GIVE_ROWS), :], pair.at[unit]
        own = z * size
        keep, away_half = own + p * half, own + (1 - p) * half
        base, away = keep + q * quarter, keep + (1 - q) * quarter
        at_d = 3 * size
        z1 = copy(unit, "z1", out.at[pl.ds(0, 3 * size), :], line.at[pl.ds(0, 3 * size), :], inward)
        z2 = copy(unit, "z2", out.at[pl.ds(0, 2 * size), :], line.at[pl.ds(3 * size, 2 * size), :], across)
        z3 = copy(unit, "z3", out.at[pl.ds(2 * size, size), :], line.at[pl.ds(0, size), :], outward)
        d1 = copy(unit, "d1", out.at[pl.ds(at_d, half), :], other.at[pl.ds(0, half), :], to[first])
        d2 = copy(unit, "d2", out.at[pl.ds(at_d + half, quarter), :], other.at[pl.ds(half, quarter), :], to[second])
        own_quarter = rows_of(unit, base, quarter)
        g2 = copy(unit, "g2", own_quarter, own_quarter, to[second])
        own_half = rows_of(unit, keep, half)
        g1 = copy(unit, "g1", own_half, own_half, to[first])
        if step == 0:

            @pl.when(line_end)
            def _():
                product(unit, (1 - upper) * size, 3 * size, out, 0)
                z1().start()

        elif step == 1:

            @pl.when(line_mid)
            def _():
                z1().wait_recv()
                product(unit, (1 - upper) * 2 * size, 2 * size, out, 0, line, (1 - upper) * size)
                z2().start()
                product(unit, own, size, block, own, line, upper * 2 * size)

        elif step == 2:

            @pl.when(line_mid)
            def _():
                z2().wait_recv()
                product(unit, upper * 3 * size, size, out, 2 * size, line, (3 + upper) * size)
                z3().start()
                got = (4 - upper) * size
                accumulate(unit, away_half, half, line, got + (1 - p) * half, out, at_d)
                d1().start()
                accumulate(unit, keep, half, line, got + p * half, block, keep)

        elif step == 3:

            @pl.when(line_end)
            def _():
                z3().wait_recv()
                product(unit, away_half, half, out, at_d, line, (1 - p) * half)
                d1().start()
                product(unit, keep, half, block, keep, line, p * half)

        elif step == 4:
            d1().wait_recv()
            accumulate(unit, away, quarter, other, (1 - q) * quarter, out, at_d + half)
            d2().start()
            accumulate(unit, base, quarter, other, q * quarter, block, base)
        elif step == 5:
            d2().wait_recv()
            accumulate(unit, base, quarter, other, half, block, base)
            g2().start()
        elif step == 6:
            g2().wait_recv()
            g1().start()
        elif step == 7:
            g1().wait_recv()
            gather_line(unit, 0, size, 1)
        elif step in (8, 9):
            gather_arrived(unit, 0, size, step - 7)
            gather_line(unit, 0, size, step - 6)
        else:
            gather_arrived(unit, 0, size, 3)
            finish(unit, 2 * half + 2 * quarter + 4 * size, 2 * half + 2 * quarter + 8 * size)


    for kind, a, b in program_order(units, ends):
        if kind == "task":
            tasks[a][1]()
        elif kind == "wait":
            wait_pair(a)
        elif kind == "vec":
            vec_task(a)
        elif kinds[a][0] == "Z":
            task_z(a, b)
        else:
            task_xy(a, b)
    for step in range(5):
        vec_copy(step).wait_send()


def whole_layer(layer_input, cotangent, weights, params):
    dims = tuple(w.shape for w in weights)
    at_rows = sum(rows for rows, _ in dims)
    g_cols = sum(cols for _, cols in dims)
    at_base = [sum(rows for rows, _ in dims[:m]) for m in range(4)]
    g_base = [sum(cols for _, cols in dims[:m]) for m in range(4)]
    length, width = layer_input.shape
    hidden = dims[2][1]
    blocks = hidden // width
    units = unit_table(dims)
    kinds = KINDS
    n, n_z = len(units), sum(kind[0] == "Z" for kind in kinds)
    tiles = n // 2
    hbm = pl.BlockSpec(memory_space=pl.ANY)
    vmem = pl.BlockSpec(memory_space=pltpu.VMEM)
    dma = pltpu.SemaphoreType.DMA
    small = (24, width // 2)
    got = pl.pallas_call(
        functools.partial(layer_kernel, dims, at_base, g_base),
        out_shape=[
            pltpu.VMEM((length, width), BF16),
            pltpu.VMEM((length, width), F32),
            pltpu.VMEM((n, UNIT_ROWS, UNIT_COLS), BF16),
            pltpu.VMEM(small, F32),
            jax.ShapeDtypeStruct((2, tiles, 512, UNIT_COLS), BF16),
        ],
        in_specs=[vmem, hbm] + [hbm] * 4 + [vmem] * 13,
        out_specs=[vmem] * 4 + [hbm],
        scratch_shapes=[
            pltpu.VMEM((at_rows, 2 * length), BF16),
            pltpu.VMEM((2 * length, g_cols), BF16),
            pltpu.VMEM((n * GIVE_ROWS, UNIT_COLS), BF16),
            pltpu.VMEM((n, UNIT_ROWS // 4, UNIT_COLS), BF16),
            pltpu.VMEM((n - n_z, 5 * UNIT_ROWS // 16, UNIT_COLS), BF16),
            pltpu.VMEM((n_z, 5 * UNIT_ROWS // 4, UNIT_COLS), BF16),
            pltpu.VMEM((4, 512, UNIT_COLS), BF16),
            pltpu.VMEM((3 * blocks * length, width), F32),
            pltpu.VMEM((2 * at_rows, length), BF16),
            pltpu.VMEM((length, width), BF16),
            pltpu.VMEM((blocks * length, width), BF16),
            pltpu.VMEM((length, 3 * width), BF16),
            pltpu.VMEM((width // 64, length, length), F32),
            pltpu.VMEM((length, width), F32),
            pltpu.VMEM((length, width), F32),
            pltpu.VMEM((length, width), F32),
            pltpu.VMEM((length, width), F32),
            pltpu.VMEM((16, width), F32),
            pltpu.VMEM((8, hidden), F32),
            pltpu.VMEM((length, 128), F32),
            pltpu.VMEM((24, hidden), F32),
            pltpu.VMEM((2,) + small, F32),
            pltpu.VMEM((5,) + small, F32),
            pltpu.VMEM((5,) + small, F32),
            dma((n,)),
            dma((n, 9)),
            dma((5,)),
            dma((5,)),
            dma((4, 2)),
            dma((4, 2)),
            dma((4,)),
            dma((6,)),
            dma((16,)),
            dma((16,)),
            dma((2 * tiles,)),
            dma((4,)),
            dma((2, 2)),
            dma((1,)),
        ],
        compiler_params=pltpu.CompilerParams(
            collective_id=0, has_side_effects=True, vmem_limit_bytes=50 * MIB
        ),
        name="whole_layer",
    )(layer_input, cotangent, *weights, *params)
    return got[:4]


def finish_kernel(dims, *refs):
    y_in, dx_in, res, vec = refs[0:4]
    y_out, dx_out, outs, smalls = refs[4], refs[5], refs[6:10], refs[10:23]
    wide, lines, o_sem, s_sem = refs[23], refs[24:37], refs[37], refs[38]
    slots = wide.shape[0]
    copies = [pltpu.make_async_copy(y_in, y_out, s_sem.at[13]), pltpu.make_async_copy(dx_in, dx_out, s_sem.at[14])]
    rows_of = [range(0, 2)] + [range(k, k + 1) for k in range(2, 11)] + [range(11 + 4 * k, 15 + 4 * k) for k in range(3)]
    for k, rows in enumerate(rows_of):
        if len(rows) == 4:
            for j, row in enumerate(rows):
                lines[k][:, j * vec.shape[1] : (j + 1) * vec.shape[1]] = vec[row : row + 1, :]
        else:
            lines[k][...] = vec[rows.start : rows.stop, :]
        copies.append(pltpu.make_async_copy(lines[k], smalls[k], s_sem.at[k]))
    for piece in copies:
        piece.start()
    units = unit_table(dims)

    def put(unit):
        m, row, col = units[unit]
        return pltpu.make_async_copy(
            wide.at[unit % slots], outs[m].at[pl.ds(row, UNIT_ROWS), pl.ds(col, UNIT_COLS)], o_sem.at[unit % slots]
        )

    for unit in range(len(units)):
        if unit >= slots:
            put(unit - slots).wait()

        def widen(b, _, unit=unit):
            rows = pl.ds(pl.multiple_of(b * 32, 32), 32)
            wide[unit % slots, rows, :] = res[unit, rows, :].astype(F32)
            return 0

        lax.fori_loop(0, UNIT_ROWS // 32, widen, 0)
        put(unit).start()
    for unit in range(len(units) - slots, len(units)):
        put(unit).wait()
    for piece in copies:
        piece.wait()


def write_results(got, dims):
    y, dx, _, vec = got
    half = vec.shape[1]
    small = [(2, half)] + [(1, half)] * 9 + [(1, 4 * half)] * 3
    hbm = pl.BlockSpec(memory_space=pl.ANY)
    vmem = pl.BlockSpec(memory_space=pltpu.VMEM)
    dma = pltpu.SemaphoreType.DMA
    return pl.pallas_call(
        functools.partial(finish_kernel, dims),
        out_shape=[jax.ShapeDtypeStruct(y.shape, BF16), jax.ShapeDtypeStruct(dx.shape, F32)]
        + [jax.ShapeDtypeStruct(d, F32) for d in dims]
        + [jax.ShapeDtypeStruct(s, F32) for s in small],
        in_specs=[vmem] * 4,
        out_specs=[hbm] * 19,
        scratch_shapes=[pltpu.VMEM((6, UNIT_ROWS, UNIT_COLS), F32)]
        + [pltpu.VMEM(s, F32) for s in small]
        + [dma((6,)), dma((15,))],
        compiler_params=pltpu.CompilerParams(vmem_limit_bytes=30 * MIB),
        name="write_results",
    )(*got)


def on_pair_of_cores(
    layer_input, cotangent, w_qkv, qv_bias, w_out, out_bias, head_scale, ln1_gain, ln1_bias, ln2_gain, ln2_bias,
    ln3_gain, ln3_bias, w_fc1, fc1_bias, ln4_gain, ln4_bias, w_fc2, fc2_bias,
):
    params = (
        qv_bias, out_bias, jnp.repeat(head_scale, HEAD_DIM), ln1_gain, ln1_bias, ln2_gain, ln2_bias, ln3_gain, ln3_bias,
        fc1_bias, ln4_gain, ln4_bias, fc2_bias,
    )
    params = [p.reshape(-1, p.shape[-1]) for p in params]
    weights = (w_qkv, w_out, w_fc1, w_fc2)
    got = whole_layer(layer_input, cotangent, weights, params)
    output, grad_input, qkv, out, up, down, *smalls = write_results(got, tuple(w.shape for w in weights))
    heads = smalls[2].reshape(-1, HEAD_DIM).sum(axis=-1)
    rows = [s.reshape(-1) for s in smalls]
    return (
        output, grad_input, qkv, smalls[0], out, rows[1], heads, rows[3], rows[4], rows[5], rows[6], rows[7], rows[8], up,
        rows[10], rows[11], rows[12], down, rows[9],
    )


def fits_pair(mesh):
    return mesh.shape["shard"] == 2 and mesh.shape["rep"] == 16


def solution(mesh):
    return jax.shard_map(
        on_pair_of_cores if fits_pair(mesh) else on_any_mesh,
        mesh=mesh,
        in_specs=(
            P(("rep", "shard"), None),
            P(("rep", "shard"), None),
            P("shard", None),
            P(None, "shard"),
            P("shard", None),
            P("shard"),
            P("shard"),
            P("shard"),
            P("shard"),
            P("shard"),
            P("shard"),
            P("shard"),
            P("shard"),
            P("shard", None),
            P("shard"),
            P("shard"),
            P("shard"),
            P("shard", None),
            P("shard"),
        ),
        out_specs=(
            P(("rep", "shard"), None),
            P(("rep", "shard"), None),
            P("shard", None),
            P(None, "shard"),
            P("shard", None),
            P("shard"),
            P("shard"),
            P("shard"),
            P("shard"),
            P("shard"),
            P("shard"),
            P("shard"),
            P("shard"),
            P("shard", None),
            P("shard"),
            P("shard"),
            P("shard"),
            P("shard", None),
            P("shard"),
        ),
        check_vma=False,
    )
```

```python
import functools

import jax
import jax.numpy as jnp
from jax import lax
from jax.experimental import pallas as pl
from jax.experimental.pallas import tpu as pltpu
from jax.sharding import PartitionSpec as P

D = 1024
HEADS = 16
HEAD_DIM = 64


EPS = 1e-05
NEG = -1e30


def norm_rows(v, gain, bias):
    centre = jnp.mean(v, axis=-1, keepdims=True)
    centred = v - centre
    spread = jnp.mean(centred * centred, axis=-1, keepdims=True)
    return centred * lax.rsqrt(spread + EPS) * gain + bias


def ffn_middle(hidden, gain, bias):
    return norm_rows(jax.nn.gelu(hidden, approximate=False), gain, bias)


def causal_mask(index, qblock, length):
    rows = index * qblock + lax.iota(jnp.int32, qblock)
    cols = lax.iota(jnp.int32, length)
    return (cols[None, :] <= rows[:, None])[None]


def block_scores(queries, keys_all, index, qblock, scale):
    length = keys_all.shape[0]
    scores = (
        jnp.einsum("qhd,khd->hqk", queries, keys_all, preferred_element_type=jnp.float32) * scale
    )
    return (queries, jnp.where(causal_mask(index, qblock, length), scores, NEG))


def attend_forward(queries, keys_all, values_all, scale):
    length, heads, width = queries.shape
    qblock = min(512, length)
    blocks = length // qblock

    def one_block(index):
        rows_q, scores = block_scores(queries, keys_all, index, qblock, scale)
        total = jax.nn.logsumexp(scores, axis=-1, keepdims=True)
        probs = jnp.exp(scores - total).astype(jnp.bfloat16)
        outcome = jnp.einsum("hqk,khd->qhd", probs, values_all, preferred_element_type=jnp.float32)
        return (outcome, total)

    outcome, totals = lax.map(one_block, jnp.arange(blocks, dtype=jnp.int32))
    return (outcome.reshape(length, heads, width), totals)


def attend_backward(queries, keys_all, values_all, totals, grad_out, scale):
    length, heads, width = queries.shape
    qblock = min(512, length)
    blocks = length // qblock

    def one_block(carry, index):
        grad_keys, grad_values = carry
        rows_q, scores = block_scores(queries, keys_all, index, qblock, scale)
        probs = jnp.exp(scores - totals[index])
        probs_low = probs.astype(jnp.bfloat16)
        grad_values = grad_values + jnp.einsum(
            "hqk,qhd->khd", probs_low, grad_out, preferred_element_type=jnp.float32
        )
        grad_probs = jnp.einsum(
            "qhd,khd->hqk", grad_out, values_all, preferred_element_type=jnp.float32
        )
        row_dot = jnp.sum(probs * grad_probs, axis=-1, keepdims=True)
        grad_scores = (probs * (grad_probs - row_dot)).astype(jnp.bfloat16)
        grad_rows = (
            jnp.einsum("hqk,khd->qhd", grad_scores, keys_all, preferred_element_type=jnp.float32)
            * scale
        )
        grad_keys = (
            grad_keys
            + jnp.einsum("hqk,qhd->khd", grad_scores, rows_q, preferred_element_type=jnp.float32)
            * scale
        )
        return ((grad_keys, grad_values), grad_rows)

    empty = jnp.zeros((length, heads, width), jnp.float32)
    (grad_keys, grad_values), grad_queries = lax.scan(
        one_block, (empty, empty), jnp.arange(blocks, dtype=jnp.int32)
    )
    return (grad_queries.reshape(length, heads, width), grad_keys, grad_values)


def on_any_mesh(
    layer_input,
    cotangent,
    w_qkv,
    qv_bias,
    w_out,
    out_bias,
    head_scale,
    ln1_gain,
    ln1_bias,
    ln2_gain,
    ln2_bias,
    ln3_gain,
    ln3_bias,
    w_fc1,
    fc1_bias,
    ln4_gain,
    ln4_bias,
    w_fc2,
    fc2_bias,
):
    low_qkv = w_qkv.astype(jnp.bfloat16)
    low_out = w_out.astype(jnp.bfloat16)
    low_heads = head_scale.astype(jnp.bfloat16)
    low_up = w_fc1.astype(jnp.bfloat16)
    low_down = w_fc2.astype(jnp.bfloat16)
    whole = (
        lax.all_gather(low_qkv, "shard", axis=0, tiled=True),
        lax.all_gather(qv_bias.astype(jnp.bfloat16), "shard", axis=1, tiled=True),
        lax.all_gather(low_out, "shard", axis=0, tiled=True),
        lax.all_gather(out_bias.astype(jnp.bfloat16), "shard", axis=0, tiled=True),
        lax.all_gather(low_heads, "shard", axis=0, tiled=True),
        lax.all_gather(ln1_gain.astype(jnp.bfloat16), "shard", axis=0, tiled=True),
        lax.all_gather(ln1_bias.astype(jnp.bfloat16), "shard", axis=0, tiled=True),
        lax.all_gather(ln2_gain.astype(jnp.bfloat16), "shard", axis=0, tiled=True),
        lax.all_gather(ln2_bias.astype(jnp.bfloat16), "shard", axis=0, tiled=True),
        lax.all_gather(ln3_gain.astype(jnp.bfloat16), "shard", axis=0, tiled=True),
        lax.all_gather(ln3_bias.astype(jnp.bfloat16), "shard", axis=0, tiled=True),
        lax.all_gather(low_up, "shard", axis=0, tiled=True),
        lax.all_gather(fc1_bias.astype(jnp.bfloat16), "shard", axis=0, tiled=True),
        lax.all_gather(ln4_gain.astype(jnp.bfloat16), "shard", axis=0, tiled=True),
        lax.all_gather(ln4_bias.astype(jnp.bfloat16), "shard", axis=0, tiled=True),
        lax.all_gather(low_down, "shard", axis=0, tiled=True),
        lax.all_gather(fc2_bias.astype(jnp.bfloat16), "shard", axis=0, tiled=True),
    )
    weight_qkv, weight_out, weight_up, weight_down = (whole[0], whole[2], whole[11], whole[15])
    (
        bias_qv,
        bias_out,
        head_gain,
        gain_one,
        shift_one,
        gain_two,
        shift_two,
        gain_three,
        shift_three,
        bias_up,
        gain_four,
        shift_four,
        bias_down,
    ) = tuple(
        (whole[index].astype(jnp.float32) for index in (1, 3, 4, 5, 6, 7, 8, 9, 10, 12, 13, 14, 16))
    )
    length = layer_input.shape[0]
    scale = HEAD_DIM ** (-0.5)
    inputs = layer_input.astype(jnp.float32)
    normed_one, pull_one = jax.vjp(norm_rows, inputs, gain_one, shift_one)
    act_one = normed_one.astype(jnp.bfloat16)
    bias_full = jnp.concatenate([bias_qv[0], jnp.zeros((D,), jnp.float32), bias_qv[1]])
    qkv = (jnp.dot(act_one, weight_qkv, preferred_element_type=jnp.float32) + bias_full).astype(
        jnp.bfloat16
    )
    triple = qkv.reshape(length, 3, HEADS, HEAD_DIM)
    queries = triple[:, 0]
    keys_all = triple[:, 1]
    values_all = triple[:, 2]
    attended, totals = attend_forward(queries, keys_all, values_all, scale)
    mixed = (attended * head_gain[:, None]).reshape(length, D).astype(jnp.bfloat16)
    branch = jnp.dot(mixed, weight_out, preferred_element_type=jnp.float32) + bias_out
    normed_two, pull_two = jax.vjp(norm_rows, branch, gain_two, shift_two)
    middle = inputs + normed_two
    normed_three, pull_three = jax.vjp(norm_rows, middle, gain_three, shift_three)
    act_three = normed_three.astype(jnp.bfloat16)
    hidden = jnp.dot(act_three, weight_up, preferred_element_type=jnp.float32) + bias_up
    normed_four, pull_four = jax.vjp(ffn_middle, hidden, gain_four, shift_four)
    act_four = normed_four.astype(jnp.bfloat16)
    result = middle + (
        jnp.dot(act_four, weight_down, preferred_element_type=jnp.float32) + bias_down
    )
    output = result.astype(jnp.bfloat16)
    again = (
        lax.all_gather(low_qkv, "shard", axis=0, tiled=True),
        lax.all_gather(low_out, "shard", axis=0, tiled=True),
        lax.all_gather(low_heads, "shard", axis=0, tiled=True),
        lax.all_gather(low_up, "shard", axis=0, tiled=True),
        lax.all_gather(low_down, "shard", axis=0, tiled=True),
    )
    back_qkv, back_out, back_up, back_down = (again[0], again[1], again[3], again[4])
    back_heads = again[2].astype(jnp.float32)
    cot_full = cotangent.astype(jnp.float32)
    grad_down_bias = jnp.sum(cot_full, axis=0)
    grad_down = jnp.einsum("tf,td->fd", act_four, cotangent, preferred_element_type=jnp.float32)
    grad_four = jnp.einsum("td,fd->tf", cotangent, back_down, preferred_element_type=jnp.float32)
    grad_hidden, grad_gain_four, grad_shift_four = pull_four(grad_four)
    hidden_low = grad_hidden.astype(jnp.bfloat16)
    grad_up_bias = jnp.sum(hidden_low, axis=0, dtype=jnp.float32)
    grad_up = jnp.einsum("td,tf->df", act_three, hidden_low, preferred_element_type=jnp.float32)
    grad_three = jnp.einsum("tf,df->td", hidden_low, back_up, preferred_element_type=jnp.float32)
    grad_mid_part, grad_gain_three, grad_shift_three = pull_three(grad_three)
    grad_middle = cot_full + grad_mid_part
    grad_branch, grad_gain_two, grad_shift_two = pull_two(grad_middle)
    branch_low = grad_branch.astype(jnp.bfloat16)
    grad_out_b = jnp.sum(branch_low, axis=0, dtype=jnp.float32)
    grad_out_w = jnp.einsum("td,te->de", mixed, branch_low, preferred_element_type=jnp.float32)
    grad_mixed = jnp.einsum("te,de->td", branch_low, back_out, preferred_element_type=jnp.float32)
    grad_mixed = grad_mixed.reshape(length, HEADS, HEAD_DIM)
    grad_heads = jnp.sum(grad_mixed * attended, axis=(0, 2))
    grad_attended = (grad_mixed * back_heads[:, None]).astype(jnp.bfloat16)
    grad_queries, grad_keys, grad_values = attend_backward(
        queries, keys_all, values_all, totals, grad_attended, scale
    )
    grad_qkv = (
        jnp.stack([grad_queries, grad_keys, grad_values], axis=1)
        .reshape(length, 3 * D)
        .astype(jnp.bfloat16)
    )
    grad_qv = jnp.stack(
        [
            jnp.sum(grad_qkv[:, :D], axis=0, dtype=jnp.float32),
            jnp.sum(grad_qkv[:, 2 * D :], axis=0, dtype=jnp.float32),
        ]
    )
    grad_qkv_w = jnp.einsum("td,te->de", act_one, grad_qkv, preferred_element_type=jnp.float32)
    grad_one = jnp.einsum("te,de->td", grad_qkv, back_qkv, preferred_element_type=jnp.float32)
    grad_in_part, grad_gain_one, grad_shift_one = pull_one(grad_one)
    grad_input = grad_middle + grad_in_part
    shares = (
        lax.psum_scatter(grad_qkv_w, "shard", scatter_dimension=0, tiled=True),
        lax.psum_scatter(grad_qv, "shard", scatter_dimension=1, tiled=True),
        lax.psum_scatter(grad_out_w, "shard", scatter_dimension=0, tiled=True),
        lax.psum_scatter(grad_out_b, "shard", scatter_dimension=0, tiled=True),
        lax.psum_scatter(grad_heads, "shard", scatter_dimension=0, tiled=True),
        lax.psum_scatter(grad_gain_one, "shard", scatter_dimension=0, tiled=True),
        lax.psum_scatter(grad_shift_one, "shard", scatter_dimension=0, tiled=True),
        lax.psum_scatter(grad_gain_two, "shard", scatter_dimension=0, tiled=True),
        lax.psum_scatter(grad_shift_two, "shard", scatter_dimension=0, tiled=True),
        lax.psum_scatter(grad_gain_three, "shard", scatter_dimension=0, tiled=True),
        lax.psum_scatter(grad_shift_three, "shard", scatter_dimension=0, tiled=True),
        lax.psum_scatter(grad_up, "shard", scatter_dimension=0, tiled=True),
        lax.psum_scatter(grad_up_bias, "shard", scatter_dimension=0, tiled=True),
        lax.psum_scatter(grad_gain_four, "shard", scatter_dimension=0, tiled=True),
        lax.psum_scatter(grad_shift_four, "shard", scatter_dimension=0, tiled=True),
        lax.psum_scatter(grad_down, "shard", scatter_dimension=0, tiled=True),
        lax.psum_scatter(grad_down_bias, "shard", scatter_dimension=0, tiled=True),
    )
    summed = lax.psum(
        (
            shares[0],
            shares[1],
            shares[2],
            shares[3],
            shares[4],
            shares[5],
            shares[6],
            shares[7],
            shares[8],
            shares[9],
            shares[10],
            shares[11],
            shares[12],
            shares[13],
            shares[14],
            shares[15],
            shares[16],
        ),
        "rep",
    )
    return (output, grad_input) + tuple(summed)


MESH = pl.DeviceIdType.MESH
BF16 = jnp.bfloat16
F32 = jnp.float32
UNIT_ROWS = 256
UNIT_COLS = 1024
MIB = 1 << 20
SLOT = {
    "d1": 0, "d2": 1, "z1": 2, "z3": 2, "z2": 3, "u1": 4, "w1": 4, "u2": 5, "w2": 5, "u3": 6, "w3": 6, "g1": 7, "g2": 8,
}


def unit_table(dims):
    table = []
    for matrix in (3, 2, 1, 0):
        rows, cols = dims[matrix]
        for col in range(0, cols, UNIT_COLS):
            for row in range(0, rows, UNIT_ROWS):
                table.append((matrix, row, col))
    return table


KINDS = (
    "X", "ZY", "ZY", "Y", "X", "Y", "X", "Y", "ZY", "X", "Y", "Y", "X", "Y", "ZY", "X", "ZY", "X", "X", "Y",
    "X", "Y", "X", "ZY",
)
TASK, VECTORS = 24, 25
ORDER = (
    0, 7, 1, 6, 24, 24, 24, 24, 5, 24, 24, 24, 24, 24, 2, 3, 4, 24, 24, 24, 24, 7, 1, 24, 0, 9, 14, 24, 6, 5, 4,
    10, 24, 24, 2, 0, 24, 7, 24, 3, 17, 4, 11, 24, 14, 24, 15, 3, 5, 8, 9, 1, 10, 24, 4, 6, 24, 7, 3, 17, 0, 11,
    1, 21, 2, 4, 12, 14, 5, 0, 7, 15, 8, 1, 10, 11, 24, 9, 17, 3, 2, 13, 18, 5, 11, 0, 4, 14, 21, 24, 20, 7, 8,
    5, 24, 15, 3, 6, 11, 17, 9, 7, 16, 1, 6, 4, 19, 2, 15, 3, 17, 14, 13, 12, 5, 6, 17, 9, 4, 7, 11, 0, 18, 22,
    15, 14, 5, 1, 7, 4, 10, 0, 9, 8, 17, 15, 6, 23, 16, 0, 3, 11, 2, 6, 24, 10, 15, 1, 22, 19, 9, 21, 12, 3, 18,
    16, 20, 6, 23, 11, 4, 1, 15, 8, 13, 17, 25, 9, 14, 7, 10, 19, 2, 20, 21, 11, 23, 18, 17, 10, 25, 8, 1, 6,
    22, 21, 19, 9, 13, 23, 2, 3, 22, 10, 0, 5, 15, 12, 20, 19, 21, 13, 23, 21, 10, 16, 18, 12, 22, 12, 13, 2,
    11, 9, 21, 18, 19, 21, 23, 16, 20, 22, 18, 19, 15, 20, 3, 5, 7, 2, 14, 13, 18, 20, 23, 22, 12, 8, 16, 19,
    18, 19, 20, 25, 5, 13, 1, 10, 14, 17, 13, 12, 8, 22, 16, 0, 20, 25, 2, 23, 22, 8, 9, 18, 16, 12, 23, 11, 20,
    21, 6, 14, 18, 22, 12, 19, 14, 16, 21, 16, 13, 4, 23, 20, 16, 8, 23, 15, 22, 19, 10, 25, 17, 8, 13, 12,
)


GIVE_ROWS = 240


def program_order(units, ends):
    order, task, vector, waited, step = [], 0, 0, {3}, [0] * len(units)
    order.append(("wait", 3, 0))
    for entry in ORDER:
        if entry == TASK:
            order.append(("task", task, 0))
            task += 1
            continue
        if entry == VECTORS:
            order.append(("vec", vector, 0))
            vector += 1
            continue
        m = units[entry][0]
        if m not in waited:
            assert task >= ends[m]
            order.append(("wait", m, 0))
            waited.add(m)
        order.append(("sum", entry, step[entry]))
        step[entry] += 1
    return order


PAIRS = 2


def fold(v):
    total = v[0:8]
    for k in range(1, v.shape[0] // 8):
        total = total + v[8 * k : 8 * k + 8]
    return total


def layer_kernel(dims, at_base, g_base, *refs):
    x_in, cot_in, weights, params = refs[0], refs[1], refs[2:6], refs[6:19]
    y_out, dx_out, res, vec_out, tiles_hbm = refs[19:24]
    (
        at, g, give, pair, line_xy, line_z, ring, big, left, act, hid, qkv, probs, attended, branch, middle, dmid,
        late_in, vec_w, vec_h, rstd4, sums4, vec_in, vec_own, vec_got,
        send, recv, v_send, v_recv, p_send, p_recv, l_sem, w_in, w_keep, w_send, w_recv, t_sem, s_sem, e_sem,
    ) = refs[24:]
    r = lax.axis_index("rep")
    c = lax.axis_index("shard")
    x, y, z = r % 2, (r // 2) % 2, r // 4
    core = {"shard": 1 - c}
    to = {
        "X": {"rep": r + 1 - 2 * x},
        "Y": {"rep": r + 2 - 4 * y},
        "U": {"rep": r + 4},
        "D": {"rep": r - 4},
    }
    line_end = (z == 0) | (z == 3)
    line_mid = (z == 1) | (z == 2)
    outward = {"rep": r + 4 * (2 * (z // 2) - 1)}
    inward = {"rep": r + 4 * (1 - 2 * (z // 2))}
    across = {"rep": r + 4 * (3 - 2 * z)}
    upper = z // 2
    length = x_in.shape[0]
    width = x_in.shape[1]
    half_w = width // 2
    hidden = dims[2][1]
    half_h = hidden // 2
    blocks = hidden // width
    TILE = 512

    tile_of = []
    for m, (rows, cols) in enumerate(dims):
        for row in range(0, rows, TILE):
            for col in range(0, cols, UNIT_COLS):
                tile_of.append((m, row, col))
    first_tile = [min(t for t, v in enumerate(tile_of) if v[0] == m) for m in range(4)]
    parts = 2 * len(tile_of)
    slots_f, slots_b, late, slots_l, slots_g = 6, 16, 16, 3, 7

    def part_read(i):
        m, row, col = tile_of[i // 2]
        return pltpu.make_async_copy(
            weights[m].at[pl.ds(row + (i % 2) * 256, 256), pl.ds(col, UNIT_COLS)],
            late_in.at[pl.ds((i % slots_l) * 256, 256), :] if i >= late else big.at[pl.ds((i % slots_f) * 256, 256), :],
            w_in.at[slots_f + i % slots_l if i >= late else i % slots_f],
        )

    def low_row(i):
        return 240 * 16 + (i - late) % slots_g * 256 if i >= late else i * 256

    def part_low(i):
        return low_buf.at[pl.ds(low_row(i), 256), :]

    low_buf = give

    def part_place(i):
        return tiles_hbm.at[c, i // 2, pl.ds((i % 2) * 256, 256), :]

    def part_keep(i):
        return pltpu.make_async_copy(part_low(i), part_place(i), w_keep.at[i % slots_b])

    def part_give(i):
        return pltpu.make_async_remote_copy(
            src_ref=part_low(i), dst_ref=part_place(i), send_sem=w_send.at[i % slots_b], recv_sem=w_recv.at[i],
            device_id=core, device_id_type=MESH,
        )

    def part_got(i):
        return pltpu.make_async_remote_copy(
            src_ref=part_low(i), dst_ref=tiles_hbm.at[1 - c, i // 2, pl.ds((i % 2) * 256, 256), :],
            send_sem=w_send.at[i % slots_b], recv_sem=w_recv.at[i], device_id=core, device_id_type=MESH,
        )

    for i in range(slots_f):
        part_read(i).start()

    barrier = pltpu.get_barrier_semaphore()
    for peer in (core, to["X"], to["Y"]):
        pl.semaphore_signal(barrier, inc=1, device_id=peer, device_id_type=MESH)

    @pl.when(z < 3)
    def _():
        pl.semaphore_signal(barrier, inc=1, device_id=to["U"], device_id_type=MESH)

    @pl.when(z > 0)
    def _():
        pl.semaphore_signal(barrier, inc=1, device_id=to["D"], device_id_type=MESH)

    @pl.when(line_end)
    def _():
        pl.semaphore_signal(barrier, inc=1, device_id=across, device_id_type=MESH)

    narrow = (0, 0, 2, 3, 4, 5, 6, 7, 8, 9, 10)

    def rounded(v):
        return v.astype(BF16).astype(F32)

    lane_w = pl.ds(pl.multiple_of(c * half_w, half_w), half_w)
    lane_h = pl.ds(pl.multiple_of(c * half_h, half_h), half_h)
    (qv_ref, ob_ref, hs_ref, g1_ref, b1_ref, g2_ref, b2_ref, g3_ref, b3_ref, ub_ref, g4_ref, b4_ref, db_ref) = params
    vec_w[0:2, lane_w] = rounded(qv_ref[...])
    for row, ref in zip((2, 4, 5, 6, 7, 8, 9, 10), (ob_ref, g1_ref, b1_ref, g2_ref, b2_ref, g3_ref, b3_ref, db_ref)):
        vec_w[row : row + 1, lane_w] = rounded(ref[...])
    head_of = lax.broadcasted_iota(jnp.int32, (1, half_w), 1) // 64
    spread = jnp.zeros((1, half_w), F32)
    for h in range(half_w // 64):
        spread = jnp.where(head_of == h, rounded(hs_ref[0:1, h : h + 1]), spread)
    vec_w[3:4, lane_w] = spread
    for row, ref in enumerate((ub_ref, g4_ref, b4_ref)):
        vec_h[row : row + 1, lane_h] = rounded(ref[...])
    QB, VB, OB, HS, G1, B1, G2, B2, G3, B3, DB = range(11)
    UB, G4, B4 = range(3)

    def small_copy(k, give_it):
        ref, lane, far = ((vec_w, lane_w, 1 - c), (vec_h, lane_h, 1 - c))[k]
        size = half_w if k == 0 else half_h
        other = pl.ds(pl.multiple_of((1 - c) * size, size), size)
        here = ref.at[:, lane]
        return pltpu.make_async_remote_copy(
            src_ref=here, dst_ref=here if give_it else ref.at[:, other], send_sem=s_sem.at[k, 0], recv_sem=s_sem.at[k, 1],
            device_id=core, device_id_type=MESH,
        )

    e_copy = pltpu.make_async_copy(cot_in, g.at[pl.ds(0, length), pl.ds(g_base[3], width)], e_sem.at[0])
    e_copy.start()

    def left_own(m):
        rows = dims[m][0]
        return pltpu.make_async_copy(
            left.at[pl.ds(pl.multiple_of(2 * at_base[m] + c * rows, 512), rows), :],
            at.at[pl.ds(at_base[m], rows), pl.ds(0, length)],
            l_sem.at[m],
        )

    def left_far(m):
        rows = dims[m][0]
        return pltpu.make_async_remote_copy(
            src_ref=left.at[pl.ds(pl.multiple_of(2 * at_base[m] + (1 - c) * rows, 512), rows), :],
            dst_ref=at.at[pl.ds(at_base[m], rows), pl.ds(length, length)],
            send_sem=p_send.at[m, 0], recv_sem=p_recv.at[m, 0], device_id=core, device_id_type=MESH,
        )

    def right_far(m):
        cols = pl.ds(g_base[m], dims[m][1])
        return pltpu.make_async_remote_copy(
            src_ref=g.at[pl.ds(0, length), cols], dst_ref=g.at[pl.ds(length, length), cols],
            send_sem=p_send.at[m, 1], recv_sem=p_recv.at[m, 1], device_id=core, device_id_type=MESH,
        )

    def start_left(m):
        left_own(m).start()
        left_far(m).start()

    def wait_pair(m):
        left_own(m).wait()
        left_far(m).wait()
        right_far(m).wait()

    converted, kept_parts, given_parts = [0], set(), set()

    def kept(i):
        if i not in kept_parts:
            kept_parts.add(i)
            part_keep(i).wait()

    def given(i):
        if i not in given_parts:
            given_parts.add(i)
            part_give(i).wait_send()

    def convert_parts(upto):
        for i in range(converted[0], upto):
            part_read(i).wait()
            if i >= slots_b:
                kept(i - slots_b)
            if i == late:
                for k in range(late):
                    kept(k)
                    given(k)
            if i >= late + slots_g:
                kept(i - slots_g)
                given(i - slots_g)
            source, first = (late_in, i % slots_l * 256) if i >= late else (big, i % slots_f * 256)

            def convert(b, _, i=i, source=source, first=first):
                rows = pl.multiple_of(first + b * 32, 32)
                low = pl.multiple_of(low_row(i) + b * 32, 32)
                low_buf[pl.ds(low, 32), :] = source[pl.ds(rows, 32), :].astype(BF16)
                return 0

            lax.fori_loop(0, 8, convert, 0)
            part_keep(i).start()
            if i == 0:
                pl.semaphore_wait(barrier, 5)
                small_copy(0, True).start()
                small_copy(1, True).start()
            part_give(i).start()
            if i >= late and i + slots_l < parts:
                part_read(i + slots_l).start()
            if i + slots_f < late:
                part_read(i + slots_f).start()
            if i == late - slots_f:
                for k in range(slots_l):
                    part_read(late + k).start()
        converted[0] = max(converted[0], upto)

    convert_parts(2)
    e_copy.wait()
    right_far(3).start()
    convert_parts(4)

    def tile(m, half, index):
        return (half, first_tile[m] + index)

    stream = []
    for m in (0, 1, 2):
        for index in range(dims[m][1] // UNIT_COLS):
            stream += [tile(m, 0, index), tile(m, 1, index)]
    per_half = dims[3][0] // TILE
    stream += [tile(3, h, k) for h in range(2) for k in range(per_half)]
    for m in (2, 1, 0):
        for index in range(dims[m][1] // UNIT_COLS):
            stream += [tile(m, 0, index), tile(m, 1, index)]
    slots_t = 4
    here = set()

    def tile_load(i):
        half, t = stream[i]
        return pltpu.make_async_copy(
            tiles_hbm.at[half, t], ring.at[i % slots_t], t_sem.at[i % slots_t]
        )

    def tile_start(i):
        half, t = stream[i]
        if (1, t) not in here:
            here.add((1, t))
            convert_parts(2 * t + 2)
            for k in (2 * t, 2 * t + 1):
                kept(k)
                part_got(k).wait_recv()
        tile_load(i).start()

    at_tile, started, allowed_to = [0], [0], [0]

    def fill(limit=None):
        if limit is not None:
            allowed_to[0] = limit
        while started[0] < min(at_tile[0] + slots_t, allowed_to[0], len(stream)):
            tile_start(started[0])
            started[0] += 1

    def next_tile(ahead=0):
        i = at_tile[0] + ahead
        assert i < started[0]
        tile_load(i).wait()
        return ring.at[i % slots_t]

    def done_tile(count=1):
        at_tile[0] += count
        fill()

    def mean(v):
        return jnp.sum(v, axis=-1, keepdims=True) / v.shape[-1]

    def normal(v):
        centred = v - mean(v)
        scale = lax.rsqrt(mean(centred * centred) + 1e-05)
        return centred * scale, scale

    def each(fn, step=32, init=0, unroll=1):
        def body(i, carry):
            return fn(pl.ds(pl.multiple_of(i * step, step), step), carry)

        return lax.fori_loop(0, length // step, body, init, unroll=unroll)

    def w_row(i):
        return vec_w[i : i + 1, :]

    def turn(source, m, block=0):
        for k in range(width // 256):
            row = 2 * at_base[m] + block * width + k * 256
            left[row : row + 256, :] = jnp.transpose(source[:, k * 256 : (k + 1) * 256])

    NT = (((1,), (1,)), ((), ()))
    TN = (((0,), (0,)), ((), ()))

    def nt(a, b):
        return lax.dot_general(a, b, NT, preferred_element_type=F32)

    def tn(a, b):
        return lax.dot_general(a, b, TN, preferred_element_type=F32)

    def product_pair(source, write):
        first, second = next_tile(), next_tile(1)
        for k in range(UNIT_COLS // 256):
            cols = slice(k * 256, (k + 1) * 256)
            value = jnp.dot(source[:, 0:half_w], first[:, cols], preferred_element_type=F32)
            value = value + jnp.dot(source[:, half_w:width], second[:, cols], preferred_element_type=F32)
            write(cols, value)
        done_tile(2)

    small_copy(0, True).wait_send()
    small_copy(1, True).wait_send()
    small_copy(0, False).wait_recv()
    small_copy(1, False).wait_recv()

    def first_norm(rows, _):
        hat, _s = normal(x_in[rows, :].astype(F32))
        act[rows, :] = (hat * w_row(G1) + w_row(B1)).astype(BF16)
        return 0

    each(first_norm, unroll=2)
    fill(8)
    for index in range(3):

        def put_qkv(cols, value, index=index):
            if index == 0:
                value = value + vec_w[QB : QB + 1, cols]
            if index == 2:
                value = value + vec_w[VB : VB + 1, cols]
            qkv[:, index * width + cols.start : index * width + cols.stop] = value.astype(BF16)

        product_pair(act, put_qkv)
        convert_parts(10 + 2 * index)
    turn(act, 0)
    start_left(0)
    convert_parts(16)

    low_lane = lax.broadcasted_iota(jnp.int32, (length, 128), 1) < 64
    allowed = lax.broadcasted_iota(jnp.int32, (length, length), 1) <= lax.broadcasted_iota(
        jnp.int32, (length, length), 0
    )
    scale = 64 ** (-0.5)
    keep_lane = (low_lane.astype(F32).astype(BF16), jnp.logical_not(low_lane).astype(F32).astype(BF16))

    def split_heads(v):
        return jnp.concatenate([v * keep_lane[0], v * keep_lane[1]], axis=0)

    def attend(p):
        q = qkv[:, pl.ds(pl.multiple_of(p * 128, 128), 128)]
        k = qkv[:, pl.ds(pl.multiple_of(width + p * 128, 128), 128)]
        v = qkv[:, pl.ds(pl.multiple_of(2 * width + p * 128, 128), 128)]
        both = nt(q, split_heads(k)) * scale
        got = []
        for h in range(2):
            scores = jnp.where(allowed, both[:, h * length : (h + 1) * length], -1e30)
            top = jnp.max(scores, axis=-1, keepdims=True)
            lse = top + jnp.log(jnp.sum(jnp.exp(scores - top), axis=-1, keepdims=True))
            got.append(jnp.exp(scores - lse))
        prob = jnp.concatenate(got, axis=1)
        probs[p] = prob
        value = jnp.dot(prob.astype(BF16), split_heads(v), preferred_element_type=F32)
        cols = pl.ds(pl.multiple_of(p * 128, 128), 128)
        attended[:, cols] = value
        act[:, cols] = (value * vec_w[HS : HS + 1, cols]).astype(BF16)

    def attend_some(i, _):
        for n in range(PAIRS):
            attend(i * PAIRS + n)
        return 0

    lax.fori_loop(0, width // 128 // PAIRS, attend_some, 0)
    fill(10)

    def put_branch(cols, value):
        branch[:, cols] = value + vec_w[OB : OB + 1, cols]

    product_pair(act, put_branch)
    fill(16)
    turn(act, 1)
    start_left(1)

    def second_norm(rows, _):
        hat, _s = normal(branch[rows, :])
        mid = x_in[rows, :].astype(F32) + (hat * w_row(G2) + w_row(B2))
        middle[rows, :] = mid
        hat, _s = normal(mid)
        act[rows, :] = (hat * w_row(G3) + w_row(B3)).astype(BF16)
        return 0

    each(second_norm, unroll=2)
    U0, H0, D0 = 0, blocks * length, 2 * blocks * length
    for j in range(blocks):

        def put_hidden(cols, value, j=j):
            wide = slice(j * width + cols.start, j * width + cols.stop)
            big[U0 + j * length : U0 + (j + 1) * length, cols] = value + vec_h[UB : UB + 1, wide]

        product_pair(act, put_hidden)
    turn(act, 2)
    start_left(2)
    root_half = 0.7071067811865476

    def near(base, start):
        return pl.ds(pl.multiple_of(base + start, 16), 16)

    def hidden_norm(rows, _):
        total = jnp.zeros((16, 1), F32)
        for j in range(blocks):
            u = big[near(U0 + j * length, rows.start), :]
            h = u * (1.0 + lax.erf(u * root_half)) * 0.5
            big[near(H0 + j * length, rows.start), :] = h
            total = total + jnp.sum(h, axis=-1, keepdims=True)
        centre = total / hidden
        total = jnp.zeros((16, 1), F32)
        for j in range(blocks):
            h = big[near(H0 + j * length, rows.start), :] - centre
            total = total + jnp.sum(h * h, axis=-1, keepdims=True)
        s = lax.rsqrt(total / hidden + 1e-05)
        rstd4[rows, :] = jnp.broadcast_to(s, (16, 128))
        for j in range(blocks):
            at_h = near(H0 + j * length, rows.start)
            hat = (big[at_h, :] - centre) * s
            big[at_h, :] = hat
            cols = slice(j * width, (j + 1) * width)
            hid[near(j * length, rows.start), :] = (
                hat * vec_h[G4 : G4 + 1, cols] + vec_h[B4 : B4 + 1, cols]
            ).astype(BF16)
        return 0

    each(hidden_norm, 16)
    for j in range(blocks):
        turn(hid.at[pl.ds(j * length, length), :], 3, j)
    start_left(3)
    convert_parts(parts)

    tasks = []
    zeros8 = jnp.zeros((8, width), F32)
    dirs = g.at[pl.ds(0, length), :]

    def put_sum(row, value):
        line = jnp.sum(value, axis=0, keepdims=True)
        vec_in[0, row : row + 1, :] = line[:, 0:half_w]
        vec_in[1, row : row + 1, :] = line[:, half_w:width]

    def task_down(h, k):
        def run():
            w = next_tile()
            row = h * dims[3][0] + k * TILE
            j, lane = row // width, row % width
            if h == 0 and k == 0:
                y_acc[...] = middle[...] + w_row(DB)
            for n in range(TILE // 256):
                big[D0 + j * length : D0 + (j + 1) * length, lane + n * 256 : lane + (n + 1) * 256] = nt(
                    dirs[:, g_base[3] : g_base[3] + width], w[n * 256 : (n + 1) * 256, :]
                )

            for n in range(width // 256):
                cols = slice(n * 256, (n + 1) * 256)
                y_acc[:, cols] += jnp.dot(
                    hid[j * length : (j + 1) * length, lane : lane + TILE], w[:, cols], preferred_element_type=F32
                )
            done_tile()
            if h == 1 and k == per_half - 1:
                y_out[...] = y_acc[...].astype(BF16)

        return run

    y_acc = dmid
    for h in range(2):
        for k in range(per_half):
            tasks.append((1.2, task_down(h, k)))

    def task_hidden(first, count):
        def run():
            if first == 0:
                sums4[...] = jnp.zeros_like(sums4)

                def e_sum(rows, carry):
                    return carry + fold(dirs[rows, g_base[3] : g_base[3] + width].astype(F32))

                put_sum(DB, each(e_sum, 32, zeros8))

            def body(i, _):
                at_r = pl.multiple_of(first + i * 16, 16)
                one = jnp.zeros((16, 1), F32)
                two = jnp.zeros((16, 1), F32)
                for j in range(blocks):
                    gain = vec_h[G4 : G4 + 1, j * width : (j + 1) * width]
                    d = big[near(D0 + j * length, at_r), :] * gain
                    hat = big[near(H0 + j * length, at_r), :]
                    one = one + jnp.sum(d, axis=-1, keepdims=True)
                    two = two + jnp.sum(d * hat, axis=-1, keepdims=True)
                one, two = one / hidden, two / hidden
                s = rstd4[pl.ds(at_r, 16), 0:1]
                for j in range(blocks):
                    cols = slice(j * width, (j + 1) * width)
                    da = big[near(D0 + j * length, at_r), :]
                    hat = big[near(H0 + j * length, at_r), :]
                    u = big[near(U0 + j * length, at_r), :]
                    dh = s * (da * vec_h[G4 : G4 + 1, cols] - one - hat * two)
                    slope = 0.5 * (1.0 + lax.erf(u * root_half)) + u * (jnp.exp(u * u * -0.5) * 0.3989422804014327)
                    du = (dh * slope).astype(BF16)
                    g[pl.ds(at_r, 16), g_base[2] + j * width : g_base[2] + (j + 1) * width] = du
                    sums4[0:8, cols] += fold(du.astype(F32))
                    sums4[8:16, cols] += fold(da * hat)
                    sums4[16:24, cols] += fold(da)
                return 0

            lax.fori_loop(0, count // 16, body, 0)
            if first + count == length:
                for i in range(3):
                    line = jnp.sum(sums4[8 * i : 8 * i + 8, :], axis=0, keepdims=True)
                    for n in range(hidden // half_w):
                        hh, k = divmod(n, half_h // half_w)
                        vec_in[hh, 11 + 4 * i + k : 12 + 4 * i + k, :] = line[:, n * half_w : (n + 1) * half_w]
                right_far(2).start()

        return run

    for first in range(0, length, 32):
        tasks.append((3.0, task_hidden(first, 32)))

    def add_pair(acc, index_of, cols_of, count, width_to):
        def make(index):
            def run():
                for h in range(2):
                    w = next_tile()
                    for n in range(TILE // 256):
                        cols = slice(h * half_w + n * 256, h * half_w + (n + 1) * 256)
                        value = nt(dirs[:, cols_of(index)], w[n * 256 : (n + 1) * 256, :])
                        if index == 0:
                            acc[:, cols] = value
                        else:
                            acc[:, cols] += value
                    done_tile()

            return run

        return [(1.2, make(index)) for index in range(count)]

    ends = {2: len(tasks)}
    acc = big.at[pl.ds(U0, length), :]
    tasks += add_pair(acc, None, lambda j: slice(g_base[2] + j * width, g_base[2] + (j + 1) * width), blocks, width)

    def task_norms():
        def body(rows, carry):
            s3g, s3b, s2g, s2b, sob = carry
            da = acc[rows, :]
            hat, s = normal(middle[rows, :])
            d = da * w_row(G3)
            d_mid = dirs[rows, g_base[3] : g_base[3] + width].astype(F32) + s * (d - mean(d) - hat * mean(d * hat))
            dmid[rows, :] = d_mid
            s3g, s3b = s3g + fold(da * hat), s3b + fold(da)
            hat, s = normal(branch[rows, :])
            d = d_mid * w_row(G2)
            dy = (s * (d - mean(d) - hat * mean(d * hat))).astype(BF16)
            s2g, s2b = s2g + fold(d_mid * hat), s2b + fold(d_mid)
            g[rows, g_base[1] : g_base[1] + width] = dy
            return (s3g, s3b, s2g, s2b, sob + fold(dy.astype(F32)))

        got = each(body, 16, (zeros8,) * 5)
        for row, value in zip((G3, B3, G2, B2, OB), got):
            put_sum(row, value)
        right_far(1).start()

    tasks.append((2.5, task_norms))
    ends[1] = len(tasks)
    d_mixed = big.at[pl.ds(U0 + length, length), :]
    tasks += add_pair(d_mixed, None, lambda j: slice(g_base[1], g_base[1] + width), 1, width)

    def task_heads():
        def body(rows, carry):
            d = d_mixed[rows, :]
            act[rows, :] = (d * w_row(HS)).astype(BF16)
            return carry + fold(d * attended[rows, :])

        put_sum(HS, each(body, 32, zeros8))

    tasks.append((0.6, task_heads))

    def task_attend(first, count):
        def run():
            def pair_of_heads(p):
                q_cols = pl.ds(pl.multiple_of(p * 128, 128), 128)
                k_cols = pl.ds(pl.multiple_of(width + p * 128, 128), 128)
                v_cols = pl.ds(pl.multiple_of(2 * width + p * 128, 128), 128)
                q, k, v, do = qkv[:, q_cols], qkv[:, k_cols], qkv[:, v_cols], act[:, q_cols]
                prob = probs[p]
                dv = tn(prob.astype(BF16), do)
                dp = nt(do, split_heads(v))
                ds = []
                for h in range(2):
                    own = slice(h * length, (h + 1) * length)
                    dot = jnp.sum(prob[:, own] * dp[:, own], axis=-1, keepdims=True)
                    ds.append(prob[:, own] * (dp[:, own] - dot))
                ds = jnp.concatenate(ds, axis=1).astype(BF16)
                dq = jnp.dot(ds, split_heads(k), preferred_element_type=F32) * scale
                dk = tn(ds, q) * scale
                g[0:length, q_cols] = dq.astype(BF16)
                g[0:length, k_cols] = jnp.where(low_lane, dk[0:length], dk[length : 2 * length]).astype(BF16)
                g[0:length, v_cols] = jnp.where(low_lane, dv[0:length], dv[length : 2 * length]).astype(BF16)

            for n in range(count):
                pair_of_heads(first + n)
            if first + count == width // 128:

                def sums(rows, carry):
                    a, b = carry
                    return (
                        a + fold(g[rows, 0:width].astype(F32)),
                        b + fold(g[rows, 2 * width : 3 * width].astype(F32)),
                    )

                a, b = each(sums, 32, (zeros8, zeros8))
                put_sum(QB, a)
                put_sum(VB, b)
                right_far(0).start()

        return run

    for first in range(0, width // 128, 2):
        tasks.append((3.0, task_attend(first, 2)))
    ends[0] = len(tasks)
    d_first = big.at[pl.ds(U0 + 2 * length, length), :]
    tasks += add_pair(d_first, None, lambda j: slice(j * width, (j + 1) * width), 3, width)

    def task_last():
        def body(rows, carry):
            sg, sb = carry
            da = d_first[rows, :]
            hat, s = normal(x_in[rows, :].astype(F32))
            d = da * w_row(G1)
            dx_out[rows, :] = dmid[rows, :] + s * (d - mean(d) - hat * mean(d * hat))
            return (sg + fold(da * hat), sb + fold(da))

        sg, sb = each(body, 16, (zeros8, zeros8))
        put_sum(G1, sg)
        put_sum(B1, sb)
        vec_in[0, 23:24, :] = jnp.zeros((1, half_w), F32)
        vec_in[1, 23:24, :] = jnp.zeros((1, half_w), F32)
        vec_copy(0).start()

    tasks.append((1.5, task_last))

    vec_steps = (core, to["X"], to["Y"], {"rep": r + 4 * (1 - 2 * (z % 2))}, across)

    def vec_copy(step):
        source = vec_in.at[1 - c] if step == 0 else vec_own.at[step]
        return pltpu.make_async_remote_copy(
            src_ref=source, dst_ref=vec_got.at[step], send_sem=v_send.at[step], recv_sem=v_recv.at[step],
            device_id=vec_steps[step], device_id_type=MESH,
        )

    def vec_task(k):
        vec_copy(k).wait_recv()
        total = (vec_in[c] if k == 0 else vec_own[k]) + vec_got[k]
        if k < 4:
            vec_own[k + 1] = total
            vec_copy(k + 1).start()
        else:
            vec_out[...] = total

    units = unit_table(dims)
    kinds = KINDS
    xy_at, z_at = {}, {}
    for unit, kind in enumerate(kinds):
        (z_at if kind[0] == "Z" else xy_at)[unit] = len(z_at) if kind[0] == "Z" else len(xy_at)

    def copy(unit, name, source, dest, device):
        return functools.partial(
            pltpu.make_async_remote_copy,
            src_ref=source, dst_ref=dest, send_sem=send.at[unit], recv_sem=recv.at[unit, SLOT[name]],
            device_id=device, device_id_type=MESH,
        )

    def rows_of(unit, start, count):
        if not isinstance(start, int):
            start = pl.multiple_of(start, 16)
        return res.at[unit, pl.ds(start, count), :]

    def product(unit, start, count, dest, dest_start, got=None, got_start=0):
        m, row, col = units[unit]
        step = 128 if count % 128 == 0 else min(count, 64)

        def block(index, _):
            part, strip = index // (UNIT_COLS // 256), index % (UNIT_COLS // 256)
            cols = pl.ds(pl.multiple_of(strip * 256, 256), 256)
            value = jnp.dot(
                at[pl.ds(pl.multiple_of(at_base[m] + row + start + part * step, 16), step), :],
                g[:, pl.ds(pl.multiple_of(g_base[m] + col + strip * 256, 256), 256)],
                preferred_element_type=F32,
            )
            if got is not None:
                value = value + got[pl.ds(pl.multiple_of(got_start + part * step, 16), step), cols].astype(F32)
            dest[pl.ds(pl.multiple_of(dest_start + part * step, 16), step), cols] = value.astype(BF16)
            return 0

        lax.fori_loop(0, (count // step) * (UNIT_COLS // 256), block, 0)

    def accumulate(unit, start, count, got, got_start, dest, dest_start):
        def block(strip, _):
            cols = pl.ds(pl.multiple_of(strip * 256, 256), 256)
            value = res[unit, pl.ds(pl.multiple_of(start, 16), count), cols].astype(F32)
            value = value + got[pl.ds(pl.multiple_of(got_start, 16), count), cols].astype(F32)
            dest[pl.ds(pl.multiple_of(dest_start, 16), count), cols] = value.astype(BF16)
            return 0

        lax.fori_loop(0, UNIT_COLS // 256, block, 0)

    def gather_line(unit, base, size, level):
        up, down = "u%d" % level, "w%d" % level
        low, high = z - (level - 1), z + (level - 1)

        @pl.when((low >= 0) & (z < 3))
        def _():
            part = rows_of(unit, base + low * size, size)
            copy(unit, up, part, part, to["U"])().start()

        @pl.when((high <= 3) & (z > 0))
        def _():
            part = rows_of(unit, base + high * size, size)
            copy(unit, down, part, part, to["D"])().start()

    def gather_arrived(unit, base, size, level):
        def wait(chunks):
            part = give.at[pl.ds(0, chunks * size), :]
            copy(unit, "u%d" % level, part, part, to["U"])().wait_recv()

        if level == 1:
            pl.when(line_mid)(lambda: wait(2))
        if level == 2:
            wait(1)
        else:
            pl.when(line_end)(lambda: wait(1))

    def finish(unit, ends, mids):
        def wait(rows):
            part = give.at[pl.ds(0, rows), :]
            copy(unit, "d1", part, part, to["X"])().wait_send()

        pl.when(line_end)(lambda: wait(ends))
        pl.when(line_mid)(lambda: wait(mids))

    def task_xy(unit, step):
        half, quarter, size = UNIT_ROWS // 2, UNIT_ROWS // 4, UNIT_ROWS // 16
        first, second = ("X", "Y") if kinds[unit] == "X" else ("Y", "X")
        p, q = (x, y) if kinds[unit] == "X" else (y, x)
        line, block, out, other = line_xy.at[xy_at[unit]], res.at[unit], give.at[pl.ds(unit * GIVE_ROWS, GIVE_ROWS), :], pair.at[unit]
        keep, away_half = p * half, (1 - p) * half
        base = keep + q * quarter
        away = keep + (1 - q) * quarter
        at_z = half + quarter
        d1 = copy(unit, "d1", out.at[pl.ds(0, half), :], rows_of(unit, away_half, half), to[first])
        d2 = copy(unit, "d2", out.at[pl.ds(half, quarter), :], other.at[pl.ds(0, quarter), :], to[second])
        z1 = copy(unit, "z1", out.at[pl.ds(at_z, 3 * size), :], line.at[pl.ds(0, 3 * size), :], inward)
        z2 = copy(unit, "z2", out.at[pl.ds(at_z, 2 * size), :], line.at[pl.ds(3 * size, 2 * size), :], across)
        z3 = copy(unit, "z3", out.at[pl.ds(at_z + 2 * size, size), :], line.at[pl.ds(0, size), :], outward)
        own_quarter = rows_of(unit, base, quarter)
        g2 = copy(unit, "g2", own_quarter, own_quarter, to[second])
        own_half = rows_of(unit, keep, half)
        g1 = copy(unit, "g1", own_half, own_half, to[first])
        own = base + z * size
        if step == 0:
            product(unit, away_half, half, out, 0)
            d1().start()
        elif step == 1:
            d1().wait_recv()
            product(unit, away, quarter, out, half, block, away)
            d2().start()
            product(unit, base, quarter, block, base, block, base)
        elif step == 2:
            d2().wait_recv()

            @pl.when(line_end)
            def _():
                skip = (1 - upper) * size
                accumulate(unit, base + skip, 3 * size, other, skip, out, at_z)
                z1().start()
                accumulate(unit, own, size, other, z * size, block, own)

            @pl.when(line_mid)
            def _():
                accumulate(unit, base, quarter, other, 0, block, base)

        elif step == 3:

            @pl.when(line_mid)
            def _():
                z1().wait_recv()
                accumulate(unit, base + (1 - upper) * 2 * size, 2 * size, line, (1 - upper) * size, out, at_z)
                z2().start()
                accumulate(unit, own, size, line, upper * 2 * size, block, own)

        elif step == 4:

            @pl.when(line_mid)
            def _():
                z2().wait_recv()
                accumulate(unit, base + upper * 3 * size, size, line, (3 + upper) * size, out, at_z + 2 * size)
                z3().start()
                accumulate(unit, own, size, line, (4 - upper) * size, block, own)
                gather_line(unit, base, size, 1)

        elif step == 5:

            @pl.when(line_end)
            def _():
                z3().wait_recv()
                accumulate(unit, own, size, line, 0, block, own)
                gather_line(unit, base, size, 1)

        elif step in (6, 7):
            gather_arrived(unit, base, size, step - 5)
            gather_line(unit, base, size, step - 4)
        elif step == 8:
            gather_arrived(unit, base, size, 3)
            g2().start()
        elif step == 9:
            g2().wait_recv()
            g1().start()
        else:
            g1().wait_recv()
            finish(unit, 2 * half + 2 * quarter + 4 * size, 2 * half + 2 * quarter + 8 * size)

    def task_z(unit, step):
        size, half, quarter = UNIT_ROWS // 4, UNIT_ROWS // 8, UNIT_ROWS // 16
        first, second = ("X", "Y") if kinds[unit] == "ZX" else ("Y", "X")
        p, q = (x, y) if kinds[unit] == "ZX" else (y, x)
        line, block, out, other = line_z.at[z_at[unit]], res.at[unit], give.at[pl.ds(unit * GIVE_ROWS, GIVE_ROWS), :], pair.at[unit]
        own = z * size
        keep, away_half = own + p * half, own + (1 - p) * half
        base, away = keep + q * quarter, keep + (1 - q) * quarter
        at_d = 3 * size
        z1 = copy(unit, "z1", out.at[pl.ds(0, 3 * size), :], line.at[pl.ds(0, 3 * size), :], inward)
        z2 = copy(unit, "z2", out.at[pl.ds(0, 2 * size), :], line.at[pl.ds(3 * size, 2 * size), :], across)
        z3 = copy(unit, "z3", out.at[pl.ds(2 * size, size), :], line.at[pl.ds(0, size), :], outward)
        d1 = copy(unit, "d1", out.at[pl.ds(at_d, half), :], other.at[pl.ds(0, half), :], to[first])
        d2 = copy(unit, "d2", out.at[pl.ds(at_d + half, quarter), :], other.at[pl.ds(half, quarter), :], to[second])
        own_quarter = rows_of(unit, base, quarter)
        g2 = copy(unit, "g2", own_quarter, own_quarter, to[second])
        own_half = rows_of(unit, keep, half)
        g1 = copy(unit, "g1", own_half, own_half, to[first])
        if step == 0:

            @pl.when(line_end)
            def _():
                product(unit, (1 - upper) * size, 3 * size, out, 0)
                z1().start()

        elif step == 1:

            @pl.when(line_mid)
            def _():
                z1().wait_recv()
                product(unit, (1 - upper) * 2 * size, 2 * size, out, 0, line, (1 - upper) * size)
                z2().start()
                product(unit, own, size, block, own, line, upper * 2 * size)

        elif step == 2:

            @pl.when(line_mid)
            def _():
                z2().wait_recv()
                product(unit, upper * 3 * size, size, out, 2 * size, line, (3 + upper) * size)
                z3().start()
                got = (4 - upper) * size
                accumulate(unit, away_half, half, line, got + (1 - p) * half, out, at_d)
                d1().start()
                accumulate(unit, keep, half, line, got + p * half, block, keep)

        elif step == 3:

            @pl.when(line_end)
            def _():
                z3().wait_recv()
                product(unit, away_half, half, out, at_d, line, (1 - p) * half)
                d1().start()
                product(unit, keep, half, block, keep, line, p * half)

        elif step == 4:
            d1().wait_recv()
            accumulate(unit, away, quarter, other, (1 - q) * quarter, out, at_d + half)
            d2().start()
            accumulate(unit, base, quarter, other, q * quarter, block, base)
        elif step == 5:
            d2().wait_recv()
            accumulate(unit, base, quarter, other, half, block, base)
            g2().start()
        elif step == 6:
            g2().wait_recv()
            g1().start()
        elif step == 7:
            g1().wait_recv()
            gather_line(unit, 0, size, 1)
        elif step in (8, 9):
            gather_arrived(unit, 0, size, step - 7)
            gather_line(unit, 0, size, step - 6)
        else:
            gather_arrived(unit, 0, size, 3)
            finish(unit, 2 * half + 2 * quarter + 4 * size, 2 * half + 2 * quarter + 8 * size)


    for kind, a, b in program_order(units, ends):
        if kind == "task":
            if a == 0:
                fill(len(stream))
            tasks[a][1]()
        elif kind == "wait":
            wait_pair(a)
            if a == 1:
                for k in range(parts):
                    given(k)
        elif kind == "vec":
            vec_task(a)
        elif kinds[a][0] == "Z":
            task_z(a, b)
        else:
            task_xy(a, b)
    for step in range(5):
        vec_copy(step).wait_send()


def whole_layer(layer_input, cotangent, weights, params):
    dims = tuple(w.shape for w in weights)
    at_rows = sum(rows for rows, _ in dims)
    g_cols = sum(cols for _, cols in dims)
    at_base = [sum(rows for rows, _ in dims[:m]) for m in range(4)]
    g_base = [sum(cols for _, cols in dims[:m]) for m in range(4)]
    length, width = layer_input.shape
    hidden = dims[2][1]
    blocks = hidden // width
    units = unit_table(dims)
    kinds = KINDS
    n, n_z = len(units), sum(kind[0] == "Z" for kind in kinds)
    tiles = n // 2
    hbm = pl.BlockSpec(memory_space=pl.ANY)
    vmem = pl.BlockSpec(memory_space=pltpu.VMEM)
    dma = pltpu.SemaphoreType.DMA
    small = (24, width // 2)
    got = pl.pallas_call(
        functools.partial(layer_kernel, dims, at_base, g_base),
        out_shape=[
            pltpu.VMEM((length, width), BF16),
            pltpu.VMEM((length, width), F32),
            pltpu.VMEM((n, UNIT_ROWS, UNIT_COLS), BF16),
            pltpu.VMEM(small, F32),
            jax.ShapeDtypeStruct((2, tiles, 512, UNIT_COLS), BF16),
        ],
        in_specs=[vmem, hbm] + [hbm] * 4 + [vmem] * 13,
        out_specs=[vmem] * 4 + [hbm],
        scratch_shapes=[
            pltpu.VMEM((at_rows, 2 * length), BF16),
            pltpu.VMEM((2 * length, g_cols), BF16),
            pltpu.VMEM((n * GIVE_ROWS, UNIT_COLS), BF16),
            pltpu.VMEM((n, UNIT_ROWS // 4, UNIT_COLS), BF16),
            pltpu.VMEM((n - n_z, 5 * UNIT_ROWS // 16, UNIT_COLS), BF16),
            pltpu.VMEM((n_z, 5 * UNIT_ROWS // 4, UNIT_COLS), BF16),
            pltpu.VMEM((4, 512, UNIT_COLS), BF16),
            pltpu.VMEM((3 * blocks * length, width), F32),
            pltpu.VMEM((2 * at_rows, length), BF16),
            pltpu.VMEM((length, width), BF16),
            pltpu.VMEM((blocks * length, width), BF16),
            pltpu.VMEM((length, 3 * width), BF16),
            pltpu.VMEM((width // 128, length, 2 * length), F32),
            pltpu.VMEM((length, width), F32),
            pltpu.VMEM((length, width), F32),
            pltpu.VMEM((length, width), F32),
            pltpu.VMEM((length, width), F32),
            pltpu.VMEM((3 * 256, UNIT_COLS), F32),
            pltpu.VMEM((16, width), F32),
            pltpu.VMEM((8, hidden), F32),
            pltpu.VMEM((length, 128), F32),
            pltpu.VMEM((24, hidden), F32),
            pltpu.VMEM((2,) + small, F32),
            pltpu.VMEM((5,) + small, F32),
            pltpu.VMEM((5,) + small, F32),
            dma((n,)),
            dma((n, 9)),
            dma((5,)),
            dma((5,)),
            dma((4, 2)),
            dma((4, 2)),
            dma((4,)),
            dma((10,)),
            dma((16,)),
            dma((16,)),
            dma((2 * tiles,)),
            dma((4,)),
            dma((2, 2)),
            dma((1,)),
        ],
        compiler_params=pltpu.CompilerParams(
            collective_id=0, has_side_effects=True, vmem_limit_bytes=50 * MIB
        ),
        name="whole_layer",
    )(layer_input, cotangent, *weights, *params)
    return got[:4]


def finish_kernel(dims, *refs):
    y_in, dx_in, res, vec = refs[0:4]
    y_out, dx_out, outs, smalls = refs[4], refs[5], refs[6:10], refs[10:23]
    wide, lines, o_sem, s_sem = refs[23], refs[24:37], refs[37], refs[38]
    slots = wide.shape[0]
    copies = [pltpu.make_async_copy(y_in, y_out, s_sem.at[13]), pltpu.make_async_copy(dx_in, dx_out, s_sem.at[14])]
    rows_of = [range(0, 2)] + [range(k, k + 1) for k in range(2, 11)] + [range(11 + 4 * k, 15 + 4 * k) for k in range(3)]
    for k, rows in enumerate(rows_of):
        if k == 2:
            head_of = lax.broadcasted_iota(jnp.int32, (1, vec.shape[1]), 1) // 64
            lane = lax.broadcasted_iota(jnp.int32, lines[k].shape, 1)
            total = jnp.zeros(lines[k].shape, F32)
            for h in range(vec.shape[1] // 64):
                one = jnp.sum(jnp.where(head_of == h, vec[3:4, :], 0.0), axis=-1, keepdims=True)
                total = jnp.where(lane == h, one, total)
            lines[k][...] = total
        elif len(rows) == 4:
            for j, row in enumerate(rows):
                lines[k][:, j * vec.shape[1] : (j + 1) * vec.shape[1]] = vec[row : row + 1, :]
        else:
            lines[k][...] = vec[rows.start : rows.stop, :]
        copies.append(pltpu.make_async_copy(lines[k], smalls[k], s_sem.at[k]))
    for piece in copies:
        piece.start()
    units = unit_table(dims)

    def put(unit):
        m, row, col = units[unit]
        return pltpu.make_async_copy(
            wide.at[unit % slots], outs[m].at[pl.ds(row, UNIT_ROWS), pl.ds(col, UNIT_COLS)], o_sem.at[unit % slots]
        )

    for unit in range(len(units)):
        if unit >= slots:
            put(unit - slots).wait()

        def widen(b, _, unit=unit):
            rows = pl.ds(pl.multiple_of(b * 32, 32), 32)
            wide[unit % slots, rows, :] = res[unit, rows, :].astype(F32)
            return 0

        lax.fori_loop(0, UNIT_ROWS // 32, widen, 0)
        put(unit).start()
    for unit in range(len(units) - slots, len(units)):
        put(unit).wait()
    for piece in copies:
        piece.wait()


def write_results(got, dims):
    y, dx, _, vec = got
    half = vec.shape[1]
    small = [(2, half), (1, half), (1, half // 64)] + [(1, half)] * 7 + [(1, 4 * half)] * 3
    hbm = pl.BlockSpec(memory_space=pl.ANY)
    vmem = pl.BlockSpec(memory_space=pltpu.VMEM)
    dma = pltpu.SemaphoreType.DMA
    return pl.pallas_call(
        functools.partial(finish_kernel, dims),
        out_shape=[jax.ShapeDtypeStruct(y.shape, BF16), jax.ShapeDtypeStruct(dx.shape, F32)]
        + [jax.ShapeDtypeStruct(d, F32) for d in dims]
        + [jax.ShapeDtypeStruct(s, F32) for s in small],
        in_specs=[vmem] * 4,
        out_specs=[hbm] * 19,
        scratch_shapes=[pltpu.VMEM((6, UNIT_ROWS, UNIT_COLS), F32)]
        + [pltpu.VMEM(s, F32) for s in small]
        + [dma((6,)), dma((15,))],
        compiler_params=pltpu.CompilerParams(vmem_limit_bytes=30 * MIB),
        name="write_results",
    )(*got)


def on_pair_of_cores(
    layer_input, cotangent, w_qkv, qv_bias, w_out, out_bias, head_scale, ln1_gain, ln1_bias, ln2_gain, ln2_bias,
    ln3_gain, ln3_bias, w_fc1, fc1_bias, ln4_gain, ln4_bias, w_fc2, fc2_bias,
):
    params = (
        qv_bias, out_bias, head_scale, ln1_gain, ln1_bias, ln2_gain, ln2_bias, ln3_gain, ln3_bias,
        fc1_bias, ln4_gain, ln4_bias, fc2_bias,
    )
    params = [p.reshape(-1, p.shape[-1]) for p in params]
    weights = (w_qkv, w_out, w_fc1, w_fc2)
    got = whole_layer(layer_input, cotangent, weights, params)
    output, grad_input, qkv, out, up, down, *smalls = write_results(got, tuple(w.shape for w in weights))
    rows = [s.reshape(-1) for s in smalls]
    return (
        output, grad_input, qkv, smalls[0], out, rows[1], rows[2], rows[3], rows[4], rows[5], rows[6], rows[7], rows[8], up,
        rows[10], rows[11], rows[12], down, rows[9],
    )


def fits_pair(mesh):
    return mesh.shape["shard"] == 2 and mesh.shape["rep"] == 16


def solution(mesh):
    return jax.shard_map(
        on_pair_of_cores if fits_pair(mesh) else on_any_mesh,
        mesh=mesh,
        in_specs=(
            P(("rep", "shard"), None),
            P(("rep", "shard"), None),
            P("shard", None),
            P(None, "shard"),
            P("shard", None),
            P("shard"),
            P("shard"),
            P("shard"),
            P("shard"),
            P("shard"),
            P("shard"),
            P("shard"),
            P("shard"),
            P("shard", None),
            P("shard"),
            P("shard"),
            P("shard"),
            P("shard", None),
            P("shard"),
        ),
        out_specs=(
            P(("rep", "shard"), None),
            P(("rep", "shard"), None),
            P("shard", None),
            P(None, "shard"),
            P("shard", None),
            P("shard"),
            P("shard"),
            P("shard"),
            P("shard"),
            P("shard"),
            P("shard"),
            P("shard"),
            P("shard"),
            P("shard", None),
            P("shard"),
            P("shard"),
            P("shard"),
            P("shard", None),
            P("shard"),
        ),
        check_vma=False,
    )
```

```python
import functools

import jax
import jax.numpy as jnp
from jax import lax
from jax.experimental import pallas as pl
from jax.experimental.pallas import tpu as pltpu
from jax.sharding import PartitionSpec as P

D = 1024
HEADS = 16
HEAD_DIM = 64


EPS = 1e-05
NEG = -1e30


def norm_rows(v, gain, bias):
    centre = jnp.mean(v, axis=-1, keepdims=True)
    centred = v - centre
    spread = jnp.mean(centred * centred, axis=-1, keepdims=True)
    return centred * lax.rsqrt(spread + EPS) * gain + bias


def ffn_middle(hidden, gain, bias):
    return norm_rows(jax.nn.gelu(hidden, approximate=False), gain, bias)


def causal_mask(index, qblock, length):
    rows = index * qblock + lax.iota(jnp.int32, qblock)
    cols = lax.iota(jnp.int32, length)
    return (cols[None, :] <= rows[:, None])[None]


def block_scores(queries, keys_all, index, qblock, scale):
    length = keys_all.shape[0]
    scores = (
        jnp.einsum("qhd,khd->hqk", queries, keys_all, preferred_element_type=jnp.float32) * scale
    )
    return (queries, jnp.where(causal_mask(index, qblock, length), scores, NEG))


def attend_forward(queries, keys_all, values_all, scale):
    length, heads, width = queries.shape
    qblock = min(512, length)
    blocks = length // qblock

    def one_block(index):
        rows_q, scores = block_scores(queries, keys_all, index, qblock, scale)
        total = jax.nn.logsumexp(scores, axis=-1, keepdims=True)
        probs = jnp.exp(scores - total).astype(jnp.bfloat16)
        outcome = jnp.einsum("hqk,khd->qhd", probs, values_all, preferred_element_type=jnp.float32)
        return (outcome, total)

    outcome, totals = lax.map(one_block, jnp.arange(blocks, dtype=jnp.int32))
    return (outcome.reshape(length, heads, width), totals)


def attend_backward(queries, keys_all, values_all, totals, grad_out, scale):
    length, heads, width = queries.shape
    qblock = min(512, length)
    blocks = length // qblock

    def one_block(carry, index):
        grad_keys, grad_values = carry
        rows_q, scores = block_scores(queries, keys_all, index, qblock, scale)
        probs = jnp.exp(scores - totals[index])
        probs_low = probs.astype(jnp.bfloat16)
        grad_values = grad_values + jnp.einsum(
            "hqk,qhd->khd", probs_low, grad_out, preferred_element_type=jnp.float32
        )
        grad_probs = jnp.einsum(
            "qhd,khd->hqk", grad_out, values_all, preferred_element_type=jnp.float32
        )
        row_dot = jnp.sum(probs * grad_probs, axis=-1, keepdims=True)
        grad_scores = (probs * (grad_probs - row_dot)).astype(jnp.bfloat16)
        grad_rows = (
            jnp.einsum("hqk,khd->qhd", grad_scores, keys_all, preferred_element_type=jnp.float32)
            * scale
        )
        grad_keys = (
            grad_keys
            + jnp.einsum("hqk,qhd->khd", grad_scores, rows_q, preferred_element_type=jnp.float32)
            * scale
        )
        return ((grad_keys, grad_values), grad_rows)

    empty = jnp.zeros((length, heads, width), jnp.float32)
    (grad_keys, grad_values), grad_queries = lax.scan(
        one_block, (empty, empty), jnp.arange(blocks, dtype=jnp.int32)
    )
    return (grad_queries.reshape(length, heads, width), grad_keys, grad_values)


def on_any_mesh(
    layer_input,
    cotangent,
    w_qkv,
    qv_bias,
    w_out,
    out_bias,
    head_scale,
    ln1_gain,
    ln1_bias,
    ln2_gain,
    ln2_bias,
    ln3_gain,
    ln3_bias,
    w_fc1,
    fc1_bias,
    ln4_gain,
    ln4_bias,
    w_fc2,
    fc2_bias,
):
    low_qkv = w_qkv.astype(jnp.bfloat16)
    low_out = w_out.astype(jnp.bfloat16)
    low_heads = head_scale.astype(jnp.bfloat16)
    low_up = w_fc1.astype(jnp.bfloat16)
    low_down = w_fc2.astype(jnp.bfloat16)
    whole = (
        lax.all_gather(low_qkv, "shard", axis=0, tiled=True),
        lax.all_gather(qv_bias.astype(jnp.bfloat16), "shard", axis=1, tiled=True),
        lax.all_gather(low_out, "shard", axis=0, tiled=True),
        lax.all_gather(out_bias.astype(jnp.bfloat16), "shard", axis=0, tiled=True),
        lax.all_gather(low_heads, "shard", axis=0, tiled=True),
        lax.all_gather(ln1_gain.astype(jnp.bfloat16), "shard", axis=0, tiled=True),
        lax.all_gather(ln1_bias.astype(jnp.bfloat16), "shard", axis=0, tiled=True),
        lax.all_gather(ln2_gain.astype(jnp.bfloat16), "shard", axis=0, tiled=True),
        lax.all_gather(ln2_bias.astype(jnp.bfloat16), "shard", axis=0, tiled=True),
        lax.all_gather(ln3_gain.astype(jnp.bfloat16), "shard", axis=0, tiled=True),
        lax.all_gather(ln3_bias.astype(jnp.bfloat16), "shard", axis=0, tiled=True),
        lax.all_gather(low_up, "shard", axis=0, tiled=True),
        lax.all_gather(fc1_bias.astype(jnp.bfloat16), "shard", axis=0, tiled=True),
        lax.all_gather(ln4_gain.astype(jnp.bfloat16), "shard", axis=0, tiled=True),
        lax.all_gather(ln4_bias.astype(jnp.bfloat16), "shard", axis=0, tiled=True),
        lax.all_gather(low_down, "shard", axis=0, tiled=True),
        lax.all_gather(fc2_bias.astype(jnp.bfloat16), "shard", axis=0, tiled=True),
    )
    weight_qkv, weight_out, weight_up, weight_down = (whole[0], whole[2], whole[11], whole[15])
    (
        bias_qv,
        bias_out,
        head_gain,
        gain_one,
        shift_one,
        gain_two,
        shift_two,
        gain_three,
        shift_three,
        bias_up,
        gain_four,
        shift_four,
        bias_down,
    ) = tuple(
        (whole[index].astype(jnp.float32) for index in (1, 3, 4, 5, 6, 7, 8, 9, 10, 12, 13, 14, 16))
    )
    length = layer_input.shape[0]
    scale = HEAD_DIM ** (-0.5)
    inputs = layer_input.astype(jnp.float32)
    normed_one, pull_one = jax.vjp(norm_rows, inputs, gain_one, shift_one)
    act_one = normed_one.astype(jnp.bfloat16)
    bias_full = jnp.concatenate([bias_qv[0], jnp.zeros((D,), jnp.float32), bias_qv[1]])
    qkv = (jnp.dot(act_one, weight_qkv, preferred_element_type=jnp.float32) + bias_full).astype(
        jnp.bfloat16
    )
    triple = qkv.reshape(length, 3, HEADS, HEAD_DIM)
    queries = triple[:, 0]
    keys_all = triple[:, 1]
    values_all = triple[:, 2]
    attended, totals = attend_forward(queries, keys_all, values_all, scale)
    mixed = (attended * head_gain[:, None]).reshape(length, D).astype(jnp.bfloat16)
    branch = jnp.dot(mixed, weight_out, preferred_element_type=jnp.float32) + bias_out
    normed_two, pull_two = jax.vjp(norm_rows, branch, gain_two, shift_two)
    middle = inputs + normed_two
    normed_three, pull_three = jax.vjp(norm_rows, middle, gain_three, shift_three)
    act_three = normed_three.astype(jnp.bfloat16)
    hidden = jnp.dot(act_three, weight_up, preferred_element_type=jnp.float32) + bias_up
    normed_four, pull_four = jax.vjp(ffn_middle, hidden, gain_four, shift_four)
    act_four = normed_four.astype(jnp.bfloat16)
    result = middle + (
        jnp.dot(act_four, weight_down, preferred_element_type=jnp.float32) + bias_down
    )
    output = result.astype(jnp.bfloat16)
    again = (
        lax.all_gather(low_qkv, "shard", axis=0, tiled=True),
        lax.all_gather(low_out, "shard", axis=0, tiled=True),
        lax.all_gather(low_heads, "shard", axis=0, tiled=True),
        lax.all_gather(low_up, "shard", axis=0, tiled=True),
        lax.all_gather(low_down, "shard", axis=0, tiled=True),
    )
    back_qkv, back_out, back_up, back_down = (again[0], again[1], again[3], again[4])
    back_heads = again[2].astype(jnp.float32)
    cot_full = cotangent.astype(jnp.float32)
    grad_down_bias = jnp.sum(cot_full, axis=0)
    grad_down = jnp.einsum("tf,td->fd", act_four, cotangent, preferred_element_type=jnp.float32)
    grad_four = jnp.einsum("td,fd->tf", cotangent, back_down, preferred_element_type=jnp.float32)
    grad_hidden, grad_gain_four, grad_shift_four = pull_four(grad_four)
    hidden_low = grad_hidden.astype(jnp.bfloat16)
    grad_up_bias = jnp.sum(hidden_low, axis=0, dtype=jnp.float32)
    grad_up = jnp.einsum("td,tf->df", act_three, hidden_low, preferred_element_type=jnp.float32)
    grad_three = jnp.einsum("tf,df->td", hidden_low, back_up, preferred_element_type=jnp.float32)
    grad_mid_part, grad_gain_three, grad_shift_three = pull_three(grad_three)
    grad_middle = cot_full + grad_mid_part
    grad_branch, grad_gain_two, grad_shift_two = pull_two(grad_middle)
    branch_low = grad_branch.astype(jnp.bfloat16)
    grad_out_b = jnp.sum(branch_low, axis=0, dtype=jnp.float32)
    grad_out_w = jnp.einsum("td,te->de", mixed, branch_low, preferred_element_type=jnp.float32)
    grad_mixed = jnp.einsum("te,de->td", branch_low, back_out, preferred_element_type=jnp.float32)
    grad_mixed = grad_mixed.reshape(length, HEADS, HEAD_DIM)
    grad_heads = jnp.sum(grad_mixed * attended, axis=(0, 2))
    grad_attended = (grad_mixed * back_heads[:, None]).astype(jnp.bfloat16)
    grad_queries, grad_keys, grad_values = attend_backward(
        queries, keys_all, values_all, totals, grad_attended, scale
    )
    grad_qkv = (
        jnp.stack([grad_queries, grad_keys, grad_values], axis=1)
        .reshape(length, 3 * D)
        .astype(jnp.bfloat16)
    )
    grad_qv = jnp.stack(
        [
            jnp.sum(grad_qkv[:, :D], axis=0, dtype=jnp.float32),
            jnp.sum(grad_qkv[:, 2 * D :], axis=0, dtype=jnp.float32),
        ]
    )
    grad_qkv_w = jnp.einsum("td,te->de", act_one, grad_qkv, preferred_element_type=jnp.float32)
    grad_one = jnp.einsum("te,de->td", grad_qkv, back_qkv, preferred_element_type=jnp.float32)
    grad_in_part, grad_gain_one, grad_shift_one = pull_one(grad_one)
    grad_input = grad_middle + grad_in_part
    shares = (
        lax.psum_scatter(grad_qkv_w, "shard", scatter_dimension=0, tiled=True),
        lax.psum_scatter(grad_qv, "shard", scatter_dimension=1, tiled=True),
        lax.psum_scatter(grad_out_w, "shard", scatter_dimension=0, tiled=True),
        lax.psum_scatter(grad_out_b, "shard", scatter_dimension=0, tiled=True),
        lax.psum_scatter(grad_heads, "shard", scatter_dimension=0, tiled=True),
        lax.psum_scatter(grad_gain_one, "shard", scatter_dimension=0, tiled=True),
        lax.psum_scatter(grad_shift_one, "shard", scatter_dimension=0, tiled=True),
        lax.psum_scatter(grad_gain_two, "shard", scatter_dimension=0, tiled=True),
        lax.psum_scatter(grad_shift_two, "shard", scatter_dimension=0, tiled=True),
        lax.psum_scatter(grad_gain_three, "shard", scatter_dimension=0, tiled=True),
        lax.psum_scatter(grad_shift_three, "shard", scatter_dimension=0, tiled=True),
        lax.psum_scatter(grad_up, "shard", scatter_dimension=0, tiled=True),
        lax.psum_scatter(grad_up_bias, "shard", scatter_dimension=0, tiled=True),
        lax.psum_scatter(grad_gain_four, "shard", scatter_dimension=0, tiled=True),
        lax.psum_scatter(grad_shift_four, "shard", scatter_dimension=0, tiled=True),
        lax.psum_scatter(grad_down, "shard", scatter_dimension=0, tiled=True),
        lax.psum_scatter(grad_down_bias, "shard", scatter_dimension=0, tiled=True),
    )
    summed = lax.psum(
        (
            shares[0],
            shares[1],
            shares[2],
            shares[3],
            shares[4],
            shares[5],
            shares[6],
            shares[7],
            shares[8],
            shares[9],
            shares[10],
            shares[11],
            shares[12],
            shares[13],
            shares[14],
            shares[15],
            shares[16],
        ),
        "rep",
    )
    return (output, grad_input) + tuple(summed)


MESH = pl.DeviceIdType.MESH
BF16 = jnp.bfloat16
F32 = jnp.float32
UNIT_ROWS = 256
UNIT_COLS = 1024
MIB = 1 << 20
SLOT = {
    "d1": 0, "d2": 1, "z1": 2, "z3": 2, "z2": 3, "u1": 4, "w1": 4, "u2": 5, "w2": 5, "u3": 6, "w3": 6, "g1": 7, "g2": 8,
}


def unit_table(dims):
    table = []
    for matrix in (3, 2, 1, 0):
        rows, cols = dims[matrix]
        for col in range(0, cols, UNIT_COLS):
            for row in range(0, rows, UNIT_ROWS):
                table.append((matrix, row, col))
    return table


KINDS = (
    "YA", "YA", "YA", "XA", "XA", "YA", "XA", "XA", "ZX", "X", "X", "X", "Y", "Y", "ZY", "ZY", "X", "Y", "X",
    "ZY", "Y", "Y", "X", "ZX",
)
TASK, VECTORS = 24, 25
ORDER = (
    5, 7, 3, 24, 24, 2, 1, 0, 6, 24, 24, 24, 5, 24, 3, 24, 2, 24, 24, 5, 24, 24, 3, 4, 24, 0, 2, 6, 15, 5, 11,
    14, 13, 1, 4, 24, 24, 12, 3, 9, 5, 10, 2, 24, 24, 24, 24, 24, 24, 2, 15, 16, 6, 11, 17, 24, 24, 4, 24, 6,
    14, 3, 2, 11, 1, 7, 12, 3, 2, 20, 0, 23, 11, 6, 18, 13, 4, 9, 24, 3, 0, 11, 6, 16, 14, 5, 22, 15, 24, 21,
    20, 19, 3, 0, 1, 14, 9, 17, 23, 6, 15, 3, 2, 0, 24, 11, 18, 1, 5, 14, 2, 10, 4, 22, 19, 6, 4, 20, 23, 21,
    24, 1, 6, 11, 7, 4, 14, 17, 3, 5, 2, 9, 0, 10, 15, 19, 20, 13, 16, 7, 1, 14, 9, 23, 6, 17, 20, 0, 11, 15, 1,
    10, 18, 12, 23, 13, 7, 17, 11, 0, 19, 20, 2, 16, 9, 25, 4, 13, 1, 22, 7, 20, 4, 10, 9, 21, 12, 22, 20, 17,
    0, 10, 23, 11, 16, 13, 3, 8, 7, 12, 19, 17, 10, 16, 13, 12, 14, 18, 7, 20, 6, 9, 4, 15, 25, 17, 1, 15, 22,
    23, 18, 10, 9, 25, 8, 17, 16, 7, 19, 10, 13, 12, 21, 5, 13, 1, 18, 15, 17, 9, 8, 20, 12, 18, 21, 22, 19, 10,
    13, 15, 8, 22, 21, 14, 21, 25, 7, 16, 8, 14, 21, 22, 19, 16, 12, 8, 22, 21, 23, 5, 0, 8, 19, 18, 16, 23, 8,
    18, 14, 10, 4, 21, 25, 23, 9, 12, 19, 22, 23, 20, 15, 18, 8, 19, 16, 13, 22, 11, 8, 5, 17, 21, 12, 7, 8, 18,
)


GIVE_ROWS = 240


def program_order(units, ends):
    order, task, vector, waited, step = [], 0, 0, {3}, [0] * len(units)
    order.append(("wait", 3, 0))
    for entry in ORDER:
        if entry == TASK:
            order.append(("task", task, 0))
            task += 1
            continue
        if entry == VECTORS:
            order.append(("vec", vector, 0))
            vector += 1
            continue
        m = units[entry][0]
        if m not in waited:
            assert task >= ends[m]
            order.append(("wait", m, 0))
            waited.add(m)
        order.append(("sum", entry, step[entry]))
        step[entry] += 1
    return order


PAIRS = 2


def fold(v):
    total = v[0:8]
    for k in range(1, v.shape[0] // 8):
        total = total + v[8 * k : 8 * k + 8]
    return total


def layer_kernel(dims, at_base, g_base, *refs):
    x_in, cot_in, weights, params = refs[0], refs[1], refs[2:6], refs[6:19]
    y_out, dx_out, res, vec_out, tiles_hbm = refs[19:24]
    (
        at, g, give, pair, line_xy, line_z, ring, big, left, act, hid, qkv, probs, attended, branch, middle, dmid,
        late_in, near_left, near_right, vec_w, vec_h, rstd4, sums4, vec_in, vec_own, vec_got,
        send, recv, v_send, v_recv, p_send, p_recv, l_sem, w_in, w_keep, w_send, w_recv, t_sem, s_sem, e_sem, n_send, n_recv,
    ) = refs[24:]
    r = lax.axis_index("rep")
    c = lax.axis_index("shard")
    x, y, z = r % 2, (r // 2) % 2, r // 4
    core = {"shard": 1 - c}
    to = {
        "X": {"rep": r + 1 - 2 * x},
        "Y": {"rep": r + 2 - 4 * y},
        "U": {"rep": r + 4},
        "D": {"rep": r - 4},
    }
    line_end = (z == 0) | (z == 3)
    line_mid = (z == 1) | (z == 2)
    outward = {"rep": r + 4 * (2 * (z // 2) - 1)}
    inward = {"rep": r + 4 * (1 - 2 * (z // 2))}
    across = {"rep": r + 4 * (3 - 2 * z)}
    upper = z // 2
    length = x_in.shape[0]
    width = x_in.shape[1]
    half_w = width // 2
    hidden = dims[2][1]
    half_h = hidden // 2
    blocks = hidden // width
    TILE = 512

    tile_of = []
    for m, (rows, cols) in enumerate(dims):
        for row in range(0, rows, TILE):
            for col in range(0, cols, UNIT_COLS):
                tile_of.append((m, row, col))
    first_tile = [min(t for t, v in enumerate(tile_of) if v[0] == m) for m in range(4)]
    parts = 2 * len(tile_of)
    slots_f, slots_b, late, slots_l, slots_g = 6, 16, 16, 2, 7

    def part_read(i):
        m, row, col = tile_of[i // 2]
        return pltpu.make_async_copy(
            weights[m].at[pl.ds(row + (i % 2) * 256, 256), pl.ds(col, UNIT_COLS)],
            late_in.at[pl.ds((i % slots_l) * 256, 256), :] if i >= late else big.at[pl.ds((i % slots_f) * 256, 256), :],
            w_in.at[slots_f + i % slots_l if i >= late else i % slots_f],
        )

    def low_row(i):
        return 240 * 16 + (i - late) % slots_g * 256 if i >= late else i * 256

    def part_low(i):
        return low_buf.at[pl.ds(low_row(i), 256), :]

    low_buf = give

    def part_place(i):
        return tiles_hbm.at[c, i // 2, pl.ds((i % 2) * 256, 256), :]

    def part_keep(i):
        return pltpu.make_async_copy(part_low(i), part_place(i), w_keep.at[i % slots_b])

    def part_give(i):
        return pltpu.make_async_remote_copy(
            src_ref=part_low(i), dst_ref=part_place(i), send_sem=w_send.at[i % slots_b], recv_sem=w_recv.at[i],
            device_id=core, device_id_type=MESH,
        )

    def part_got(i):
        return pltpu.make_async_remote_copy(
            src_ref=part_low(i), dst_ref=tiles_hbm.at[1 - c, i // 2, pl.ds((i % 2) * 256, 256), :],
            send_sem=w_send.at[i % slots_b], recv_sem=w_recv.at[i], device_id=core, device_id_type=MESH,
        )

    for i in range(slots_f):
        part_read(i).start()

    barrier = pltpu.get_barrier_semaphore()
    for peer in (core, to["X"], to["Y"]):
        pl.semaphore_signal(barrier, inc=1, device_id=peer, device_id_type=MESH)

    @pl.when(z < 3)
    def _():
        pl.semaphore_signal(barrier, inc=1, device_id=to["U"], device_id_type=MESH)

    @pl.when(z > 0)
    def _():
        pl.semaphore_signal(barrier, inc=1, device_id=to["D"], device_id_type=MESH)

    @pl.when(line_end)
    def _():
        pl.semaphore_signal(barrier, inc=1, device_id=across, device_id_type=MESH)

    narrow = (0, 0, 2, 3, 4, 5, 6, 7, 8, 9, 10)

    def rounded(v):
        return v.astype(BF16).astype(F32)

    lane_w = pl.ds(pl.multiple_of(c * half_w, half_w), half_w)
    lane_h = pl.ds(pl.multiple_of(c * half_h, half_h), half_h)
    (qv_ref, ob_ref, hs_ref, g1_ref, b1_ref, g2_ref, b2_ref, g3_ref, b3_ref, ub_ref, g4_ref, b4_ref, db_ref) = params
    vec_w[0:2, lane_w] = rounded(qv_ref[...])
    for row, ref in zip((2, 4, 5, 6, 7, 8, 9, 10), (ob_ref, g1_ref, b1_ref, g2_ref, b2_ref, g3_ref, b3_ref, db_ref)):
        vec_w[row : row + 1, lane_w] = rounded(ref[...])
    head_of = lax.broadcasted_iota(jnp.int32, (1, half_w), 1) // 64
    spread = jnp.zeros((1, half_w), F32)
    for h in range(half_w // 64):
        spread = jnp.where(head_of == h, rounded(hs_ref[0:1, h : h + 1]), spread)
    vec_w[3:4, lane_w] = spread
    for row, ref in enumerate((ub_ref, g4_ref, b4_ref)):
        vec_h[row : row + 1, lane_h] = rounded(ref[...])
    QB, VB, OB, HS, G1, B1, G2, B2, G3, B3, DB = range(11)
    UB, G4, B4 = range(3)

    def small_copy(k, give_it):
        ref, lane, far = ((vec_w, lane_w, 1 - c), (vec_h, lane_h, 1 - c))[k]
        size = half_w if k == 0 else half_h
        other = pl.ds(pl.multiple_of((1 - c) * size, size), size)
        here = ref.at[:, lane]
        return pltpu.make_async_remote_copy(
            src_ref=here, dst_ref=here if give_it else ref.at[:, other], send_sem=s_sem.at[k, 0], recv_sem=s_sem.at[k, 1],
            device_id=core, device_id_type=MESH,
        )

    e_copy = pltpu.make_async_copy(cot_in, g.at[pl.ds(0, length), pl.ds(g_base[3], width)], e_sem.at[0])
    e_copy.start()

    def left_own(m):
        rows = dims[m][0]
        return pltpu.make_async_copy(
            left.at[pl.ds(pl.multiple_of(2 * at_base[m] + c * rows, 512), rows), :],
            at.at[pl.ds(at_base[m], rows), pl.ds(0, length)],
            l_sem.at[m],
        )

    def left_far(m):
        rows = dims[m][0]
        return pltpu.make_async_remote_copy(
            src_ref=left.at[pl.ds(pl.multiple_of(2 * at_base[m] + (1 - c) * rows, 512), rows), :],
            dst_ref=at.at[pl.ds(at_base[m], rows), pl.ds(length, length)],
            send_sem=p_send.at[m, 0], recv_sem=p_recv.at[m, 0], device_id=core, device_id_type=MESH,
        )

    def right_far(m):
        cols = pl.ds(g_base[m], dims[m][1])
        return pltpu.make_async_remote_copy(
            src_ref=g.at[pl.ds(0, length), cols], dst_ref=g.at[pl.ds(length, length), cols],
            send_sem=p_send.at[m, 1], recv_sem=p_recv.at[m, 1], device_id=core, device_id_type=MESH,
        )

    def start_left(m):
        left_own(m).start()
        left_far(m).start()

    def wait_pair(m):
        left_own(m).wait()
        left_far(m).wait()
        right_far(m).wait()

    converted, kept_parts, given_parts = [0], set(), set()

    def kept(i):
        if i not in kept_parts:
            kept_parts.add(i)
            part_keep(i).wait()

    def given(i):
        if i not in given_parts:
            given_parts.add(i)
            part_give(i).wait_send()

    def convert_parts(upto):
        for i in range(converted[0], upto):
            part_read(i).wait()
            if i >= slots_b:
                kept(i - slots_b)
            if i == late:
                for k in range(late):
                    kept(k)
                    given(k)
            if i >= late + slots_g:
                kept(i - slots_g)
                given(i - slots_g)
            source, first = (late_in, i % slots_l * 256) if i >= late else (big, i % slots_f * 256)

            def convert(b, _, i=i, source=source, first=first):
                rows = pl.multiple_of(first + b * 32, 32)
                low = pl.multiple_of(low_row(i) + b * 32, 32)
                low_buf[pl.ds(low, 32), :] = source[pl.ds(rows, 32), :].astype(BF16)
                return 0

            lax.fori_loop(0, 8, convert, 0)
            part_keep(i).start()
            if i == 0:
                pl.semaphore_wait(barrier, 5)
                small_copy(0, True).start()
                small_copy(1, True).start()
            part_give(i).start()
            if i >= late and i + slots_l < parts:
                part_read(i + slots_l).start()
            if i + slots_f < late:
                part_read(i + slots_f).start()
            if i == late - slots_f:
                for k in range(slots_l):
                    part_read(late + k).start()
        converted[0] = max(converted[0], upto)

    def cotangent_copy(k, relay):
        here, there = pl.ds(0, length), pl.ds(length, length)
        cols = pl.ds(g_base[3], width)
        return pltpu.make_async_remote_copy(
            src_ref=near_right.at[k, here, :] if relay else g.at[here, cols],
            dst_ref=near_right.at[k, there if relay else here, :],
            send_sem=n_send.at[k, int(relay)], recv_sem=n_recv.at[k, int(relay)],
            device_id=core if relay else to["XY"[k]], device_id_type=MESH,
        )

    convert_parts(2)
    e_copy.wait()
    right_far(3).start()
    cotangent_copy(0, False).start()
    cotangent_copy(1, False).start()
    convert_parts(4)

    def tile(m, half, index):
        return (half, first_tile[m] + index)

    stream = []
    for m in (0, 1, 2):
        for index in range(dims[m][1] // UNIT_COLS):
            stream += [tile(m, 0, index), tile(m, 1, index)]
    per_half = dims[3][0] // TILE
    stream += [tile(3, h, k) for h in range(2) for k in range(per_half)]
    for m in (2, 1, 0):
        for index in range(dims[m][1] // UNIT_COLS):
            stream += [tile(m, 0, index), tile(m, 1, index)]
    slots_t = 4
    here = set()

    def tile_load(i):
        half, t = stream[i]
        return pltpu.make_async_copy(
            tiles_hbm.at[half, t], ring.at[i % slots_t], t_sem.at[i % slots_t]
        )

    def tile_start(i):
        half, t = stream[i]
        if (1, t) not in here:
            here.add((1, t))
            convert_parts(2 * t + 2)
            for k in (2 * t, 2 * t + 1):
                kept(k)
                part_got(k).wait_recv()
        tile_load(i).start()

    at_tile, started, allowed_to = [0], [0], [0]

    def fill(limit=None):
        if limit is not None:
            allowed_to[0] = limit
        while started[0] < min(at_tile[0] + slots_t, allowed_to[0], len(stream)):
            tile_start(started[0])
            started[0] += 1

    def next_tile(ahead=0):
        i = at_tile[0] + ahead
        assert i < started[0]
        tile_load(i).wait()
        return ring.at[i % slots_t]

    def done_tile(count=1):
        at_tile[0] += count
        fill()

    def mean(v):
        return jnp.sum(v, axis=-1, keepdims=True) / v.shape[-1]

    def normal(v):
        centred = v - mean(v)
        scale = lax.rsqrt(mean(centred * centred) + 1e-05)
        return centred * scale, scale

    def each(fn, step=32, init=0, unroll=1):
        def body(i, carry):
            return fn(pl.ds(pl.multiple_of(i * step, step), step), carry)

        return lax.fori_loop(0, length // step, body, init, unroll=unroll)

    def w_row(i):
        return vec_w[i : i + 1, :]

    def turn(source, m, block=0):
        for k in range(width // 256):
            row = 2 * at_base[m] + block * width + k * 256
            left[row : row + 256, :] = jnp.transpose(source[:, k * 256 : (k + 1) * 256])

    NT = (((1,), (1,)), ((), ()))
    TN = (((0,), (0,)), ((), ()))

    def nt(a, b):
        return lax.dot_general(a, b, NT, preferred_element_type=F32)

    def tn(a, b):
        return lax.dot_general(a, b, TN, preferred_element_type=F32)

    def product_pair(source, write):
        first, second = next_tile(), next_tile(1)
        for k in range(UNIT_COLS // 256):
            cols = slice(k * 256, (k + 1) * 256)
            value = jnp.dot(source[:, 0:half_w], first[:, cols], preferred_element_type=F32)
            value = value + jnp.dot(source[:, half_w:width], second[:, cols], preferred_element_type=F32)
            write(cols, value)
        done_tile(2)

    small_copy(0, True).wait_send()
    small_copy(1, True).wait_send()
    small_copy(0, False).wait_recv()
    small_copy(1, False).wait_recv()

    def first_norm(rows, _):
        hat, _s = normal(x_in[rows, :].astype(F32))
        act[rows, :] = (hat * w_row(G1) + w_row(B1)).astype(BF16)
        return 0

    each(first_norm, unroll=2)
    fill(8)
    for index in range(3):

        def put_qkv(cols, value, index=index):
            if index == 0:
                value = value + vec_w[QB : QB + 1, cols]
            if index == 2:
                value = value + vec_w[VB : VB + 1, cols]
            qkv[:, index * width + cols.start : index * width + cols.stop] = value.astype(BF16)

        product_pair(act, put_qkv)
        convert_parts(10 + 2 * index)
    turn(act, 0)
    start_left(0)
    convert_parts(16)

    low_lane = lax.broadcasted_iota(jnp.int32, (length, 128), 1) < 64
    allowed = lax.broadcasted_iota(jnp.int32, (length, length), 1) <= lax.broadcasted_iota(
        jnp.int32, (length, length), 0
    )
    scale = 64 ** (-0.5)
    keep_lane = (low_lane.astype(F32).astype(BF16), jnp.logical_not(low_lane).astype(F32).astype(BF16))

    def split_heads(v):
        return jnp.concatenate([v * keep_lane[0], v * keep_lane[1]], axis=0)

    def attend(p):
        q = qkv[:, pl.ds(pl.multiple_of(p * 128, 128), 128)]
        k = qkv[:, pl.ds(pl.multiple_of(width + p * 128, 128), 128)]
        v = qkv[:, pl.ds(pl.multiple_of(2 * width + p * 128, 128), 128)]
        both = nt(q, split_heads(k)) * scale
        got = []
        for h in range(2):
            scores = jnp.where(allowed, both[:, h * length : (h + 1) * length], -1e30)
            top = jnp.max(scores, axis=-1, keepdims=True)
            lse = top + jnp.log(jnp.sum(jnp.exp(scores - top), axis=-1, keepdims=True))
            got.append(jnp.exp(scores - lse))
        prob = jnp.concatenate(got, axis=1)
        probs[p] = prob
        value = jnp.dot(prob.astype(BF16), split_heads(v), preferred_element_type=F32)
        cols = pl.ds(pl.multiple_of(p * 128, 128), 128)
        attended[:, cols] = value
        act[:, cols] = (value * vec_w[HS : HS + 1, cols]).astype(BF16)

    def attend_some(i, _):
        for n in range(PAIRS):
            attend(i * PAIRS + n)
        return 0

    lax.fori_loop(0, width // 128 // PAIRS, attend_some, 0)
    fill(10)
    for k in range(2):
        cotangent_copy(k, False).wait()
        cotangent_copy(k, True).start()

    def put_branch(cols, value):
        branch[:, cols] = value + vec_w[OB : OB + 1, cols]

    product_pair(act, put_branch)
    fill(16)
    turn(act, 1)
    start_left(1)

    def second_norm(rows, _):
        hat, _s = normal(branch[rows, :])
        mid = x_in[rows, :].astype(F32) + (hat * w_row(G2) + w_row(B2))
        middle[rows, :] = mid
        hat, _s = normal(mid)
        act[rows, :] = (hat * w_row(G3) + w_row(B3)).astype(BF16)
        return 0

    each(second_norm, unroll=2)
    U0, H0, D0 = 0, blocks * length, 2 * blocks * length
    for j in range(blocks):

        def put_hidden(cols, value, j=j):
            wide = slice(j * width + cols.start, j * width + cols.stop)
            big[U0 + j * length : U0 + (j + 1) * length, cols] = value + vec_h[UB : UB + 1, wide]

        product_pair(act, put_hidden)
    turn(act, 2)
    start_left(2)
    root_half = 0.7071067811865476

    def near(base, start):
        return pl.ds(pl.multiple_of(base + start, 16), 16)

    def hidden_norm(rows, _):
        total = jnp.zeros((16, 1), F32)
        for j in range(blocks):
            u = big[near(U0 + j * length, rows.start), :]
            h = u * (1.0 + lax.erf(u * root_half)) * 0.5
            big[near(H0 + j * length, rows.start), :] = h
            total = total + jnp.sum(h, axis=-1, keepdims=True)
        centre = total / hidden
        total = jnp.zeros((16, 1), F32)
        for j in range(blocks):
            h = big[near(H0 + j * length, rows.start), :] - centre
            total = total + jnp.sum(h * h, axis=-1, keepdims=True)
        s = lax.rsqrt(total / hidden + 1e-05)
        rstd4[rows, :] = jnp.broadcast_to(s, (16, 128))
        for j in range(blocks):
            at_h = near(H0 + j * length, rows.start)
            hat = (big[at_h, :] - centre) * s
            big[at_h, :] = hat
            cols = slice(j * width, (j + 1) * width)
            hid[near(j * length, rows.start), :] = (
                hat * vec_h[G4 : G4 + 1, cols] + vec_h[B4 : B4 + 1, cols]
            ).astype(BF16)
        return 0

    each(hidden_norm, 16)
    for j in range(blocks):
        turn(hid.at[pl.ds(j * length, length), :], 3, j)
    start_left(3)
    convert_parts(parts)

    tasks = []
    zeros8 = jnp.zeros((8, width), F32)
    dirs = g.at[pl.ds(0, length), :]

    def put_sum(row, value):
        line = jnp.sum(value, axis=0, keepdims=True)
        vec_in[0, row : row + 1, :] = line[:, 0:half_w]
        vec_in[1, row : row + 1, :] = line[:, half_w:width]

    def task_down(h, k):
        def run():
            w = next_tile()
            row = h * dims[3][0] + k * TILE
            j, lane = row // width, row % width
            if h == 0 and k == 0:
                y_acc[...] = middle[...] + w_row(DB)
            for n in range(TILE // 256):
                big[D0 + j * length : D0 + (j + 1) * length, lane + n * 256 : lane + (n + 1) * 256] = nt(
                    dirs[:, g_base[3] : g_base[3] + width], w[n * 256 : (n + 1) * 256, :]
                )

            for n in range(width // 256):
                cols = slice(n * 256, (n + 1) * 256)
                y_acc[:, cols] += jnp.dot(
                    hid[j * length : (j + 1) * length, lane : lane + TILE], w[:, cols], preferred_element_type=F32
                )
            done_tile()
            if h == 1 and k == per_half - 1:
                y_out[...] = y_acc[...].astype(BF16)

        return run

    y_acc = dmid
    for h in range(2):
        for k in range(per_half):
            tasks.append((1.2, task_down(h, k)))

    def task_hidden(first, count):
        def run():
            if first == 0:
                sums4[...] = jnp.zeros_like(sums4)

                def e_sum(rows, carry):
                    return carry + fold(dirs[rows, g_base[3] : g_base[3] + width].astype(F32))

                put_sum(DB, each(e_sum, 32, zeros8))

            def body(i, _):
                at_r = pl.multiple_of(first + i * 16, 16)
                one = jnp.zeros((16, 1), F32)
                two = jnp.zeros((16, 1), F32)
                for j in range(blocks):
                    gain = vec_h[G4 : G4 + 1, j * width : (j + 1) * width]
                    d = big[near(D0 + j * length, at_r), :] * gain
                    hat = big[near(H0 + j * length, at_r), :]
                    one = one + jnp.sum(d, axis=-1, keepdims=True)
                    two = two + jnp.sum(d * hat, axis=-1, keepdims=True)
                one, two = one / hidden, two / hidden
                s = rstd4[pl.ds(at_r, 16), 0:1]
                for j in range(blocks):
                    cols = slice(j * width, (j + 1) * width)
                    da = big[near(D0 + j * length, at_r), :]
                    hat = big[near(H0 + j * length, at_r), :]
                    u = big[near(U0 + j * length, at_r), :]
                    dh = s * (da * vec_h[G4 : G4 + 1, cols] - one - hat * two)
                    slope = 0.5 * (1.0 + lax.erf(u * root_half)) + u * (jnp.exp(u * u * -0.5) * 0.3989422804014327)
                    du = (dh * slope).astype(BF16)
                    g[pl.ds(at_r, 16), g_base[2] + j * width : g_base[2] + (j + 1) * width] = du
                    sums4[0:8, cols] += fold(du.astype(F32))
                    sums4[8:16, cols] += fold(da * hat)
                    sums4[16:24, cols] += fold(da)
                return 0

            lax.fori_loop(0, count // 16, body, 0)
            if first + count == length:
                for i in range(3):
                    line = jnp.sum(sums4[8 * i : 8 * i + 8, :], axis=0, keepdims=True)
                    for n in range(hidden // half_w):
                        hh, k = divmod(n, half_h // half_w)
                        vec_in[hh, 11 + 4 * i + k : 12 + 4 * i + k, :] = line[:, n * half_w : (n + 1) * half_w]
                right_far(2).start()

        return run

    for first in range(0, length, 32):
        tasks.append((3.0, task_hidden(first, 32)))

    def add_pair(acc, index_of, cols_of, count, width_to):
        def make(index):
            def run():
                for h in range(2):
                    w = next_tile()
                    for n in range(TILE // 256):
                        cols = slice(h * half_w + n * 256, h * half_w + (n + 1) * 256)
                        value = nt(dirs[:, cols_of(index)], w[n * 256 : (n + 1) * 256, :])
                        if index == 0:
                            acc[:, cols] = value
                        else:
                            acc[:, cols] += value
                    done_tile()

            return run

        return [(1.2, make(index)) for index in range(count)]

    ends = {2: len(tasks)}
    acc = big.at[pl.ds(U0, length), :]
    tasks += add_pair(acc, None, lambda j: slice(g_base[2] + j * width, g_base[2] + (j + 1) * width), blocks, width)

    def task_norms():
        def body(rows, carry):
            s3g, s3b, s2g, s2b, sob = carry
            da = acc[rows, :]
            hat, s = normal(middle[rows, :])
            d = da * w_row(G3)
            d_mid = dirs[rows, g_base[3] : g_base[3] + width].astype(F32) + s * (d - mean(d) - hat * mean(d * hat))
            dmid[rows, :] = d_mid
            s3g, s3b = s3g + fold(da * hat), s3b + fold(da)
            hat, s = normal(branch[rows, :])
            d = d_mid * w_row(G2)
            dy = (s * (d - mean(d) - hat * mean(d * hat))).astype(BF16)
            s2g, s2b = s2g + fold(d_mid * hat), s2b + fold(d_mid)
            g[rows, g_base[1] : g_base[1] + width] = dy
            return (s3g, s3b, s2g, s2b, sob + fold(dy.astype(F32)))

        got = each(body, 16, (zeros8,) * 5)
        for row, value in zip((G3, B3, G2, B2, OB), got):
            put_sum(row, value)
        right_far(1).start()

    tasks.append((2.5, task_norms))
    ends[1] = len(tasks)
    d_mixed = big.at[pl.ds(U0 + length, length), :]
    tasks += add_pair(d_mixed, None, lambda j: slice(g_base[1], g_base[1] + width), 1, width)

    def task_heads():
        def body(rows, carry):
            d = d_mixed[rows, :]
            act[rows, :] = (d * w_row(HS)).astype(BF16)
            return carry + fold(d * attended[rows, :])

        put_sum(HS, each(body, 32, zeros8))

    tasks.append((0.6, task_heads))

    def task_attend(first, count):
        def run():
            def pair_of_heads(p):
                q_cols = pl.ds(pl.multiple_of(p * 128, 128), 128)
                k_cols = pl.ds(pl.multiple_of(width + p * 128, 128), 128)
                v_cols = pl.ds(pl.multiple_of(2 * width + p * 128, 128), 128)
                q, k, v, do = qkv[:, q_cols], qkv[:, k_cols], qkv[:, v_cols], act[:, q_cols]
                prob = probs[p]
                dv = tn(prob.astype(BF16), do)
                dp = nt(do, split_heads(v))
                ds = []
                for h in range(2):
                    own = slice(h * length, (h + 1) * length)
                    dot = jnp.sum(prob[:, own] * dp[:, own], axis=-1, keepdims=True)
                    ds.append(prob[:, own] * (dp[:, own] - dot))
                ds = jnp.concatenate(ds, axis=1).astype(BF16)
                dq = jnp.dot(ds, split_heads(k), preferred_element_type=F32) * scale
                dk = tn(ds, q) * scale
                g[0:length, q_cols] = dq.astype(BF16)
                g[0:length, k_cols] = jnp.where(low_lane, dk[0:length], dk[length : 2 * length]).astype(BF16)
                g[0:length, v_cols] = jnp.where(low_lane, dv[0:length], dv[length : 2 * length]).astype(BF16)

            for n in range(count):
                pair_of_heads(first + n)
            if first + count == width // 128:

                def sums(rows, carry):
                    a, b = carry
                    return (
                        a + fold(g[rows, 0:width].astype(F32)),
                        b + fold(g[rows, 2 * width : 3 * width].astype(F32)),
                    )

                a, b = each(sums, 32, (zeros8, zeros8))
                put_sum(QB, a)
                put_sum(VB, b)
                right_far(0).start()

        return run

    for first in range(0, width // 128, 2):
        tasks.append((3.0, task_attend(first, 2)))
    ends[0] = len(tasks)
    d_first = big.at[pl.ds(U0 + 2 * length, length), :]
    tasks += add_pair(d_first, None, lambda j: slice(j * width, (j + 1) * width), 3, width)

    def task_last():
        def body(rows, carry):
            sg, sb = carry
            da = d_first[rows, :]
            hat, s = normal(x_in[rows, :].astype(F32))
            d = da * w_row(G1)
            dx_out[rows, :] = dmid[rows, :] + s * (d - mean(d) - hat * mean(d * hat))
            return (sg + fold(da * hat), sb + fold(da))

        sg, sb = each(body, 16, (zeros8, zeros8))
        put_sum(G1, sg)
        put_sum(B1, sb)
        vec_in[0, 23:24, :] = jnp.zeros((1, half_w), F32)
        vec_in[1, 23:24, :] = jnp.zeros((1, half_w), F32)
        vec_copy(0).start()

    tasks.append((1.5, task_last))

    vec_steps = (core, to["X"], to["Y"], {"rep": r + 4 * (1 - 2 * (z % 2))}, across)

    def vec_copy(step):
        source = vec_in.at[1 - c] if step == 0 else vec_own.at[step]
        return pltpu.make_async_remote_copy(
            src_ref=source, dst_ref=vec_got.at[step], send_sem=v_send.at[step], recv_sem=v_recv.at[step],
            device_id=vec_steps[step], device_id_type=MESH,
        )

    def vec_task(k):
        vec_copy(k).wait_recv()
        total = (vec_in[c] if k == 0 else vec_own[k]) + vec_got[k]
        if k < 4:
            vec_own[k + 1] = total
            vec_copy(k + 1).start()
        else:
            vec_out[...] = total

    units = unit_table(dims)
    kinds = KINDS
    xy_at, z_at = {}, {}
    for unit, kind in enumerate(kinds):
        (z_at if kind[0] == "Z" else xy_at)[unit] = len(z_at) if kind[0] == "Z" else len(xy_at)

    def copy(unit, name, source, dest, device):
        return functools.partial(
            pltpu.make_async_remote_copy,
            src_ref=source, dst_ref=dest, send_sem=send.at[unit], recv_sem=recv.at[unit, SLOT[name]],
            device_id=device, device_id_type=MESH,
        )

    def rows_of(unit, start, count):
        if not isinstance(start, int):
            start = pl.multiple_of(start, 16)
        return res.at[unit, pl.ds(start, count), :]

    def product(unit, start, count, dest, dest_start, got=None, got_start=0, near=None, near_start=0):
        m, row, col = units[unit]
        step = 128 if count % 128 == 0 else min(count, 64)

        def block(index, _):
            part, strip = index // (UNIT_COLS // 256), index % (UNIT_COLS // 256)
            cols = pl.ds(pl.multiple_of(strip * 256, 256), 256)
            value = jnp.dot(
                at[pl.ds(pl.multiple_of(at_base[m] + row + start + part * step, 16), step), :],
                g[:, pl.ds(pl.multiple_of(g_base[m] + col + strip * 256, 256), 256)],
                preferred_element_type=F32,
            )
            if near is not None:
                value = value + jnp.dot(
                    near_left[unit, pl.ds(pl.multiple_of(near_start + part * step, 16), step), :],
                    near[:, pl.ds(pl.multiple_of(col + strip * 256, 256), 256)],
                    preferred_element_type=F32,
                )
            if got is not None:
                value = value + got[pl.ds(pl.multiple_of(got_start + part * step, 16), step), cols].astype(F32)
            dest[pl.ds(pl.multiple_of(dest_start + part * step, 16), step), cols] = value.astype(BF16)
            return 0

        lax.fori_loop(0, (count // step) * (UNIT_COLS // 256), block, 0)

    def accumulate(unit, start, count, got, got_start, dest, dest_start):
        def block(strip, _):
            cols = pl.ds(pl.multiple_of(strip * 256, 256), 256)
            value = res[unit, pl.ds(pl.multiple_of(start, 16), count), cols].astype(F32)
            value = value + got[pl.ds(pl.multiple_of(got_start, 16), count), cols].astype(F32)
            dest[pl.ds(pl.multiple_of(dest_start, 16), count), cols] = value.astype(BF16)
            return 0

        lax.fori_loop(0, UNIT_COLS // 256, block, 0)

    def gather_line(unit, base, size, level):
        up, down = "u%d" % level, "w%d" % level
        low, high = z - (level - 1), z + (level - 1)

        @pl.when((low >= 0) & (z < 3))
        def _():
            part = rows_of(unit, base + low * size, size)
            copy(unit, up, part, part, to["U"])().start()

        @pl.when((high <= 3) & (z > 0))
        def _():
            part = rows_of(unit, base + high * size, size)
            copy(unit, down, part, part, to["D"])().start()

    def gather_arrived(unit, base, size, level):
        def wait(chunks):
            part = give.at[pl.ds(0, chunks * size), :]
            copy(unit, "u%d" % level, part, part, to["U"])().wait_recv()

        if level == 1:
            pl.when(line_mid)(lambda: wait(2))
        if level == 2:
            wait(1)
        else:
            pl.when(line_end)(lambda: wait(1))

    def finish(unit, ends, mids):
        def wait(rows):
            part = give.at[pl.ds(0, rows), :]
            copy(unit, "d1", part, part, to["X"])().wait_send()

        pl.when(line_end)(lambda: wait(ends))
        pl.when(line_mid)(lambda: wait(mids))

    def task_xy(unit, step):
        half, quarter, size = UNIT_ROWS // 2, UNIT_ROWS // 4, UNIT_ROWS // 16
        first, second = ("X", "Y") if kinds[unit][0] == "X" else ("Y", "X")
        p, q = (x, y) if kinds[unit][0] == "X" else (y, x)
        by_tokens = kinds[unit] in ("XA", "YA")
        line, block, out, other = line_xy.at[xy_at[unit]], res.at[unit], give.at[pl.ds(unit * GIVE_ROWS, GIVE_ROWS), :], pair.at[unit]
        keep, away_half = p * half, (1 - p) * half
        base = keep + q * quarter
        away = keep + (1 - q) * quarter
        at_z = half + quarter
        if by_tokens:
            m, row, _ = units[unit]
            give_left = at.at[pl.ds(pl.multiple_of(at_base[m] + row + away_half, 128), half), :]
            d1 = copy(unit, "d1", give_left, near_left.at[unit], to[first])
        else:
            d1 = copy(unit, "d1", out.at[pl.ds(0, half), :], rows_of(unit, away_half, half), to[first])
        d2 = copy(unit, "d2", out.at[pl.ds(half, quarter), :], other.at[pl.ds(0, quarter), :], to[second])
        z1 = copy(unit, "z1", out.at[pl.ds(at_z, 3 * size), :], line.at[pl.ds(0, 3 * size), :], inward)
        z2 = copy(unit, "z2", out.at[pl.ds(at_z, 2 * size), :], line.at[pl.ds(3 * size, 2 * size), :], across)
        z3 = copy(unit, "z3", out.at[pl.ds(at_z + 2 * size, size), :], line.at[pl.ds(0, size), :], outward)
        own_quarter = rows_of(unit, base, quarter)
        g2 = copy(unit, "g2", own_quarter, own_quarter, to[second])
        own_half = rows_of(unit, keep, half)
        g1 = copy(unit, "g1", own_half, own_half, to[first])
        own = base + z * size
        if step == 0 and by_tokens:
            d1().start()
        elif step == 1 and by_tokens:
            d1().wait_recv()
            near = near_right.at["XY".index(first)]
            product(unit, away, quarter, out, half, near=near, near_start=(1 - q) * quarter)
            d2().start()
            product(unit, base, quarter, block, base, near=near, near_start=q * quarter)
        elif step == 0:
            product(unit, away_half, half, out, 0)
            d1().start()
        elif step == 1:
            d1().wait_recv()
            product(unit, away, quarter, out, half, block, away)
            d2().start()
            product(unit, base, quarter, block, base, block, base)
        elif step == 2:
            d2().wait_recv()

            @pl.when(line_end)
            def _():
                skip = (1 - upper) * size
                accumulate(unit, base + skip, 3 * size, other, skip, out, at_z)
                z1().start()
                accumulate(unit, own, size, other, z * size, block, own)

            @pl.when(line_mid)
            def _():
                accumulate(unit, base, quarter, other, 0, block, base)

        elif step == 3:

            @pl.when(line_mid)
            def _():
                z1().wait_recv()
                accumulate(unit, base + (1 - upper) * 2 * size, 2 * size, line, (1 - upper) * size, out, at_z)
                z2().start()
                accumulate(unit, own, size, line, upper * 2 * size, block, own)

        elif step == 4:

            @pl.when(line_mid)
            def _():
                z2().wait_recv()
                accumulate(unit, base + upper * 3 * size, size, line, (3 + upper) * size, out, at_z + 2 * size)
                z3().start()
                accumulate(unit, own, size, line, (4 - upper) * size, block, own)
                gather_line(unit, base, size, 1)

        elif step == 5:

            @pl.when(line_end)
            def _():
                z3().wait_recv()
                accumulate(unit, own, size, line, 0, block, own)
                gather_line(unit, base, size, 1)

        elif step in (6, 7):
            gather_arrived(unit, base, size, step - 5)
            gather_line(unit, base, size, step - 4)
        elif step == 8:
            gather_arrived(unit, base, size, 3)
            g2().start()
        elif step == 9:
            g2().wait_recv()
            g1().start()
        else:
            g1().wait_recv()
            sent = 2 * quarter + half + (half // 4 if by_tokens else half)
            finish(unit, sent + 4 * size, sent + 8 * size)

    def task_z(unit, step):
        size, half, quarter = UNIT_ROWS // 4, UNIT_ROWS // 8, UNIT_ROWS // 16
        first, second = ("X", "Y") if kinds[unit] == "ZX" else ("Y", "X")
        p, q = (x, y) if kinds[unit] == "ZX" else (y, x)
        line, block, out, other = line_z.at[z_at[unit]], res.at[unit], give.at[pl.ds(unit * GIVE_ROWS, GIVE_ROWS), :], pair.at[unit]
        own = z * size
        keep, away_half = own + p * half, own + (1 - p) * half
        base, away = keep + q * quarter, keep + (1 - q) * quarter
        at_d = 3 * size
        z1 = copy(unit, "z1", out.at[pl.ds(0, 3 * size), :], line.at[pl.ds(0, 3 * size), :], inward)
        z2 = copy(unit, "z2", out.at[pl.ds(0, 2 * size), :], line.at[pl.ds(3 * size, 2 * size), :], across)
        z3 = copy(unit, "z3", out.at[pl.ds(2 * size, size), :], line.at[pl.ds(0, size), :], outward)
        d1 = copy(unit, "d1", out.at[pl.ds(at_d, half), :], other.at[pl.ds(0, half), :], to[first])
        d2 = copy(unit, "d2", out.at[pl.ds(at_d + half, quarter), :], other.at[pl.ds(half, quarter), :], to[second])
        own_quarter = rows_of(unit, base, quarter)
        g2 = copy(unit, "g2", own_quarter, own_quarter, to[second])
        own_half = rows_of(unit, keep, half)
        g1 = copy(unit, "g1", own_half, own_half, to[first])
        if step == 0:

            @pl.when(line_end)
            def _():
                product(unit, (1 - upper) * size, 3 * size, out, 0)
                z1().start()

        elif step == 1:

            @pl.when(line_mid)
            def _():
                z1().wait_recv()
                product(unit, (1 - upper) * 2 * size, 2 * size, out, 0, line, (1 - upper) * size)
                z2().start()
                product(unit, own, size, block, own, line, upper * 2 * size)

        elif step == 2:

            @pl.when(line_mid)
            def _():
                z2().wait_recv()
                product(unit, upper * 3 * size, size, out, 2 * size, line, (3 + upper) * size)
                z3().start()
                got = (4 - upper) * size
                accumulate(unit, away_half, half, line, got + (1 - p) * half, out, at_d)
                d1().start()
                accumulate(unit, keep, half, line, got + p * half, block, keep)

        elif step == 3:

            @pl.when(line_end)
            def _():
                z3().wait_recv()
                product(unit, away_half, half, out, at_d, line, (1 - p) * half)
                d1().start()
                product(unit, keep, half, block, keep, line, p * half)

        elif step == 4:
            d1().wait_recv()
            accumulate(unit, away, quarter, other, (1 - q) * quarter, out, at_d + half)
            d2().start()
            accumulate(unit, base, quarter, other, q * quarter, block, base)
        elif step == 5:
            d2().wait_recv()
            accumulate(unit, base, quarter, other, half, block, base)
            g2().start()
        elif step == 6:
            g2().wait_recv()
            g1().start()
        elif step == 7:
            g1().wait_recv()
            gather_line(unit, 0, size, 1)
        elif step in (8, 9):
            gather_arrived(unit, 0, size, step - 7)
            gather_line(unit, 0, size, step - 6)
        else:
            gather_arrived(unit, 0, size, 3)
            finish(unit, 2 * half + 2 * quarter + 4 * size, 2 * half + 2 * quarter + 8 * size)


    for kind, a, b in program_order(units, ends):
        if kind == "task":
            if a == 0:
                fill(len(stream))
            tasks[a][1]()
        elif kind == "wait":
            wait_pair(a)
            if a == 3:
                for k in range(2):
                    cotangent_copy(k, True).wait()
            if a == 1:
                for k in range(parts):
                    given(k)
        elif kind == "vec":
            vec_task(a)
        elif kinds[a][0] == "Z":
            task_z(a, b)
        else:
            task_xy(a, b)
    for step in range(5):
        vec_copy(step).wait_send()


def whole_layer(layer_input, cotangent, weights, params):
    dims = tuple(w.shape for w in weights)
    at_rows = sum(rows for rows, _ in dims)
    g_cols = sum(cols for _, cols in dims)
    at_base = [sum(rows for rows, _ in dims[:m]) for m in range(4)]
    g_base = [sum(cols for _, cols in dims[:m]) for m in range(4)]
    length, width = layer_input.shape
    hidden = dims[2][1]
    blocks = hidden // width
    units = unit_table(dims)
    kinds = KINDS
    n, n_z = len(units), sum(kind[0] == "Z" for kind in kinds)
    tiles = n // 2
    hbm = pl.BlockSpec(memory_space=pl.ANY)
    vmem = pl.BlockSpec(memory_space=pltpu.VMEM)
    dma = pltpu.SemaphoreType.DMA
    small = (24, width // 2)
    got = pl.pallas_call(
        functools.partial(layer_kernel, dims, at_base, g_base),
        out_shape=[
            pltpu.VMEM((length, width), BF16),
            pltpu.VMEM((length, width), F32),
            pltpu.VMEM((n, UNIT_ROWS, UNIT_COLS), BF16),
            pltpu.VMEM(small, F32),
            jax.ShapeDtypeStruct((2, tiles, 512, UNIT_COLS), BF16),
        ],
        in_specs=[vmem, hbm] + [hbm] * 4 + [vmem] * 13,
        out_specs=[vmem] * 4 + [hbm],
        scratch_shapes=[
            pltpu.VMEM((at_rows, 2 * length), BF16),
            pltpu.VMEM((2 * length, g_cols), BF16),
            pltpu.VMEM((n * GIVE_ROWS, UNIT_COLS), BF16),
            pltpu.VMEM((n, UNIT_ROWS // 4, UNIT_COLS), BF16),
            pltpu.VMEM((n - n_z, 5 * UNIT_ROWS // 16, UNIT_COLS), BF16),
            pltpu.VMEM((n_z, 5 * UNIT_ROWS // 4, UNIT_COLS), BF16),
            pltpu.VMEM((4, 512, UNIT_COLS), BF16),
            pltpu.VMEM((3 * blocks * length, width), F32),
            pltpu.VMEM((2 * at_rows, length), BF16),
            pltpu.VMEM((length, width), BF16),
            pltpu.VMEM((blocks * length, width), BF16),
            pltpu.VMEM((length, 3 * width), BF16),
            pltpu.VMEM((width // 128, length, 2 * length), F32),
            pltpu.VMEM((length, width), F32),
            pltpu.VMEM((length, width), F32),
            pltpu.VMEM((length, width), F32),
            pltpu.VMEM((length, width), F32),
            pltpu.VMEM((2 * 256, UNIT_COLS), F32),
            pltpu.VMEM((dims[3][0] // UNIT_ROWS, UNIT_ROWS // 2, 2 * length), BF16),
            pltpu.VMEM((2, 2 * length, width), BF16),
            pltpu.VMEM((16, width), F32),
            pltpu.VMEM((8, hidden), F32),
            pltpu.VMEM((length, 128), F32),
            pltpu.VMEM((24, hidden), F32),
            pltpu.VMEM((2,) + small, F32),
            pltpu.VMEM((5,) + small, F32),
            pltpu.VMEM((5,) + small, F32),
            dma((n,)),
            dma((n, 9)),
            dma((5,)),
            dma((5,)),
            dma((4, 2)),
            dma((4, 2)),
            dma((4,)),
            dma((10,)),
            dma((16,)),
            dma((16,)),
            dma((2 * tiles,)),
            dma((4,)),
            dma((2, 2)),
            dma((1,)),
            dma((2, 2)),
            dma((2, 2)),
        ],
        compiler_params=pltpu.CompilerParams(
            collective_id=0, has_side_effects=True, vmem_limit_bytes=50 * MIB
        ),
        name="whole_layer",
    )(layer_input, cotangent, *weights, *params)
    return got[:4]


def finish_kernel(dims, *refs):
    y_in, dx_in, res, vec = refs[0:4]
    y_out, dx_out, outs, smalls = refs[4], refs[5], refs[6:10], refs[10:23]
    wide, lines, o_sem, s_sem = refs[23], refs[24:37], refs[37], refs[38]
    slots = wide.shape[0]
    copies = [pltpu.make_async_copy(y_in, y_out, s_sem.at[13]), pltpu.make_async_copy(dx_in, dx_out, s_sem.at[14])]
    rows_of = [range(0, 2)] + [range(k, k + 1) for k in range(2, 11)] + [range(11 + 4 * k, 15 + 4 * k) for k in range(3)]
    for k, rows in enumerate(rows_of):
        if k == 2:
            head_of = lax.broadcasted_iota(jnp.int32, (1, vec.shape[1]), 1) // 64
            lane = lax.broadcasted_iota(jnp.int32, lines[k].shape, 1)
            total = jnp.zeros(lines[k].shape, F32)
            for h in range(vec.shape[1] // 64):
                one = jnp.sum(jnp.where(head_of == h, vec[3:4, :], 0.0), axis=-1, keepdims=True)
                total = jnp.where(lane == h, one, total)
            lines[k][...] = total
        elif len(rows) == 4:
            for j, row in enumerate(rows):
                lines[k][:, j * vec.shape[1] : (j + 1) * vec.shape[1]] = vec[row : row + 1, :]
        else:
            lines[k][...] = vec[rows.start : rows.stop, :]
        copies.append(pltpu.make_async_copy(lines[k], smalls[k], s_sem.at[k]))
    for piece in copies:
        piece.start()
    units = unit_table(dims)

    def put(unit):
        m, row, col = units[unit]
        return pltpu.make_async_copy(
            wide.at[unit % slots], outs[m].at[pl.ds(row, UNIT_ROWS), pl.ds(col, UNIT_COLS)], o_sem.at[unit % slots]
        )

    for unit in range(len(units)):
        if unit >= slots:
            put(unit - slots).wait()

        def widen(b, _, unit=unit):
            rows = pl.ds(pl.multiple_of(b * 32, 32), 32)
            wide[unit % slots, rows, :] = res[unit, rows, :].astype(F32)
            return 0

        lax.fori_loop(0, UNIT_ROWS // 32, widen, 0)
        put(unit).start()
    for unit in range(len(units) - slots, len(units)):
        put(unit).wait()
    for piece in copies:
        piece.wait()


def write_results(got, dims):
    y, dx, _, vec = got
    half = vec.shape[1]
    small = [(2, half), (1, half), (1, half // 64)] + [(1, half)] * 7 + [(1, 4 * half)] * 3
    hbm = pl.BlockSpec(memory_space=pl.ANY)
    vmem = pl.BlockSpec(memory_space=pltpu.VMEM)
    dma = pltpu.SemaphoreType.DMA
    return pl.pallas_call(
        functools.partial(finish_kernel, dims),
        out_shape=[jax.ShapeDtypeStruct(y.shape, BF16), jax.ShapeDtypeStruct(dx.shape, F32)]
        + [jax.ShapeDtypeStruct(d, F32) for d in dims]
        + [jax.ShapeDtypeStruct(s, F32) for s in small],
        in_specs=[vmem] * 4,
        out_specs=[hbm] * 19,
        scratch_shapes=[pltpu.VMEM((6, UNIT_ROWS, UNIT_COLS), F32)]
        + [pltpu.VMEM(s, F32) for s in small]
        + [dma((6,)), dma((15,))],
        compiler_params=pltpu.CompilerParams(vmem_limit_bytes=30 * MIB),
        name="write_results",
    )(*got)


def on_pair_of_cores(
    layer_input, cotangent, w_qkv, qv_bias, w_out, out_bias, head_scale, ln1_gain, ln1_bias, ln2_gain, ln2_bias,
    ln3_gain, ln3_bias, w_fc1, fc1_bias, ln4_gain, ln4_bias, w_fc2, fc2_bias,
):
    params = (
        qv_bias, out_bias, head_scale, ln1_gain, ln1_bias, ln2_gain, ln2_bias, ln3_gain, ln3_bias,
        fc1_bias, ln4_gain, ln4_bias, fc2_bias,
    )
    params = [p.reshape(-1, p.shape[-1]) for p in params]
    weights = (w_qkv, w_out, w_fc1, w_fc2)
    got = whole_layer(layer_input, cotangent, weights, params)
    output, grad_input, qkv, out, up, down, *smalls = write_results(got, tuple(w.shape for w in weights))
    rows = [s.reshape(-1) for s in smalls]
    return (
        output, grad_input, qkv, smalls[0], out, rows[1], rows[2], rows[3], rows[4], rows[5], rows[6], rows[7], rows[8], up,
        rows[10], rows[11], rows[12], down, rows[9],
    )


def fits_pair(mesh):
    return mesh.shape["shard"] == 2 and mesh.shape["rep"] == 16


def solution(mesh):
    return jax.shard_map(
        on_pair_of_cores if fits_pair(mesh) else on_any_mesh,
        mesh=mesh,
        in_specs=(
            P(("rep", "shard"), None),
            P(("rep", "shard"), None),
            P("shard", None),
            P(None, "shard"),
            P("shard", None),
            P("shard"),
            P("shard"),
            P("shard"),
            P("shard"),
            P("shard"),
            P("shard"),
            P("shard"),
            P("shard"),
            P("shard", None),
            P("shard"),
            P("shard"),
            P("shard"),
            P("shard", None),
            P("shard"),
        ),
        out_specs=(
            P(("rep", "shard"), None),
            P(("rep", "shard"), None),
            P("shard", None),
            P(None, "shard"),
            P("shard", None),
            P("shard"),
            P("shard"),
            P("shard"),
            P("shard"),
            P("shard"),
            P("shard"),
            P("shard"),
            P("shard"),
            P("shard", None),
            P("shard"),
            P("shard"),
            P("shard"),
            P("shard", None),
            P("shard"),
        ),
        check_vma=False,
    )
```

```python
import functools

import jax
import jax.numpy as jnp
from jax import lax
from jax.experimental import pallas as pl
from jax.experimental.pallas import tpu as pltpu
from jax.sharding import PartitionSpec as P

D = 1024
HEADS = 16
HEAD_DIM = 64


EPS = 1e-05
NEG = -1e30


def norm_rows(v, gain, bias):
    centre = jnp.mean(v, axis=-1, keepdims=True)
    centred = v - centre
    spread = jnp.mean(centred * centred, axis=-1, keepdims=True)
    return centred * lax.rsqrt(spread + EPS) * gain + bias


def ffn_middle(hidden, gain, bias):
    return norm_rows(jax.nn.gelu(hidden, approximate=False), gain, bias)


def causal_mask(index, qblock, length):
    rows = index * qblock + lax.iota(jnp.int32, qblock)
    cols = lax.iota(jnp.int32, length)
    return (cols[None, :] <= rows[:, None])[None]


def block_scores(queries, keys_all, index, qblock, scale):
    length = keys_all.shape[0]
    scores = (
        jnp.einsum("qhd,khd->hqk", queries, keys_all, preferred_element_type=jnp.float32) * scale
    )
    return (queries, jnp.where(causal_mask(index, qblock, length), scores, NEG))


def attend_forward(queries, keys_all, values_all, scale):
    length, heads, width = queries.shape
    qblock = min(512, length)
    blocks = length // qblock

    def one_block(index):
        rows_q, scores = block_scores(queries, keys_all, index, qblock, scale)
        total = jax.nn.logsumexp(scores, axis=-1, keepdims=True)
        probs = jnp.exp(scores - total).astype(jnp.bfloat16)
        outcome = jnp.einsum("hqk,khd->qhd", probs, values_all, preferred_element_type=jnp.float32)
        return (outcome, total)

    outcome, totals = lax.map(one_block, jnp.arange(blocks, dtype=jnp.int32))
    return (outcome.reshape(length, heads, width), totals)


def attend_backward(queries, keys_all, values_all, totals, grad_out, scale):
    length, heads, width = queries.shape
    qblock = min(512, length)
    blocks = length // qblock

    def one_block(carry, index):
        grad_keys, grad_values = carry
        rows_q, scores = block_scores(queries, keys_all, index, qblock, scale)
        probs = jnp.exp(scores - totals[index])
        probs_low = probs.astype(jnp.bfloat16)
        grad_values = grad_values + jnp.einsum(
            "hqk,qhd->khd", probs_low, grad_out, preferred_element_type=jnp.float32
        )
        grad_probs = jnp.einsum(
            "qhd,khd->hqk", grad_out, values_all, preferred_element_type=jnp.float32
        )
        row_dot = jnp.sum(probs * grad_probs, axis=-1, keepdims=True)
        grad_scores = (probs * (grad_probs - row_dot)).astype(jnp.bfloat16)
        grad_rows = (
            jnp.einsum("hqk,khd->qhd", grad_scores, keys_all, preferred_element_type=jnp.float32)
            * scale
        )
        grad_keys = (
            grad_keys
            + jnp.einsum("hqk,qhd->khd", grad_scores, rows_q, preferred_element_type=jnp.float32)
            * scale
        )
        return ((grad_keys, grad_values), grad_rows)

    empty = jnp.zeros((length, heads, width), jnp.float32)
    (grad_keys, grad_values), grad_queries = lax.scan(
        one_block, (empty, empty), jnp.arange(blocks, dtype=jnp.int32)
    )
    return (grad_queries.reshape(length, heads, width), grad_keys, grad_values)


def on_any_mesh(
    layer_input,
    cotangent,
    w_qkv,
    qv_bias,
    w_out,
    out_bias,
    head_scale,
    ln1_gain,
    ln1_bias,
    ln2_gain,
    ln2_bias,
    ln3_gain,
    ln3_bias,
    w_fc1,
    fc1_bias,
    ln4_gain,
    ln4_bias,
    w_fc2,
    fc2_bias,
):
    low_qkv = w_qkv.astype(jnp.bfloat16)
    low_out = w_out.astype(jnp.bfloat16)
    low_heads = head_scale.astype(jnp.bfloat16)
    low_up = w_fc1.astype(jnp.bfloat16)
    low_down = w_fc2.astype(jnp.bfloat16)
    whole = (
        lax.all_gather(low_qkv, "shard", axis=0, tiled=True),
        lax.all_gather(qv_bias.astype(jnp.bfloat16), "shard", axis=1, tiled=True),
        lax.all_gather(low_out, "shard", axis=0, tiled=True),
        lax.all_gather(out_bias.astype(jnp.bfloat16), "shard", axis=0, tiled=True),
        lax.all_gather(low_heads, "shard", axis=0, tiled=True),
        lax.all_gather(ln1_gain.astype(jnp.bfloat16), "shard", axis=0, tiled=True),
        lax.all_gather(ln1_bias.astype(jnp.bfloat16), "shard", axis=0, tiled=True),
        lax.all_gather(ln2_gain.astype(jnp.bfloat16), "shard", axis=0, tiled=True),
        lax.all_gather(ln2_bias.astype(jnp.bfloat16), "shard", axis=0, tiled=True),
        lax.all_gather(ln3_gain.astype(jnp.bfloat16), "shard", axis=0, tiled=True),
        lax.all_gather(ln3_bias.astype(jnp.bfloat16), "shard", axis=0, tiled=True),
        lax.all_gather(low_up, "shard", axis=0, tiled=True),
        lax.all_gather(fc1_bias.astype(jnp.bfloat16), "shard", axis=0, tiled=True),
        lax.all_gather(ln4_gain.astype(jnp.bfloat16), "shard", axis=0, tiled=True),
        lax.all_gather(ln4_bias.astype(jnp.bfloat16), "shard", axis=0, tiled=True),
        lax.all_gather(low_down, "shard", axis=0, tiled=True),
        lax.all_gather(fc2_bias.astype(jnp.bfloat16), "shard", axis=0, tiled=True),
    )
    weight_qkv, weight_out, weight_up, weight_down = (whole[0], whole[2], whole[11], whole[15])
    (
        bias_qv,
        bias_out,
        head_gain,
        gain_one,
        shift_one,
        gain_two,
        shift_two,
        gain_three,
        shift_three,
        bias_up,
        gain_four,
        shift_four,
        bias_down,
    ) = tuple(
        (whole[index].astype(jnp.float32) for index in (1, 3, 4, 5, 6, 7, 8, 9, 10, 12, 13, 14, 16))
    )
    length = layer_input.shape[0]
    scale = HEAD_DIM ** (-0.5)
    inputs = layer_input.astype(jnp.float32)
    normed_one, pull_one = jax.vjp(norm_rows, inputs, gain_one, shift_one)
    act_one = normed_one.astype(jnp.bfloat16)
    bias_full = jnp.concatenate([bias_qv[0], jnp.zeros((D,), jnp.float32), bias_qv[1]])
    qkv = (jnp.dot(act_one, weight_qkv, preferred_element_type=jnp.float32) + bias_full).astype(
        jnp.bfloat16
    )
    triple = qkv.reshape(length, 3, HEADS, HEAD_DIM)
    queries = triple[:, 0]
    keys_all = triple[:, 1]
    values_all = triple[:, 2]
    attended, totals = attend_forward(queries, keys_all, values_all, scale)
    mixed = (attended * head_gain[:, None]).reshape(length, D).astype(jnp.bfloat16)
    branch = jnp.dot(mixed, weight_out, preferred_element_type=jnp.float32) + bias_out
    normed_two, pull_two = jax.vjp(norm_rows, branch, gain_two, shift_two)
    middle = inputs + normed_two
    normed_three, pull_three = jax.vjp(norm_rows, middle, gain_three, shift_three)
    act_three = normed_three.astype(jnp.bfloat16)
    hidden = jnp.dot(act_three, weight_up, preferred_element_type=jnp.float32) + bias_up
    normed_four, pull_four = jax.vjp(ffn_middle, hidden, gain_four, shift_four)
    act_four = normed_four.astype(jnp.bfloat16)
    result = middle + (
        jnp.dot(act_four, weight_down, preferred_element_type=jnp.float32) + bias_down
    )
    output = result.astype(jnp.bfloat16)
    again = (
        lax.all_gather(low_qkv, "shard", axis=0, tiled=True),
        lax.all_gather(low_out, "shard", axis=0, tiled=True),
        lax.all_gather(low_heads, "shard", axis=0, tiled=True),
        lax.all_gather(low_up, "shard", axis=0, tiled=True),
        lax.all_gather(low_down, "shard", axis=0, tiled=True),
    )
    back_qkv, back_out, back_up, back_down = (again[0], again[1], again[3], again[4])
    back_heads = again[2].astype(jnp.float32)
    cot_full = cotangent.astype(jnp.float32)
    grad_down_bias = jnp.sum(cot_full, axis=0)
    grad_down = jnp.einsum("tf,td->fd", act_four, cotangent, preferred_element_type=jnp.float32)
    grad_four = jnp.einsum("td,fd->tf", cotangent, back_down, preferred_element_type=jnp.float32)
    grad_hidden, grad_gain_four, grad_shift_four = pull_four(grad_four)
    hidden_low = grad_hidden.astype(jnp.bfloat16)
    grad_up_bias = jnp.sum(hidden_low, axis=0, dtype=jnp.float32)
    grad_up = jnp.einsum("td,tf->df", act_three, hidden_low, preferred_element_type=jnp.float32)
    grad_three = jnp.einsum("tf,df->td", hidden_low, back_up, preferred_element_type=jnp.float32)
    grad_mid_part, grad_gain_three, grad_shift_three = pull_three(grad_three)
    grad_middle = cot_full + grad_mid_part
    grad_branch, grad_gain_two, grad_shift_two = pull_two(grad_middle)
    branch_low = grad_branch.astype(jnp.bfloat16)
    grad_out_b = jnp.sum(branch_low, axis=0, dtype=jnp.float32)
    grad_out_w = jnp.einsum("td,te->de", mixed, branch_low, preferred_element_type=jnp.float32)
    grad_mixed = jnp.einsum("te,de->td", branch_low, back_out, preferred_element_type=jnp.float32)
    grad_mixed = grad_mixed.reshape(length, HEADS, HEAD_DIM)
    grad_heads = jnp.sum(grad_mixed * attended, axis=(0, 2))
    grad_attended = (grad_mixed * back_heads[:, None]).astype(jnp.bfloat16)
    grad_queries, grad_keys, grad_values = attend_backward(
        queries, keys_all, values_all, totals, grad_attended, scale
    )
    grad_qkv = (
        jnp.stack([grad_queries, grad_keys, grad_values], axis=1)
        .reshape(length, 3 * D)
        .astype(jnp.bfloat16)
    )
    grad_qv = jnp.stack(
        [
            jnp.sum(grad_qkv[:, :D], axis=0, dtype=jnp.float32),
            jnp.sum(grad_qkv[:, 2 * D :], axis=0, dtype=jnp.float32),
        ]
    )
    grad_qkv_w = jnp.einsum("td,te->de", act_one, grad_qkv, preferred_element_type=jnp.float32)
    grad_one = jnp.einsum("te,de->td", grad_qkv, back_qkv, preferred_element_type=jnp.float32)
    grad_in_part, grad_gain_one, grad_shift_one = pull_one(grad_one)
    grad_input = grad_middle + grad_in_part
    shares = (
        lax.psum_scatter(grad_qkv_w, "shard", scatter_dimension=0, tiled=True),
        lax.psum_scatter(grad_qv, "shard", scatter_dimension=1, tiled=True),
        lax.psum_scatter(grad_out_w, "shard", scatter_dimension=0, tiled=True),
        lax.psum_scatter(grad_out_b, "shard", scatter_dimension=0, tiled=True),
        lax.psum_scatter(grad_heads, "shard", scatter_dimension=0, tiled=True),
        lax.psum_scatter(grad_gain_one, "shard", scatter_dimension=0, tiled=True),
        lax.psum_scatter(grad_shift_one, "shard", scatter_dimension=0, tiled=True),
        lax.psum_scatter(grad_gain_two, "shard", scatter_dimension=0, tiled=True),
        lax.psum_scatter(grad_shift_two, "shard", scatter_dimension=0, tiled=True),
        lax.psum_scatter(grad_gain_three, "shard", scatter_dimension=0, tiled=True),
        lax.psum_scatter(grad_shift_three, "shard", scatter_dimension=0, tiled=True),
        lax.psum_scatter(grad_up, "shard", scatter_dimension=0, tiled=True),
        lax.psum_scatter(grad_up_bias, "shard", scatter_dimension=0, tiled=True),
        lax.psum_scatter(grad_gain_four, "shard", scatter_dimension=0, tiled=True),
        lax.psum_scatter(grad_shift_four, "shard", scatter_dimension=0, tiled=True),
        lax.psum_scatter(grad_down, "shard", scatter_dimension=0, tiled=True),
        lax.psum_scatter(grad_down_bias, "shard", scatter_dimension=0, tiled=True),
    )
    summed = lax.psum(
        (
            shares[0],
            shares[1],
            shares[2],
            shares[3],
            shares[4],
            shares[5],
            shares[6],
            shares[7],
            shares[8],
            shares[9],
            shares[10],
            shares[11],
            shares[12],
            shares[13],
            shares[14],
            shares[15],
            shares[16],
        ),
        "rep",
    )
    return (output, grad_input) + tuple(summed)


MESH = pl.DeviceIdType.MESH
BF16 = jnp.bfloat16
F32 = jnp.float32
UNIT_ROWS = 256
UNIT_COLS = 1024
MIB = 1 << 20
SLOT = {
    "d1": 0, "d2": 1, "z1": 2, "z3": 2, "z2": 3, "u1": 4, "w1": 4, "u2": 5, "w2": 5, "u3": 6, "w3": 6, "g1": 7, "g2": 8,
}


def unit_table(dims):
    table = []
    for matrix in (3, 2, 1, 0):
        rows, cols = dims[matrix]
        for col in range(0, cols, UNIT_COLS):
            for row in range(0, rows, UNIT_ROWS):
                table.append((matrix, row, col))
    return table


KINDS = (
    "QX", "QX", "QX", "QY", "QY", "QY", "QY", "QY", "Y", "X", "X", "Y", "ZY", "ZY", "X", "Y", "X", "X", "ZY",
    "Y", "Y", "X", "ZY", "X",
)
TASK, VECTORS = 24, 25
ORDER = (
    1, 5, 24, 2, 3, 5, 0, 24, 4, 0, 4, 24, 2, 24, 24, 1, 24, 24, 24, 24, 24, 24, 24, 6, 5, 7, 4, 10, 6, 8, 11,
    7, 13, 2, 24, 24, 14, 15, 24, 5, 4, 24, 24, 24, 5, 0, 9, 10, 4, 16, 17, 5, 13, 7, 2, 24, 12, 24, 14, 24, 24,
    4, 9, 7, 5, 24, 16, 6, 8, 7, 0, 3, 10, 19, 12, 20, 2, 23, 21, 5, 1, 9, 0, 5, 10, 7, 13, 0, 4, 12, 6, 1, 2,
    2, 9, 8, 3, 23, 0, 13, 16, 17, 4, 24, 11, 16, 22, 4, 6, 12, 7, 8, 5, 13, 24, 0, 3, 21, 9, 15, 2, 6, 16, 20,
    24, 8, 11, 13, 17, 7, 2, 16, 3, 12, 7, 22, 10, 4, 6, 15, 19, 16, 3, 11, 24, 12, 8, 8, 0, 3, 14, 15, 1, 7,
    10, 2, 20, 22, 23, 11, 17, 10, 15, 9, 1, 19, 21, 14, 25, 18, 12, 0, 20, 3, 10, 1, 13, 16, 6, 22, 21, 3, 8,
    19, 20, 1, 10, 22, 9, 16, 23, 21, 6, 20, 19, 8, 13, 7, 1, 6, 22, 23, 11, 20, 16, 18, 17, 14, 10, 23, 9, 25,
    1, 11, 23, 17, 15, 12, 4, 19, 3, 18, 19, 14, 21, 11, 22, 9, 25, 5, 16, 18, 20, 23, 8, 11, 20, 19, 15, 17,
    17, 18, 14, 17, 19, 23, 21, 12, 14, 21, 6, 18, 9, 12, 15, 17, 14, 18, 3, 0, 25, 10, 19, 21, 15, 13, 20, 23,
    22, 9, 2, 18, 13, 22, 14, 15, 22, 13, 17, 1, 19, 21, 18, 12, 20, 11, 18, 25, 8, 18, 23, 22, 14, 15, 21, 11,
)


GIVE_ROWS = 240


def program_order(units, ends):
    order, task, vector, waited, step = [], 0, 0, {3}, [0] * len(units)
    order.append(("wait", 3, 0))
    for entry in ORDER:
        if entry == TASK:
            order.append(("task", task, 0))
            task += 1
            continue
        if entry == VECTORS:
            order.append(("vec", vector, 0))
            vector += 1
            continue
        m = units[entry][0]
        if m not in waited:
            assert task >= ends[m]
            order.append(("wait", m, 0))
            waited.add(m)
        order.append(("sum", entry, step[entry]))
        step[entry] += 1
    return order


PAIRS = 2


def fold(v):
    total = v[0:8]
    for k in range(1, v.shape[0] // 8):
        total = total + v[8 * k : 8 * k + 8]
    return total


def layer_kernel(dims, at_base, g_base, *refs):
    x_in, cot_in, weights, params = refs[0], refs[1], refs[2:6], refs[6:19]
    y_out, dx_out, res, vec_out, tiles_hbm = refs[19:24]
    (
        at, g, give, pair, line_xy, line_z, ring, big, left, act, hid, qkv, probs, attended, branch, middle, dmid,
        late_in, near_left, near_right, vec_w, vec_h, rstd4, sums4, vec_in, vec_own, vec_got,
        send, recv, v_send, v_recv, p_send, p_recv, l_sem, w_in, w_keep, w_send, w_recv, t_sem, s_sem, e_sem, n_send, n_recv,
    ) = refs[24:]
    r = lax.axis_index("rep")
    c = lax.axis_index("shard")
    x, y, z = r % 2, (r // 2) % 2, r // 4
    core = {"shard": 1 - c}
    to = {
        "X": {"rep": r + 1 - 2 * x},
        "Y": {"rep": r + 2 - 4 * y},
        "U": {"rep": r + 4},
        "D": {"rep": r - 4},
        "XY": {"rep": r + 3 - 2 * x - 4 * y},
    }
    line_end = (z == 0) | (z == 3)
    line_mid = (z == 1) | (z == 2)
    outward = {"rep": r + 4 * (2 * (z // 2) - 1)}
    inward = {"rep": r + 4 * (1 - 2 * (z // 2))}
    across = {"rep": r + 4 * (3 - 2 * z)}
    upper = z // 2
    length = x_in.shape[0]
    width = x_in.shape[1]
    half_w = width // 2
    hidden = dims[2][1]
    half_h = hidden // 2
    blocks = hidden // width
    TILE = 512

    tile_of = []
    for m, (rows, cols) in enumerate(dims):
        for row in range(0, rows, TILE):
            for col in range(0, cols, UNIT_COLS):
                tile_of.append((m, row, col))
    first_tile = [min(t for t, v in enumerate(tile_of) if v[0] == m) for m in range(4)]
    parts = 2 * len(tile_of)
    slots_f, slots_b, late, slots_l, slots_g = 6, 16, 16, 2, 7

    def part_read(i):
        m, row, col = tile_of[i // 2]
        return pltpu.make_async_copy(
            weights[m].at[pl.ds(row + (i % 2) * 256, 256), pl.ds(col, UNIT_COLS)],
            late_in.at[pl.ds((i % slots_l) * 256, 256), :] if i >= late else big.at[pl.ds((i % slots_f) * 256, 256), :],
            w_in.at[slots_f + i % slots_l if i >= late else i % slots_f],
        )

    def low_row(i):
        return 240 * 16 + (i - late) % slots_g * 256 if i >= late else i * 256

    def part_low(i):
        return low_buf.at[pl.ds(low_row(i), 256), :]

    low_buf = give

    def part_place(i):
        return tiles_hbm.at[c, i // 2, pl.ds((i % 2) * 256, 256), :]

    def part_keep(i):
        return pltpu.make_async_copy(part_low(i), part_place(i), w_keep.at[i % slots_b])

    def part_give(i):
        return pltpu.make_async_remote_copy(
            src_ref=part_low(i), dst_ref=part_place(i), send_sem=w_send.at[i % slots_b], recv_sem=w_recv.at[i],
            device_id=core, device_id_type=MESH,
        )

    def part_got(i):
        return pltpu.make_async_remote_copy(
            src_ref=part_low(i), dst_ref=tiles_hbm.at[1 - c, i // 2, pl.ds((i % 2) * 256, 256), :],
            send_sem=w_send.at[i % slots_b], recv_sem=w_recv.at[i], device_id=core, device_id_type=MESH,
        )

    for i in range(slots_f):
        part_read(i).start()

    barrier = pltpu.get_barrier_semaphore()
    for peer in (core, to["X"], to["Y"], to["XY"]):
        pl.semaphore_signal(barrier, inc=1, device_id=peer, device_id_type=MESH)

    @pl.when(z < 3)
    def _():
        pl.semaphore_signal(barrier, inc=1, device_id=to["U"], device_id_type=MESH)

    @pl.when(z > 0)
    def _():
        pl.semaphore_signal(barrier, inc=1, device_id=to["D"], device_id_type=MESH)

    @pl.when(line_end)
    def _():
        pl.semaphore_signal(barrier, inc=1, device_id=across, device_id_type=MESH)

    narrow = (0, 0, 2, 3, 4, 5, 6, 7, 8, 9, 10)

    def rounded(v):
        return v.astype(BF16).astype(F32)

    lane_w = pl.ds(pl.multiple_of(c * half_w, half_w), half_w)
    lane_h = pl.ds(pl.multiple_of(c * half_h, half_h), half_h)
    (qv_ref, ob_ref, hs_ref, g1_ref, b1_ref, g2_ref, b2_ref, g3_ref, b3_ref, ub_ref, g4_ref, b4_ref, db_ref) = params
    vec_w[0:2, lane_w] = rounded(qv_ref[...])
    for row, ref in zip((2, 4, 5, 6, 7, 8, 9, 10), (ob_ref, g1_ref, b1_ref, g2_ref, b2_ref, g3_ref, b3_ref, db_ref)):
        vec_w[row : row + 1, lane_w] = rounded(ref[...])
    head_of = lax.broadcasted_iota(jnp.int32, (1, half_w), 1) // 64
    spread = jnp.zeros((1, half_w), F32)
    for h in range(half_w // 64):
        spread = jnp.where(head_of == h, rounded(hs_ref[0:1, h : h + 1]), spread)
    vec_w[3:4, lane_w] = spread
    for row, ref in enumerate((ub_ref, g4_ref, b4_ref)):
        vec_h[row : row + 1, lane_h] = rounded(ref[...])
    QB, VB, OB, HS, G1, B1, G2, B2, G3, B3, DB = range(11)
    UB, G4, B4 = range(3)

    def small_copy(k, give_it):
        ref, lane, far = ((vec_w, lane_w, 1 - c), (vec_h, lane_h, 1 - c))[k]
        size = half_w if k == 0 else half_h
        other = pl.ds(pl.multiple_of((1 - c) * size, size), size)
        here = ref.at[:, lane]
        return pltpu.make_async_remote_copy(
            src_ref=here, dst_ref=here if give_it else ref.at[:, other], send_sem=s_sem.at[k, 0], recv_sem=s_sem.at[k, 1],
            device_id=core, device_id_type=MESH,
        )

    e_copy = pltpu.make_async_copy(cot_in, g.at[pl.ds(0, length), pl.ds(g_base[3], width)], e_sem.at[0])
    e_copy.start()

    def left_own(m):
        rows = dims[m][0]
        return pltpu.make_async_copy(
            left.at[pl.ds(pl.multiple_of(2 * at_base[m] + c * rows, 512), rows), :],
            at.at[pl.ds(at_base[m], rows), pl.ds(0, length)],
            l_sem.at[m],
        )

    def left_far(m):
        rows = dims[m][0]
        return pltpu.make_async_remote_copy(
            src_ref=left.at[pl.ds(pl.multiple_of(2 * at_base[m] + (1 - c) * rows, 512), rows), :],
            dst_ref=at.at[pl.ds(at_base[m], rows), pl.ds(length, length)],
            send_sem=p_send.at[m, 0], recv_sem=p_recv.at[m, 0], device_id=core, device_id_type=MESH,
        )

    def right_far(m):
        cols = pl.ds(g_base[m], dims[m][1])
        return pltpu.make_async_remote_copy(
            src_ref=g.at[pl.ds(0, length), cols], dst_ref=g.at[pl.ds(length, length), cols],
            send_sem=p_send.at[m, 1], recv_sem=p_recv.at[m, 1], device_id=core, device_id_type=MESH,
        )

    def start_left(m):
        left_own(m).start()
        left_far(m).start()

    def wait_pair(m):
        left_own(m).wait()
        left_far(m).wait()
        right_far(m).wait()

    converted, kept_parts, given_parts = [0], set(), set()

    def kept(i):
        if i not in kept_parts:
            kept_parts.add(i)
            part_keep(i).wait()

    def given(i):
        if i not in given_parts:
            given_parts.add(i)
            part_give(i).wait_send()

    def convert_parts(upto):
        for i in range(converted[0], upto):
            part_read(i).wait()
            if i >= slots_b:
                kept(i - slots_b)
            if i == late:
                for k in range(late):
                    kept(k)
                    given(k)
            if i >= late + slots_g:
                kept(i - slots_g)
                given(i - slots_g)
            source, first = (late_in, i % slots_l * 256) if i >= late else (big, i % slots_f * 256)

            def convert(b, _, i=i, source=source, first=first):
                rows = pl.multiple_of(first + b * 32, 32)
                low = pl.multiple_of(low_row(i) + b * 32, 32)
                low_buf[pl.ds(low, 32), :] = source[pl.ds(rows, 32), :].astype(BF16)
                return 0

            lax.fori_loop(0, 8, convert, 0)
            part_keep(i).start()
            if i == 0:
                pl.semaphore_wait(barrier, 6)
                small_copy(0, True).start()
                small_copy(1, True).start()
            part_give(i).start()
            if i >= late and i + slots_l < parts:
                part_read(i + slots_l).start()
            if i + slots_f < late:
                part_read(i + slots_f).start()
            if i == late - slots_f:
                for k in range(slots_l):
                    part_read(late + k).start()
        converted[0] = max(converted[0], upto)

    def cotangent_copy(k, relay):
        here, there = pl.ds(0, length), pl.ds(length, length)
        cols = pl.ds(g_base[3], width)
        return pltpu.make_async_remote_copy(
            src_ref=near_right.at[k, here, :] if relay else near_right.at[0, here, :] if k == 2 else g.at[here, cols],
            dst_ref=near_right.at[k, there if relay else here, :],
            send_sem=n_send.at[k, int(relay)], recv_sem=n_recv.at[k, int(relay)],
            device_id=core if relay else to["XYY"[k]], device_id_type=MESH,
        )

    convert_parts(2)
    e_copy.wait()
    right_far(3).start()
    cotangent_copy(0, False).start()
    cotangent_copy(1, False).start()
    convert_parts(4)

    def tile(m, half, index):
        return (half, first_tile[m] + index)

    stream = []
    for m in (0, 1, 2):
        for index in range(dims[m][1] // UNIT_COLS):
            stream += [tile(m, 0, index), tile(m, 1, index)]
    per_half = dims[3][0] // TILE
    stream += [tile(3, h, k) for h in range(2) for k in range(per_half)]
    for m in (2, 1, 0):
        for index in range(dims[m][1] // UNIT_COLS):
            stream += [tile(m, 0, index), tile(m, 1, index)]
    slots_t = 4
    here = set()

    def tile_load(i):
        half, t = stream[i]
        return pltpu.make_async_copy(
            tiles_hbm.at[half, t], ring.at[i % slots_t], t_sem.at[i % slots_t]
        )

    def tile_start(i):
        half, t = stream[i]
        if (1, t) not in here:
            here.add((1, t))
            convert_parts(2 * t + 2)
            for k in (2 * t, 2 * t + 1):
                kept(k)
                part_got(k).wait_recv()
        tile_load(i).start()

    at_tile, started, allowed_to = [0], [0], [0]

    def fill(limit=None):
        if limit is not None:
            allowed_to[0] = limit
        while started[0] < min(at_tile[0] + slots_t, allowed_to[0], len(stream)):
            tile_start(started[0])
            started[0] += 1

    def next_tile(ahead=0):
        i = at_tile[0] + ahead
        assert i < started[0]
        tile_load(i).wait()
        return ring.at[i % slots_t]

    def done_tile(count=1):
        at_tile[0] += count
        fill()

    def mean(v):
        return jnp.sum(v, axis=-1, keepdims=True) / v.shape[-1]

    def normal(v):
        centred = v - mean(v)
        scale = lax.rsqrt(mean(centred * centred) + 1e-05)
        return centred * scale, scale

    def each(fn, step=32, init=0, unroll=1):
        def body(i, carry):
            return fn(pl.ds(pl.multiple_of(i * step, step), step), carry)

        return lax.fori_loop(0, length // step, body, init, unroll=unroll)

    def w_row(i):
        return vec_w[i : i + 1, :]

    def turn(source, m, block=0):
        for k in range(width // 256):
            row = 2 * at_base[m] + block * width + k * 256
            left[row : row + 256, :] = jnp.transpose(source[:, k * 256 : (k + 1) * 256])

    NT = (((1,), (1,)), ((), ()))
    TN = (((0,), (0,)), ((), ()))

    def nt(a, b):
        return lax.dot_general(a, b, NT, preferred_element_type=F32)

    def tn(a, b):
        return lax.dot_general(a, b, TN, preferred_element_type=F32)

    def product_pair(source, write):
        first, second = next_tile(), next_tile(1)
        for k in range(UNIT_COLS // 256):
            cols = slice(k * 256, (k + 1) * 256)
            value = jnp.dot(source[:, 0:half_w], first[:, cols], preferred_element_type=F32)
            value = value + jnp.dot(source[:, half_w:width], second[:, cols], preferred_element_type=F32)
            write(cols, value)
        done_tile(2)

    small_copy(0, True).wait_send()
    small_copy(1, True).wait_send()
    small_copy(0, False).wait_recv()
    small_copy(1, False).wait_recv()

    def first_norm(rows, _):
        hat, _s = normal(x_in[rows, :].astype(F32))
        act[rows, :] = (hat * w_row(G1) + w_row(B1)).astype(BF16)
        return 0

    each(first_norm, unroll=2)
    fill(8)
    for index in range(3):

        def put_qkv(cols, value, index=index):
            if index == 0:
                value = value + vec_w[QB : QB + 1, cols]
            if index == 2:
                value = value + vec_w[VB : VB + 1, cols]
            qkv[:, index * width + cols.start : index * width + cols.stop] = value.astype(BF16)

        product_pair(act, put_qkv)
        convert_parts(10 + 2 * index)
    turn(act, 0)
    start_left(0)
    convert_parts(16)
    for k in range(2):
        cotangent_copy(k, False).wait()
        cotangent_copy(k, True).start()
    cotangent_copy(2, False).start()

    low_lane = lax.broadcasted_iota(jnp.int32, (length, 128), 1) < 64
    allowed = lax.broadcasted_iota(jnp.int32, (length, length), 1) <= lax.broadcasted_iota(
        jnp.int32, (length, length), 0
    )
    scale = 64 ** (-0.5)
    keep_lane = (low_lane.astype(F32).astype(BF16), jnp.logical_not(low_lane).astype(F32).astype(BF16))

    def split_heads(v):
        return jnp.concatenate([v * keep_lane[0], v * keep_lane[1]], axis=0)

    def attend(p):
        q = qkv[:, pl.ds(pl.multiple_of(p * 128, 128), 128)]
        k = qkv[:, pl.ds(pl.multiple_of(width + p * 128, 128), 128)]
        v = qkv[:, pl.ds(pl.multiple_of(2 * width + p * 128, 128), 128)]
        both = nt(q, split_heads(k)) * scale
        got = []
        for h in range(2):
            scores = jnp.where(allowed, both[:, h * length : (h + 1) * length], -1e30)
            top = jnp.max(scores, axis=-1, keepdims=True)
            lse = top + jnp.log(jnp.sum(jnp.exp(scores - top), axis=-1, keepdims=True))
            got.append(jnp.exp(scores - lse))
        prob = jnp.concatenate(got, axis=1)
        probs[p] = prob
        value = jnp.dot(prob.astype(BF16), split_heads(v), preferred_element_type=F32)
        cols = pl.ds(pl.multiple_of(p * 128, 128), 128)
        attended[:, cols] = value
        act[:, cols] = (value * vec_w[HS : HS + 1, cols]).astype(BF16)

    def attend_some(i, _):
        for n in range(PAIRS):
            attend(i * PAIRS + n)
        return 0

    lax.fori_loop(0, width // 128 // PAIRS, attend_some, 0)
    fill(10)

    def put_branch(cols, value):
        branch[:, cols] = value + vec_w[OB : OB + 1, cols]

    product_pair(act, put_branch)
    fill(16)
    turn(act, 1)
    start_left(1)

    def second_norm(rows, _):
        hat, _s = normal(branch[rows, :])
        mid = x_in[rows, :].astype(F32) + (hat * w_row(G2) + w_row(B2))
        middle[rows, :] = mid
        hat, _s = normal(mid)
        act[rows, :] = (hat * w_row(G3) + w_row(B3)).astype(BF16)
        return 0

    each(second_norm, unroll=2)
    U0, H0, D0 = 0, blocks * length, 2 * blocks * length
    for j in range(blocks):

        def put_hidden(cols, value, j=j):
            wide = slice(j * width + cols.start, j * width + cols.stop)
            big[U0 + j * length : U0 + (j + 1) * length, cols] = value + vec_h[UB : UB + 1, wide]

        product_pair(act, put_hidden)
    turn(act, 2)
    start_left(2)
    root_half = 0.7071067811865476

    def near(base, start):
        return pl.ds(pl.multiple_of(base + start, 16), 16)

    def hidden_norm(rows, _):
        total = jnp.zeros((16, 1), F32)
        for j in range(blocks):
            u = big[near(U0 + j * length, rows.start), :]
            h = u * (1.0 + lax.erf(u * root_half)) * 0.5
            big[near(H0 + j * length, rows.start), :] = h
            total = total + jnp.sum(h, axis=-1, keepdims=True)
        centre = total / hidden
        total = jnp.zeros((16, 1), F32)
        for j in range(blocks):
            h = big[near(H0 + j * length, rows.start), :] - centre
            total = total + jnp.sum(h * h, axis=-1, keepdims=True)
        s = lax.rsqrt(total / hidden + 1e-05)
        rstd4[rows, :] = jnp.broadcast_to(s, (16, 128))
        for j in range(blocks):
            at_h = near(H0 + j * length, rows.start)
            hat = (big[at_h, :] - centre) * s
            big[at_h, :] = hat
            cols = slice(j * width, (j + 1) * width)
            hid[near(j * length, rows.start), :] = (
                hat * vec_h[G4 : G4 + 1, cols] + vec_h[B4 : B4 + 1, cols]
            ).astype(BF16)
        return 0

    cotangent_copy(2, False).wait()
    cotangent_copy(2, True).start()
    each(hidden_norm, 16)
    for j in range(blocks):
        turn(hid.at[pl.ds(j * length, length), :], 3, j)
    start_left(3)
    convert_parts(parts)

    tasks = []
    zeros8 = jnp.zeros((8, width), F32)
    dirs = g.at[pl.ds(0, length), :]

    def put_sum(row, value):
        line = jnp.sum(value, axis=0, keepdims=True)
        vec_in[0, row : row + 1, :] = line[:, 0:half_w]
        vec_in[1, row : row + 1, :] = line[:, half_w:width]

    def task_down(h, k):
        def run():
            w = next_tile()
            row = h * dims[3][0] + k * TILE
            j, lane = row // width, row % width
            if h == 0 and k == 0:
                y_acc[...] = middle[...] + w_row(DB)
            for n in range(TILE // 256):
                big[D0 + j * length : D0 + (j + 1) * length, lane + n * 256 : lane + (n + 1) * 256] = nt(
                    dirs[:, g_base[3] : g_base[3] + width], w[n * 256 : (n + 1) * 256, :]
                )

            for n in range(width // 256):
                cols = slice(n * 256, (n + 1) * 256)
                y_acc[:, cols] += jnp.dot(
                    hid[j * length : (j + 1) * length, lane : lane + TILE], w[:, cols], preferred_element_type=F32
                )
            done_tile()
            if h == 1 and k == per_half - 1:
                y_out[...] = y_acc[...].astype(BF16)

        return run

    y_acc = dmid
    for h in range(2):
        for k in range(per_half):
            tasks.append((1.2, task_down(h, k)))

    def task_hidden(first, count):
        def run():
            if first == 0:
                sums4[...] = jnp.zeros_like(sums4)

                def e_sum(rows, carry):
                    return carry + fold(dirs[rows, g_base[3] : g_base[3] + width].astype(F32))

                put_sum(DB, each(e_sum, 32, zeros8))

            def body(i, _):
                at_r = pl.multiple_of(first + i * 16, 16)
                one = jnp.zeros((16, 1), F32)
                two = jnp.zeros((16, 1), F32)
                for j in range(blocks):
                    gain = vec_h[G4 : G4 + 1, j * width : (j + 1) * width]
                    d = big[near(D0 + j * length, at_r), :] * gain
                    hat = big[near(H0 + j * length, at_r), :]
                    one = one + jnp.sum(d, axis=-1, keepdims=True)
                    two = two + jnp.sum(d * hat, axis=-1, keepdims=True)
                one, two = one / hidden, two / hidden
                s = rstd4[pl.ds(at_r, 16), 0:1]
                for j in range(blocks):
                    cols = slice(j * width, (j + 1) * width)
                    da = big[near(D0 + j * length, at_r), :]
                    hat = big[near(H0 + j * length, at_r), :]
                    u = big[near(U0 + j * length, at_r), :]
                    dh = s * (da * vec_h[G4 : G4 + 1, cols] - one - hat * two)
                    slope = 0.5 * (1.0 + lax.erf(u * root_half)) + u * (jnp.exp(u * u * -0.5) * 0.3989422804014327)
                    du = (dh * slope).astype(BF16)
                    g[pl.ds(at_r, 16), g_base[2] + j * width : g_base[2] + (j + 1) * width] = du
                    sums4[0:8, cols] += fold(du.astype(F32))
                    sums4[8:16, cols] += fold(da * hat)
                    sums4[16:24, cols] += fold(da)
                return 0

            lax.fori_loop(0, count // 16, body, 0)
            if first + count == length:
                for i in range(3):
                    line = jnp.sum(sums4[8 * i : 8 * i + 8, :], axis=0, keepdims=True)
                    for n in range(hidden // half_w):
                        hh, k = divmod(n, half_h // half_w)
                        vec_in[hh, 11 + 4 * i + k : 12 + 4 * i + k, :] = line[:, n * half_w : (n + 1) * half_w]
                right_far(2).start()

        return run

    for first in range(0, length, 32):
        tasks.append((3.0, task_hidden(first, 32)))

    def add_pair(acc, index_of, cols_of, count, width_to):
        def make(index):
            def run():
                for h in range(2):
                    w = next_tile()
                    for n in range(TILE // 256):
                        cols = slice(h * half_w + n * 256, h * half_w + (n + 1) * 256)
                        value = nt(dirs[:, cols_of(index)], w[n * 256 : (n + 1) * 256, :])
                        if index == 0:
                            acc[:, cols] = value
                        else:
                            acc[:, cols] += value
                    done_tile()

            return run

        return [(1.2, make(index)) for index in range(count)]

    ends = {2: len(tasks)}
    acc = big.at[pl.ds(U0, length), :]
    tasks += add_pair(acc, None, lambda j: slice(g_base[2] + j * width, g_base[2] + (j + 1) * width), blocks, width)

    def task_norms():
        def body(rows, carry):
            s3g, s3b, s2g, s2b, sob = carry
            da = acc[rows, :]
            hat, s = normal(middle[rows, :])
            d = da * w_row(G3)
            d_mid = dirs[rows, g_base[3] : g_base[3] + width].astype(F32) + s * (d - mean(d) - hat * mean(d * hat))
            dmid[rows, :] = d_mid
            s3g, s3b = s3g + fold(da * hat), s3b + fold(da)
            hat, s = normal(branch[rows, :])
            d = d_mid * w_row(G2)
            dy = (s * (d - mean(d) - hat * mean(d * hat))).astype(BF16)
            s2g, s2b = s2g + fold(d_mid * hat), s2b + fold(d_mid)
            g[rows, g_base[1] : g_base[1] + width] = dy
            return (s3g, s3b, s2g, s2b, sob + fold(dy.astype(F32)))

        got = each(body, 16, (zeros8,) * 5)
        for row, value in zip((G3, B3, G2, B2, OB), got):
            put_sum(row, value)
        right_far(1).start()

    tasks.append((2.5, task_norms))
    ends[1] = len(tasks)
    d_mixed = big.at[pl.ds(U0 + length, length), :]
    tasks += add_pair(d_mixed, None, lambda j: slice(g_base[1], g_base[1] + width), 1, width)

    def task_heads():
        def body(rows, carry):
            d = d_mixed[rows, :]
            act[rows, :] = (d * w_row(HS)).astype(BF16)
            return carry + fold(d * attended[rows, :])

        put_sum(HS, each(body, 32, zeros8))

    tasks.append((0.6, task_heads))

    def task_attend(first, count):
        def run():
            def pair_of_heads(p):
                q_cols = pl.ds(pl.multiple_of(p * 128, 128), 128)
                k_cols = pl.ds(pl.multiple_of(width + p * 128, 128), 128)
                v_cols = pl.ds(pl.multiple_of(2 * width + p * 128, 128), 128)
                q, k, v, do = qkv[:, q_cols], qkv[:, k_cols], qkv[:, v_cols], act[:, q_cols]
                prob = probs[p]
                dv = tn(prob.astype(BF16), do)
                dp = nt(do, split_heads(v))
                ds = []
                for h in range(2):
                    own = slice(h * length, (h + 1) * length)
                    dot = jnp.sum(prob[:, own] * dp[:, own], axis=-1, keepdims=True)
                    ds.append(prob[:, own] * (dp[:, own] - dot))
                ds = jnp.concatenate(ds, axis=1).astype(BF16)
                dq = jnp.dot(ds, split_heads(k), preferred_element_type=F32) * scale
                dk = tn(ds, q) * scale
                g[0:length, q_cols] = dq.astype(BF16)
                g[0:length, k_cols] = jnp.where(low_lane, dk[0:length], dk[length : 2 * length]).astype(BF16)
                g[0:length, v_cols] = jnp.where(low_lane, dv[0:length], dv[length : 2 * length]).astype(BF16)

            for n in range(count):
                pair_of_heads(first + n)
            if first + count == width // 128:

                def sums(rows, carry):
                    a, b = carry
                    return (
                        a + fold(g[rows, 0:width].astype(F32)),
                        b + fold(g[rows, 2 * width : 3 * width].astype(F32)),
                    )

                a, b = each(sums, 32, (zeros8, zeros8))
                put_sum(QB, a)
                put_sum(VB, b)
                right_far(0).start()

        return run

    for first in range(0, width // 128, 2):
        tasks.append((3.0, task_attend(first, 2)))
    ends[0] = len(tasks)
    d_first = big.at[pl.ds(U0 + 2 * length, length), :]
    tasks += add_pair(d_first, None, lambda j: slice(j * width, (j + 1) * width), 3, width)

    def task_last():
        def body(rows, carry):
            sg, sb = carry
            da = d_first[rows, :]
            hat, s = normal(x_in[rows, :].astype(F32))
            d = da * w_row(G1)
            dx_out[rows, :] = dmid[rows, :] + s * (d - mean(d) - hat * mean(d * hat))
            return (sg + fold(da * hat), sb + fold(da))

        sg, sb = each(body, 16, (zeros8, zeros8))
        put_sum(G1, sg)
        put_sum(B1, sb)
        vec_in[0, 23:24, :] = jnp.zeros((1, half_w), F32)
        vec_in[1, 23:24, :] = jnp.zeros((1, half_w), F32)
        vec_copy(0).start()

    tasks.append((1.5, task_last))

    vec_steps = (core, to["X"], to["Y"], {"rep": r + 4 * (1 - 2 * (z % 2))}, across)

    def vec_copy(step):
        source = vec_in.at[1 - c] if step == 0 else vec_own.at[step]
        return pltpu.make_async_remote_copy(
            src_ref=source, dst_ref=vec_got.at[step], send_sem=v_send.at[step], recv_sem=v_recv.at[step],
            device_id=vec_steps[step], device_id_type=MESH,
        )

    def vec_task(k):
        vec_copy(k).wait_recv()
        total = (vec_in[c] if k == 0 else vec_own[k]) + vec_got[k]
        if k < 4:
            vec_own[k + 1] = total
            vec_copy(k + 1).start()
        else:
            vec_out[...] = total

    units = unit_table(dims)
    kinds = KINDS
    xy_at, z_at = {}, {}
    for unit, kind in enumerate(kinds):
        (z_at if kind[0] == "Z" else xy_at)[unit] = len(z_at) if kind[0] == "Z" else len(xy_at)

    def copy(unit, name, source, dest, device):
        return functools.partial(
            pltpu.make_async_remote_copy,
            src_ref=source, dst_ref=dest, send_sem=send.at[unit], recv_sem=recv.at[unit, SLOT[name]],
            device_id=device, device_id_type=MESH,
        )

    def rows_of(unit, start, count):
        if not isinstance(start, int):
            start = pl.multiple_of(start, 16)
        return res.at[unit, pl.ds(start, count), :]

    def product(unit, start, count, dest, dest_start, got=None, got_start=0, near_start=None):
        m, row, col = units[unit]
        step = 128 if count % 128 == 0 else min(count, 64)

        def block(index, _):
            part, strip = index // (UNIT_COLS // 256), index % (UNIT_COLS // 256)
            cols = pl.ds(pl.multiple_of(strip * 256, 256), 256)
            value = jnp.dot(
                at[pl.ds(pl.multiple_of(at_base[m] + row + start + part * step, 16), step), :],
                g[:, pl.ds(pl.multiple_of(g_base[m] + col + strip * 256, 256), 256)],
                preferred_element_type=F32,
            )
            if near_start is not None:
                for peer in range(3):
                    rows = peer * (UNIT_ROWS // 4) + near_start + part * step
                    value = value + jnp.dot(
                        near_left[unit, pl.ds(pl.multiple_of(rows, 16), step), :],
                        near_right[peer, :, pl.ds(pl.multiple_of(col + strip * 256, 256), 256)],
                        preferred_element_type=F32,
                    )
            if got is not None:
                value = value + got[pl.ds(pl.multiple_of(got_start + part * step, 16), step), cols].astype(F32)
            dest[pl.ds(pl.multiple_of(dest_start + part * step, 16), step), cols] = value.astype(BF16)
            return 0

        lax.fori_loop(0, (count // step) * (UNIT_COLS // 256), block, 0)

    def accumulate(unit, start, count, got, got_start, dest, dest_start):
        def block(strip, _):
            cols = pl.ds(pl.multiple_of(strip * 256, 256), 256)
            value = res[unit, pl.ds(pl.multiple_of(start, 16), count), cols].astype(F32)
            value = value + got[pl.ds(pl.multiple_of(got_start, 16), count), cols].astype(F32)
            dest[pl.ds(pl.multiple_of(dest_start, 16), count), cols] = value.astype(BF16)
            return 0

        lax.fori_loop(0, UNIT_COLS // 256, block, 0)

    def gather_line(unit, base, size, level):
        up, down = "u%d" % level, "w%d" % level
        low, high = z - (level - 1), z + (level - 1)

        @pl.when((low >= 0) & (z < 3))
        def _():
            part = rows_of(unit, base + low * size, size)
            copy(unit, up, part, part, to["U"])().start()

        @pl.when((high <= 3) & (z > 0))
        def _():
            part = rows_of(unit, base + high * size, size)
            copy(unit, down, part, part, to["D"])().start()

    def gather_arrived(unit, base, size, level):
        def wait(chunks):
            part = give.at[pl.ds(0, chunks * size), :]
            copy(unit, "u%d" % level, part, part, to["U"])().wait_recv()

        if level == 1:
            pl.when(line_mid)(lambda: wait(2))
        if level == 2:
            wait(1)
        else:
            pl.when(line_end)(lambda: wait(1))

    def finish(unit, ends, mids):
        def wait(rows):
            part = give.at[pl.ds(0, rows), :]
            copy(unit, "d1", part, part, to["X"])().wait_send()

        pl.when(line_end)(lambda: wait(ends))
        pl.when(line_mid)(lambda: wait(mids))

    def task_xy(unit, step):
        half, quarter, size = UNIT_ROWS // 2, UNIT_ROWS // 4, UNIT_ROWS // 16
        first, second = ("X", "Y") if kinds[unit][-1] == "X" else ("Y", "X")
        p, q = (x, y) if first == "X" else (y, x)
        by_tokens = kinds[unit][0] == "Q"
        line, block, out, other = line_xy.at[xy_at[unit]], res.at[unit], give.at[pl.ds(unit * GIVE_ROWS, GIVE_ROWS), :], pair.at[unit]
        keep, away_half = p * half, (1 - p) * half
        base = keep + q * quarter
        away = keep + (1 - q) * quarter
        at_z = half + quarter
        d1 = copy(unit, "d1", out.at[pl.ds(0, half), :], rows_of(unit, away_half, half), to[first])

        def left_for(peer):
            m, row, _ = units[unit]
            px, py = ((1 - x, y), (x, 1 - y), (1 - x, 1 - y))[peer]
            at_p, at_q = (px, py) if first == "X" else (py, px)
            rows = pl.ds(pl.multiple_of(at_base[m] + row + at_p * half + at_q * quarter, quarter), quarter)
            dest = near_left.at[unit, pl.ds(peer * quarter, quarter), :]
            return copy(unit, "d1", at.at[rows, :], dest, to[("X", "Y", "XY")[peer]])

        d2 = copy(unit, "d2", out.at[pl.ds(half, quarter), :], other.at[pl.ds(0, quarter), :], to[second])
        z1 = copy(unit, "z1", out.at[pl.ds(at_z, 3 * size), :], line.at[pl.ds(0, 3 * size), :], inward)
        z2 = copy(unit, "z2", out.at[pl.ds(at_z, 2 * size), :], line.at[pl.ds(3 * size, 2 * size), :], across)
        z3 = copy(unit, "z3", out.at[pl.ds(at_z + 2 * size, size), :], line.at[pl.ds(0, size), :], outward)
        own_quarter = rows_of(unit, base, quarter)
        g2 = copy(unit, "g2", own_quarter, own_quarter, to[second])
        own_half = rows_of(unit, keep, half)
        g1 = copy(unit, "g1", own_half, own_half, to[first])
        own = base + z * size
        if step == 0 and by_tokens:
            for peer in range(3):
                left_for(peer)().start()
        elif step == 1 and by_tokens:
            pass
        elif step == 2 and by_tokens:
            arrived = near_left.at[unit]
            copy(unit, "d1", arrived, arrived, to["X"])().wait_recv()

            product(unit, base, quarter, block, base, near_start=0)

            @pl.when(line_end)
            def _():
                from_row = pl.multiple_of(base + (1 - upper) * size, 16)
                for n in range(3):
                    out[at_z + n * size : at_z + (n + 1) * size, :] = block[pl.ds(from_row + n * size, size), :]
                z1().start()

        elif step == 0:
            product(unit, away_half, half, out, 0)
            d1().start()
        elif step == 1:
            d1().wait_recv()
            product(unit, away, quarter, out, half, block, away)
            d2().start()
            product(unit, base, quarter, block, base, block, base)
        elif step == 2:
            d2().wait_recv()

            @pl.when(line_end)
            def _():
                skip = (1 - upper) * size
                accumulate(unit, base + skip, 3 * size, other, skip, out, at_z)
                z1().start()
                accumulate(unit, own, size, other, z * size, block, own)

            @pl.when(line_mid)
            def _():
                accumulate(unit, base, quarter, other, 0, block, base)

        elif step == 3:

            @pl.when(line_mid)
            def _():
                z1().wait_recv()
                accumulate(unit, base + (1 - upper) * 2 * size, 2 * size, line, (1 - upper) * size, out, at_z)
                z2().start()
                accumulate(unit, own, size, line, upper * 2 * size, block, own)

        elif step == 4:

            @pl.when(line_mid)
            def _():
                z2().wait_recv()
                accumulate(unit, base + upper * 3 * size, size, line, (3 + upper) * size, out, at_z + 2 * size)
                z3().start()
                accumulate(unit, own, size, line, (4 - upper) * size, block, own)
                gather_line(unit, base, size, 1)

        elif step == 5:

            @pl.when(line_end)
            def _():
                z3().wait_recv()
                accumulate(unit, own, size, line, 0, block, own)
                gather_line(unit, base, size, 1)

        elif step in (6, 7):
            gather_arrived(unit, base, size, step - 5)
            gather_line(unit, base, size, step - 4)
        elif step == 8:
            gather_arrived(unit, base, size, 3)
            g2().start()
        elif step == 9:
            g2().wait_recv()
            g1().start()
        else:
            g1().wait_recv()
            sent = half + quarter + (3 * size if by_tokens else half + quarter)
            finish(unit, sent + 4 * size, sent + 8 * size)

    def task_z(unit, step):
        size, half, quarter = UNIT_ROWS // 4, UNIT_ROWS // 8, UNIT_ROWS // 16
        first, second = ("X", "Y") if kinds[unit] == "ZX" else ("Y", "X")
        p, q = (x, y) if kinds[unit] == "ZX" else (y, x)
        line, block, out, other = line_z.at[z_at[unit]], res.at[unit], give.at[pl.ds(unit * GIVE_ROWS, GIVE_ROWS), :], pair.at[unit]
        own = z * size
        keep, away_half = own + p * half, own + (1 - p) * half
        base, away = keep + q * quarter, keep + (1 - q) * quarter
        at_d = 3 * size
        z1 = copy(unit, "z1", out.at[pl.ds(0, 3 * size), :], line.at[pl.ds(0, 3 * size), :], inward)
        z2 = copy(unit, "z2", out.at[pl.ds(0, 2 * size), :], line.at[pl.ds(3 * size, 2 * size), :], across)
        z3 = copy(unit, "z3", out.at[pl.ds(2 * size, size), :], line.at[pl.ds(0, size), :], outward)
        d1 = copy(unit, "d1", out.at[pl.ds(at_d, half), :], other.at[pl.ds(0, half), :], to[first])
        d2 = copy(unit, "d2", out.at[pl.ds(at_d + half, quarter), :], other.at[pl.ds(half, quarter), :], to[second])
        own_quarter = rows_of(unit, base, quarter)
        g2 = copy(unit, "g2", own_quarter, own_quarter, to[second])
        own_half = rows_of(unit, keep, half)
        g1 = copy(unit, "g1", own_half, own_half, to[first])
        if step == 0:

            @pl.when(line_end)
            def _():
                product(unit, (1 - upper) * size, 3 * size, out, 0)
                z1().start()

        elif step == 1:

            @pl.when(line_mid)
            def _():
                z1().wait_recv()
                product(unit, (1 - upper) * 2 * size, 2 * size, out, 0, line, (1 - upper) * size)
                z2().start()
                product(unit, own, size, block, own, line, upper * 2 * size)

        elif step == 2:

            @pl.when(line_mid)
            def _():
                z2().wait_recv()
                product(unit, upper * 3 * size, size, out, 2 * size, line, (3 + upper) * size)
                z3().start()
                got = (4 - upper) * size
                accumulate(unit, away_half, half, line, got + (1 - p) * half, out, at_d)
                d1().start()
                accumulate(unit, keep, half, line, got + p * half, block, keep)

        elif step == 3:

            @pl.when(line_end)
            def _():
                z3().wait_recv()
                product(unit, away_half, half, out, at_d, line, (1 - p) * half)
                d1().start()
                product(unit, keep, half, block, keep, line, p * half)

        elif step == 4:
            d1().wait_recv()
            accumulate(unit, away, quarter, other, (1 - q) * quarter, out, at_d + half)
            d2().start()
            accumulate(unit, base, quarter, other, q * quarter, block, base)
        elif step == 5:
            d2().wait_recv()
            accumulate(unit, base, quarter, other, half, block, base)
            g2().start()
        elif step == 6:
            g2().wait_recv()
            g1().start()
        elif step == 7:
            g1().wait_recv()
            gather_line(unit, 0, size, 1)
        elif step in (8, 9):
            gather_arrived(unit, 0, size, step - 7)
            gather_line(unit, 0, size, step - 6)
        else:
            gather_arrived(unit, 0, size, 3)
            finish(unit, 2 * half + 2 * quarter + 4 * size, 2 * half + 2 * quarter + 8 * size)


    for kind, a, b in program_order(units, ends):
        if kind == "task":
            if a == 0:
                fill(len(stream))
            tasks[a][1]()
        elif kind == "wait":
            wait_pair(a)
            if a == 3:
                for k in range(3):
                    cotangent_copy(k, True).wait()
            if a == 1:
                for k in range(parts):
                    given(k)
        elif kind == "vec":
            vec_task(a)
        elif kinds[a][0] == "Z":
            task_z(a, b)
        else:
            task_xy(a, b)
    for step in range(5):
        vec_copy(step).wait_send()


def whole_layer(layer_input, cotangent, weights, params):
    dims = tuple(w.shape for w in weights)
    at_rows = sum(rows for rows, _ in dims)
    g_cols = sum(cols for _, cols in dims)
    at_base = [sum(rows for rows, _ in dims[:m]) for m in range(4)]
    g_base = [sum(cols for _, cols in dims[:m]) for m in range(4)]
    length, width = layer_input.shape
    hidden = dims[2][1]
    blocks = hidden // width
    units = unit_table(dims)
    kinds = KINDS
    n, n_z = len(units), sum(kind[0] == "Z" for kind in kinds)
    tiles = n // 2
    hbm = pl.BlockSpec(memory_space=pl.ANY)
    vmem = pl.BlockSpec(memory_space=pltpu.VMEM)
    dma = pltpu.SemaphoreType.DMA
    small = (24, width // 2)
    got = pl.pallas_call(
        functools.partial(layer_kernel, dims, at_base, g_base),
        out_shape=[
            pltpu.VMEM((length, width), BF16),
            pltpu.VMEM((length, width), F32),
            pltpu.VMEM((n, UNIT_ROWS, UNIT_COLS), BF16),
            pltpu.VMEM(small, F32),
            jax.ShapeDtypeStruct((2, tiles, 512, UNIT_COLS), BF16),
        ],
        in_specs=[vmem, hbm] + [hbm] * 4 + [vmem] * 13,
        out_specs=[vmem] * 4 + [hbm],
        scratch_shapes=[
            pltpu.VMEM((at_rows, 2 * length), BF16),
            pltpu.VMEM((2 * length, g_cols), BF16),
            pltpu.VMEM((n * GIVE_ROWS, UNIT_COLS), BF16),
            pltpu.VMEM((n, UNIT_ROWS // 4, UNIT_COLS), BF16),
            pltpu.VMEM((n - n_z, 5 * UNIT_ROWS // 16, UNIT_COLS), BF16),
            pltpu.VMEM((n_z, 5 * UNIT_ROWS // 4, UNIT_COLS), BF16),
            pltpu.VMEM((4, 512, UNIT_COLS), BF16),
            pltpu.VMEM((3 * blocks * length, width), F32),
            pltpu.VMEM((2 * at_rows, length), BF16),
            pltpu.VMEM((length, width), BF16),
            pltpu.VMEM((blocks * length, width), BF16),
            pltpu.VMEM((length, 3 * width), BF16),
            pltpu.VMEM((width // 128, length, 2 * length), F32),
            pltpu.VMEM((length, width), F32),
            pltpu.VMEM((length, width), F32),
            pltpu.VMEM((length, width), F32),
            pltpu.VMEM((length, width), F32),
            pltpu.VMEM((2 * 256, UNIT_COLS), F32),
            pltpu.VMEM((dims[3][0] // UNIT_ROWS, 3 * UNIT_ROWS // 4, 2 * length), BF16),
            pltpu.VMEM((3, 2 * length, width), BF16),
            pltpu.VMEM((16, width), F32),
            pltpu.VMEM((8, hidden), F32),
            pltpu.VMEM((length, 128), F32),
            pltpu.VMEM((24, hidden), F32),
            pltpu.VMEM((2,) + small, F32),
            pltpu.VMEM((5,) + small, F32),
            pltpu.VMEM((5,) + small, F32),
            dma((n,)),
            dma((n, 9)),
            dma((5,)),
            dma((5,)),
            dma((4, 2)),
            dma((4, 2)),
            dma((4,)),
            dma((10,)),
            dma((16,)),
            dma((16,)),
            dma((2 * tiles,)),
            dma((4,)),
            dma((2, 2)),
            dma((1,)),
            dma((3, 2)),
            dma((3, 2)),
        ],
        compiler_params=pltpu.CompilerParams(
            collective_id=0, has_side_effects=True, vmem_limit_bytes=50 * MIB + 786432
        ),
        name="whole_layer",
    )(layer_input, cotangent, *weights, *params)
    return got[:4]


def finish_kernel(dims, *refs):
    y_in, dx_in, res, vec = refs[0:4]
    y_out, dx_out, outs, smalls = refs[4], refs[5], refs[6:10], refs[10:23]
    wide, lines, o_sem, s_sem = refs[23], refs[24:37], refs[37], refs[38]
    slots = wide.shape[0]
    copies = [pltpu.make_async_copy(y_in, y_out, s_sem.at[13]), pltpu.make_async_copy(dx_in, dx_out, s_sem.at[14])]
    rows_of = [range(0, 2)] + [range(k, k + 1) for k in range(2, 11)] + [range(11 + 4 * k, 15 + 4 * k) for k in range(3)]
    for k, rows in enumerate(rows_of):
        if k == 2:
            head_of = lax.broadcasted_iota(jnp.int32, (1, vec.shape[1]), 1) // 64
            lane = lax.broadcasted_iota(jnp.int32, lines[k].shape, 1)
            total = jnp.zeros(lines[k].shape, F32)
            for h in range(vec.shape[1] // 64):
                one = jnp.sum(jnp.where(head_of == h, vec[3:4, :], 0.0), axis=-1, keepdims=True)
                total = jnp.where(lane == h, one, total)
            lines[k][...] = total
        elif len(rows) == 4:
            for j, row in enumerate(rows):
                lines[k][:, j * vec.shape[1] : (j + 1) * vec.shape[1]] = vec[row : row + 1, :]
        else:
            lines[k][...] = vec[rows.start : rows.stop, :]
        copies.append(pltpu.make_async_copy(lines[k], smalls[k], s_sem.at[k]))
    for piece in copies:
        piece.start()
    units = unit_table(dims)

    def put(unit):
        m, row, col = units[unit]
        return pltpu.make_async_copy(
            wide.at[unit % slots], outs[m].at[pl.ds(row, UNIT_ROWS), pl.ds(col, UNIT_COLS)], o_sem.at[unit % slots]
        )

    for unit in range(len(units)):
        if unit >= slots:
            put(unit - slots).wait()

        def widen(b, _, unit=unit):
            rows = pl.ds(pl.multiple_of(b * 32, 32), 32)
            wide[unit % slots, rows, :] = res[unit, rows, :].astype(F32)
            return 0

        lax.fori_loop(0, UNIT_ROWS // 32, widen, 0)
        put(unit).start()
    for unit in range(len(units) - slots, len(units)):
        put(unit).wait()
    for piece in copies:
        piece.wait()


def write_results(got, dims):
    y, dx, _, vec = got
    half = vec.shape[1]
    small = [(2, half), (1, half), (1, half // 64)] + [(1, half)] * 7 + [(1, 4 * half)] * 3
    hbm = pl.BlockSpec(memory_space=pl.ANY)
    vmem = pl.BlockSpec(memory_space=pltpu.VMEM)
    dma = pltpu.SemaphoreType.DMA
    return pl.pallas_call(
        functools.partial(finish_kernel, dims),
        out_shape=[jax.ShapeDtypeStruct(y.shape, BF16), jax.ShapeDtypeStruct(dx.shape, F32)]
        + [jax.ShapeDtypeStruct(d, F32) for d in dims]
        + [jax.ShapeDtypeStruct(s, F32) for s in small],
        in_specs=[vmem] * 4,
        out_specs=[hbm] * 19,
        scratch_shapes=[pltpu.VMEM((6, UNIT_ROWS, UNIT_COLS), F32)]
        + [pltpu.VMEM(s, F32) for s in small]
        + [dma((6,)), dma((15,))],
        compiler_params=pltpu.CompilerParams(vmem_limit_bytes=30 * MIB),
        name="write_results",
    )(*got)


def on_pair_of_cores(
    layer_input, cotangent, w_qkv, qv_bias, w_out, out_bias, head_scale, ln1_gain, ln1_bias, ln2_gain, ln2_bias,
    ln3_gain, ln3_bias, w_fc1, fc1_bias, ln4_gain, ln4_bias, w_fc2, fc2_bias,
):
    params = (
        qv_bias, out_bias, head_scale, ln1_gain, ln1_bias, ln2_gain, ln2_bias, ln3_gain, ln3_bias,
        fc1_bias, ln4_gain, ln4_bias, fc2_bias,
    )
    params = [p.reshape(-1, p.shape[-1]) for p in params]
    weights = (w_qkv, w_out, w_fc1, w_fc2)
    got = whole_layer(layer_input, cotangent, weights, params)
    output, grad_input, qkv, out, up, down, *smalls = write_results(got, tuple(w.shape for w in weights))
    rows = [s.reshape(-1) for s in smalls]
    return (
        output, grad_input, qkv, smalls[0], out, rows[1], rows[2], rows[3], rows[4], rows[5], rows[6], rows[7], rows[8], up,
        rows[10], rows[11], rows[12], down, rows[9],
    )


def fits_pair(mesh):
    return mesh.shape["shard"] == 2 and mesh.shape["rep"] == 16


def solution(mesh):
    return jax.shard_map(
        on_pair_of_cores if fits_pair(mesh) else on_any_mesh,
        mesh=mesh,
        in_specs=(
            P(("rep", "shard"), None),
            P(("rep", "shard"), None),
            P("shard", None),
            P(None, "shard"),
            P("shard", None),
            P("shard"),
            P("shard"),
            P("shard"),
            P("shard"),
            P("shard"),
            P("shard"),
            P("shard"),
            P("shard"),
            P("shard", None),
            P("shard"),
            P("shard"),
            P("shard"),
            P("shard", None),
            P("shard"),
        ),
        out_specs=(
            P(("rep", "shard"), None),
            P(("rep", "shard"), None),
            P("shard", None),
            P(None, "shard"),
            P("shard", None),
            P("shard"),
            P("shard"),
            P("shard"),
            P("shard"),
            P("shard"),
            P("shard"),
            P("shard"),
            P("shard"),
            P("shard", None),
            P("shard"),
            P("shard"),
            P("shard"),
            P("shard", None),
            P("shard"),
        ),
        check_vma=False,
    )
```

```python
import functools

import jax
import jax.numpy as jnp
from jax import lax
from jax.experimental import pallas as pl
from jax.experimental.pallas import tpu as pltpu
from jax.sharding import PartitionSpec as P

D = 1024
HEADS = 16
HEAD_DIM = 64


EPS = 1e-05
NEG = -1e30


def norm_rows(v, gain, bias):
    centre = jnp.mean(v, axis=-1, keepdims=True)
    centred = v - centre
    spread = jnp.mean(centred * centred, axis=-1, keepdims=True)
    return centred * lax.rsqrt(spread + EPS) * gain + bias


def ffn_middle(hidden, gain, bias):
    return norm_rows(jax.nn.gelu(hidden, approximate=False), gain, bias)


def causal_mask(index, qblock, length):
    rows = index * qblock + lax.iota(jnp.int32, qblock)
    cols = lax.iota(jnp.int32, length)
    return (cols[None, :] <= rows[:, None])[None]


def block_scores(queries, keys_all, index, qblock, scale):
    length = keys_all.shape[0]
    scores = (
        jnp.einsum("qhd,khd->hqk", queries, keys_all, preferred_element_type=jnp.float32) * scale
    )
    return (queries, jnp.where(causal_mask(index, qblock, length), scores, NEG))


def attend_forward(queries, keys_all, values_all, scale):
    length, heads, width = queries.shape
    qblock = min(512, length)
    blocks = length // qblock

    def one_block(index):
        rows_q, scores = block_scores(queries, keys_all, index, qblock, scale)
        total = jax.nn.logsumexp(scores, axis=-1, keepdims=True)
        probs = jnp.exp(scores - total).astype(jnp.bfloat16)
        outcome = jnp.einsum("hqk,khd->qhd", probs, values_all, preferred_element_type=jnp.float32)
        return (outcome, total)

    outcome, totals = lax.map(one_block, jnp.arange(blocks, dtype=jnp.int32))
    return (outcome.reshape(length, heads, width), totals)


def attend_backward(queries, keys_all, values_all, totals, grad_out, scale):
    length, heads, width = queries.shape
    qblock = min(512, length)
    blocks = length // qblock

    def one_block(carry, index):
        grad_keys, grad_values = carry
        rows_q, scores = block_scores(queries, keys_all, index, qblock, scale)
        probs = jnp.exp(scores - totals[index])
        probs_low = probs.astype(jnp.bfloat16)
        grad_values = grad_values + jnp.einsum(
            "hqk,qhd->khd", probs_low, grad_out, preferred_element_type=jnp.float32
        )
        grad_probs = jnp.einsum(
            "qhd,khd->hqk", grad_out, values_all, preferred_element_type=jnp.float32
        )
        row_dot = jnp.sum(probs * grad_probs, axis=-1, keepdims=True)
        grad_scores = (probs * (grad_probs - row_dot)).astype(jnp.bfloat16)
        grad_rows = (
            jnp.einsum("hqk,khd->qhd", grad_scores, keys_all, preferred_element_type=jnp.float32)
            * scale
        )
        grad_keys = (
            grad_keys
            + jnp.einsum("hqk,qhd->khd", grad_scores, rows_q, preferred_element_type=jnp.float32)
            * scale
        )
        return ((grad_keys, grad_values), grad_rows)

    empty = jnp.zeros((length, heads, width), jnp.float32)
    (grad_keys, grad_values), grad_queries = lax.scan(
        one_block, (empty, empty), jnp.arange(blocks, dtype=jnp.int32)
    )
    return (grad_queries.reshape(length, heads, width), grad_keys, grad_values)


def on_any_mesh(
    layer_input,
    cotangent,
    w_qkv,
    qv_bias,
    w_out,
    out_bias,
    head_scale,
    ln1_gain,
    ln1_bias,
    ln2_gain,
    ln2_bias,
    ln3_gain,
    ln3_bias,
    w_fc1,
    fc1_bias,
    ln4_gain,
    ln4_bias,
    w_fc2,
    fc2_bias,
):
    low_qkv = w_qkv.astype(jnp.bfloat16)
    low_out = w_out.astype(jnp.bfloat16)
    low_heads = head_scale.astype(jnp.bfloat16)
    low_up = w_fc1.astype(jnp.bfloat16)
    low_down = w_fc2.astype(jnp.bfloat16)
    whole = (
        lax.all_gather(low_qkv, "shard", axis=0, tiled=True),
        lax.all_gather(qv_bias.astype(jnp.bfloat16), "shard", axis=1, tiled=True),
        lax.all_gather(low_out, "shard", axis=0, tiled=True),
        lax.all_gather(out_bias.astype(jnp.bfloat16), "shard", axis=0, tiled=True),
        lax.all_gather(low_heads, "shard", axis=0, tiled=True),
        lax.all_gather(ln1_gain.astype(jnp.bfloat16), "shard", axis=0, tiled=True),
        lax.all_gather(ln1_bias.astype(jnp.bfloat16), "shard", axis=0, tiled=True),
        lax.all_gather(ln2_gain.astype(jnp.bfloat16), "shard", axis=0, tiled=True),
        lax.all_gather(ln2_bias.astype(jnp.bfloat16), "shard", axis=0, tiled=True),
        lax.all_gather(ln3_gain.astype(jnp.bfloat16), "shard", axis=0, tiled=True),
        lax.all_gather(ln3_bias.astype(jnp.bfloat16), "shard", axis=0, tiled=True),
        lax.all_gather(low_up, "shard", axis=0, tiled=True),
        lax.all_gather(fc1_bias.astype(jnp.bfloat16), "shard", axis=0, tiled=True),
        lax.all_gather(ln4_gain.astype(jnp.bfloat16), "shard", axis=0, tiled=True),
        lax.all_gather(ln4_bias.astype(jnp.bfloat16), "shard", axis=0, tiled=True),
        lax.all_gather(low_down, "shard", axis=0, tiled=True),
        lax.all_gather(fc2_bias.astype(jnp.bfloat16), "shard", axis=0, tiled=True),
    )
    weight_qkv, weight_out, weight_up, weight_down = (whole[0], whole[2], whole[11], whole[15])
    (
        bias_qv,
        bias_out,
        head_gain,
        gain_one,
        shift_one,
        gain_two,
        shift_two,
        gain_three,
        shift_three,
        bias_up,
        gain_four,
        shift_four,
        bias_down,
    ) = tuple(
        (whole[index].astype(jnp.float32) for index in (1, 3, 4, 5, 6, 7, 8, 9, 10, 12, 13, 14, 16))
    )
    length = layer_input.shape[0]
    scale = HEAD_DIM ** (-0.5)
    inputs = layer_input.astype(jnp.float32)
    normed_one, pull_one = jax.vjp(norm_rows, inputs, gain_one, shift_one)
    act_one = normed_one.astype(jnp.bfloat16)
    bias_full = jnp.concatenate([bias_qv[0], jnp.zeros((D,), jnp.float32), bias_qv[1]])
    qkv = (jnp.dot(act_one, weight_qkv, preferred_element_type=jnp.float32) + bias_full).astype(
        jnp.bfloat16
    )
    triple = qkv.reshape(length, 3, HEADS, HEAD_DIM)
    queries = triple[:, 0]
    keys_all = triple[:, 1]
    values_all = triple[:, 2]
    attended, totals = attend_forward(queries, keys_all, values_all, scale)
    mixed = (attended * head_gain[:, None]).reshape(length, D).astype(jnp.bfloat16)
    branch = jnp.dot(mixed, weight_out, preferred_element_type=jnp.float32) + bias_out
    normed_two, pull_two = jax.vjp(norm_rows, branch, gain_two, shift_two)
    middle = inputs + normed_two
    normed_three, pull_three = jax.vjp(norm_rows, middle, gain_three, shift_three)
    act_three = normed_three.astype(jnp.bfloat16)
    hidden = jnp.dot(act_three, weight_up, preferred_element_type=jnp.float32) + bias_up
    normed_four, pull_four = jax.vjp(ffn_middle, hidden, gain_four, shift_four)
    act_four = normed_four.astype(jnp.bfloat16)
    result = middle + (
        jnp.dot(act_four, weight_down, preferred_element_type=jnp.float32) + bias_down
    )
    output = result.astype(jnp.bfloat16)
    again = (
        lax.all_gather(low_qkv, "shard", axis=0, tiled=True),
        lax.all_gather(low_out, "shard", axis=0, tiled=True),
        lax.all_gather(low_heads, "shard", axis=0, tiled=True),
        lax.all_gather(low_up, "shard", axis=0, tiled=True),
        lax.all_gather(low_down, "shard", axis=0, tiled=True),
    )
    back_qkv, back_out, back_up, back_down = (again[0], again[1], again[3], again[4])
    back_heads = again[2].astype(jnp.float32)
    cot_full = cotangent.astype(jnp.float32)
    grad_down_bias = jnp.sum(cot_full, axis=0)
    grad_down = jnp.einsum("tf,td->fd", act_four, cotangent, preferred_element_type=jnp.float32)
    grad_four = jnp.einsum("td,fd->tf", cotangent, back_down, preferred_element_type=jnp.float32)
    grad_hidden, grad_gain_four, grad_shift_four = pull_four(grad_four)
    hidden_low = grad_hidden.astype(jnp.bfloat16)
    grad_up_bias = jnp.sum(hidden_low, axis=0, dtype=jnp.float32)
    grad_up = jnp.einsum("td,tf->df", act_three, hidden_low, preferred_element_type=jnp.float32)
    grad_three = jnp.einsum("tf,df->td", hidden_low, back_up, preferred_element_type=jnp.float32)
    grad_mid_part, grad_gain_three, grad_shift_three = pull_three(grad_three)
    grad_middle = cot_full + grad_mid_part
    grad_branch, grad_gain_two, grad_shift_two = pull_two(grad_middle)
    branch_low = grad_branch.astype(jnp.bfloat16)
    grad_out_b = jnp.sum(branch_low, axis=0, dtype=jnp.float32)
    grad_out_w = jnp.einsum("td,te->de", mixed, branch_low, preferred_element_type=jnp.float32)
    grad_mixed = jnp.einsum("te,de->td", branch_low, back_out, preferred_element_type=jnp.float32)
    grad_mixed = grad_mixed.reshape(length, HEADS, HEAD_DIM)
    grad_heads = jnp.sum(grad_mixed * attended, axis=(0, 2))
    grad_attended = (grad_mixed * back_heads[:, None]).astype(jnp.bfloat16)
    grad_queries, grad_keys, grad_values = attend_backward(
        queries, keys_all, values_all, totals, grad_attended, scale
    )
    grad_qkv = (
        jnp.stack([grad_queries, grad_keys, grad_values], axis=1)
        .reshape(length, 3 * D)
        .astype(jnp.bfloat16)
    )
    grad_qv = jnp.stack(
        [
            jnp.sum(grad_qkv[:, :D], axis=0, dtype=jnp.float32),
            jnp.sum(grad_qkv[:, 2 * D :], axis=0, dtype=jnp.float32),
        ]
    )
    grad_qkv_w = jnp.einsum("td,te->de", act_one, grad_qkv, preferred_element_type=jnp.float32)
    grad_one = jnp.einsum("te,de->td", grad_qkv, back_qkv, preferred_element_type=jnp.float32)
    grad_in_part, grad_gain_one, grad_shift_one = pull_one(grad_one)
    grad_input = grad_middle + grad_in_part
    shares = (
        lax.psum_scatter(grad_qkv_w, "shard", scatter_dimension=0, tiled=True),
        lax.psum_scatter(grad_qv, "shard", scatter_dimension=1, tiled=True),
        lax.psum_scatter(grad_out_w, "shard", scatter_dimension=0, tiled=True),
        lax.psum_scatter(grad_out_b, "shard", scatter_dimension=0, tiled=True),
        lax.psum_scatter(grad_heads, "shard", scatter_dimension=0, tiled=True),
        lax.psum_scatter(grad_gain_one, "shard", scatter_dimension=0, tiled=True),
        lax.psum_scatter(grad_shift_one, "shard", scatter_dimension=0, tiled=True),
        lax.psum_scatter(grad_gain_two, "shard", scatter_dimension=0, tiled=True),
        lax.psum_scatter(grad_shift_two, "shard", scatter_dimension=0, tiled=True),
        lax.psum_scatter(grad_gain_three, "shard", scatter_dimension=0, tiled=True),
        lax.psum_scatter(grad_shift_three, "shard", scatter_dimension=0, tiled=True),
        lax.psum_scatter(grad_up, "shard", scatter_dimension=0, tiled=True),
        lax.psum_scatter(grad_up_bias, "shard", scatter_dimension=0, tiled=True),
        lax.psum_scatter(grad_gain_four, "shard", scatter_dimension=0, tiled=True),
        lax.psum_scatter(grad_shift_four, "shard", scatter_dimension=0, tiled=True),
        lax.psum_scatter(grad_down, "shard", scatter_dimension=0, tiled=True),
        lax.psum_scatter(grad_down_bias, "shard", scatter_dimension=0, tiled=True),
    )
    summed = lax.psum(
        (
            shares[0],
            shares[1],
            shares[2],
            shares[3],
            shares[4],
            shares[5],
            shares[6],
            shares[7],
            shares[8],
            shares[9],
            shares[10],
            shares[11],
            shares[12],
            shares[13],
            shares[14],
            shares[15],
            shares[16],
        ),
        "rep",
    )
    return (output, grad_input) + tuple(summed)


MESH = pl.DeviceIdType.MESH
BF16 = jnp.bfloat16
F32 = jnp.float32
UNIT_ROWS = 256
UNIT_COLS = 1024
MIB = 1 << 20
SLOT = {
    "d1": 0, "d2": 1, "z1": 2, "z3": 2, "z2": 3, "u1": 4, "w1": 4, "u2": 5, "w2": 5, "u3": 6, "w3": 6, "g1": 7, "g2": 8,
}


def unit_table(dims):
    table = []
    for matrix in (3, 2, 1, 0):
        rows, cols = dims[matrix]
        for col in range(0, cols, UNIT_COLS):
            for row in range(0, rows, UNIT_ROWS):
                table.append((matrix, row, col))
    return table


KINDS = (
    "QX", "QX", "QX", "QY", "QY", "QY", "QY", "QY", "Y", "X", "X", "Y", "ZY", "ZY", "X", "Y", "X", "X", "ZY",
    "Y", "Y", "X", "ZY", "X",
)
TASK, VECTORS = 24, 25
ORDER = (
    1, 5, 24, 2, 3, 5, 0, 24, 4, 0, 4, 24, 2, 24, 24, 1, 24, 24, 24, 24, 24, 24, 24, 6, 5, 7, 4, 10, 6, 8, 11,
    7, 13, 2, 24, 24, 14, 15, 24, 5, 4, 24, 24, 24, 5, 0, 9, 10, 4, 16, 17, 5, 13, 7, 2, 24, 12, 24, 14, 24, 24,
    4, 9, 7, 5, 24, 16, 6, 8, 7, 0, 3, 10, 19, 12, 20, 2, 23, 21, 5, 1, 9, 0, 5, 10, 7, 13, 0, 4, 12, 6, 1, 2,
    2, 9, 8, 3, 23, 0, 13, 16, 17, 4, 24, 11, 16, 22, 4, 6, 12, 7, 8, 5, 13, 24, 0, 3, 21, 9, 15, 2, 6, 16, 20,
    24, 8, 11, 13, 17, 7, 2, 16, 3, 12, 7, 22, 10, 4, 6, 15, 19, 16, 3, 11, 24, 12, 8, 8, 0, 3, 14, 15, 1, 7,
    10, 2, 20, 22, 23, 11, 17, 10, 15, 9, 1, 19, 21, 14, 25, 18, 12, 0, 20, 3, 10, 1, 13, 16, 6, 22, 21, 3, 8,
    19, 20, 1, 10, 22, 9, 16, 23, 21, 6, 20, 19, 8, 13, 7, 1, 6, 22, 23, 11, 20, 16, 18, 17, 14, 10, 23, 9, 25,
    1, 11, 23, 17, 15, 12, 4, 19, 3, 18, 19, 14, 21, 11, 22, 9, 25, 5, 16, 18, 20, 23, 8, 11, 20, 19, 15, 17,
    17, 18, 14, 17, 19, 23, 21, 12, 14, 21, 6, 18, 9, 12, 15, 17, 14, 18, 3, 0, 25, 10, 19, 21, 15, 13, 20, 23,
    22, 9, 2, 18, 13, 22, 14, 15, 22, 13, 17, 1, 19, 21, 18, 12, 20, 11, 18, 25, 8, 18, 23, 22, 14, 15, 21, 11,
)


GIVE_ROWS = 240


def program_order(units, ends):
    order, task, vector, waited, step = [], 0, 0, {3}, [0] * len(units)
    order.append(("wait", 3, 0))
    for entry in ORDER:
        if entry == TASK:
            order.append(("task", task, 0))
            task += 1
            continue
        if entry == VECTORS:
            order.append(("vec", vector, 0))
            vector += 1
            continue
        m = units[entry][0]
        if m not in waited:
            assert task >= ends[m]
            order.append(("wait", m, 0))
            waited.add(m)
        order.append(("sum", entry, step[entry]))
        step[entry] += 1
    return order


PAIRS = 2


def fold(v):
    total = v[0:8]
    for k in range(1, v.shape[0] // 8):
        total = total + v[8 * k : 8 * k + 8]
    return total


def layer_kernel(dims, at_base, g_base, *refs):
    x_in, cot_in, weights, params = refs[0], refs[1], refs[2:6], refs[6:19]
    y_out, dx_out, res, vec_out, tiles_hbm = refs[19:24]
    (
        at, g, give, pair, line_xy, line_z, ring, big, left, act, hid, qkv, probs, attended, branch, middle, dmid,
        late_in, near_left, near_right, vec_w, vec_h, rstd4, sums4, vec_in, vec_own, vec_got,
        send, recv, v_send, v_recv, p_send, p_recv, l_sem, w_in, w_keep, w_send, w_recv, w_store, t_sem, s_sem, e_sem, n_send, n_recv,
    ) = refs[24:]
    r = lax.axis_index("rep")
    c = lax.axis_index("shard")
    x, y, z = r % 2, (r // 2) % 2, r // 4
    core = {"shard": 1 - c}
    to = {
        "X": {"rep": r + 1 - 2 * x},
        "Y": {"rep": r + 2 - 4 * y},
        "U": {"rep": r + 4},
        "D": {"rep": r - 4},
        "XY": {"rep": r + 3 - 2 * x - 4 * y},
    }
    line_end = (z == 0) | (z == 3)
    line_mid = (z == 1) | (z == 2)
    outward = {"rep": r + 4 * (2 * (z // 2) - 1)}
    inward = {"rep": r + 4 * (1 - 2 * (z // 2))}
    across = {"rep": r + 4 * (3 - 2 * z)}
    upper = z // 2
    length = x_in.shape[0]
    width = x_in.shape[1]
    half_w = width // 2
    hidden = dims[2][1]
    half_h = hidden // 2
    blocks = hidden // width
    TILE = 512

    tile_of = []
    for m, (rows, cols) in enumerate(dims):
        for row in range(0, rows, TILE):
            for col in range(0, cols, UNIT_COLS):
                tile_of.append((m, row, col))
    first_tile = [min(t for t, v in enumerate(tile_of) if v[0] == m) for m in range(4)]
    parts = 2 * len(tile_of)
    slots_f, slots_b, late, slots_l, slots_g = 6, 16, 16, 2, 7

    def part_read(i):
        m, row, col = tile_of[i // 2]
        return pltpu.make_async_copy(
            weights[m].at[pl.ds(row + (i % 2) * 256, 256), pl.ds(col, UNIT_COLS)],
            late_in.at[pl.ds((i % slots_l) * 256, 256), :] if i >= late else big.at[pl.ds((i % slots_f) * 256, 256), :],
            w_in.at[slots_f + i % slots_l if i >= late else i % slots_f],
        )

    def low_row(i):
        return 240 * 16 + (i - late) % slots_g * 256 if i >= late else i * 256

    def part_low(i):
        return low_buf.at[pl.ds(low_row(i), 256), :]

    low_buf = give

    def part_place(i):
        return tiles_hbm.at[c, i // 2, pl.ds((i % 2) * 256, 256), :]

    def part_keep(i):
        return pltpu.make_async_copy(part_low(i), part_place(i), w_keep.at[i % slots_b])

    def part_landing(i):
        if i < 8:
            return res.at[i]
        return ring.at[(i - 8) // 2, pl.ds((i % 2) * 256, 256), :]

    def part_store(i):
        far = tiles_hbm.at[1 - c, i // 2, pl.ds((i % 2) * 256, 256), :]
        return pltpu.make_async_copy(part_landing(i), far, w_store.at[i])

    def part_give(i):
        return pltpu.make_async_remote_copy(
            src_ref=part_low(i), dst_ref=part_landing(i) if i < late else part_place(i), send_sem=w_send.at[i % slots_b], recv_sem=w_recv.at[i],
            device_id=core, device_id_type=MESH,
        )

    def part_got(i):
        return pltpu.make_async_remote_copy(
            src_ref=part_low(i),
            dst_ref=part_landing(i) if i < late else tiles_hbm.at[1 - c, i // 2, pl.ds((i % 2) * 256, 256), :],
            send_sem=w_send.at[i % slots_b], recv_sem=w_recv.at[i], device_id=core, device_id_type=MESH,
        )

    for i in range(slots_f):
        part_read(i).start()

    barrier = pltpu.get_barrier_semaphore()
    for peer in (core, to["X"], to["Y"], to["XY"]):
        pl.semaphore_signal(barrier, inc=1, device_id=peer, device_id_type=MESH)

    @pl.when(z < 3)
    def _():
        pl.semaphore_signal(barrier, inc=1, device_id=to["U"], device_id_type=MESH)

    @pl.when(z > 0)
    def _():
        pl.semaphore_signal(barrier, inc=1, device_id=to["D"], device_id_type=MESH)

    @pl.when(line_end)
    def _():
        pl.semaphore_signal(barrier, inc=1, device_id=across, device_id_type=MESH)

    narrow = (0, 0, 2, 3, 4, 5, 6, 7, 8, 9, 10)

    def rounded(v):
        return v.astype(BF16).astype(F32)

    lane_w = pl.ds(pl.multiple_of(c * half_w, half_w), half_w)
    lane_h = pl.ds(pl.multiple_of(c * half_h, half_h), half_h)
    (qv_ref, ob_ref, hs_ref, g1_ref, b1_ref, g2_ref, b2_ref, g3_ref, b3_ref, ub_ref, g4_ref, b4_ref, db_ref) = params
    vec_w[0:2, lane_w] = rounded(qv_ref[...])
    for row, ref in zip((2, 4, 5, 6, 7, 8, 9, 10), (ob_ref, g1_ref, b1_ref, g2_ref, b2_ref, g3_ref, b3_ref, db_ref)):
        vec_w[row : row + 1, lane_w] = rounded(ref[...])
    head_of = lax.broadcasted_iota(jnp.int32, (1, half_w), 1) // 64
    spread = jnp.zeros((1, half_w), F32)
    for h in range(half_w // 64):
        spread = jnp.where(head_of == h, rounded(hs_ref[0:1, h : h + 1]), spread)
    vec_w[3:4, lane_w] = spread
    for row, ref in enumerate((ub_ref, g4_ref, b4_ref)):
        vec_h[row : row + 1, lane_h] = rounded(ref[...])
    QB, VB, OB, HS, G1, B1, G2, B2, G3, B3, DB = range(11)
    UB, G4, B4 = range(3)

    def small_copy(k, give_it):
        ref, lane, far = ((vec_w, lane_w, 1 - c), (vec_h, lane_h, 1 - c))[k]
        size = half_w if k == 0 else half_h
        other = pl.ds(pl.multiple_of((1 - c) * size, size), size)
        here = ref.at[:, lane]
        return pltpu.make_async_remote_copy(
            src_ref=here, dst_ref=here if give_it else ref.at[:, other], send_sem=s_sem.at[k, 0], recv_sem=s_sem.at[k, 1],
            device_id=core, device_id_type=MESH,
        )

    e_copy = pltpu.make_async_copy(cot_in, g.at[pl.ds(0, length), pl.ds(g_base[3], width)], e_sem.at[0])
    e_copy.start()

    def left_own(m):
        rows = dims[m][0]
        return pltpu.make_async_copy(
            left.at[pl.ds(pl.multiple_of(2 * at_base[m] + c * rows, 512), rows), :],
            at.at[pl.ds(at_base[m], rows), pl.ds(0, length)],
            l_sem.at[m],
        )

    def left_far(m):
        rows = dims[m][0]
        return pltpu.make_async_remote_copy(
            src_ref=left.at[pl.ds(pl.multiple_of(2 * at_base[m] + (1 - c) * rows, 512), rows), :],
            dst_ref=at.at[pl.ds(at_base[m], rows), pl.ds(length, length)],
            send_sem=p_send.at[m, 0], recv_sem=p_recv.at[m, 0], device_id=core, device_id_type=MESH,
        )

    def right_far(m):
        cols = pl.ds(g_base[m], dims[m][1])
        return pltpu.make_async_remote_copy(
            src_ref=g.at[pl.ds(0, length), cols], dst_ref=g.at[pl.ds(length, length), cols],
            send_sem=p_send.at[m, 1], recv_sem=p_recv.at[m, 1], device_id=core, device_id_type=MESH,
        )

    def start_left(m):
        left_own(m).start()
        left_far(m).start()

    def wait_pair(m):
        left_own(m).wait()
        left_far(m).wait()
        right_far(m).wait()

    converted, kept_parts, given_parts = [0], set(), set()

    def kept(i):
        if i not in kept_parts:
            kept_parts.add(i)
            part_keep(i).wait()

    def given(i):
        if i not in given_parts:
            given_parts.add(i)
            part_give(i).wait_send()

    def convert_parts(upto):
        for i in range(converted[0], upto):
            part_read(i).wait()
            if i >= slots_b:
                kept(i - slots_b)
            if i == late:
                for k in range(late):
                    kept(k)
                    given(k)
            if i >= late + slots_g:
                kept(i - slots_g)
                given(i - slots_g)
            source, first = (late_in, i % slots_l * 256) if i >= late else (big, i % slots_f * 256)

            def convert(b, _, i=i, source=source, first=first):
                rows = pl.multiple_of(first + b * 32, 32)
                low = pl.multiple_of(low_row(i) + b * 32, 32)
                low_buf[pl.ds(low, 32), :] = source[pl.ds(rows, 32), :].astype(BF16)
                return 0

            lax.fori_loop(0, 8, convert, 0)
            part_keep(i).start()
            if i == 0:
                pl.semaphore_wait(barrier, 6)
                small_copy(0, True).start()
                small_copy(1, True).start()
            part_give(i).start()
            if i >= late and i + slots_l < parts:
                part_read(i + slots_l).start()
            if i + slots_f < late:
                part_read(i + slots_f).start()
            if i == late - slots_f:
                for k in range(slots_l):
                    part_read(late + k).start()
        converted[0] = max(converted[0], upto)

    def cotangent_copy(k, relay):
        here, there = pl.ds(0, length), pl.ds(length, length)
        cols = pl.ds(g_base[3], width)
        return pltpu.make_async_remote_copy(
            src_ref=near_right.at[k, here, :] if relay else near_right.at[0, here, :] if k == 2 else g.at[here, cols],
            dst_ref=near_right.at[k, there if relay else here, :],
            send_sem=n_send.at[k, int(relay)], recv_sem=n_recv.at[k, int(relay)],
            device_id=core if relay else to["XYY"[k]], device_id_type=MESH,
        )

    convert_parts(2)
    e_copy.wait()
    right_far(3).start()
    cotangent_copy(0, False).start()
    cotangent_copy(1, False).start()
    convert_parts(4)

    def tile(m, half, index):
        return (half, first_tile[m] + index)

    stream = []
    per_half = dims[3][0] // TILE
    stream += [tile(3, h, k) for h in range(2) for k in range(per_half)]
    for m in (2, 1, 0):
        for index in range(dims[m][1] // UNIT_COLS):
            stream += [tile(m, 0, index), tile(m, 1, index)]
    slots_t = 4
    here = set()

    def tile_load(i):
        half, t = stream[i]
        return pltpu.make_async_copy(
            tiles_hbm.at[half, t], ring.at[i % slots_t], t_sem.at[i % slots_t]
        )

    def tile_start(i):
        half, t = stream[i]
        if (1, t) not in here:
            here.add((1, t))
            convert_parts(2 * t + 2)
            for k in (2 * t, 2 * t + 1):
                kept(k)
                if k >= late:
                    part_got(k).wait_recv()
        tile_load(i).start()

    at_tile, started, allowed_to = [0], [0], [0]

    def fill(limit=None):
        if limit is not None:
            allowed_to[0] = limit
        while started[0] < min(at_tile[0] + slots_t, allowed_to[0], len(stream)):
            tile_start(started[0])
            started[0] += 1

    def next_tile(ahead=0):
        i = at_tile[0] + ahead
        assert i < started[0]
        tile_load(i).wait()
        return ring.at[i % slots_t]

    def done_tile(count=1):
        at_tile[0] += count
        fill()

    def mean(v):
        return jnp.sum(v, axis=-1, keepdims=True) / v.shape[-1]

    def normal(v):
        centred = v - mean(v)
        scale = lax.rsqrt(mean(centred * centred) + 1e-05)
        return centred * scale, scale

    def each(fn, step=32, init=0, unroll=1):
        def body(i, carry):
            return fn(pl.ds(pl.multiple_of(i * step, step), step), carry)

        return lax.fori_loop(0, length // step, body, init, unroll=unroll)

    def w_row(i):
        return vec_w[i : i + 1, :]

    def turn(source, m, block=0):
        for k in range(width // 256):
            row = 2 * at_base[m] + block * width + k * 256
            left[row : row + 256, :] = jnp.transpose(source[:, k * 256 : (k + 1) * 256])

    NT = (((1,), (1,)), ((), ()))
    TN = (((0,), (0,)), ((), ()))

    def nt(a, b):
        return lax.dot_general(a, b, NT, preferred_element_type=F32)

    def tn(a, b):
        return lax.dot_general(a, b, TN, preferred_element_type=F32)

    def product_pair(source, write, t):
        convert_parts(2 * t + 2)
        for i in (2 * t, 2 * t + 1):
            part_got(i).wait_recv()
            part_store(i).start()
        far = (part_landing(2 * t), part_landing(2 * t + 1))
        for k in range(UNIT_COLS // 256):
            cols = slice(k * 256, (k + 1) * 256)
            own = low_buf[512 * t : 512 * (t + 1), cols]
            value = jnp.dot(source[:, lane_w], own, preferred_element_type=F32)
            for n in range(2):
                lanes = pl.ds(pl.multiple_of((1 - c) * half_w + n * 256, 256), 256)
                value = value + jnp.dot(source[:, lanes], far[n][:, cols], preferred_element_type=F32)
            write(cols, value)

    small_copy(0, True).wait_send()
    small_copy(1, True).wait_send()
    small_copy(0, False).wait_recv()
    small_copy(1, False).wait_recv()

    def first_norm(rows, _):
        hat, _s = normal(x_in[rows, :].astype(F32))
        act[rows, :] = (hat * w_row(G1) + w_row(B1)).astype(BF16)
        return 0

    each(first_norm, unroll=2)
    for index in range(3):

        def put_qkv(cols, value, index=index):
            if index == 0:
                value = value + vec_w[QB : QB + 1, cols]
            if index == 2:
                value = value + vec_w[VB : VB + 1, cols]
            qkv[:, index * width + cols.start : index * width + cols.stop] = value.astype(BF16)

        product_pair(act, put_qkv, first_tile[0] + index)
        convert_parts(10 + 2 * index)
    turn(act, 0)
    start_left(0)
    convert_parts(16)
    for k in range(2):
        cotangent_copy(k, False).wait()
        cotangent_copy(k, True).start()
    cotangent_copy(2, False).start()

    low_lane = lax.broadcasted_iota(jnp.int32, (length, 128), 1) < 64
    allowed = lax.broadcasted_iota(jnp.int32, (length, length), 1) <= lax.broadcasted_iota(
        jnp.int32, (length, length), 0
    )
    scale = 64 ** (-0.5)
    keep_lane = (low_lane.astype(F32).astype(BF16), jnp.logical_not(low_lane).astype(F32).astype(BF16))

    def split_heads(v):
        return jnp.concatenate([v * keep_lane[0], v * keep_lane[1]], axis=0)

    def attend(p):
        q = qkv[:, pl.ds(pl.multiple_of(p * 128, 128), 128)]
        k = qkv[:, pl.ds(pl.multiple_of(width + p * 128, 128), 128)]
        v = qkv[:, pl.ds(pl.multiple_of(2 * width + p * 128, 128), 128)]
        both = nt(q, split_heads(k)) * scale
        got = []
        for h in range(2):
            scores = jnp.where(allowed, both[:, h * length : (h + 1) * length], -1e30)
            top = jnp.max(scores, axis=-1, keepdims=True)
            lse = top + jnp.log(jnp.sum(jnp.exp(scores - top), axis=-1, keepdims=True))
            got.append(jnp.exp(scores - lse))
        prob = jnp.concatenate(got, axis=1)
        probs[p] = prob
        value = jnp.dot(prob.astype(BF16), split_heads(v), preferred_element_type=F32)
        cols = pl.ds(pl.multiple_of(p * 128, 128), 128)
        attended[:, cols] = value
        act[:, cols] = (value * vec_w[HS : HS + 1, cols]).astype(BF16)

    def attend_some(i, _):
        for n in range(PAIRS):
            attend(i * PAIRS + n)
        return 0

    lax.fori_loop(0, width // 128 // PAIRS, attend_some, 0)

    def put_branch(cols, value):
        branch[:, cols] = value + vec_w[OB : OB + 1, cols]

    product_pair(act, put_branch, first_tile[1])
    turn(act, 1)
    start_left(1)

    def second_norm(rows, _):
        hat, _s = normal(branch[rows, :])
        mid = x_in[rows, :].astype(F32) + (hat * w_row(G2) + w_row(B2))
        middle[rows, :] = mid
        hat, _s = normal(mid)
        act[rows, :] = (hat * w_row(G3) + w_row(B3)).astype(BF16)
        return 0

    each(second_norm, unroll=2)
    U0, H0, D0 = 0, blocks * length, 2 * blocks * length
    for j in range(blocks):

        def put_hidden(cols, value, j=j):
            wide = slice(j * width + cols.start, j * width + cols.stop)
            big[U0 + j * length : U0 + (j + 1) * length, cols] = value + vec_h[UB : UB + 1, wide]

        product_pair(act, put_hidden, first_tile[2] + j)
    turn(act, 2)
    start_left(2)
    root_half = 0.7071067811865476

    def near(base, start):
        return pl.ds(pl.multiple_of(base + start, 16), 16)

    def hidden_norm(rows, _):
        total = jnp.zeros((16, 1), F32)
        for j in range(blocks):
            u = big[near(U0 + j * length, rows.start), :]
            h = u * (1.0 + lax.erf(u * root_half)) * 0.5
            big[near(H0 + j * length, rows.start), :] = h
            total = total + jnp.sum(h, axis=-1, keepdims=True)
        centre = total / hidden
        total = jnp.zeros((16, 1), F32)
        for j in range(blocks):
            h = big[near(H0 + j * length, rows.start), :] - centre
            total = total + jnp.sum(h * h, axis=-1, keepdims=True)
        s = lax.rsqrt(total / hidden + 1e-05)
        rstd4[rows, :] = jnp.broadcast_to(s, (16, 128))
        for j in range(blocks):
            at_h = near(H0 + j * length, rows.start)
            hat = (big[at_h, :] - centre) * s
            big[at_h, :] = hat
            cols = slice(j * width, (j + 1) * width)
            hid[near(j * length, rows.start), :] = (
                hat * vec_h[G4 : G4 + 1, cols] + vec_h[B4 : B4 + 1, cols]
            ).astype(BF16)
        return 0

    cotangent_copy(2, False).wait()
    cotangent_copy(2, True).start()
    each(hidden_norm, 16)
    for j in range(blocks):
        turn(hid.at[pl.ds(j * length, length), :], 3, j)
    start_left(3)
    convert_parts(parts)
    for i in range(late):
        part_store(i).wait()

    tasks = []
    zeros8 = jnp.zeros((8, width), F32)
    dirs = g.at[pl.ds(0, length), :]

    def put_sum(row, value):
        line = jnp.sum(value, axis=0, keepdims=True)
        vec_in[0, row : row + 1, :] = line[:, 0:half_w]
        vec_in[1, row : row + 1, :] = line[:, half_w:width]

    def task_down(h, k):
        def run():
            w = next_tile()
            row = h * dims[3][0] + k * TILE
            j, lane = row // width, row % width
            if h == 0 and k == 0:
                y_acc[...] = middle[...] + w_row(DB)
            for n in range(TILE // 256):
                big[D0 + j * length : D0 + (j + 1) * length, lane + n * 256 : lane + (n + 1) * 256] = nt(
                    dirs[:, g_base[3] : g_base[3] + width], w[n * 256 : (n + 1) * 256, :]
                )

            for n in range(width // 256):
                cols = slice(n * 256, (n + 1) * 256)
                y_acc[:, cols] += jnp.dot(
                    hid[j * length : (j + 1) * length, lane : lane + TILE], w[:, cols], preferred_element_type=F32
                )
            done_tile()
            if h == 1 and k == per_half - 1:
                y_out[...] = y_acc[...].astype(BF16)

        return run

    y_acc = dmid
    for h in range(2):
        for k in range(per_half):
            tasks.append((1.2, task_down(h, k)))

    def task_hidden(first, count):
        def run():
            if first == 0:
                sums4[...] = jnp.zeros_like(sums4)

                def e_sum(rows, carry):
                    return carry + fold(dirs[rows, g_base[3] : g_base[3] + width].astype(F32))

                put_sum(DB, each(e_sum, 32, zeros8))

            def body(i, _):
                at_r = pl.multiple_of(first + i * 16, 16)
                one = jnp.zeros((16, 1), F32)
                two = jnp.zeros((16, 1), F32)
                for j in range(blocks):
                    gain = vec_h[G4 : G4 + 1, j * width : (j + 1) * width]
                    d = big[near(D0 + j * length, at_r), :] * gain
                    hat = big[near(H0 + j * length, at_r), :]
                    one = one + jnp.sum(d, axis=-1, keepdims=True)
                    two = two + jnp.sum(d * hat, axis=-1, keepdims=True)
                one, two = one / hidden, two / hidden
                s = rstd4[pl.ds(at_r, 16), 0:1]
                for j in range(blocks):
                    cols = slice(j * width, (j + 1) * width)
                    da = big[near(D0 + j * length, at_r), :]
                    hat = big[near(H0 + j * length, at_r), :]
                    u = big[near(U0 + j * length, at_r), :]
                    dh = s * (da * vec_h[G4 : G4 + 1, cols] - one - hat * two)
                    slope = 0.5 * (1.0 + lax.erf(u * root_half)) + u * (jnp.exp(u * u * -0.5) * 0.3989422804014327)
                    du = (dh * slope).astype(BF16)
                    g[pl.ds(at_r, 16), g_base[2] + j * width : g_base[2] + (j + 1) * width] = du
                    sums4[0:8, cols] += fold(du.astype(F32))
                    sums4[8:16, cols] += fold(da * hat)
                    sums4[16:24, cols] += fold(da)
                return 0

            lax.fori_loop(0, count // 16, body, 0)
            if first + count == length:
                for i in range(3):
                    line = jnp.sum(sums4[8 * i : 8 * i + 8, :], axis=0, keepdims=True)
                    for n in range(hidden // half_w):
                        hh, k = divmod(n, half_h // half_w)
                        vec_in[hh, 11 + 4 * i + k : 12 + 4 * i + k, :] = line[:, n * half_w : (n + 1) * half_w]
                right_far(2).start()

        return run

    for first in range(0, length, 32):
        tasks.append((3.0, task_hidden(first, 32)))

    def add_pair(acc, index_of, cols_of, count, width_to):
        def make(index):
            def run():
                for h in range(2):
                    w = next_tile()
                    for n in range(TILE // 256):
                        cols = slice(h * half_w + n * 256, h * half_w + (n + 1) * 256)
                        value = nt(dirs[:, cols_of(index)], w[n * 256 : (n + 1) * 256, :])
                        if index == 0:
                            acc[:, cols] = value
                        else:
                            acc[:, cols] += value
                    done_tile()

            return run

        return [(1.2, make(index)) for index in range(count)]

    ends = {2: len(tasks)}
    acc = big.at[pl.ds(U0, length), :]
    tasks += add_pair(acc, None, lambda j: slice(g_base[2] + j * width, g_base[2] + (j + 1) * width), blocks, width)

    def task_norms():
        def body(rows, carry):
            s3g, s3b, s2g, s2b, sob = carry
            da = acc[rows, :]
            hat, s = normal(middle[rows, :])
            d = da * w_row(G3)
            d_mid = dirs[rows, g_base[3] : g_base[3] + width].astype(F32) + s * (d - mean(d) - hat * mean(d * hat))
            dmid[rows, :] = d_mid
            s3g, s3b = s3g + fold(da * hat), s3b + fold(da)
            hat, s = normal(branch[rows, :])
            d = d_mid * w_row(G2)
            dy = (s * (d - mean(d) - hat * mean(d * hat))).astype(BF16)
            s2g, s2b = s2g + fold(d_mid * hat), s2b + fold(d_mid)
            g[rows, g_base[1] : g_base[1] + width] = dy
            return (s3g, s3b, s2g, s2b, sob + fold(dy.astype(F32)))

        got = each(body, 16, (zeros8,) * 5)
        for row, value in zip((G3, B3, G2, B2, OB), got):
            put_sum(row, value)
        right_far(1).start()

    tasks.append((2.5, task_norms))
    ends[1] = len(tasks)
    d_mixed = big.at[pl.ds(U0 + length, length), :]
    tasks += add_pair(d_mixed, None, lambda j: slice(g_base[1], g_base[1] + width), 1, width)

    def task_heads():
        def body(rows, carry):
            d = d_mixed[rows, :]
            act[rows, :] = (d * w_row(HS)).astype(BF16)
            return carry + fold(d * attended[rows, :])

        put_sum(HS, each(body, 32, zeros8))

    tasks.append((0.6, task_heads))

    def task_attend(first, count):
        def run():
            def pair_of_heads(p):
                q_cols = pl.ds(pl.multiple_of(p * 128, 128), 128)
                k_cols = pl.ds(pl.multiple_of(width + p * 128, 128), 128)
                v_cols = pl.ds(pl.multiple_of(2 * width + p * 128, 128), 128)
                q, k, v, do = qkv[:, q_cols], qkv[:, k_cols], qkv[:, v_cols], act[:, q_cols]
                prob = probs[p]
                dv = tn(prob.astype(BF16), do)
                dp = nt(do, split_heads(v))
                ds = []
                for h in range(2):
                    own = slice(h * length, (h + 1) * length)
                    dot = jnp.sum(prob[:, own] * dp[:, own], axis=-1, keepdims=True)
                    ds.append(prob[:, own] * (dp[:, own] - dot))
                ds = jnp.concatenate(ds, axis=1).astype(BF16)
                dq = jnp.dot(ds, split_heads(k), preferred_element_type=F32) * scale
                dk = tn(ds, q) * scale
                g[0:length, q_cols] = dq.astype(BF16)
                g[0:length, k_cols] = jnp.where(low_lane, dk[0:length], dk[length : 2 * length]).astype(BF16)
                g[0:length, v_cols] = jnp.where(low_lane, dv[0:length], dv[length : 2 * length]).astype(BF16)

            for n in range(count):
                pair_of_heads(first + n)
            if first + count == width // 128:

                def sums(rows, carry):
                    a, b = carry
                    return (
                        a + fold(g[rows, 0:width].astype(F32)),
                        b + fold(g[rows, 2 * width : 3 * width].astype(F32)),
                    )

                a, b = each(sums, 32, (zeros8, zeros8))
                put_sum(QB, a)
                put_sum(VB, b)
                right_far(0).start()

        return run

    for first in range(0, width // 128, 2):
        tasks.append((3.0, task_attend(first, 2)))
    ends[0] = len(tasks)
    d_first = big.at[pl.ds(U0 + 2 * length, length), :]
    tasks += add_pair(d_first, None, lambda j: slice(j * width, (j + 1) * width), 3, width)

    def task_last():
        def body(rows, carry):
            sg, sb = carry
            da = d_first[rows, :]
            hat, s = normal(x_in[rows, :].astype(F32))
            d = da * w_row(G1)
            dx_out[rows, :] = dmid[rows, :] + s * (d - mean(d) - hat * mean(d * hat))
            return (sg + fold(da * hat), sb + fold(da))

        sg, sb = each(body, 16, (zeros8, zeros8))
        put_sum(G1, sg)
        put_sum(B1, sb)
        vec_in[0, 23:24, :] = jnp.zeros((1, half_w), F32)
        vec_in[1, 23:24, :] = jnp.zeros((1, half_w), F32)
        vec_copy(0).start()

    tasks.append((1.5, task_last))

    vec_steps = (core, to["X"], to["Y"], {"rep": r + 4 * (1 - 2 * (z % 2))}, across)

    def vec_copy(step):
        source = vec_in.at[1 - c] if step == 0 else vec_own.at[step]
        return pltpu.make_async_remote_copy(
            src_ref=source, dst_ref=vec_got.at[step], send_sem=v_send.at[step], recv_sem=v_recv.at[step],
            device_id=vec_steps[step], device_id_type=MESH,
        )

    def vec_task(k):
        vec_copy(k).wait_recv()
        total = (vec_in[c] if k == 0 else vec_own[k]) + vec_got[k]
        if k < 4:
            vec_own[k + 1] = total
            vec_copy(k + 1).start()
        else:
            vec_out[...] = total

    units = unit_table(dims)
    kinds = KINDS
    xy_at, z_at = {}, {}
    for unit, kind in enumerate(kinds):
        (z_at if kind[0] == "Z" else xy_at)[unit] = len(z_at) if kind[0] == "Z" else len(xy_at)

    def copy(unit, name, source, dest, device):
        return functools.partial(
            pltpu.make_async_remote_copy,
            src_ref=source, dst_ref=dest, send_sem=send.at[unit], recv_sem=recv.at[unit, SLOT[name]],
            device_id=device, device_id_type=MESH,
        )

    def rows_of(unit, start, count):
        if not isinstance(start, int):
            start = pl.multiple_of(start, 16)
        return res.at[unit, pl.ds(start, count), :]

    def product(unit, start, count, dest, dest_start, got=None, got_start=0, near_start=None):
        m, row, col = units[unit]
        step = 128 if count % 128 == 0 else min(count, 64)

        def block(index, _):
            part, strip = index // (UNIT_COLS // 256), index % (UNIT_COLS // 256)
            cols = pl.ds(pl.multiple_of(strip * 256, 256), 256)
            value = jnp.dot(
                at[pl.ds(pl.multiple_of(at_base[m] + row + start + part * step, 16), step), :],
                g[:, pl.ds(pl.multiple_of(g_base[m] + col + strip * 256, 256), 256)],
                preferred_element_type=F32,
            )
            if near_start is not None:
                for peer in range(3):
                    rows = peer * (UNIT_ROWS // 4) + near_start + part * step
                    value = value + jnp.dot(
                        near_left[unit, pl.ds(pl.multiple_of(rows, 16), step), :],
                        near_right[peer, :, pl.ds(pl.multiple_of(col + strip * 256, 256), 256)],
                        preferred_element_type=F32,
                    )
            if got is not None:
                value = value + got[pl.ds(pl.multiple_of(got_start + part * step, 16), step), cols].astype(F32)
            dest[pl.ds(pl.multiple_of(dest_start + part * step, 16), step), cols] = value.astype(BF16)
            return 0

        lax.fori_loop(0, (count // step) * (UNIT_COLS // 256), block, 0)

    def accumulate(unit, start, count, got, got_start, dest, dest_start):
        def block(strip, _):
            cols = pl.ds(pl.multiple_of(strip * 256, 256), 256)
            value = res[unit, pl.ds(pl.multiple_of(start, 16), count), cols].astype(F32)
            value = value + got[pl.ds(pl.multiple_of(got_start, 16), count), cols].astype(F32)
            dest[pl.ds(pl.multiple_of(dest_start, 16), count), cols] = value.astype(BF16)
            return 0

        lax.fori_loop(0, UNIT_COLS // 256, block, 0)

    def gather_line(unit, base, size, level):
        up, down = "u%d" % level, "w%d" % level
        low, high = z - (level - 1), z + (level - 1)

        @pl.when((low >= 0) & (z < 3))
        def _():
            part = rows_of(unit, base + low * size, size)
            copy(unit, up, part, part, to["U"])().start()

        @pl.when((high <= 3) & (z > 0))
        def _():
            part = rows_of(unit, base + high * size, size)
            copy(unit, down, part, part, to["D"])().start()

    def gather_arrived(unit, base, size, level):
        def wait(chunks):
            part = give.at[pl.ds(0, chunks * size), :]
            copy(unit, "u%d" % level, part, part, to["U"])().wait_recv()

        if level == 1:
            pl.when(line_mid)(lambda: wait(2))
        if level == 2:
            wait(1)
        else:
            pl.when(line_end)(lambda: wait(1))

    def finish(unit, ends, mids):
        def wait(rows):
            part = give.at[pl.ds(0, rows), :]
            copy(unit, "d1", part, part, to["X"])().wait_send()

        pl.when(line_end)(lambda: wait(ends))
        pl.when(line_mid)(lambda: wait(mids))

    def task_xy(unit, step):
        half, quarter, size = UNIT_ROWS // 2, UNIT_ROWS // 4, UNIT_ROWS // 16
        first, second = ("X", "Y") if kinds[unit][-1] == "X" else ("Y", "X")
        p, q = (x, y) if first == "X" else (y, x)
        by_tokens = kinds[unit][0] == "Q"
        line, block, out, other = line_xy.at[xy_at[unit]], res.at[unit], give.at[pl.ds(unit * GIVE_ROWS, GIVE_ROWS), :], pair.at[unit]
        keep, away_half = p * half, (1 - p) * half
        base = keep + q * quarter
        away = keep + (1 - q) * quarter
        at_z = half + quarter
        d1 = copy(unit, "d1", out.at[pl.ds(0, half), :], rows_of(unit, away_half, half), to[first])

        def left_for(peer):
            m, row, _ = units[unit]
            px, py = ((1 - x, y), (x, 1 - y), (1 - x, 1 - y))[peer]
            at_p, at_q = (px, py) if first == "X" else (py, px)
            rows = pl.ds(pl.multiple_of(at_base[m] + row + at_p * half + at_q * quarter, quarter), quarter)
            dest = near_left.at[unit, pl.ds(peer * quarter, quarter), :]
            return copy(unit, "d1", at.at[rows, :], dest, to[("X", "Y", "XY")[peer]])

        d2 = copy(unit, "d2", out.at[pl.ds(half, quarter), :], other.at[pl.ds(0, quarter), :], to[second])
        z1 = copy(unit, "z1", out.at[pl.ds(at_z, 3 * size), :], line.at[pl.ds(0, 3 * size), :], inward)
        z2 = copy(unit, "z2", out.at[pl.ds(at_z, 2 * size), :], line.at[pl.ds(3 * size, 2 * size), :], across)
        z3 = copy(unit, "z3", out.at[pl.ds(at_z + 2 * size, size), :], line.at[pl.ds(0, size), :], outward)
        own_quarter = rows_of(unit, base, quarter)
        g2 = copy(unit, "g2", own_quarter, own_quarter, to[second])
        own_half = rows_of(unit, keep, half)
        g1 = copy(unit, "g1", own_half, own_half, to[first])
        own = base + z * size
        if step == 0 and by_tokens:
            for peer in range(3):
                left_for(peer)().start()
        elif step == 1 and by_tokens:
            pass
        elif step == 2 and by_tokens:
            arrived = near_left.at[unit]
            copy(unit, "d1", arrived, arrived, to["X"])().wait_recv()

            product(unit, base, quarter, block, base, near_start=0)

            @pl.when(line_end)
            def _():
                from_row = pl.multiple_of(base + (1 - upper) * size, 16)
                for n in range(3):
                    out[at_z + n * size : at_z + (n + 1) * size, :] = block[pl.ds(from_row + n * size, size), :]
                z1().start()

        elif step == 0:
            product(unit, away_half, half, out, 0)
            d1().start()
        elif step == 1:
            d1().wait_recv()
            product(unit, away, quarter, out, half, block, away)
            d2().start()
            product(unit, base, quarter, block, base, block, base)
        elif step == 2:
            d2().wait_recv()

            @pl.when(line_end)
            def _():
                skip = (1 - upper) * size
                accumulate(unit, base + skip, 3 * size, other, skip, out, at_z)
                z1().start()
                accumulate(unit, own, size, other, z * size, block, own)

            @pl.when(line_mid)
            def _():
                accumulate(unit, base, quarter, other, 0, block, base)

        elif step == 3:

            @pl.when(line_mid)
            def _():
                z1().wait_recv()
                accumulate(unit, base + (1 - upper) * 2 * size, 2 * size, line, (1 - upper) * size, out, at_z)
                z2().start()
                accumulate(unit, own, size, line, upper * 2 * size, block, own)

        elif step == 4:

            @pl.when(line_mid)
            def _():
                z2().wait_recv()
                accumulate(unit, base + upper * 3 * size, size, line, (3 + upper) * size, out, at_z + 2 * size)
                z3().start()
                accumulate(unit, own, size, line, (4 - upper) * size, block, own)
                gather_line(unit, base, size, 1)

        elif step == 5:

            @pl.when(line_end)
            def _():
                z3().wait_recv()
                accumulate(unit, own, size, line, 0, block, own)
                gather_line(unit, base, size, 1)

        elif step in (6, 7):
            gather_arrived(unit, base, size, step - 5)
            gather_line(unit, base, size, step - 4)
        elif step == 8:
            gather_arrived(unit, base, size, 3)
            g2().start()
        elif step == 9:
            g2().wait_recv()
            g1().start()
        else:
            g1().wait_recv()
            sent = half + quarter + (3 * size if by_tokens else half + quarter)
            finish(unit, sent + 4 * size, sent + 8 * size)

    def task_z(unit, step):
        size, half, quarter = UNIT_ROWS // 4, UNIT_ROWS // 8, UNIT_ROWS // 16
        first, second = ("X", "Y") if kinds[unit] == "ZX" else ("Y", "X")
        p, q = (x, y) if kinds[unit] == "ZX" else (y, x)
        line, block, out, other = line_z.at[z_at[unit]], res.at[unit], give.at[pl.ds(unit * GIVE_ROWS, GIVE_ROWS), :], pair.at[unit]
        own = z * size
        keep, away_half = own + p * half, own + (1 - p) * half
        base, away = keep + q * quarter, keep + (1 - q) * quarter
        at_d = 3 * size
        z1 = copy(unit, "z1", out.at[pl.ds(0, 3 * size), :], line.at[pl.ds(0, 3 * size), :], inward)
        z2 = copy(unit, "z2", out.at[pl.ds(0, 2 * size), :], line.at[pl.ds(3 * size, 2 * size), :], across)
        z3 = copy(unit, "z3", out.at[pl.ds(2 * size, size), :], line.at[pl.ds(0, size), :], outward)
        d1 = copy(unit, "d1", out.at[pl.ds(at_d, half), :], other.at[pl.ds(0, half), :], to[first])
        d2 = copy(unit, "d2", out.at[pl.ds(at_d + half, quarter), :], other.at[pl.ds(half, quarter), :], to[second])
        own_quarter = rows_of(unit, base, quarter)
        g2 = copy(unit, "g2", own_quarter, own_quarter, to[second])
        own_half = rows_of(unit, keep, half)
        g1 = copy(unit, "g1", own_half, own_half, to[first])
        if step == 0:

            @pl.when(line_end)
            def _():
                product(unit, (1 - upper) * size, 3 * size, out, 0)
                z1().start()

        elif step == 1:

            @pl.when(line_mid)
            def _():
                z1().wait_recv()
                product(unit, (1 - upper) * 2 * size, 2 * size, out, 0, line, (1 - upper) * size)
                z2().start()
                product(unit, own, size, block, own, line, upper * 2 * size)

        elif step == 2:

            @pl.when(line_mid)
            def _():
                z2().wait_recv()
                product(unit, upper * 3 * size, size, out, 2 * size, line, (3 + upper) * size)
                z3().start()
                got = (4 - upper) * size
                accumulate(unit, away_half, half, line, got + (1 - p) * half, out, at_d)
                d1().start()
                accumulate(unit, keep, half, line, got + p * half, block, keep)

        elif step == 3:

            @pl.when(line_end)
            def _():
                z3().wait_recv()
                product(unit, away_half, half, out, at_d, line, (1 - p) * half)
                d1().start()
                product(unit, keep, half, block, keep, line, p * half)

        elif step == 4:
            d1().wait_recv()
            accumulate(unit, away, quarter, other, (1 - q) * quarter, out, at_d + half)
            d2().start()
            accumulate(unit, base, quarter, other, q * quarter, block, base)
        elif step == 5:
            d2().wait_recv()
            accumulate(unit, base, quarter, other, half, block, base)
            g2().start()
        elif step == 6:
            g2().wait_recv()
            g1().start()
        elif step == 7:
            g1().wait_recv()
            gather_line(unit, 0, size, 1)
        elif step in (8, 9):
            gather_arrived(unit, 0, size, step - 7)
            gather_line(unit, 0, size, step - 6)
        else:
            gather_arrived(unit, 0, size, 3)
            finish(unit, 2 * half + 2 * quarter + 4 * size, 2 * half + 2 * quarter + 8 * size)


    for kind, a, b in program_order(units, ends):
        if kind == "task":
            if a == 0:
                fill(len(stream))
            tasks[a][1]()
        elif kind == "wait":
            wait_pair(a)
            if a == 3:
                for k in range(3):
                    cotangent_copy(k, True).wait()
            if a == 1:
                for k in range(parts):
                    given(k)
        elif kind == "vec":
            vec_task(a)
        elif kinds[a][0] == "Z":
            task_z(a, b)
        else:
            task_xy(a, b)
    for step in range(5):
        vec_copy(step).wait_send()


def whole_layer(layer_input, cotangent, weights, params):
    dims = tuple(w.shape for w in weights)
    at_rows = sum(rows for rows, _ in dims)
    g_cols = sum(cols for _, cols in dims)
    at_base = [sum(rows for rows, _ in dims[:m]) for m in range(4)]
    g_base = [sum(cols for _, cols in dims[:m]) for m in range(4)]
    length, width = layer_input.shape
    hidden = dims[2][1]
    blocks = hidden // width
    units = unit_table(dims)
    kinds = KINDS
    n, n_z = len(units), sum(kind[0] == "Z" for kind in kinds)
    tiles = n // 2
    hbm = pl.BlockSpec(memory_space=pl.ANY)
    vmem = pl.BlockSpec(memory_space=pltpu.VMEM)
    dma = pltpu.SemaphoreType.DMA
    small = (24, width // 2)
    got = pl.pallas_call(
        functools.partial(layer_kernel, dims, at_base, g_base),
        out_shape=[
            pltpu.VMEM((length, width), BF16),
            pltpu.VMEM((length, width), F32),
            pltpu.VMEM((n, UNIT_ROWS, UNIT_COLS), BF16),
            pltpu.VMEM(small, F32),
            jax.ShapeDtypeStruct((2, tiles, 512, UNIT_COLS), BF16),
        ],
        in_specs=[vmem, hbm] + [hbm] * 4 + [vmem] * 13,
        out_specs=[vmem] * 4 + [hbm],
        scratch_shapes=[
            pltpu.VMEM((at_rows, 2 * length), BF16),
            pltpu.VMEM((2 * length, g_cols), BF16),
            pltpu.VMEM((n * GIVE_ROWS, UNIT_COLS), BF16),
            pltpu.VMEM((n, UNIT_ROWS // 4, UNIT_COLS), BF16),
            pltpu.VMEM((n - n_z, 5 * UNIT_ROWS // 16, UNIT_COLS), BF16),
            pltpu.VMEM((n_z, 5 * UNIT_ROWS // 4, UNIT_COLS), BF16),
            pltpu.VMEM((4, 512, UNIT_COLS), BF16),
            pltpu.VMEM((3 * blocks * length, width), F32),
            pltpu.VMEM((2 * at_rows, length), BF16),
            pltpu.VMEM((length, width), BF16),
            pltpu.VMEM((blocks * length, width), BF16),
            pltpu.VMEM((length, 3 * width), BF16),
            pltpu.VMEM((width // 128, length, 2 * length), F32),
            pltpu.VMEM((length, width), F32),
            pltpu.VMEM((length, width), F32),
            pltpu.VMEM((length, width), F32),
            pltpu.VMEM((length, width), F32),
            pltpu.VMEM((2 * 256, UNIT_COLS), F32),
            pltpu.VMEM((dims[3][0] // UNIT_ROWS, 3 * UNIT_ROWS // 4, 2 * length), BF16),
            pltpu.VMEM((3, 2 * length, width), BF16),
            pltpu.VMEM((16, width), F32),
            pltpu.VMEM((8, hidden), F32),
            pltpu.VMEM((length, 128), F32),
            pltpu.VMEM((24, hidden), F32),
            pltpu.VMEM((2,) + small, F32),
            pltpu.VMEM((5,) + small, F32),
            pltpu.VMEM((5,) + small, F32),
            dma((n,)),
            dma((n, 9)),
            dma((5,)),
            dma((5,)),
            dma((4, 2)),
            dma((4, 2)),
            dma((4,)),
            dma((10,)),
            dma((16,)),
            dma((16,)),
            dma((2 * tiles,)),
            dma((16,)),
            dma((4,)),
            dma((2, 2)),
            dma((1,)),
            dma((3, 2)),
            dma((3, 2)),
        ],
        compiler_params=pltpu.CompilerParams(
            collective_id=0, has_side_effects=True, vmem_limit_bytes=50 * MIB + 786432
        ),
        name="whole_layer",
    )(layer_input, cotangent, *weights, *params)
    return got[:4]


def finish_kernel(dims, *refs):
    y_in, dx_in, res, vec = refs[0:4]
    y_out, dx_out, outs, smalls = refs[4], refs[5], refs[6:10], refs[10:23]
    wide, lines, o_sem, s_sem = refs[23], refs[24:37], refs[37], refs[38]
    slots = wide.shape[0]
    copies = [pltpu.make_async_copy(y_in, y_out, s_sem.at[13]), pltpu.make_async_copy(dx_in, dx_out, s_sem.at[14])]
    rows_of = [range(0, 2)] + [range(k, k + 1) for k in range(2, 11)] + [range(11 + 4 * k, 15 + 4 * k) for k in range(3)]
    for k, rows in enumerate(rows_of):
        if k == 2:
            head_of = lax.broadcasted_iota(jnp.int32, (1, vec.shape[1]), 1) // 64
            lane = lax.broadcasted_iota(jnp.int32, lines[k].shape, 1)
            total = jnp.zeros(lines[k].shape, F32)
            for h in range(vec.shape[1] // 64):
                one = jnp.sum(jnp.where(head_of == h, vec[3:4, :], 0.0), axis=-1, keepdims=True)
                total = jnp.where(lane == h, one, total)
            lines[k][...] = total
        elif len(rows) == 4:
            for j, row in enumerate(rows):
                lines[k][:, j * vec.shape[1] : (j + 1) * vec.shape[1]] = vec[row : row + 1, :]
        else:
            lines[k][...] = vec[rows.start : rows.stop, :]
        copies.append(pltpu.make_async_copy(lines[k], smalls[k], s_sem.at[k]))
    for piece in copies:
        piece.start()
    units = unit_table(dims)

    def put(unit):
        m, row, col = units[unit]
        return pltpu.make_async_copy(
            wide.at[unit % slots], outs[m].at[pl.ds(row, UNIT_ROWS), pl.ds(col, UNIT_COLS)], o_sem.at[unit % slots]
        )

    for unit in range(len(units)):
        if unit >= slots:
            put(unit - slots).wait()

        def widen(b, _, unit=unit):
            rows = pl.ds(pl.multiple_of(b * 32, 32), 32)
            wide[unit % slots, rows, :] = res[unit, rows, :].astype(F32)
            return 0

        lax.fori_loop(0, UNIT_ROWS // 32, widen, 0)
        put(unit).start()
    for unit in range(len(units) - slots, len(units)):
        put(unit).wait()
    for piece in copies:
        piece.wait()


def write_results(got, dims):
    y, dx, _, vec = got
    half = vec.shape[1]
    small = [(2, half), (1, half), (1, half // 64)] + [(1, half)] * 7 + [(1, 4 * half)] * 3
    hbm = pl.BlockSpec(memory_space=pl.ANY)
    vmem = pl.BlockSpec(memory_space=pltpu.VMEM)
    dma = pltpu.SemaphoreType.DMA
    return pl.pallas_call(
        functools.partial(finish_kernel, dims),
        out_shape=[jax.ShapeDtypeStruct(y.shape, BF16), jax.ShapeDtypeStruct(dx.shape, F32)]
        + [jax.ShapeDtypeStruct(d, F32) for d in dims]
        + [jax.ShapeDtypeStruct(s, F32) for s in small],
        in_specs=[vmem] * 4,
        out_specs=[hbm] * 19,
        scratch_shapes=[pltpu.VMEM((6, UNIT_ROWS, UNIT_COLS), F32)]
        + [pltpu.VMEM(s, F32) for s in small]
        + [dma((6,)), dma((15,))],
        compiler_params=pltpu.CompilerParams(vmem_limit_bytes=30 * MIB),
        name="write_results",
    )(*got)


def on_pair_of_cores(
    layer_input, cotangent, w_qkv, qv_bias, w_out, out_bias, head_scale, ln1_gain, ln1_bias, ln2_gain, ln2_bias,
    ln3_gain, ln3_bias, w_fc1, fc1_bias, ln4_gain, ln4_bias, w_fc2, fc2_bias,
):
    params = (
        qv_bias, out_bias, head_scale, ln1_gain, ln1_bias, ln2_gain, ln2_bias, ln3_gain, ln3_bias,
        fc1_bias, ln4_gain, ln4_bias, fc2_bias,
    )
    params = [p.reshape(-1, p.shape[-1]) for p in params]
    weights = (w_qkv, w_out, w_fc1, w_fc2)
    got = whole_layer(layer_input, cotangent, weights, params)
    output, grad_input, qkv, out, up, down, *smalls = write_results(got, tuple(w.shape for w in weights))
    rows = [s.reshape(-1) for s in smalls]
    return (
        output, grad_input, qkv, smalls[0], out, rows[1], rows[2], rows[3], rows[4], rows[5], rows[6], rows[7], rows[8], up,
        rows[10], rows[11], rows[12], down, rows[9],
    )


def fits_pair(mesh):
    return mesh.shape["shard"] == 2 and mesh.shape["rep"] == 16


def solution(mesh):
    return jax.shard_map(
        on_pair_of_cores if fits_pair(mesh) else on_any_mesh,
        mesh=mesh,
        in_specs=(
            P(("rep", "shard"), None),
            P(("rep", "shard"), None),
            P("shard", None),
            P(None, "shard"),
            P("shard", None),
            P("shard"),
            P("shard"),
            P("shard"),
            P("shard"),
            P("shard"),
            P("shard"),
            P("shard"),
            P("shard"),
            P("shard", None),
            P("shard"),
            P("shard"),
            P("shard"),
            P("shard", None),
            P("shard"),
        ),
        out_specs=(
            P(("rep", "shard"), None),
            P(("rep", "shard"), None),
            P("shard", None),
            P(None, "shard"),
            P("shard", None),
            P("shard"),
            P("shard"),
            P("shard"),
            P("shard"),
            P("shard"),
            P("shard"),
            P("shard"),
            P("shard"),
            P("shard", None),
            P("shard"),
            P("shard"),
            P("shard"),
            P("shard", None),
            P("shard"),
        ),
        check_vma=False,
    )
```

```python
import functools

import jax
import jax.numpy as jnp
from jax import lax
from jax.experimental import pallas as pl
from jax.experimental.pallas import tpu as pltpu
from jax.sharding import PartitionSpec as P

D = 1024
HEADS = 16
HEAD_DIM = 64


EPS = 1e-05
NEG = -1e30


def norm_rows(v, gain, bias):
    centre = jnp.mean(v, axis=-1, keepdims=True)
    centred = v - centre
    spread = jnp.mean(centred * centred, axis=-1, keepdims=True)
    return centred * lax.rsqrt(spread + EPS) * gain + bias


def ffn_middle(hidden, gain, bias):
    return norm_rows(jax.nn.gelu(hidden, approximate=False), gain, bias)


def causal_mask(index, qblock, length):
    rows = index * qblock + lax.iota(jnp.int32, qblock)
    cols = lax.iota(jnp.int32, length)
    return (cols[None, :] <= rows[:, None])[None]


def block_scores(queries, keys_all, index, qblock, scale):
    length = keys_all.shape[0]
    scores = (
        jnp.einsum("qhd,khd->hqk", queries, keys_all, preferred_element_type=jnp.float32) * scale
    )
    return (queries, jnp.where(causal_mask(index, qblock, length), scores, NEG))


def attend_forward(queries, keys_all, values_all, scale):
    length, heads, width = queries.shape
    qblock = min(512, length)
    blocks = length // qblock

    def one_block(index):
        rows_q, scores = block_scores(queries, keys_all, index, qblock, scale)
        total = jax.nn.logsumexp(scores, axis=-1, keepdims=True)
        probs = jnp.exp(scores - total).astype(jnp.bfloat16)
        outcome = jnp.einsum("hqk,khd->qhd", probs, values_all, preferred_element_type=jnp.float32)
        return (outcome, total)

    outcome, totals = lax.map(one_block, jnp.arange(blocks, dtype=jnp.int32))
    return (outcome.reshape(length, heads, width), totals)


def attend_backward(queries, keys_all, values_all, totals, grad_out, scale):
    length, heads, width = queries.shape
    qblock = min(512, length)
    blocks = length // qblock

    def one_block(carry, index):
        grad_keys, grad_values = carry
        rows_q, scores = block_scores(queries, keys_all, index, qblock, scale)
        probs = jnp.exp(scores - totals[index])
        probs_low = probs.astype(jnp.bfloat16)
        grad_values = grad_values + jnp.einsum(
            "hqk,qhd->khd", probs_low, grad_out, preferred_element_type=jnp.float32
        )
        grad_probs = jnp.einsum(
            "qhd,khd->hqk", grad_out, values_all, preferred_element_type=jnp.float32
        )
        row_dot = jnp.sum(probs * grad_probs, axis=-1, keepdims=True)
        grad_scores = (probs * (grad_probs - row_dot)).astype(jnp.bfloat16)
        grad_rows = (
            jnp.einsum("hqk,khd->qhd", grad_scores, keys_all, preferred_element_type=jnp.float32)
            * scale
        )
        grad_keys = (
            grad_keys
            + jnp.einsum("hqk,qhd->khd", grad_scores, rows_q, preferred_element_type=jnp.float32)
            * scale
        )
        return ((grad_keys, grad_values), grad_rows)

    empty = jnp.zeros((length, heads, width), jnp.float32)
    (grad_keys, grad_values), grad_queries = lax.scan(
        one_block, (empty, empty), jnp.arange(blocks, dtype=jnp.int32)
    )
    return (grad_queries.reshape(length, heads, width), grad_keys, grad_values)


def on_any_mesh(
    layer_input,
    cotangent,
    w_qkv,
    qv_bias,
    w_out,
    out_bias,
    head_scale,
    ln1_gain,
    ln1_bias,
    ln2_gain,
    ln2_bias,
    ln3_gain,
    ln3_bias,
    w_fc1,
    fc1_bias,
    ln4_gain,
    ln4_bias,
    w_fc2,
    fc2_bias,
):
    low_qkv = w_qkv.astype(jnp.bfloat16)
    low_out = w_out.astype(jnp.bfloat16)
    low_heads = head_scale.astype(jnp.bfloat16)
    low_up = w_fc1.astype(jnp.bfloat16)
    low_down = w_fc2.astype(jnp.bfloat16)
    whole = (
        lax.all_gather(low_qkv, "shard", axis=0, tiled=True),
        lax.all_gather(qv_bias.astype(jnp.bfloat16), "shard", axis=1, tiled=True),
        lax.all_gather(low_out, "shard", axis=0, tiled=True),
        lax.all_gather(out_bias.astype(jnp.bfloat16), "shard", axis=0, tiled=True),
        lax.all_gather(low_heads, "shard", axis=0, tiled=True),
        lax.all_gather(ln1_gain.astype(jnp.bfloat16), "shard", axis=0, tiled=True),
        lax.all_gather(ln1_bias.astype(jnp.bfloat16), "shard", axis=0, tiled=True),
        lax.all_gather(ln2_gain.astype(jnp.bfloat16), "shard", axis=0, tiled=True),
        lax.all_gather(ln2_bias.astype(jnp.bfloat16), "shard", axis=0, tiled=True),
        lax.all_gather(ln3_gain.astype(jnp.bfloat16), "shard", axis=0, tiled=True),
        lax.all_gather(ln3_bias.astype(jnp.bfloat16), "shard", axis=0, tiled=True),
        lax.all_gather(low_up, "shard", axis=0, tiled=True),
        lax.all_gather(fc1_bias.astype(jnp.bfloat16), "shard", axis=0, tiled=True),
        lax.all_gather(ln4_gain.astype(jnp.bfloat16), "shard", axis=0, tiled=True),
        lax.all_gather(ln4_bias.astype(jnp.bfloat16), "shard", axis=0, tiled=True),
        lax.all_gather(low_down, "shard", axis=0, tiled=True),
        lax.all_gather(fc2_bias.astype(jnp.bfloat16), "shard", axis=0, tiled=True),
    )
    weight_qkv, weight_out, weight_up, weight_down = (whole[0], whole[2], whole[11], whole[15])
    (
        bias_qv,
        bias_out,
        head_gain,
        gain_one,
        shift_one,
        gain_two,
        shift_two,
        gain_three,
        shift_three,
        bias_up,
        gain_four,
        shift_four,
        bias_down,
    ) = tuple(
        (whole[index].astype(jnp.float32) for index in (1, 3, 4, 5, 6, 7, 8, 9, 10, 12, 13, 14, 16))
    )
    length = layer_input.shape[0]
    scale = HEAD_DIM ** (-0.5)
    inputs = layer_input.astype(jnp.float32)
    normed_one, pull_one = jax.vjp(norm_rows, inputs, gain_one, shift_one)
    act_one = normed_one.astype(jnp.bfloat16)
    bias_full = jnp.concatenate([bias_qv[0], jnp.zeros((D,), jnp.float32), bias_qv[1]])
    qkv = (jnp.dot(act_one, weight_qkv, preferred_element_type=jnp.float32) + bias_full).astype(
        jnp.bfloat16
    )
    triple = qkv.reshape(length, 3, HEADS, HEAD_DIM)
    queries = triple[:, 0]
    keys_all = triple[:, 1]
    values_all = triple[:, 2]
    attended, totals = attend_forward(queries, keys_all, values_all, scale)
    mixed = (attended * head_gain[:, None]).reshape(length, D).astype(jnp.bfloat16)
    branch = jnp.dot(mixed, weight_out, preferred_element_type=jnp.float32) + bias_out
    normed_two, pull_two = jax.vjp(norm_rows, branch, gain_two, shift_two)
    middle = inputs + normed_two
    normed_three, pull_three = jax.vjp(norm_rows, middle, gain_three, shift_three)
    act_three = normed_three.astype(jnp.bfloat16)
    hidden = jnp.dot(act_three, weight_up, preferred_element_type=jnp.float32) + bias_up
    normed_four, pull_four = jax.vjp(ffn_middle, hidden, gain_four, shift_four)
    act_four = normed_four.astype(jnp.bfloat16)
    result = middle + (
        jnp.dot(act_four, weight_down, preferred_element_type=jnp.float32) + bias_down
    )
    output = result.astype(jnp.bfloat16)
    again = (
        lax.all_gather(low_qkv, "shard", axis=0, tiled=True),
        lax.all_gather(low_out, "shard", axis=0, tiled=True),
        lax.all_gather(low_heads, "shard", axis=0, tiled=True),
        lax.all_gather(low_up, "shard", axis=0, tiled=True),
        lax.all_gather(low_down, "shard", axis=0, tiled=True),
    )
    back_qkv, back_out, back_up, back_down = (again[0], again[1], again[3], again[4])
    back_heads = again[2].astype(jnp.float32)
    cot_full = cotangent.astype(jnp.float32)
    grad_down_bias = jnp.sum(cot_full, axis=0)
    grad_down = jnp.einsum("tf,td->fd", act_four, cotangent, preferred_element_type=jnp.float32)
    grad_four = jnp.einsum("td,fd->tf", cotangent, back_down, preferred_element_type=jnp.float32)
    grad_hidden, grad_gain_four, grad_shift_four = pull_four(grad_four)
    hidden_low = grad_hidden.astype(jnp.bfloat16)
    grad_up_bias = jnp.sum(hidden_low, axis=0, dtype=jnp.float32)
    grad_up = jnp.einsum("td,tf->df", act_three, hidden_low, preferred_element_type=jnp.float32)
    grad_three = jnp.einsum("tf,df->td", hidden_low, back_up, preferred_element_type=jnp.float32)
    grad_mid_part, grad_gain_three, grad_shift_three = pull_three(grad_three)
    grad_middle = cot_full + grad_mid_part
    grad_branch, grad_gain_two, grad_shift_two = pull_two(grad_middle)
    branch_low = grad_branch.astype(jnp.bfloat16)
    grad_out_b = jnp.sum(branch_low, axis=0, dtype=jnp.float32)
    grad_out_w = jnp.einsum("td,te->de", mixed, branch_low, preferred_element_type=jnp.float32)
    grad_mixed = jnp.einsum("te,de->td", branch_low, back_out, preferred_element_type=jnp.float32)
    grad_mixed = grad_mixed.reshape(length, HEADS, HEAD_DIM)
    grad_heads = jnp.sum(grad_mixed * attended, axis=(0, 2))
    grad_attended = (grad_mixed * back_heads[:, None]).astype(jnp.bfloat16)
    grad_queries, grad_keys, grad_values = attend_backward(
        queries, keys_all, values_all, totals, grad_attended, scale
    )
    grad_qkv = (
        jnp.stack([grad_queries, grad_keys, grad_values], axis=1)
        .reshape(length, 3 * D)
        .astype(jnp.bfloat16)
    )
    grad_qv = jnp.stack(
        [
            jnp.sum(grad_qkv[:, :D], axis=0, dtype=jnp.float32),
            jnp.sum(grad_qkv[:, 2 * D :], axis=0, dtype=jnp.float32),
        ]
    )
    grad_qkv_w = jnp.einsum("td,te->de", act_one, grad_qkv, preferred_element_type=jnp.float32)
    grad_one = jnp.einsum("te,de->td", grad_qkv, back_qkv, preferred_element_type=jnp.float32)
    grad_in_part, grad_gain_one, grad_shift_one = pull_one(grad_one)
    grad_input = grad_middle + grad_in_part
    shares = (
        lax.psum_scatter(grad_qkv_w, "shard", scatter_dimension=0, tiled=True),
        lax.psum_scatter(grad_qv, "shard", scatter_dimension=1, tiled=True),
        lax.psum_scatter(grad_out_w, "shard", scatter_dimension=0, tiled=True),
        lax.psum_scatter(grad_out_b, "shard", scatter_dimension=0, tiled=True),
        lax.psum_scatter(grad_heads, "shard", scatter_dimension=0, tiled=True),
        lax.psum_scatter(grad_gain_one, "shard", scatter_dimension=0, tiled=True),
        lax.psum_scatter(grad_shift_one, "shard", scatter_dimension=0, tiled=True),
        lax.psum_scatter(grad_gain_two, "shard", scatter_dimension=0, tiled=True),
        lax.psum_scatter(grad_shift_two, "shard", scatter_dimension=0, tiled=True),
        lax.psum_scatter(grad_gain_three, "shard", scatter_dimension=0, tiled=True),
        lax.psum_scatter(grad_shift_three, "shard", scatter_dimension=0, tiled=True),
        lax.psum_scatter(grad_up, "shard", scatter_dimension=0, tiled=True),
        lax.psum_scatter(grad_up_bias, "shard", scatter_dimension=0, tiled=True),
        lax.psum_scatter(grad_gain_four, "shard", scatter_dimension=0, tiled=True),
        lax.psum_scatter(grad_shift_four, "shard", scatter_dimension=0, tiled=True),
        lax.psum_scatter(grad_down, "shard", scatter_dimension=0, tiled=True),
        lax.psum_scatter(grad_down_bias, "shard", scatter_dimension=0, tiled=True),
    )
    summed = lax.psum(
        (
            shares[0],
            shares[1],
            shares[2],
            shares[3],
            shares[4],
            shares[5],
            shares[6],
            shares[7],
            shares[8],
            shares[9],
            shares[10],
            shares[11],
            shares[12],
            shares[13],
            shares[14],
            shares[15],
            shares[16],
        ),
        "rep",
    )
    return (output, grad_input) + tuple(summed)


MESH = pl.DeviceIdType.MESH
BF16 = jnp.bfloat16
F32 = jnp.float32
UNIT_ROWS = 256
UNIT_COLS = 1024
MIB = 1 << 20
SLOT = {
    "d1": 0, "d2": 1, "z1": 2, "z3": 2, "z2": 3, "u1": 4, "w1": 4, "u2": 5, "w2": 5, "u3": 6, "w3": 6, "g1": 7, "g2": 8,
}


def unit_table(dims):
    table = []
    for matrix in (3, 2, 1, 0):
        rows, cols = dims[matrix]
        for col in range(0, cols, UNIT_COLS):
            for row in range(0, rows, UNIT_ROWS):
                table.append((matrix, row, col))
    return table


KINDS = (
    "QX", "QX", "QX", "QY", "QY", "QY", "QY", "QY", "Y", "X", "X", "Y", "ZY", "ZY", "X", "Y", "X", "X", "ZY",
    "Y", "Y", "X", "ZY", "X",
)
TASK, VECTORS = 24, 25
ORDER = (
    1, 5, 24, 2, 3, 5, 0, 24, 4, 0, 4, 24, 2, 24, 24, 1, 24, 24, 24, 24, 24, 24, 24, 6, 5, 7, 4, 10, 6, 8, 11,
    7, 13, 2, 24, 24, 14, 15, 24, 5, 4, 24, 24, 24, 5, 0, 9, 10, 4, 16, 17, 5, 13, 7, 2, 24, 12, 24, 14, 24, 24,
    4, 9, 7, 5, 24, 16, 6, 8, 7, 0, 3, 10, 19, 12, 20, 2, 23, 21, 5, 1, 9, 0, 5, 10, 7, 13, 0, 4, 12, 6, 1, 2,
    2, 9, 8, 3, 23, 0, 13, 16, 17, 4, 24, 11, 16, 22, 4, 6, 12, 7, 8, 5, 13, 24, 0, 3, 21, 9, 15, 2, 6, 16, 20,
    24, 8, 11, 13, 17, 7, 2, 16, 3, 12, 7, 22, 10, 4, 6, 15, 19, 16, 3, 11, 24, 12, 8, 8, 0, 3, 14, 15, 1, 7,
    10, 2, 20, 22, 23, 11, 17, 10, 15, 9, 1, 19, 21, 14, 25, 18, 12, 0, 20, 3, 10, 1, 13, 16, 6, 22, 21, 3, 8,
    19, 20, 1, 10, 22, 9, 16, 23, 21, 6, 20, 19, 8, 13, 7, 1, 6, 22, 23, 11, 20, 16, 18, 17, 14, 10, 23, 9, 25,
    1, 11, 23, 17, 15, 12, 4, 19, 3, 18, 19, 14, 21, 11, 22, 9, 25, 5, 16, 18, 20, 23, 8, 11, 20, 19, 15, 17,
    17, 18, 14, 17, 19, 23, 21, 12, 14, 21, 6, 18, 9, 12, 15, 17, 14, 18, 3, 0, 25, 10, 19, 21, 15, 13, 20, 23,
    22, 9, 2, 18, 13, 22, 14, 15, 22, 13, 17, 1, 19, 21, 18, 12, 20, 11, 18, 25, 8, 18, 23, 22, 14, 15, 21, 11,
)


GIVE_ROWS = 240


def program_order(units, ends):
    order, task, vector, waited, step = [], 0, 0, {3}, [0] * len(units)
    order.append(("wait", 3, 0))
    for entry in ORDER:
        if entry == TASK:
            order.append(("task", task, 0))
            task += 1
            continue
        if entry == VECTORS:
            order.append(("vec", vector, 0))
            vector += 1
            continue
        m = units[entry][0]
        if m not in waited:
            assert task >= ends[m]
            order.append(("wait", m, 0))
            waited.add(m)
        order.append(("sum", entry, step[entry]))
        step[entry] += 1
    return order


PAIRS = 2


def fold(v):
    total = v[0:8]
    for k in range(1, v.shape[0] // 8):
        total = total + v[8 * k : 8 * k + 8]
    return total


def layer_kernel(dims, at_base, g_base, *refs):
    x_in, cot_in, weights, params = refs[0], refs[1], refs[2:6], refs[6:19]
    y_out, dx_out, res, vec_out, tiles_hbm = refs[19:24]
    (
        at, g, give, pair, line_xy, line_z, ring, big, left, act, hid, qkv, probs, attended, branch, middle, dmid,
        late_in, near_left, near_right, vec_w, vec_h, rstd4, sums4, vec_in, vec_own, vec_got,
        send, recv, v_send, v_recv, p_send, p_recv, l_sem, w_in, w_keep, w_send, w_recv, w_store, t_sem, s_sem, e_sem, n_send, n_recv,
    ) = refs[24:]
    r = lax.axis_index("rep")
    c = lax.axis_index("shard")
    x, y, z = r % 2, (r // 2) % 2, r // 4
    core = {"shard": 1 - c}
    to = {
        "X": {"rep": r + 1 - 2 * x},
        "Y": {"rep": r + 2 - 4 * y},
        "U": {"rep": r + 4},
        "D": {"rep": r - 4},
        "XY": {"rep": r + 3 - 2 * x - 4 * y},
    }
    line_end = (z == 0) | (z == 3)
    line_mid = (z == 1) | (z == 2)
    outward = {"rep": r + 4 * (2 * (z // 2) - 1)}
    inward = {"rep": r + 4 * (1 - 2 * (z // 2))}
    across = {"rep": r + 4 * (3 - 2 * z)}
    upper = z // 2
    length = x_in.shape[0]
    width = x_in.shape[1]
    half_w = width // 2
    hidden = dims[2][1]
    half_h = hidden // 2
    blocks = hidden // width
    TILE = 512

    tile_of = []
    for m, (rows, cols) in enumerate(dims):
        for row in range(0, rows, TILE):
            for col in range(0, cols, UNIT_COLS):
                tile_of.append((m, row, col))
    first_tile = [min(t for t, v in enumerate(tile_of) if v[0] == m) for m in range(4)]
    parts = 2 * len(tile_of)
    slots_f, slots_b, late, slots_l, slots_g = 6, 16, 16, 2, 6

    def part_read(i):
        m, row, col = tile_of[i // 2]
        return pltpu.make_async_copy(
            weights[m].at[pl.ds(row + (i % 2) * 256, 256), pl.ds(col, UNIT_COLS)],
            late_in.at[pl.ds((i % slots_l) * 256, 256), :] if i >= late else big.at[pl.ds((i % slots_f) * 256, 256), :],
            w_in.at[slots_f + i % slots_l if i >= late else i % slots_f],
        )

    def low_row(i):
        return (late + (i - late) % slots_g) * 256 if i >= late else i * 256

    def part_low(i):
        return low_buf.at[pl.ds(low_row(i), 256), :]

    low_buf = give

    def part_place(i):
        return tiles_hbm.at[c, i // 2, pl.ds((i % 2) * 256, 256), :]

    def part_keep(i):
        return pltpu.make_async_copy(part_low(i), part_place(i), w_keep.at[i % slots_b])

    def part_landing(i):
        if i < 8:
            return res.at[i]
        return ring.at[(i - 8) // 2, pl.ds((i % 2) * 256, 256), :]

    def part_store(i):
        far = tiles_hbm.at[1 - c, i // 2, pl.ds((i % 2) * 256, 256), :]
        return pltpu.make_async_copy(part_landing(i), far, w_store.at[i])

    def part_give(i):
        return pltpu.make_async_remote_copy(
            src_ref=part_low(i), dst_ref=part_landing(i) if i < late else part_place(i), send_sem=w_send.at[i % slots_b], recv_sem=w_recv.at[i],
            device_id=core, device_id_type=MESH,
        )

    def part_got(i):
        return pltpu.make_async_remote_copy(
            src_ref=part_low(i),
            dst_ref=part_landing(i) if i < late else tiles_hbm.at[1 - c, i // 2, pl.ds((i % 2) * 256, 256), :],
            send_sem=w_send.at[i % slots_b], recv_sem=w_recv.at[i], device_id=core, device_id_type=MESH,
        )

    for i in range(slots_f):
        part_read(i).start()

    barrier = pltpu.get_barrier_semaphore()
    for peer in (core, to["X"], to["Y"], to["XY"]):
        pl.semaphore_signal(barrier, inc=1, device_id=peer, device_id_type=MESH)

    @pl.when(z < 3)
    def _():
        pl.semaphore_signal(barrier, inc=1, device_id=to["U"], device_id_type=MESH)

    @pl.when(z > 0)
    def _():
        pl.semaphore_signal(barrier, inc=1, device_id=to["D"], device_id_type=MESH)

    @pl.when(line_end)
    def _():
        pl.semaphore_signal(barrier, inc=1, device_id=across, device_id_type=MESH)

    narrow = (0, 0, 2, 3, 4, 5, 6, 7, 8, 9, 10)

    def rounded(v):
        return v.astype(BF16).astype(F32)

    lane_w = pl.ds(pl.multiple_of(c * half_w, half_w), half_w)
    lane_h = pl.ds(pl.multiple_of(c * half_h, half_h), half_h)
    (qv_ref, ob_ref, hs_ref, g1_ref, b1_ref, g2_ref, b2_ref, g3_ref, b3_ref, ub_ref, g4_ref, b4_ref, db_ref) = params
    vec_w[0:2, lane_w] = rounded(qv_ref[...])
    for row, ref in zip((2, 4, 5, 6, 7, 8, 9, 10), (ob_ref, g1_ref, b1_ref, g2_ref, b2_ref, g3_ref, b3_ref, db_ref)):
        vec_w[row : row + 1, lane_w] = rounded(ref[...])
    head_of = lax.broadcasted_iota(jnp.int32, (1, half_w), 1) // 64
    spread = jnp.zeros((1, half_w), F32)
    for h in range(half_w // 64):
        spread = jnp.where(head_of == h, rounded(hs_ref[0:1, h : h + 1]), spread)
    vec_w[3:4, lane_w] = spread
    for row, ref in enumerate((ub_ref, g4_ref, b4_ref)):
        vec_h[row : row + 1, lane_h] = rounded(ref[...])
    QB, VB, OB, HS, G1, B1, G2, B2, G3, B3, DB = range(11)
    UB, G4, B4 = range(3)

    def small_copy(k, give_it):
        ref, lane, far = ((vec_w, lane_w, 1 - c), (vec_h, lane_h, 1 - c))[k]
        size = half_w if k == 0 else half_h
        other = pl.ds(pl.multiple_of((1 - c) * size, size), size)
        here = ref.at[:, lane]
        return pltpu.make_async_remote_copy(
            src_ref=here, dst_ref=here if give_it else ref.at[:, other], send_sem=s_sem.at[k, 0], recv_sem=s_sem.at[k, 1],
            device_id=core, device_id_type=MESH,
        )

    e_copy = pltpu.make_async_copy(cot_in, g.at[pl.ds(0, length), pl.ds(g_base[3], width)], e_sem.at[0])
    e_copy.start()

    def left_own(m):
        rows = dims[m][0]
        return pltpu.make_async_copy(
            left.at[pl.ds(pl.multiple_of(2 * at_base[m] + c * rows, 512), rows), :],
            at.at[pl.ds(at_base[m], rows), pl.ds(0, length)],
            l_sem.at[m],
        )

    def left_far(m):
        rows = dims[m][0]
        return pltpu.make_async_remote_copy(
            src_ref=left.at[pl.ds(pl.multiple_of(2 * at_base[m] + (1 - c) * rows, 512), rows), :],
            dst_ref=at.at[pl.ds(at_base[m], rows), pl.ds(length, length)],
            send_sem=p_send.at[m, 0], recv_sem=p_recv.at[m, 0], device_id=core, device_id_type=MESH,
        )

    def right_far(m):
        cols = pl.ds(g_base[m], dims[m][1])
        return pltpu.make_async_remote_copy(
            src_ref=g.at[pl.ds(0, length), cols], dst_ref=g.at[pl.ds(length, length), cols],
            send_sem=p_send.at[m, 1], recv_sem=p_recv.at[m, 1], device_id=core, device_id_type=MESH,
        )

    def start_left(m):
        left_own(m).start()
        left_far(m).start()

    def wait_pair(m):
        left_own(m).wait()
        left_far(m).wait()
        right_far(m).wait()

    converted, kept_parts, given_parts = [0], set(), set()

    def kept(i):
        if i not in kept_parts:
            kept_parts.add(i)
            part_keep(i).wait()

    def given(i):
        if i not in given_parts:
            given_parts.add(i)
            part_give(i).wait_send()

    def convert_parts(upto):
        for i in range(converted[0], upto):
            part_read(i).wait()
            if i >= slots_b:
                kept(i - slots_b)
                given(i - slots_b)
            if i >= late + slots_g:
                kept(i - slots_g)
                given(i - slots_g)
            source, first = (late_in, i % slots_l * 256) if i >= late else (big, i % slots_f * 256)

            def convert(b, _, i=i, source=source, first=first):
                rows = pl.multiple_of(first + b * 32, 32)
                low = pl.multiple_of(low_row(i) + b * 32, 32)
                low_buf[pl.ds(low, 32), :] = source[pl.ds(rows, 32), :].astype(BF16)
                return 0

            lax.fori_loop(0, 8, convert, 0)
            part_keep(i).start()
            if i == 0:
                pl.semaphore_wait(barrier, 6)
                small_copy(0, True).start()
                small_copy(1, True).start()
            part_give(i).start()
            if i >= late and i + slots_l < parts:
                part_read(i + slots_l).start()
            if i + slots_f < late:
                part_read(i + slots_f).start()
            if i == late - slots_f:
                for k in range(slots_l):
                    part_read(late + k).start()
        converted[0] = max(converted[0], upto)

    def cotangent_copy(k, relay):
        here, there = pl.ds(0, length), pl.ds(length, length)
        cols = pl.ds(g_base[3], width)
        return pltpu.make_async_remote_copy(
            src_ref=near_right.at[k, here, :] if relay else near_right.at[0, here, :] if k == 2 else g.at[here, cols],
            dst_ref=near_right.at[k, there if relay else here, :],
            send_sem=n_send.at[k, int(relay)], recv_sem=n_recv.at[k, int(relay)],
            device_id=core if relay else to["XYY"[k]], device_id_type=MESH,
        )

    convert_parts(2)
    e_copy.wait()
    right_far(3).start()
    cotangent_copy(0, False).start()
    cotangent_copy(1, False).start()
    convert_parts(4)

    def tile(m, half, index):
        return (half, first_tile[m] + index)

    stream = []
    per_half = dims[3][0] // TILE
    stream += [tile(3, h, k) for h in range(2) for k in range(per_half)]
    for m in (2, 1, 0):
        for index in range(dims[m][1] // UNIT_COLS):
            stream += [tile(m, 0, index), tile(m, 1, index)]
    slots_t = 4
    here = set()

    def tile_load(i):
        half, t = stream[i]
        return pltpu.make_async_copy(
            tiles_hbm.at[half, t], ring.at[i % slots_t], t_sem.at[i % slots_t]
        )

    def tile_start(i):
        half, t = stream[i]
        if (1, t) not in here:
            here.add((1, t))
            convert_parts(2 * t + 2)
            for k in (2 * t, 2 * t + 1):
                kept(k)
                if k >= late:
                    part_got(k).wait_recv()
        tile_load(i).start()

    at_tile, started, allowed_to = [0], [0], [0]

    def fill(limit=None):
        if limit is not None:
            allowed_to[0] = limit
        while started[0] < min(at_tile[0] + slots_t, allowed_to[0], len(stream)):
            tile_start(started[0])
            started[0] += 1

    def next_tile(ahead=0):
        i = at_tile[0] + ahead
        assert i < started[0]
        tile_load(i).wait()
        return ring.at[i % slots_t]

    def done_tile(count=1):
        at_tile[0] += count
        fill()

    def mean(v):
        return jnp.sum(v, axis=-1, keepdims=True) / v.shape[-1]

    def normal(v):
        centred = v - mean(v)
        scale = lax.rsqrt(mean(centred * centred) + 1e-05)
        return centred * scale, scale

    def each(fn, step=32, init=0, unroll=1):
        def body(i, carry):
            return fn(pl.ds(pl.multiple_of(i * step, step), step), carry)

        return lax.fori_loop(0, length // step, body, init, unroll=unroll)

    def w_row(i):
        return vec_w[i : i + 1, :]

    def turn(source, m, block=0):
        for k in range(width // 256):
            row = 2 * at_base[m] + block * width + k * 256
            left[row : row + 256, :] = jnp.transpose(source[:, k * 256 : (k + 1) * 256])

    NT = (((1,), (1,)), ((), ()))
    TN = (((0,), (0,)), ((), ()))

    def nt(a, b):
        return lax.dot_general(a, b, NT, preferred_element_type=F32)

    def tn(a, b):
        return lax.dot_general(a, b, TN, preferred_element_type=F32)

    def product_pair(source, write, t):
        convert_parts(2 * t + 2)
        for i in (2 * t, 2 * t + 1):
            part_got(i).wait_recv()
            part_store(i).start()
        far = (part_landing(2 * t), part_landing(2 * t + 1))
        for k in range(UNIT_COLS // 256):
            cols = slice(k * 256, (k + 1) * 256)
            own = low_buf[512 * t : 512 * (t + 1), cols]
            value = jnp.dot(source[:, lane_w], own, preferred_element_type=F32)
            for n in range(2):
                lanes = pl.ds(pl.multiple_of((1 - c) * half_w + n * 256, 256), 256)
                value = value + jnp.dot(source[:, lanes], far[n][:, cols], preferred_element_type=F32)
            write(cols, value)

    small_copy(0, True).wait_send()
    small_copy(1, True).wait_send()
    small_copy(0, False).wait_recv()
    small_copy(1, False).wait_recv()

    def first_norm(rows, _):
        hat, _s = normal(x_in[rows, :].astype(F32))
        act[rows, :] = (hat * w_row(G1) + w_row(B1)).astype(BF16)
        return 0

    each(first_norm, unroll=2)
    for index in range(3):

        def put_qkv(cols, value, index=index):
            if index == 0:
                value = value + vec_w[QB : QB + 1, cols]
            if index == 2:
                value = value + vec_w[VB : VB + 1, cols]
            qkv[:, index * width + cols.start : index * width + cols.stop] = value.astype(BF16)

        product_pair(act, put_qkv, first_tile[0] + index)
        convert_parts(10 + 2 * index)
    turn(act, 0)
    start_left(0)
    convert_parts(16)
    for k in range(2):
        cotangent_copy(k, False).wait()
        cotangent_copy(k, True).start()
    cotangent_copy(2, False).start()

    low_lane = lax.broadcasted_iota(jnp.int32, (length, 128), 1) < 64
    allowed = lax.broadcasted_iota(jnp.int32, (length, length), 1) <= lax.broadcasted_iota(
        jnp.int32, (length, length), 0
    )
    scale = 64 ** (-0.5)
    keep_lane = (low_lane.astype(F32).astype(BF16), jnp.logical_not(low_lane).astype(F32).astype(BF16))

    def split_heads(v):
        return jnp.concatenate([v * keep_lane[0], v * keep_lane[1]], axis=0)

    def attend(p):
        q = qkv[:, pl.ds(pl.multiple_of(p * 128, 128), 128)]
        k = qkv[:, pl.ds(pl.multiple_of(width + p * 128, 128), 128)]
        v = qkv[:, pl.ds(pl.multiple_of(2 * width + p * 128, 128), 128)]
        both = nt(q, split_heads(k)) * scale
        got = []
        for h in range(2):
            scores = jnp.where(allowed, both[:, h * length : (h + 1) * length], -1e30)
            top = jnp.max(scores, axis=-1, keepdims=True)
            lse = top + jnp.log(jnp.sum(jnp.exp(scores - top), axis=-1, keepdims=True))
            got.append(jnp.exp(scores - lse))
        prob = jnp.concatenate(got, axis=1)
        probs[p] = prob
        value = jnp.dot(prob.astype(BF16), split_heads(v), preferred_element_type=F32)
        cols = pl.ds(pl.multiple_of(p * 128, 128), 128)
        attended[:, cols] = value
        act[:, cols] = (value * vec_w[HS : HS + 1, cols]).astype(BF16)

    def attend_some(i, _):
        for n in range(PAIRS):
            attend(i * PAIRS + n)
        return 0

    lax.fori_loop(0, width // 128 // PAIRS, attend_some, 0)

    def put_branch(cols, value):
        branch[:, cols] = value + vec_w[OB : OB + 1, cols]

    product_pair(act, put_branch, first_tile[1])
    turn(act, 1)
    start_left(1)

    def second_norm(rows, _):
        hat, _s = normal(branch[rows, :])
        mid = x_in[rows, :].astype(F32) + (hat * w_row(G2) + w_row(B2))
        middle[rows, :] = mid
        hat, _s = normal(mid)
        act[rows, :] = (hat * w_row(G3) + w_row(B3)).astype(BF16)
        return 0

    each(second_norm, unroll=2)
    U0, H0, D0 = 0, blocks * length, 2 * blocks * length
    for j in range(blocks):

        def put_hidden(cols, value, j=j):
            wide = slice(j * width + cols.start, j * width + cols.stop)
            big[U0 + j * length : U0 + (j + 1) * length, cols] = value + vec_h[UB : UB + 1, wide]

        product_pair(act, put_hidden, first_tile[2] + j)
        convert_parts(min(late + 2 * (j + 1), late + slots_g))
    turn(act, 2)
    start_left(2)
    root_half = 0.7071067811865476

    def near(base, start):
        return pl.ds(pl.multiple_of(base + start, 16), 16)

    def hidden_norm(rows, _):
        total = jnp.zeros((16, 1), F32)
        for j in range(blocks):
            u = big[near(U0 + j * length, rows.start), :]
            h = u * (1.0 + lax.erf(u * root_half)) * 0.5
            big[near(H0 + j * length, rows.start), :] = h
            total = total + jnp.sum(h, axis=-1, keepdims=True)
        centre = total / hidden
        total = jnp.zeros((16, 1), F32)
        for j in range(blocks):
            h = big[near(H0 + j * length, rows.start), :] - centre
            total = total + jnp.sum(h * h, axis=-1, keepdims=True)
        s = lax.rsqrt(total / hidden + 1e-05)
        rstd4[rows, :] = jnp.broadcast_to(s, (16, 128))
        for j in range(blocks):
            at_h = near(H0 + j * length, rows.start)
            hat = (big[at_h, :] - centre) * s
            big[at_h, :] = hat
            cols = slice(j * width, (j + 1) * width)
            hid[near(j * length, rows.start), :] = (
                hat * vec_h[G4 : G4 + 1, cols] + vec_h[B4 : B4 + 1, cols]
            ).astype(BF16)
        return 0

    cotangent_copy(2, False).wait()
    cotangent_copy(2, True).start()
    each(hidden_norm, 16)
    for j in range(blocks):
        turn(hid.at[pl.ds(j * length, length), :], 3, j)
    start_left(3)
    convert_parts(parts)
    for i in range(late):
        part_store(i).wait()
        kept(i)
        given(i)

    tasks = []
    zeros8 = jnp.zeros((8, width), F32)
    dirs = g.at[pl.ds(0, length), :]

    def put_sum(row, value):
        line = jnp.sum(value, axis=0, keepdims=True)
        vec_in[0, row : row + 1, :] = line[:, 0:half_w]
        vec_in[1, row : row + 1, :] = line[:, half_w:width]

    def task_down(h, k):
        def run():
            w = next_tile()
            row = h * dims[3][0] + k * TILE
            j, lane = row // width, row % width
            if h == 0 and k == 0:
                y_acc[...] = middle[...] + w_row(DB)
            for n in range(TILE // 256):
                big[D0 + j * length : D0 + (j + 1) * length, lane + n * 256 : lane + (n + 1) * 256] = nt(
                    dirs[:, g_base[3] : g_base[3] + width], w[n * 256 : (n + 1) * 256, :]
                )

            for n in range(width // 256):
                cols = slice(n * 256, (n + 1) * 256)
                y_acc[:, cols] += jnp.dot(
                    hid[j * length : (j + 1) * length, lane : lane + TILE], w[:, cols], preferred_element_type=F32
                )
            done_tile()
            if h == 1 and k == per_half - 1:
                y_out[...] = y_acc[...].astype(BF16)

        return run

    y_acc = dmid
    for h in range(2):
        for k in range(per_half):
            tasks.append((1.2, task_down(h, k)))

    def task_hidden(first, count):
        def run():
            if first == 0:
                sums4[...] = jnp.zeros_like(sums4)

                def e_sum(rows, carry):
                    return carry + fold(dirs[rows, g_base[3] : g_base[3] + width].astype(F32))

                put_sum(DB, each(e_sum, 32, zeros8))

            def body(i, _):
                at_r = pl.multiple_of(first + i * 16, 16)
                one = jnp.zeros((16, 1), F32)
                two = jnp.zeros((16, 1), F32)
                for j in range(blocks):
                    gain = vec_h[G4 : G4 + 1, j * width : (j + 1) * width]
                    d = big[near(D0 + j * length, at_r), :] * gain
                    hat = big[near(H0 + j * length, at_r), :]
                    one = one + jnp.sum(d, axis=-1, keepdims=True)
                    two = two + jnp.sum(d * hat, axis=-1, keepdims=True)
                one, two = one / hidden, two / hidden
                s = rstd4[pl.ds(at_r, 16), 0:1]
                for j in range(blocks):
                    cols = slice(j * width, (j + 1) * width)
                    da = big[near(D0 + j * length, at_r), :]
                    hat = big[near(H0 + j * length, at_r), :]
                    u = big[near(U0 + j * length, at_r), :]
                    dh = s * (da * vec_h[G4 : G4 + 1, cols] - one - hat * two)
                    slope = 0.5 * (1.0 + lax.erf(u * root_half)) + u * (jnp.exp(u * u * -0.5) * 0.3989422804014327)
                    du = (dh * slope).astype(BF16)
                    g[pl.ds(at_r, 16), g_base[2] + j * width : g_base[2] + (j + 1) * width] = du
                    sums4[0:8, cols] += fold(du.astype(F32))
                    sums4[8:16, cols] += fold(da * hat)
                    sums4[16:24, cols] += fold(da)
                return 0

            lax.fori_loop(0, count // 16, body, 0)
            if first + count == length:
                for i in range(3):
                    line = jnp.sum(sums4[8 * i : 8 * i + 8, :], axis=0, keepdims=True)
                    for n in range(hidden // half_w):
                        hh, k = divmod(n, half_h // half_w)
                        vec_in[hh, 11 + 4 * i + k : 12 + 4 * i + k, :] = line[:, n * half_w : (n + 1) * half_w]
                right_far(2).start()

        return run

    for first in range(0, length, 32):
        tasks.append((3.0, task_hidden(first, 32)))

    def add_pair(acc, index_of, cols_of, count, width_to):
        def make(index):
            def run():
                for h in range(2):
                    w = next_tile()
                    for n in range(TILE // 256):
                        cols = slice(h * half_w + n * 256, h * half_w + (n + 1) * 256)
                        value = nt(dirs[:, cols_of(index)], w[n * 256 : (n + 1) * 256, :])
                        if index == 0:
                            acc[:, cols] = value
                        else:
                            acc[:, cols] += value
                    done_tile()

            return run

        return [(1.2, make(index)) for index in range(count)]

    ends = {2: len(tasks)}
    acc = big.at[pl.ds(U0, length), :]
    tasks += add_pair(acc, None, lambda j: slice(g_base[2] + j * width, g_base[2] + (j + 1) * width), blocks, width)

    def task_norms():
        def body(rows, carry):
            s3g, s3b, s2g, s2b, sob = carry
            da = acc[rows, :]
            hat, s = normal(middle[rows, :])
            d = da * w_row(G3)
            d_mid = dirs[rows, g_base[3] : g_base[3] + width].astype(F32) + s * (d - mean(d) - hat * mean(d * hat))
            dmid[rows, :] = d_mid
            s3g, s3b = s3g + fold(da * hat), s3b + fold(da)
            hat, s = normal(branch[rows, :])
            d = d_mid * w_row(G2)
            dy = (s * (d - mean(d) - hat * mean(d * hat))).astype(BF16)
            s2g, s2b = s2g + fold(d_mid * hat), s2b + fold(d_mid)
            g[rows, g_base[1] : g_base[1] + width] = dy
            return (s3g, s3b, s2g, s2b, sob + fold(dy.astype(F32)))

        got = each(body, 16, (zeros8,) * 5)
        for row, value in zip((G3, B3, G2, B2, OB), got):
            put_sum(row, value)
        right_far(1).start()

    tasks.append((2.5, task_norms))
    ends[1] = len(tasks)
    d_mixed = big.at[pl.ds(U0 + length, length), :]
    tasks += add_pair(d_mixed, None, lambda j: slice(g_base[1], g_base[1] + width), 1, width)

    def task_heads():
        def body(rows, carry):
            d = d_mixed[rows, :]
            act[rows, :] = (d * w_row(HS)).astype(BF16)
            return carry + fold(d * attended[rows, :])

        put_sum(HS, each(body, 32, zeros8))

    tasks.append((0.6, task_heads))

    def task_attend(first, count):
        def run():
            def pair_of_heads(p):
                q_cols = pl.ds(pl.multiple_of(p * 128, 128), 128)
                k_cols = pl.ds(pl.multiple_of(width + p * 128, 128), 128)
                v_cols = pl.ds(pl.multiple_of(2 * width + p * 128, 128), 128)
                q, k, v, do = qkv[:, q_cols], qkv[:, k_cols], qkv[:, v_cols], act[:, q_cols]
                prob = probs[p]
                dv = tn(prob.astype(BF16), do)
                dp = nt(do, split_heads(v))
                ds = []
                for h in range(2):
                    own = slice(h * length, (h + 1) * length)
                    dot = jnp.sum(prob[:, own] * dp[:, own], axis=-1, keepdims=True)
                    ds.append(prob[:, own] * (dp[:, own] - dot))
                ds = jnp.concatenate(ds, axis=1).astype(BF16)
                dq = jnp.dot(ds, split_heads(k), preferred_element_type=F32) * scale
                dk = tn(ds, q) * scale
                g[0:length, q_cols] = dq.astype(BF16)
                g[0:length, k_cols] = jnp.where(low_lane, dk[0:length], dk[length : 2 * length]).astype(BF16)
                g[0:length, v_cols] = jnp.where(low_lane, dv[0:length], dv[length : 2 * length]).astype(BF16)

            for n in range(count):
                pair_of_heads(first + n)
            if first + count == width // 128:

                def sums(rows, carry):
                    a, b = carry
                    return (
                        a + fold(g[rows, 0:width].astype(F32)),
                        b + fold(g[rows, 2 * width : 3 * width].astype(F32)),
                    )

                a, b = each(sums, 32, (zeros8, zeros8))
                put_sum(QB, a)
                put_sum(VB, b)
                right_far(0).start()

        return run

    for first in range(0, width // 128, 2):
        tasks.append((3.0, task_attend(first, 2)))
    ends[0] = len(tasks)
    d_first = big.at[pl.ds(U0 + 2 * length, length), :]
    tasks += add_pair(d_first, None, lambda j: slice(j * width, (j + 1) * width), 3, width)

    def task_last():
        def body(rows, carry):
            sg, sb = carry
            da = d_first[rows, :]
            hat, s = normal(x_in[rows, :].astype(F32))
            d = da * w_row(G1)
            dx_out[rows, :] = dmid[rows, :] + s * (d - mean(d) - hat * mean(d * hat))
            return (sg + fold(da * hat), sb + fold(da))

        sg, sb = each(body, 16, (zeros8, zeros8))
        put_sum(G1, sg)
        put_sum(B1, sb)
        vec_in[0, 23:24, :] = jnp.zeros((1, half_w), F32)
        vec_in[1, 23:24, :] = jnp.zeros((1, half_w), F32)
        vec_copy(0).start()

    tasks.append((1.5, task_last))

    vec_steps = (core, to["X"], to["Y"], {"rep": r + 4 * (1 - 2 * (z % 2))}, across)

    def vec_copy(step):
        source = vec_in.at[1 - c] if step == 0 else vec_own.at[step]
        return pltpu.make_async_remote_copy(
            src_ref=source, dst_ref=vec_got.at[step], send_sem=v_send.at[step], recv_sem=v_recv.at[step],
            device_id=vec_steps[step], device_id_type=MESH,
        )

    def vec_task(k):
        vec_copy(k).wait_recv()
        total = (vec_in[c] if k == 0 else vec_own[k]) + vec_got[k]
        if k < 4:
            vec_own[k + 1] = total
            vec_copy(k + 1).start()
        else:
            vec_out[...] = total

    units = unit_table(dims)
    kinds = KINDS
    xy_at, z_at = {}, {}
    for unit, kind in enumerate(kinds):
        (z_at if kind[0] == "Z" else xy_at)[unit] = len(z_at) if kind[0] == "Z" else len(xy_at)

    def copy(unit, name, source, dest, device):
        return functools.partial(
            pltpu.make_async_remote_copy,
            src_ref=source, dst_ref=dest, send_sem=send.at[unit], recv_sem=recv.at[unit, SLOT[name]],
            device_id=device, device_id_type=MESH,
        )

    def rows_of(unit, start, count):
        if not isinstance(start, int):
            start = pl.multiple_of(start, 16)
        return res.at[unit, pl.ds(start, count), :]

    def product(unit, start, count, dest, dest_start, got=None, got_start=0, near_start=None):
        m, row, col = units[unit]
        step = 128 if count % 128 == 0 else min(count, 64)

        def block(index, _):
            part, strip = index // (UNIT_COLS // 256), index % (UNIT_COLS // 256)
            cols = pl.ds(pl.multiple_of(strip * 256, 256), 256)
            value = jnp.dot(
                at[pl.ds(pl.multiple_of(at_base[m] + row + start + part * step, 16), step), :],
                g[:, pl.ds(pl.multiple_of(g_base[m] + col + strip * 256, 256), 256)],
                preferred_element_type=F32,
            )
            if near_start is not None:
                for peer in range(3):
                    rows = peer * (UNIT_ROWS // 4) + near_start + part * step
                    value = value + jnp.dot(
                        near_left[unit, pl.ds(pl.multiple_of(rows, 16), step), :],
                        near_right[peer, :, pl.ds(pl.multiple_of(col + strip * 256, 256), 256)],
                        preferred_element_type=F32,
                    )
            if got is not None:
                value = value + got[pl.ds(pl.multiple_of(got_start + part * step, 16), step), cols].astype(F32)
            dest[pl.ds(pl.multiple_of(dest_start + part * step, 16), step), cols] = value.astype(BF16)
            return 0

        lax.fori_loop(0, (count // step) * (UNIT_COLS // 256), block, 0)

    def accumulate(unit, start, count, got, got_start, dest, dest_start):
        def block(strip, _):
            cols = pl.ds(pl.multiple_of(strip * 256, 256), 256)
            value = res[unit, pl.ds(pl.multiple_of(start, 16), count), cols].astype(F32)
            value = value + got[pl.ds(pl.multiple_of(got_start, 16), count), cols].astype(F32)
            dest[pl.ds(pl.multiple_of(dest_start, 16), count), cols] = value.astype(BF16)
            return 0

        lax.fori_loop(0, UNIT_COLS // 256, block, 0)

    def gather_line(unit, base, size, level):
        up, down = "u%d" % level, "w%d" % level
        low, high = z - (level - 1), z + (level - 1)

        @pl.when((low >= 0) & (z < 3))
        def _():
            part = rows_of(unit, base + low * size, size)
            copy(unit, up, part, part, to["U"])().start()

        @pl.when((high <= 3) & (z > 0))
        def _():
            part = rows_of(unit, base + high * size, size)
            copy(unit, down, part, part, to["D"])().start()

    def gather_arrived(unit, base, size, level):
        def wait(chunks):
            part = give.at[pl.ds(0, chunks * size), :]
            copy(unit, "u%d" % level, part, part, to["U"])().wait_recv()

        if level == 1:
            pl.when(line_mid)(lambda: wait(2))
        if level == 2:
            wait(1)
        else:
            pl.when(line_end)(lambda: wait(1))

    def finish(unit, ends, mids):
        def wait(rows):
            part = give.at[pl.ds(0, rows), :]
            copy(unit, "d1", part, part, to["X"])().wait_send()

        pl.when(line_end)(lambda: wait(ends))
        pl.when(line_mid)(lambda: wait(mids))

    def task_xy(unit, step):
        half, quarter, size = UNIT_ROWS // 2, UNIT_ROWS // 4, UNIT_ROWS // 16
        first, second = ("X", "Y") if kinds[unit][-1] == "X" else ("Y", "X")
        p, q = (x, y) if first == "X" else (y, x)
        by_tokens = kinds[unit][0] == "Q"
        line, block, out, other = line_xy.at[xy_at[unit]], res.at[unit], give.at[pl.ds(unit * GIVE_ROWS, GIVE_ROWS), :], pair.at[unit]
        keep, away_half = p * half, (1 - p) * half
        base = keep + q * quarter
        away = keep + (1 - q) * quarter
        at_z = half + quarter
        d1 = copy(unit, "d1", out.at[pl.ds(0, half), :], rows_of(unit, away_half, half), to[first])

        def left_for(peer):
            m, row, _ = units[unit]
            px, py = ((1 - x, y), (x, 1 - y), (1 - x, 1 - y))[peer]
            at_p, at_q = (px, py) if first == "X" else (py, px)
            rows = pl.ds(pl.multiple_of(at_base[m] + row + at_p * half + at_q * quarter, quarter), quarter)
            dest = near_left.at[unit, pl.ds(peer * quarter, quarter), :]
            return copy(unit, "d1", at.at[rows, :], dest, to[("X", "Y", "XY")[peer]])

        d2 = copy(unit, "d2", out.at[pl.ds(half, quarter), :], other.at[pl.ds(0, quarter), :], to[second])
        z1 = copy(unit, "z1", out.at[pl.ds(at_z, 3 * size), :], line.at[pl.ds(0, 3 * size), :], inward)
        z2 = copy(unit, "z2", out.at[pl.ds(at_z, 2 * size), :], line.at[pl.ds(3 * size, 2 * size), :], across)
        z3 = copy(unit, "z3", out.at[pl.ds(at_z + 2 * size, size), :], line.at[pl.ds(0, size), :], outward)
        own_quarter = rows_of(unit, base, quarter)
        g2 = copy(unit, "g2", own_quarter, own_quarter, to[second])
        own_half = rows_of(unit, keep, half)
        g1 = copy(unit, "g1", own_half, own_half, to[first])
        own = base + z * size
        if step == 0 and by_tokens:
            for peer in range(3):
                left_for(peer)().start()
        elif step == 1 and by_tokens:
            pass
        elif step == 2 and by_tokens:
            arrived = near_left.at[unit]
            copy(unit, "d1", arrived, arrived, to["X"])().wait_recv()

            product(unit, base, quarter, block, base, near_start=0)

            @pl.when(line_end)
            def _():
                from_row = pl.multiple_of(base + (1 - upper) * size, 16)
                for n in range(3):
                    out[at_z + n * size : at_z + (n + 1) * size, :] = block[pl.ds(from_row + n * size, size), :]
                z1().start()

        elif step == 0:
            product(unit, away_half, half, out, 0)
            d1().start()
        elif step == 1:
            d1().wait_recv()
            product(unit, away, quarter, out, half, block, away)
            d2().start()
            product(unit, base, quarter, block, base, block, base)
        elif step == 2:
            d2().wait_recv()

            @pl.when(line_end)
            def _():
                skip = (1 - upper) * size
                accumulate(unit, base + skip, 3 * size, other, skip, out, at_z)
                z1().start()
                accumulate(unit, own, size, other, z * size, block, own)

            @pl.when(line_mid)
            def _():
                accumulate(unit, base, quarter, other, 0, block, base)

        elif step == 3:

            @pl.when(line_mid)
            def _():
                z1().wait_recv()
                accumulate(unit, base + (1 - upper) * 2 * size, 2 * size, line, (1 - upper) * size, out, at_z)
                z2().start()
                accumulate(unit, own, size, line, upper * 2 * size, block, own)

        elif step == 4:

            @pl.when(line_mid)
            def _():
                z2().wait_recv()
                accumulate(unit, base + upper * 3 * size, size, line, (3 + upper) * size, out, at_z + 2 * size)
                z3().start()
                accumulate(unit, own, size, line, (4 - upper) * size, block, own)
                gather_line(unit, base, size, 1)

        elif step == 5:

            @pl.when(line_end)
            def _():
                z3().wait_recv()
                accumulate(unit, own, size, line, 0, block, own)
                gather_line(unit, base, size, 1)

        elif step in (6, 7):
            gather_arrived(unit, base, size, step - 5)
            gather_line(unit, base, size, step - 4)
        elif step == 8:
            gather_arrived(unit, base, size, 3)
            g2().start()
        elif step == 9:
            g2().wait_recv()
            g1().start()
        else:
            g1().wait_recv()
            sent = half + quarter + (3 * size if by_tokens else half + quarter)
            finish(unit, sent + 4 * size, sent + 8 * size)

    def task_z(unit, step):
        size, half, quarter = UNIT_ROWS // 4, UNIT_ROWS // 8, UNIT_ROWS // 16
        first, second = ("X", "Y") if kinds[unit] == "ZX" else ("Y", "X")
        p, q = (x, y) if kinds[unit] == "ZX" else (y, x)
        line, block, out, other = line_z.at[z_at[unit]], res.at[unit], give.at[pl.ds(unit * GIVE_ROWS, GIVE_ROWS), :], pair.at[unit]
        own = z * size
        keep, away_half = own + p * half, own + (1 - p) * half
        base, away = keep + q * quarter, keep + (1 - q) * quarter
        at_d = 3 * size
        z1 = copy(unit, "z1", out.at[pl.ds(0, 3 * size), :], line.at[pl.ds(0, 3 * size), :], inward)
        z2 = copy(unit, "z2", out.at[pl.ds(0, 2 * size), :], line.at[pl.ds(3 * size, 2 * size), :], across)
        z3 = copy(unit, "z3", out.at[pl.ds(2 * size, size), :], line.at[pl.ds(0, size), :], outward)
        d1 = copy(unit, "d1", out.at[pl.ds(at_d, half), :], other.at[pl.ds(0, half), :], to[first])
        d2 = copy(unit, "d2", out.at[pl.ds(at_d + half, quarter), :], other.at[pl.ds(half, quarter), :], to[second])
        own_quarter = rows_of(unit, base, quarter)
        g2 = copy(unit, "g2", own_quarter, own_quarter, to[second])
        own_half = rows_of(unit, keep, half)
        g1 = copy(unit, "g1", own_half, own_half, to[first])
        if step == 0:

            @pl.when(line_end)
            def _():
                product(unit, (1 - upper) * size, 3 * size, out, 0)
                z1().start()

        elif step == 1:

            @pl.when(line_mid)
            def _():
                z1().wait_recv()
                product(unit, (1 - upper) * 2 * size, 2 * size, out, 0, line, (1 - upper) * size)
                z2().start()
                product(unit, own, size, block, own, line, upper * 2 * size)

        elif step == 2:

            @pl.when(line_mid)
            def _():
                z2().wait_recv()
                product(unit, upper * 3 * size, size, out, 2 * size, line, (3 + upper) * size)
                z3().start()
                got = (4 - upper) * size
                accumulate(unit, away_half, half, line, got + (1 - p) * half, out, at_d)
                d1().start()
                accumulate(unit, keep, half, line, got + p * half, block, keep)

        elif step == 3:

            @pl.when(line_end)
            def _():
                z3().wait_recv()
                product(unit, away_half, half, out, at_d, line, (1 - p) * half)
                d1().start()
                product(unit, keep, half, block, keep, line, p * half)

        elif step == 4:
            d1().wait_recv()
            accumulate(unit, away, quarter, other, (1 - q) * quarter, out, at_d + half)
            d2().start()
            accumulate(unit, base, quarter, other, q * quarter, block, base)
        elif step == 5:
            d2().wait_recv()
            accumulate(unit, base, quarter, other, half, block, base)
            g2().start()
        elif step == 6:
            g2().wait_recv()
            g1().start()
        elif step == 7:
            g1().wait_recv()
            gather_line(unit, 0, size, 1)
        elif step in (8, 9):
            gather_arrived(unit, 0, size, step - 7)
            gather_line(unit, 0, size, step - 6)
        else:
            gather_arrived(unit, 0, size, 3)
            finish(unit, 2 * half + 2 * quarter + 4 * size, 2 * half + 2 * quarter + 8 * size)


    for kind, a, b in program_order(units, ends):
        if kind == "task":
            if a == 0:
                fill(len(stream))
            tasks[a][1]()
        elif kind == "wait":
            wait_pair(a)
            if a == 3:
                for k in range(3):
                    cotangent_copy(k, True).wait()
            if a == 1:
                for k in range(parts):
                    given(k)
        elif kind == "vec":
            vec_task(a)
        elif kinds[a][0] == "Z":
            task_z(a, b)
        else:
            task_xy(a, b)
    for step in range(5):
        vec_copy(step).wait_send()


def whole_layer(layer_input, cotangent, weights, params):
    dims = tuple(w.shape for w in weights)
    at_rows = sum(rows for rows, _ in dims)
    g_cols = sum(cols for _, cols in dims)
    at_base = [sum(rows for rows, _ in dims[:m]) for m in range(4)]
    g_base = [sum(cols for _, cols in dims[:m]) for m in range(4)]
    length, width = layer_input.shape
    hidden = dims[2][1]
    blocks = hidden // width
    units = unit_table(dims)
    kinds = KINDS
    n, n_z = len(units), sum(kind[0] == "Z" for kind in kinds)
    tiles = n // 2
    hbm = pl.BlockSpec(memory_space=pl.ANY)
    vmem = pl.BlockSpec(memory_space=pltpu.VMEM)
    dma = pltpu.SemaphoreType.DMA
    small = (24, width // 2)
    got = pl.pallas_call(
        functools.partial(layer_kernel, dims, at_base, g_base),
        out_shape=[
            pltpu.VMEM((length, width), BF16),
            pltpu.VMEM((length, width), F32),
            pltpu.VMEM((n, UNIT_ROWS, UNIT_COLS), BF16),
            pltpu.VMEM(small, F32),
            jax.ShapeDtypeStruct((2, tiles, 512, UNIT_COLS), BF16),
        ],
        in_specs=[vmem, hbm] + [hbm] * 4 + [vmem] * 13,
        out_specs=[vmem] * 4 + [hbm],
        scratch_shapes=[
            pltpu.VMEM((at_rows, 2 * length), BF16),
            pltpu.VMEM((2 * length, g_cols), BF16),
            pltpu.VMEM((n * GIVE_ROWS, UNIT_COLS), BF16),
            pltpu.VMEM((n, UNIT_ROWS // 4, UNIT_COLS), BF16),
            pltpu.VMEM((n - n_z, 5 * UNIT_ROWS // 16, UNIT_COLS), BF16),
            pltpu.VMEM((n_z, 5 * UNIT_ROWS // 4, UNIT_COLS), BF16),
            pltpu.VMEM((4, 512, UNIT_COLS), BF16),
            pltpu.VMEM((3 * blocks * length, width), F32),
            pltpu.VMEM((2 * at_rows, length), BF16),
            pltpu.VMEM((length, width), BF16),
            pltpu.VMEM((blocks * length, width), BF16),
            pltpu.VMEM((length, 3 * width), BF16),
            pltpu.VMEM((width // 128, length, 2 * length), F32),
            pltpu.VMEM((length, width), F32),
            pltpu.VMEM((length, width), F32),
            pltpu.VMEM((length, width), F32),
            pltpu.VMEM((length, width), F32),
            pltpu.VMEM((2 * 256, UNIT_COLS), F32),
            pltpu.VMEM((dims[3][0] // UNIT_ROWS, 3 * UNIT_ROWS // 4, 2 * length), BF16),
            pltpu.VMEM((3, 2 * length, width), BF16),
            pltpu.VMEM((16, width), F32),
            pltpu.VMEM((8, hidden), F32),
            pltpu.VMEM((length, 128), F32),
            pltpu.VMEM((24, hidden), F32),
            pltpu.VMEM((2,) + small, F32),
            pltpu.VMEM((5,) + small, F32),
            pltpu.VMEM((5,) + small, F32),
            dma((n,)),
            dma((n, 9)),
            dma((5,)),
            dma((5,)),
            dma((4, 2)),
            dma((4, 2)),
            dma((4,)),
            dma((10,)),
            dma((16,)),
            dma((16,)),
            dma((2 * tiles,)),
            dma((16,)),
            dma((4,)),
            dma((2, 2)),
            dma((1,)),
            dma((3, 2)),
            dma((3, 2)),
        ],
        compiler_params=pltpu.CompilerParams(
            collective_id=0, has_side_effects=True, vmem_limit_bytes=50 * MIB + 786432
        ),
        name="whole_layer",
    )(layer_input, cotangent, *weights, *params)
    return got[:4]


def finish_kernel(dims, *refs):
    y_in, dx_in, res, vec = refs[0:4]
    y_out, dx_out, outs, smalls = refs[4], refs[5], refs[6:10], refs[10:23]
    wide, lines, o_sem, s_sem = refs[23], refs[24:37], refs[37], refs[38]
    slots = wide.shape[0]
    copies = [pltpu.make_async_copy(y_in, y_out, s_sem.at[13]), pltpu.make_async_copy(dx_in, dx_out, s_sem.at[14])]
    rows_of = [range(0, 2)] + [range(k, k + 1) for k in range(2, 11)] + [range(11 + 4 * k, 15 + 4 * k) for k in range(3)]
    for k, rows in enumerate(rows_of):
        if k == 2:
            head_of = lax.broadcasted_iota(jnp.int32, (1, vec.shape[1]), 1) // 64
            lane = lax.broadcasted_iota(jnp.int32, lines[k].shape, 1)
            total = jnp.zeros(lines[k].shape, F32)
            for h in range(vec.shape[1] // 64):
                one = jnp.sum(jnp.where(head_of == h, vec[3:4, :], 0.0), axis=-1, keepdims=True)
                total = jnp.where(lane == h, one, total)
            lines[k][...] = total
        elif len(rows) == 4:
            for j, row in enumerate(rows):
                lines[k][:, j * vec.shape[1] : (j + 1) * vec.shape[1]] = vec[row : row + 1, :]
        else:
            lines[k][...] = vec[rows.start : rows.stop, :]
        copies.append(pltpu.make_async_copy(lines[k], smalls[k], s_sem.at[k]))
    for piece in copies:
        piece.start()
    units = unit_table(dims)

    def put(unit):
        m, row, col = units[unit]
        return pltpu.make_async_copy(
            wide.at[unit % slots], outs[m].at[pl.ds(row, UNIT_ROWS), pl.ds(col, UNIT_COLS)], o_sem.at[unit % slots]
        )

    for unit in range(len(units)):
        if unit >= slots:
            put(unit - slots).wait()

        def widen(b, _, unit=unit):
            rows = pl.ds(pl.multiple_of(b * 32, 32), 32)
            wide[unit % slots, rows, :] = res[unit, rows, :].astype(F32)
            return 0

        lax.fori_loop(0, UNIT_ROWS // 32, widen, 0)
        put(unit).start()
    for unit in range(len(units) - slots, len(units)):
        put(unit).wait()
    for piece in copies:
        piece.wait()


def write_results(got, dims):
    y, dx, _, vec = got
    half = vec.shape[1]
    small = [(2, half), (1, half), (1, half // 64)] + [(1, half)] * 7 + [(1, 4 * half)] * 3
    hbm = pl.BlockSpec(memory_space=pl.ANY)
    vmem = pl.BlockSpec(memory_space=pltpu.VMEM)
    dma = pltpu.SemaphoreType.DMA
    return pl.pallas_call(
        functools.partial(finish_kernel, dims),
        out_shape=[jax.ShapeDtypeStruct(y.shape, BF16), jax.ShapeDtypeStruct(dx.shape, F32)]
        + [jax.ShapeDtypeStruct(d, F32) for d in dims]
        + [jax.ShapeDtypeStruct(s, F32) for s in small],
        in_specs=[vmem] * 4,
        out_specs=[hbm] * 19,
        scratch_shapes=[pltpu.VMEM((6, UNIT_ROWS, UNIT_COLS), F32)]
        + [pltpu.VMEM(s, F32) for s in small]
        + [dma((6,)), dma((15,))],
        compiler_params=pltpu.CompilerParams(vmem_limit_bytes=30 * MIB),
        name="write_results",
    )(*got)


def on_pair_of_cores(
    layer_input, cotangent, w_qkv, qv_bias, w_out, out_bias, head_scale, ln1_gain, ln1_bias, ln2_gain, ln2_bias,
    ln3_gain, ln3_bias, w_fc1, fc1_bias, ln4_gain, ln4_bias, w_fc2, fc2_bias,
):
    params = (
        qv_bias, out_bias, head_scale, ln1_gain, ln1_bias, ln2_gain, ln2_bias, ln3_gain, ln3_bias,
        fc1_bias, ln4_gain, ln4_bias, fc2_bias,
    )
    params = [p.reshape(-1, p.shape[-1]) for p in params]
    weights = (w_qkv, w_out, w_fc1, w_fc2)
    got = whole_layer(layer_input, cotangent, weights, params)
    output, grad_input, qkv, out, up, down, *smalls = write_results(got, tuple(w.shape for w in weights))
    rows = [s.reshape(-1) for s in smalls]
    return (
        output, grad_input, qkv, smalls[0], out, rows[1], rows[2], rows[3], rows[4], rows[5], rows[6], rows[7], rows[8], up,
        rows[10], rows[11], rows[12], down, rows[9],
    )


def fits_pair(mesh):
    return mesh.shape["shard"] == 2 and mesh.shape["rep"] == 16


def solution(mesh):
    return jax.shard_map(
        on_pair_of_cores if fits_pair(mesh) else on_any_mesh,
        mesh=mesh,
        in_specs=(
            P(("rep", "shard"), None),
            P(("rep", "shard"), None),
            P("shard", None),
            P(None, "shard"),
            P("shard", None),
            P("shard"),
            P("shard"),
            P("shard"),
            P("shard"),
            P("shard"),
            P("shard"),
            P("shard"),
            P("shard"),
            P("shard", None),
            P("shard"),
            P("shard"),
            P("shard"),
            P("shard", None),
            P("shard"),
        ),
        out_specs=(
            P(("rep", "shard"), None),
            P(("rep", "shard"), None),
            P("shard", None),
            P(None, "shard"),
            P("shard", None),
            P("shard"),
            P("shard"),
            P("shard"),
            P("shard"),
            P("shard"),
            P("shard"),
            P("shard"),
            P("shard"),
            P("shard", None),
            P("shard"),
            P("shard"),
            P("shard"),
            P("shard", None),
            P("shard"),
        ),
        check_vma=False,
    )
```

```python
import functools

import jax
import jax.numpy as jnp
from jax import lax
from jax.experimental import pallas as pl
from jax.experimental.pallas import tpu as pltpu
from jax.sharding import PartitionSpec as P

D = 1024
HEADS = 16
HEAD_DIM = 64


EPS = 1e-05
NEG = -1e30


def norm_rows(v, gain, bias):
    centre = jnp.mean(v, axis=-1, keepdims=True)
    centred = v - centre
    spread = jnp.mean(centred * centred, axis=-1, keepdims=True)
    return centred * lax.rsqrt(spread + EPS) * gain + bias


def ffn_middle(hidden, gain, bias):
    return norm_rows(jax.nn.gelu(hidden, approximate=False), gain, bias)


def causal_mask(index, qblock, length):
    rows = index * qblock + lax.iota(jnp.int32, qblock)
    cols = lax.iota(jnp.int32, length)
    return (cols[None, :] <= rows[:, None])[None]


def block_scores(queries, keys_all, index, qblock, scale):
    length = keys_all.shape[0]
    scores = (
        jnp.einsum("qhd,khd->hqk", queries, keys_all, preferred_element_type=jnp.float32) * scale
    )
    return (queries, jnp.where(causal_mask(index, qblock, length), scores, NEG))


def attend_forward(queries, keys_all, values_all, scale):
    length, heads, width = queries.shape
    qblock = min(512, length)
    blocks = length // qblock

    def one_block(index):
        rows_q, scores = block_scores(queries, keys_all, index, qblock, scale)
        total = jax.nn.logsumexp(scores, axis=-1, keepdims=True)
        probs = jnp.exp(scores - total).astype(jnp.bfloat16)
        outcome = jnp.einsum("hqk,khd->qhd", probs, values_all, preferred_element_type=jnp.float32)
        return (outcome, total)

    outcome, totals = lax.map(one_block, jnp.arange(blocks, dtype=jnp.int32))
    return (outcome.reshape(length, heads, width), totals)


def attend_backward(queries, keys_all, values_all, totals, grad_out, scale):
    length, heads, width = queries.shape
    qblock = min(512, length)
    blocks = length // qblock

    def one_block(carry, index):
        grad_keys, grad_values = carry
        rows_q, scores = block_scores(queries, keys_all, index, qblock, scale)
        probs = jnp.exp(scores - totals[index])
        probs_low = probs.astype(jnp.bfloat16)
        grad_values = grad_values + jnp.einsum(
            "hqk,qhd->khd", probs_low, grad_out, preferred_element_type=jnp.float32
        )
        grad_probs = jnp.einsum(
            "qhd,khd->hqk", grad_out, values_all, preferred_element_type=jnp.float32
        )
        row_dot = jnp.sum(probs * grad_probs, axis=-1, keepdims=True)
        grad_scores = (probs * (grad_probs - row_dot)).astype(jnp.bfloat16)
        grad_rows = (
            jnp.einsum("hqk,khd->qhd", grad_scores, keys_all, preferred_element_type=jnp.float32)
            * scale
        )
        grad_keys = (
            grad_keys
            + jnp.einsum("hqk,qhd->khd", grad_scores, rows_q, preferred_element_type=jnp.float32)
            * scale
        )
        return ((grad_keys, grad_values), grad_rows)

    empty = jnp.zeros((length, heads, width), jnp.float32)
    (grad_keys, grad_values), grad_queries = lax.scan(
        one_block, (empty, empty), jnp.arange(blocks, dtype=jnp.int32)
    )
    return (grad_queries.reshape(length, heads, width), grad_keys, grad_values)


def on_any_mesh(
    layer_input,
    cotangent,
    w_qkv,
    qv_bias,
    w_out,
    out_bias,
    head_scale,
    ln1_gain,
    ln1_bias,
    ln2_gain,
    ln2_bias,
    ln3_gain,
    ln3_bias,
    w_fc1,
    fc1_bias,
    ln4_gain,
    ln4_bias,
    w_fc2,
    fc2_bias,
):
    low_qkv = w_qkv.astype(jnp.bfloat16)
    low_out = w_out.astype(jnp.bfloat16)
    low_heads = head_scale.astype(jnp.bfloat16)
    low_up = w_fc1.astype(jnp.bfloat16)
    low_down = w_fc2.astype(jnp.bfloat16)
    whole = (
        lax.all_gather(low_qkv, "shard", axis=0, tiled=True),
        lax.all_gather(qv_bias.astype(jnp.bfloat16), "shard", axis=1, tiled=True),
        lax.all_gather(low_out, "shard", axis=0, tiled=True),
        lax.all_gather(out_bias.astype(jnp.bfloat16), "shard", axis=0, tiled=True),
        lax.all_gather(low_heads, "shard", axis=0, tiled=True),
        lax.all_gather(ln1_gain.astype(jnp.bfloat16), "shard", axis=0, tiled=True),
        lax.all_gather(ln1_bias.astype(jnp.bfloat16), "shard", axis=0, tiled=True),
        lax.all_gather(ln2_gain.astype(jnp.bfloat16), "shard", axis=0, tiled=True),
        lax.all_gather(ln2_bias.astype(jnp.bfloat16), "shard", axis=0, tiled=True),
        lax.all_gather(ln3_gain.astype(jnp.bfloat16), "shard", axis=0, tiled=True),
        lax.all_gather(ln3_bias.astype(jnp.bfloat16), "shard", axis=0, tiled=True),
        lax.all_gather(low_up, "shard", axis=0, tiled=True),
        lax.all_gather(fc1_bias.astype(jnp.bfloat16), "shard", axis=0, tiled=True),
        lax.all_gather(ln4_gain.astype(jnp.bfloat16), "shard", axis=0, tiled=True),
        lax.all_gather(ln4_bias.astype(jnp.bfloat16), "shard", axis=0, tiled=True),
        lax.all_gather(low_down, "shard", axis=0, tiled=True),
        lax.all_gather(fc2_bias.astype(jnp.bfloat16), "shard", axis=0, tiled=True),
    )
    weight_qkv, weight_out, weight_up, weight_down = (whole[0], whole[2], whole[11], whole[15])
    (
        bias_qv,
        bias_out,
        head_gain,
        gain_one,
        shift_one,
        gain_two,
        shift_two,
        gain_three,
        shift_three,
        bias_up,
        gain_four,
        shift_four,
        bias_down,
    ) = tuple(
        (whole[index].astype(jnp.float32) for index in (1, 3, 4, 5, 6, 7, 8, 9, 10, 12, 13, 14, 16))
    )
    length = layer_input.shape[0]
    scale = HEAD_DIM ** (-0.5)
    inputs = layer_input.astype(jnp.float32)
    normed_one, pull_one = jax.vjp(norm_rows, inputs, gain_one, shift_one)
    act_one = normed_one.astype(jnp.bfloat16)
    bias_full = jnp.concatenate([bias_qv[0], jnp.zeros((D,), jnp.float32), bias_qv[1]])
    qkv = (jnp.dot(act_one, weight_qkv, preferred_element_type=jnp.float32) + bias_full).astype(
        jnp.bfloat16
    )
    triple = qkv.reshape(length, 3, HEADS, HEAD_DIM)
    queries = triple[:, 0]
    keys_all = triple[:, 1]
    values_all = triple[:, 2]
    attended, totals = attend_forward(queries, keys_all, values_all, scale)
    mixed = (attended * head_gain[:, None]).reshape(length, D).astype(jnp.bfloat16)
    branch = jnp.dot(mixed, weight_out, preferred_element_type=jnp.float32) + bias_out
    normed_two, pull_two = jax.vjp(norm_rows, branch, gain_two, shift_two)
    middle = inputs + normed_two
    normed_three, pull_three = jax.vjp(norm_rows, middle, gain_three, shift_three)
    act_three = normed_three.astype(jnp.bfloat16)
    hidden = jnp.dot(act_three, weight_up, preferred_element_type=jnp.float32) + bias_up
    normed_four, pull_four = jax.vjp(ffn_middle, hidden, gain_four, shift_four)
    act_four = normed_four.astype(jnp.bfloat16)
    result = middle + (
        jnp.dot(act_four, weight_down, preferred_element_type=jnp.float32) + bias_down
    )
    output = result.astype(jnp.bfloat16)
    again = (
        lax.all_gather(low_qkv, "shard", axis=0, tiled=True),
        lax.all_gather(low_out, "shard", axis=0, tiled=True),
        lax.all_gather(low_heads, "shard", axis=0, tiled=True),
        lax.all_gather(low_up, "shard", axis=0, tiled=True),
        lax.all_gather(low_down, "shard", axis=0, tiled=True),
    )
    back_qkv, back_out, back_up, back_down = (again[0], again[1], again[3], again[4])
    back_heads = again[2].astype(jnp.float32)
    cot_full = cotangent.astype(jnp.float32)
    grad_down_bias = jnp.sum(cot_full, axis=0)
    grad_down = jnp.einsum("tf,td->fd", act_four, cotangent, preferred_element_type=jnp.float32)
    grad_four = jnp.einsum("td,fd->tf", cotangent, back_down, preferred_element_type=jnp.float32)
    grad_hidden, grad_gain_four, grad_shift_four = pull_four(grad_four)
    hidden_low = grad_hidden.astype(jnp.bfloat16)
    grad_up_bias = jnp.sum(hidden_low, axis=0, dtype=jnp.float32)
    grad_up = jnp.einsum("td,tf->df", act_three, hidden_low, preferred_element_type=jnp.float32)
    grad_three = jnp.einsum("tf,df->td", hidden_low, back_up, preferred_element_type=jnp.float32)
    grad_mid_part, grad_gain_three, grad_shift_three = pull_three(grad_three)
    grad_middle = cot_full + grad_mid_part
    grad_branch, grad_gain_two, grad_shift_two = pull_two(grad_middle)
    branch_low = grad_branch.astype(jnp.bfloat16)
    grad_out_b = jnp.sum(branch_low, axis=0, dtype=jnp.float32)
    grad_out_w = jnp.einsum("td,te->de", mixed, branch_low, preferred_element_type=jnp.float32)
    grad_mixed = jnp.einsum("te,de->td", branch_low, back_out, preferred_element_type=jnp.float32)
    grad_mixed = grad_mixed.reshape(length, HEADS, HEAD_DIM)
    grad_heads = jnp.sum(grad_mixed * attended, axis=(0, 2))
    grad_attended = (grad_mixed * back_heads[:, None]).astype(jnp.bfloat16)
    grad_queries, grad_keys, grad_values = attend_backward(
        queries, keys_all, values_all, totals, grad_attended, scale
    )
    grad_qkv = (
        jnp.stack([grad_queries, grad_keys, grad_values], axis=1)
        .reshape(length, 3 * D)
        .astype(jnp.bfloat16)
    )
    grad_qv = jnp.stack(
        [
            jnp.sum(grad_qkv[:, :D], axis=0, dtype=jnp.float32),
            jnp.sum(grad_qkv[:, 2 * D :], axis=0, dtype=jnp.float32),
        ]
    )
    grad_qkv_w = jnp.einsum("td,te->de", act_one, grad_qkv, preferred_element_type=jnp.float32)
    grad_one = jnp.einsum("te,de->td", grad_qkv, back_qkv, preferred_element_type=jnp.float32)
    grad_in_part, grad_gain_one, grad_shift_one = pull_one(grad_one)
    grad_input = grad_middle + grad_in_part
    shares = (
        lax.psum_scatter(grad_qkv_w, "shard", scatter_dimension=0, tiled=True),
        lax.psum_scatter(grad_qv, "shard", scatter_dimension=1, tiled=True),
        lax.psum_scatter(grad_out_w, "shard", scatter_dimension=0, tiled=True),
        lax.psum_scatter(grad_out_b, "shard", scatter_dimension=0, tiled=True),
        lax.psum_scatter(grad_heads, "shard", scatter_dimension=0, tiled=True),
        lax.psum_scatter(grad_gain_one, "shard", scatter_dimension=0, tiled=True),
        lax.psum_scatter(grad_shift_one, "shard", scatter_dimension=0, tiled=True),
        lax.psum_scatter(grad_gain_two, "shard", scatter_dimension=0, tiled=True),
        lax.psum_scatter(grad_shift_two, "shard", scatter_dimension=0, tiled=True),
        lax.psum_scatter(grad_gain_three, "shard", scatter_dimension=0, tiled=True),
        lax.psum_scatter(grad_shift_three, "shard", scatter_dimension=0, tiled=True),
        lax.psum_scatter(grad_up, "shard", scatter_dimension=0, tiled=True),
        lax.psum_scatter(grad_up_bias, "shard", scatter_dimension=0, tiled=True),
        lax.psum_scatter(grad_gain_four, "shard", scatter_dimension=0, tiled=True),
        lax.psum_scatter(grad_shift_four, "shard", scatter_dimension=0, tiled=True),
        lax.psum_scatter(grad_down, "shard", scatter_dimension=0, tiled=True),
        lax.psum_scatter(grad_down_bias, "shard", scatter_dimension=0, tiled=True),
    )
    summed = lax.psum(
        (
            shares[0],
            shares[1],
            shares[2],
            shares[3],
            shares[4],
            shares[5],
            shares[6],
            shares[7],
            shares[8],
            shares[9],
            shares[10],
            shares[11],
            shares[12],
            shares[13],
            shares[14],
            shares[15],
            shares[16],
        ),
        "rep",
    )
    return (output, grad_input) + tuple(summed)


MESH = pl.DeviceIdType.MESH
BF16 = jnp.bfloat16
F32 = jnp.float32
UNIT_ROWS = 256
UNIT_COLS = 1024
MIB = 1 << 20
SLOT = {
    "d1": 0, "d2": 1, "z1": 2, "z3": 2, "z2": 3, "u1": 4, "w1": 4, "u2": 5, "w2": 5, "u3": 6, "w3": 6, "g1": 7, "g2": 8,
}


def unit_table(dims):
    table = []
    for matrix in (3, 2, 1, 0):
        rows, cols = dims[matrix]
        for col in range(0, cols, UNIT_COLS):
            for row in range(0, rows, UNIT_ROWS):
                table.append((matrix, row, col))
    return table


KINDS = (
    "QX", "QX", "QX", "QY", "QY", "QY", "QY", "QY", "Y", "X", "X", "Y", "ZY", "ZY", "X", "Y", "X", "X", "ZY",
    "Y", "Y", "X", "ZY", "X",
)
TASK, VECTORS = 24, 25
ORDER = (
    1, 5, 24, 2, 3, 5, 0, 24, 4, 0, 4, 24, 2, 24, 24, 1, 24, 24, 24, 24, 24, 24, 24, 6, 5, 7, 4, 10, 6, 8, 11,
    7, 13, 2, 24, 24, 14, 15, 24, 5, 4, 24, 24, 24, 5, 0, 9, 10, 4, 16, 17, 5, 13, 7, 2, 24, 12, 24, 14, 24, 24,
    4, 9, 7, 5, 24, 16, 6, 8, 7, 0, 3, 10, 19, 12, 20, 2, 23, 21, 5, 1, 9, 0, 5, 10, 7, 13, 0, 4, 12, 6, 1, 2,
    2, 9, 8, 3, 23, 0, 13, 16, 17, 4, 24, 11, 16, 22, 4, 6, 12, 7, 8, 5, 13, 24, 0, 3, 21, 9, 15, 2, 6, 16, 20,
    24, 8, 11, 13, 17, 7, 2, 16, 3, 12, 7, 22, 10, 4, 6, 15, 19, 16, 3, 11, 24, 12, 8, 8, 0, 3, 14, 15, 1, 7,
    10, 2, 20, 22, 23, 11, 17, 10, 15, 9, 1, 19, 21, 14, 25, 18, 12, 0, 20, 3, 10, 1, 13, 16, 6, 22, 21, 3, 8,
    19, 20, 1, 10, 22, 9, 16, 23, 21, 6, 20, 19, 8, 13, 7, 1, 6, 22, 23, 11, 20, 16, 18, 17, 14, 10, 23, 9, 25,
    1, 11, 23, 17, 15, 12, 4, 19, 3, 18, 19, 14, 21, 11, 22, 9, 25, 5, 16, 18, 20, 23, 8, 11, 20, 19, 15, 17,
    17, 18, 14, 17, 19, 23, 21, 12, 14, 21, 6, 18, 9, 12, 15, 17, 14, 18, 3, 0, 25, 10, 19, 21, 15, 13, 20, 23,
    22, 9, 2, 18, 13, 22, 14, 15, 22, 13, 17, 1, 19, 21, 18, 12, 20, 11, 18, 25, 8, 18, 23, 22, 14, 15, 21, 11,
)


GIVE_ROWS = 240


def program_order(units, ends):
    order, task, vector, waited, step = [], 0, 0, {3}, [0] * len(units)
    order.append(("wait", 3, 0))
    for entry in ORDER:
        if entry == TASK:
            order.append(("task", task, 0))
            task += 1
            continue
        if entry == VECTORS:
            order.append(("vec", vector, 0))
            vector += 1
            continue
        m = units[entry][0]
        if m not in waited:
            assert task >= ends[m]
            order.append(("wait", m, 0))
            waited.add(m)
        order.append(("sum", entry, step[entry]))
        step[entry] += 1
    return order


PAIRS = 4


def fold(v):
    total = v[0:8]
    for k in range(1, v.shape[0] // 8):
        total = total + v[8 * k : 8 * k + 8]
    return total


def layer_kernel(dims, at_base, g_base, *refs):
    x_in, cot_in, weights, params = refs[0], refs[1], refs[2:6], refs[6:19]
    y_out, dx_out, res, vec_out, tiles_hbm = refs[19:24]
    (
        at, g, give, pair, line_xy, line_z, ring, big, left, act, hid, qkv, probs, attended, branch, middle, dmid,
        late_in, near_left, near_right, vec_w, vec_h, rstd4, sums4, vec_in, vec_own, vec_got,
        send, recv, v_send, v_recv, p_send, p_recv, l_sem, w_in, w_keep, w_send, w_recv, w_store, t_sem, s_sem, e_sem, n_send, n_recv,
    ) = refs[24:]
    r = lax.axis_index("rep")
    c = lax.axis_index("shard")
    x, y, z = r % 2, (r // 2) % 2, r // 4
    core = {"shard": 1 - c}
    to = {
        "X": {"rep": r + 1 - 2 * x},
        "Y": {"rep": r + 2 - 4 * y},
        "U": {"rep": r + 4},
        "D": {"rep": r - 4},
        "XY": {"rep": r + 3 - 2 * x - 4 * y},
    }
    line_end = (z == 0) | (z == 3)
    line_mid = (z == 1) | (z == 2)
    outward = {"rep": r + 4 * (2 * (z // 2) - 1)}
    inward = {"rep": r + 4 * (1 - 2 * (z // 2))}
    across = {"rep": r + 4 * (3 - 2 * z)}
    upper = z // 2
    length = x_in.shape[0]
    width = x_in.shape[1]
    half_w = width // 2
    hidden = dims[2][1]
    half_h = hidden // 2
    blocks = hidden // width
    TILE = 512

    tile_of = []
    for m, (rows, cols) in enumerate(dims):
        for row in range(0, rows, TILE):
            for col in range(0, cols, UNIT_COLS):
                tile_of.append((m, row, col))
    first_tile = [min(t for t, v in enumerate(tile_of) if v[0] == m) for m in range(4)]
    parts = 2 * len(tile_of)
    slots_f, slots_b, late, slots_l, slots_g = 6, 16, 16, 2, 6

    def part_read(i):
        m, row, col = tile_of[i // 2]
        return pltpu.make_async_copy(
            weights[m].at[pl.ds(row + (i % 2) * 256, 256), pl.ds(col, UNIT_COLS)],
            late_in.at[pl.ds((i % slots_l) * 256, 256), :] if i >= late else big.at[pl.ds((i % slots_f) * 256, 256), :],
            w_in.at[slots_f + i % slots_l if i >= late else i % slots_f],
        )

    def low_row(i):
        return (late + (i - late) % slots_g) * 256 if i >= late else i * 256

    def part_low(i):
        return low_buf.at[pl.ds(low_row(i), 256), :]

    low_buf = give

    def part_place(i):
        return tiles_hbm.at[c, i // 2, pl.ds((i % 2) * 256, 256), :]

    def part_keep(i):
        return pltpu.make_async_copy(part_low(i), part_place(i), w_keep.at[i % slots_b])

    def part_landing(i):
        if i < 8:
            return res.at[i]
        return ring.at[(i - 8) // 2, pl.ds((i % 2) * 256, 256), :]

    def part_store(i):
        far = tiles_hbm.at[1 - c, i // 2, pl.ds((i % 2) * 256, 256), :]
        return pltpu.make_async_copy(part_landing(i), far, w_store.at[i])

    def part_give(i):
        return pltpu.make_async_remote_copy(
            src_ref=part_low(i), dst_ref=part_landing(i) if i < late else part_place(i), send_sem=w_send.at[i % slots_b], recv_sem=w_recv.at[i],
            device_id=core, device_id_type=MESH,
        )

    def part_got(i):
        return pltpu.make_async_remote_copy(
            src_ref=part_low(i),
            dst_ref=part_landing(i) if i < late else tiles_hbm.at[1 - c, i // 2, pl.ds((i % 2) * 256, 256), :],
            send_sem=w_send.at[i % slots_b], recv_sem=w_recv.at[i], device_id=core, device_id_type=MESH,
        )

    for i in range(slots_f):
        part_read(i).start()

    barrier = pltpu.get_barrier_semaphore()
    for peer in (core, to["X"], to["Y"], to["XY"]):
        pl.semaphore_signal(barrier, inc=1, device_id=peer, device_id_type=MESH)

    @pl.when(z < 3)
    def _():
        pl.semaphore_signal(barrier, inc=1, device_id=to["U"], device_id_type=MESH)

    @pl.when(z > 0)
    def _():
        pl.semaphore_signal(barrier, inc=1, device_id=to["D"], device_id_type=MESH)

    @pl.when(line_end)
    def _():
        pl.semaphore_signal(barrier, inc=1, device_id=across, device_id_type=MESH)

    narrow = (0, 0, 2, 3, 4, 5, 6, 7, 8, 9, 10)

    def rounded(v):
        return v.astype(BF16).astype(F32)

    lane_w = pl.ds(pl.multiple_of(c * half_w, half_w), half_w)
    lane_h = pl.ds(pl.multiple_of(c * half_h, half_h), half_h)
    (qv_ref, ob_ref, hs_ref, g1_ref, b1_ref, g2_ref, b2_ref, g3_ref, b3_ref, ub_ref, g4_ref, b4_ref, db_ref) = params
    vec_w[0:2, lane_w] = rounded(qv_ref[...])
    for row, ref in zip((2, 4, 5, 6, 7, 8, 9, 10), (ob_ref, g1_ref, b1_ref, g2_ref, b2_ref, g3_ref, b3_ref, db_ref)):
        vec_w[row : row + 1, lane_w] = rounded(ref[...])
    head_of = lax.broadcasted_iota(jnp.int32, (1, half_w), 1) // 64
    spread = jnp.zeros((1, half_w), F32)
    for h in range(half_w // 64):
        spread = jnp.where(head_of == h, rounded(hs_ref[0:1, h : h + 1]), spread)
    vec_w[3:4, lane_w] = spread
    for row, ref in enumerate((ub_ref, g4_ref, b4_ref)):
        vec_h[row : row + 1, lane_h] = rounded(ref[...])
    QB, VB, OB, HS, G1, B1, G2, B2, G3, B3, DB = range(11)
    UB, G4, B4 = range(3)

    def small_copy(k, give_it):
        ref, lane, far = ((vec_w, lane_w, 1 - c), (vec_h, lane_h, 1 - c))[k]
        size = half_w if k == 0 else half_h
        other = pl.ds(pl.multiple_of((1 - c) * size, size), size)
        here = ref.at[:, lane]
        return pltpu.make_async_remote_copy(
            src_ref=here, dst_ref=here if give_it else ref.at[:, other], send_sem=s_sem.at[k, 0], recv_sem=s_sem.at[k, 1],
            device_id=core, device_id_type=MESH,
        )

    e_copy = pltpu.make_async_copy(cot_in, g.at[pl.ds(0, length), pl.ds(g_base[3], width)], e_sem.at[0])
    e_copy.start()

    def left_own(m):
        rows = dims[m][0]
        return pltpu.make_async_copy(
            left.at[pl.ds(pl.multiple_of(2 * at_base[m] + c * rows, 512), rows), :],
            at.at[pl.ds(at_base[m], rows), pl.ds(0, length)],
            l_sem.at[m],
        )

    def left_far(m):
        rows = dims[m][0]
        return pltpu.make_async_remote_copy(
            src_ref=left.at[pl.ds(pl.multiple_of(2 * at_base[m] + (1 - c) * rows, 512), rows), :],
            dst_ref=at.at[pl.ds(at_base[m], rows), pl.ds(length, length)],
            send_sem=p_send.at[m, 0], recv_sem=p_recv.at[m, 0], device_id=core, device_id_type=MESH,
        )

    def right_far(m):
        cols = pl.ds(g_base[m], dims[m][1])
        return pltpu.make_async_remote_copy(
            src_ref=g.at[pl.ds(0, length), cols], dst_ref=g.at[pl.ds(length, length), cols],
            send_sem=p_send.at[m, 1], recv_sem=p_recv.at[m, 1], device_id=core, device_id_type=MESH,
        )

    def start_left(m):
        left_own(m).start()
        left_far(m).start()

    def wait_pair(m):
        left_own(m).wait()
        left_far(m).wait()
        right_far(m).wait()

    converted, kept_parts, given_parts = [0], set(), set()

    def kept(i):
        if i not in kept_parts:
            kept_parts.add(i)
            part_keep(i).wait()

    def given(i):
        if i not in given_parts:
            given_parts.add(i)
            part_give(i).wait_send()

    def convert_parts(upto):
        for i in range(converted[0], upto):
            part_read(i).wait()
            if i >= slots_b:
                kept(i - slots_b)
                given(i - slots_b)
            if i >= late + slots_g:
                kept(i - slots_g)
                given(i - slots_g)
            source, first = (late_in, i % slots_l * 256) if i >= late else (big, i % slots_f * 256)

            def convert(b, _, i=i, source=source, first=first):
                rows = pl.multiple_of(first + b * 32, 32)
                low = pl.multiple_of(low_row(i) + b * 32, 32)
                low_buf[pl.ds(low, 32), :] = source[pl.ds(rows, 32), :].astype(BF16)
                return 0

            lax.fori_loop(0, 8, convert, 0)
            part_keep(i).start()
            if i == 0:
                pl.semaphore_wait(barrier, 6)
                small_copy(0, True).start()
                small_copy(1, True).start()
            part_give(i).start()
            if i >= late and i + slots_l < parts:
                part_read(i + slots_l).start()
            if i + slots_f < late:
                part_read(i + slots_f).start()
            if i == late - slots_f:
                for k in range(slots_l):
                    part_read(late + k).start()
        converted[0] = max(converted[0], upto)

    def cotangent_copy(k, relay):
        here, there = pl.ds(0, length), pl.ds(length, length)
        cols = pl.ds(g_base[3], width)
        return pltpu.make_async_remote_copy(
            src_ref=near_right.at[k, here, :] if relay else near_right.at[0, here, :] if k == 2 else g.at[here, cols],
            dst_ref=near_right.at[k, there if relay else here, :],
            send_sem=n_send.at[k, int(relay)], recv_sem=n_recv.at[k, int(relay)],
            device_id=core if relay else to["XYY"[k]], device_id_type=MESH,
        )

    convert_parts(2)
    e_copy.wait()
    right_far(3).start()
    cotangent_copy(0, False).start()
    cotangent_copy(1, False).start()
    convert_parts(4)

    def tile(m, half, index):
        return (half, first_tile[m] + index)

    stream = []
    per_half = dims[3][0] // TILE
    stream += [tile(3, h, k) for h in range(2) for k in range(per_half)]
    for m in (2, 1, 0):
        for index in range(dims[m][1] // UNIT_COLS):
            stream += [tile(m, 0, index), tile(m, 1, index)]
    slots_t = 4
    here = set()

    def tile_load(i):
        half, t = stream[i]
        return pltpu.make_async_copy(
            tiles_hbm.at[half, t], ring.at[i % slots_t], t_sem.at[i % slots_t]
        )

    def tile_start(i):
        half, t = stream[i]
        if (1, t) not in here:
            here.add((1, t))
            convert_parts(2 * t + 2)
            for k in (2 * t, 2 * t + 1):
                kept(k)
                if k >= late:
                    part_got(k).wait_recv()
        tile_load(i).start()

    at_tile, started, allowed_to = [0], [0], [0]

    def fill(limit=None):
        if limit is not None:
            allowed_to[0] = limit
        while started[0] < min(at_tile[0] + slots_t, allowed_to[0], len(stream)):
            tile_start(started[0])
            started[0] += 1

    def next_tile(ahead=0):
        i = at_tile[0] + ahead
        assert i < started[0]
        tile_load(i).wait()
        return ring.at[i % slots_t]

    def done_tile(count=1):
        at_tile[0] += count
        fill()

    def mean(v):
        return jnp.sum(v, axis=-1, keepdims=True) / v.shape[-1]

    def normal(v):
        centred = v - mean(v)
        scale = lax.rsqrt(mean(centred * centred) + 1e-05)
        return centred * scale, scale

    def each(fn, step=32, init=0, unroll=1):
        def body(i, carry):
            return fn(pl.ds(pl.multiple_of(i * step, step), step), carry)

        return lax.fori_loop(0, length // step, body, init, unroll=unroll)

    def w_row(i):
        return vec_w[i : i + 1, :]

    def turn(source, m, block=0):
        for k in range(width // 256):
            row = 2 * at_base[m] + block * width + k * 256
            left[row : row + 256, :] = jnp.transpose(source[:, k * 256 : (k + 1) * 256])

    NT = (((1,), (1,)), ((), ()))
    TN = (((0,), (0,)), ((), ()))

    def nt(a, b):
        return lax.dot_general(a, b, NT, preferred_element_type=F32)

    def tn(a, b):
        return lax.dot_general(a, b, TN, preferred_element_type=F32)

    def product_pair(source, write, t):
        convert_parts(2 * t + 2)
        for i in (2 * t, 2 * t + 1):
            part_got(i).wait_recv()
            part_store(i).start()
        far = (part_landing(2 * t), part_landing(2 * t + 1))
        for k in range(UNIT_COLS // 256):
            cols = slice(k * 256, (k + 1) * 256)
            own = low_buf[512 * t : 512 * (t + 1), cols]
            value = jnp.dot(source[:, lane_w], own, preferred_element_type=F32)
            for n in range(2):
                lanes = pl.ds(pl.multiple_of((1 - c) * half_w + n * 256, 256), 256)
                value = value + jnp.dot(source[:, lanes], far[n][:, cols], preferred_element_type=F32)
            write(cols, value)

    small_copy(0, True).wait_send()
    small_copy(1, True).wait_send()
    small_copy(0, False).wait_recv()
    small_copy(1, False).wait_recv()

    def first_norm(rows, _):
        hat, _s = normal(x_in[rows, :].astype(F32))
        act[rows, :] = (hat * w_row(G1) + w_row(B1)).astype(BF16)
        return 0

    each(first_norm, unroll=2)
    for index in range(3):

        def put_qkv(cols, value, index=index):
            if index == 0:
                value = value + vec_w[QB : QB + 1, cols]
            if index == 2:
                value = value + vec_w[VB : VB + 1, cols]
            qkv[:, index * width + cols.start : index * width + cols.stop] = value.astype(BF16)

        product_pair(act, put_qkv, first_tile[0] + index)
        convert_parts(10 + 2 * index)
    turn(act, 0)
    start_left(0)
    convert_parts(16)
    for k in range(2):
        cotangent_copy(k, False).wait()
        cotangent_copy(k, True).start()
    cotangent_copy(2, False).start()

    low_lane = lax.broadcasted_iota(jnp.int32, (length, 128), 1) < 64
    allowed = lax.broadcasted_iota(jnp.int32, (length, length), 1) <= lax.broadcasted_iota(
        jnp.int32, (length, length), 0
    )
    scale = 64 ** (-0.5)
    keep_lane = (low_lane.astype(F32).astype(BF16), jnp.logical_not(low_lane).astype(F32).astype(BF16))

    def split_heads(v):
        return jnp.concatenate([v * keep_lane[0], v * keep_lane[1]], axis=0)

    def attend(p):
        q = qkv[:, pl.ds(pl.multiple_of(p * 128, 128), 128)]
        k = qkv[:, pl.ds(pl.multiple_of(width + p * 128, 128), 128)]
        v = qkv[:, pl.ds(pl.multiple_of(2 * width + p * 128, 128), 128)]
        both = nt(q, split_heads(k)) * scale
        got = []
        for h in range(2):
            scores = jnp.where(allowed, both[:, h * length : (h + 1) * length], -1e30)
            top = jnp.max(scores, axis=-1, keepdims=True)
            lse = top + jnp.log(jnp.sum(jnp.exp(scores - top), axis=-1, keepdims=True))
            got.append(jnp.exp(scores - lse))
        prob = jnp.concatenate(got, axis=1)
        probs[p] = prob
        value = jnp.dot(prob.astype(BF16), split_heads(v), preferred_element_type=F32)
        cols = pl.ds(pl.multiple_of(p * 128, 128), 128)
        attended[:, cols] = value
        act[:, cols] = (value * vec_w[HS : HS + 1, cols]).astype(BF16)

    def attend_some(i, _):
        for n in range(PAIRS):
            attend(i * PAIRS + n)
        return 0

    lax.fori_loop(0, width // 128 // PAIRS, attend_some, 0)

    def put_branch(cols, value):
        branch[:, cols] = value + vec_w[OB : OB + 1, cols]

    product_pair(act, put_branch, first_tile[1])
    turn(act, 1)
    start_left(1)

    def second_norm(rows, _):
        hat, _s = normal(branch[rows, :])
        mid = x_in[rows, :].astype(F32) + (hat * w_row(G2) + w_row(B2))
        middle[rows, :] = mid
        hat, _s = normal(mid)
        act[rows, :] = (hat * w_row(G3) + w_row(B3)).astype(BF16)
        return 0

    each(second_norm, unroll=2)
    U0, H0, D0 = 0, blocks * length, 2 * blocks * length
    for j in range(blocks):

        def put_hidden(cols, value, j=j):
            wide = slice(j * width + cols.start, j * width + cols.stop)
            big[U0 + j * length : U0 + (j + 1) * length, cols] = value + vec_h[UB : UB + 1, wide]

        product_pair(act, put_hidden, first_tile[2] + j)
        convert_parts(min(late + 2 * (j + 1), late + slots_g))
    turn(act, 2)
    start_left(2)
    root_half = 0.7071067811865476

    def near(base, start):
        return pl.ds(pl.multiple_of(base + start, 16), 16)

    def hidden_norm(rows, _):
        total = jnp.zeros((16, 1), F32)
        for j in range(blocks):
            u = big[near(U0 + j * length, rows.start), :]
            h = u * (1.0 + lax.erf(u * root_half)) * 0.5
            big[near(H0 + j * length, rows.start), :] = h
            total = total + jnp.sum(h, axis=-1, keepdims=True)
        centre = total / hidden
        total = jnp.zeros((16, 1), F32)
        for j in range(blocks):
            h = big[near(H0 + j * length, rows.start), :] - centre
            total = total + jnp.sum(h * h, axis=-1, keepdims=True)
        s = lax.rsqrt(total / hidden + 1e-05)
        rstd4[rows, :] = jnp.broadcast_to(s, (16, 128))
        for j in range(blocks):
            at_h = near(H0 + j * length, rows.start)
            hat = (big[at_h, :] - centre) * s
            big[at_h, :] = hat
            cols = slice(j * width, (j + 1) * width)
            hid[near(j * length, rows.start), :] = (
                hat * vec_h[G4 : G4 + 1, cols] + vec_h[B4 : B4 + 1, cols]
            ).astype(BF16)
        return 0

    cotangent_copy(2, False).wait()
    cotangent_copy(2, True).start()
    each(hidden_norm, 16)
    for j in range(blocks):
        turn(hid.at[pl.ds(j * length, length), :], 3, j)
    start_left(3)
    convert_parts(parts)
    for i in range(late):
        part_store(i).wait()
        kept(i)
        given(i)

    tasks = []
    zeros8 = jnp.zeros((8, width), F32)
    dirs = g.at[pl.ds(0, length), :]

    def put_sum(row, value):
        line = jnp.sum(value, axis=0, keepdims=True)
        vec_in[0, row : row + 1, :] = line[:, 0:half_w]
        vec_in[1, row : row + 1, :] = line[:, half_w:width]

    def task_down(h, k):
        def run():
            w = next_tile()
            row = h * dims[3][0] + k * TILE
            j, lane = row // width, row % width
            if h == 0 and k == 0:
                y_acc[...] = middle[...] + w_row(DB)
            for n in range(TILE // 256):
                big[D0 + j * length : D0 + (j + 1) * length, lane + n * 256 : lane + (n + 1) * 256] = nt(
                    dirs[:, g_base[3] : g_base[3] + width], w[n * 256 : (n + 1) * 256, :]
                )

            for n in range(width // 256):
                cols = slice(n * 256, (n + 1) * 256)
                y_acc[:, cols] += jnp.dot(
                    hid[j * length : (j + 1) * length, lane : lane + TILE], w[:, cols], preferred_element_type=F32
                )
            done_tile()
            if h == 1 and k == per_half - 1:
                y_out[...] = y_acc[...].astype(BF16)

        return run

    y_acc = dmid
    for h in range(2):
        for k in range(per_half):
            tasks.append((1.2, task_down(h, k)))

    def task_hidden(first, count):
        def run():
            if first == 0:
                sums4[...] = jnp.zeros_like(sums4)

                def e_sum(rows, carry):
                    return carry + fold(dirs[rows, g_base[3] : g_base[3] + width].astype(F32))

                put_sum(DB, each(e_sum, 32, zeros8))

            def body(i, _):
                at_r = pl.multiple_of(first + i * 16, 16)
                one = jnp.zeros((16, 1), F32)
                two = jnp.zeros((16, 1), F32)
                for j in range(blocks):
                    gain = vec_h[G4 : G4 + 1, j * width : (j + 1) * width]
                    d = big[near(D0 + j * length, at_r), :] * gain
                    hat = big[near(H0 + j * length, at_r), :]
                    one = one + jnp.sum(d, axis=-1, keepdims=True)
                    two = two + jnp.sum(d * hat, axis=-1, keepdims=True)
                one, two = one / hidden, two / hidden
                s = rstd4[pl.ds(at_r, 16), 0:1]
                for j in range(blocks):
                    cols = slice(j * width, (j + 1) * width)
                    da = big[near(D0 + j * length, at_r), :]
                    hat = big[near(H0 + j * length, at_r), :]
                    u = big[near(U0 + j * length, at_r), :]
                    dh = s * (da * vec_h[G4 : G4 + 1, cols] - one - hat * two)
                    slope = 0.5 * (1.0 + lax.erf(u * root_half)) + u * (jnp.exp(u * u * -0.5) * 0.3989422804014327)
                    du = (dh * slope).astype(BF16)
                    g[pl.ds(at_r, 16), g_base[2] + j * width : g_base[2] + (j + 1) * width] = du
                    sums4[0:8, cols] += fold(du.astype(F32))
                    sums4[8:16, cols] += fold(da * hat)
                    sums4[16:24, cols] += fold(da)
                return 0

            lax.fori_loop(0, count // 16, body, 0)
            if first + count == length:
                for i in range(3):
                    line = jnp.sum(sums4[8 * i : 8 * i + 8, :], axis=0, keepdims=True)
                    for n in range(hidden // half_w):
                        hh, k = divmod(n, half_h // half_w)
                        vec_in[hh, 11 + 4 * i + k : 12 + 4 * i + k, :] = line[:, n * half_w : (n + 1) * half_w]
                right_far(2).start()

        return run

    for first in range(0, length, 32):
        tasks.append((3.0, task_hidden(first, 32)))

    def add_pair(acc, index_of, cols_of, count, width_to):
        def make(index):
            def run():
                for h in range(2):
                    w = next_tile()
                    for n in range(TILE // 256):
                        cols = slice(h * half_w + n * 256, h * half_w + (n + 1) * 256)
                        value = nt(dirs[:, cols_of(index)], w[n * 256 : (n + 1) * 256, :])
                        if index == 0:
                            acc[:, cols] = value
                        else:
                            acc[:, cols] += value
                    done_tile()

            return run

        return [(1.2, make(index)) for index in range(count)]

    ends = {2: len(tasks)}
    acc = big.at[pl.ds(U0, length), :]
    tasks += add_pair(acc, None, lambda j: slice(g_base[2] + j * width, g_base[2] + (j + 1) * width), blocks, width)

    def task_norms():
        def body(rows, carry):
            s3g, s3b, s2g, s2b, sob = carry
            da = acc[rows, :]
            hat, s = normal(middle[rows, :])
            d = da * w_row(G3)
            d_mid = dirs[rows, g_base[3] : g_base[3] + width].astype(F32) + s * (d - mean(d) - hat * mean(d * hat))
            dmid[rows, :] = d_mid
            s3g, s3b = s3g + fold(da * hat), s3b + fold(da)
            hat, s = normal(branch[rows, :])
            d = d_mid * w_row(G2)
            dy = (s * (d - mean(d) - hat * mean(d * hat))).astype(BF16)
            s2g, s2b = s2g + fold(d_mid * hat), s2b + fold(d_mid)
            g[rows, g_base[1] : g_base[1] + width] = dy
            return (s3g, s3b, s2g, s2b, sob + fold(dy.astype(F32)))

        got = each(body, 16, (zeros8,) * 5)
        for row, value in zip((G3, B3, G2, B2, OB), got):
            put_sum(row, value)
        right_far(1).start()

    tasks.append((2.5, task_norms))
    ends[1] = len(tasks)
    d_mixed = big.at[pl.ds(U0 + length, length), :]
    tasks += add_pair(d_mixed, None, lambda j: slice(g_base[1], g_base[1] + width), 1, width)

    def task_heads():
        def body(rows, carry):
            d = d_mixed[rows, :]
            act[rows, :] = (d * w_row(HS)).astype(BF16)
            return carry + fold(d * attended[rows, :])

        put_sum(HS, each(body, 32, zeros8))

    tasks.append((0.6, task_heads))

    def task_attend(first, count):
        def run():
            def pair_of_heads(p):
                q_cols = pl.ds(pl.multiple_of(p * 128, 128), 128)
                k_cols = pl.ds(pl.multiple_of(width + p * 128, 128), 128)
                v_cols = pl.ds(pl.multiple_of(2 * width + p * 128, 128), 128)
                q, k, v, do = qkv[:, q_cols], qkv[:, k_cols], qkv[:, v_cols], act[:, q_cols]
                prob = probs[p]
                dv = tn(prob.astype(BF16), do)
                dp = nt(do, split_heads(v))
                ds = []
                for h in range(2):
                    own = slice(h * length, (h + 1) * length)
                    dot = jnp.sum(prob[:, own] * dp[:, own], axis=-1, keepdims=True)
                    ds.append(prob[:, own] * (dp[:, own] - dot))
                ds = jnp.concatenate(ds, axis=1).astype(BF16)
                dq = jnp.dot(ds, split_heads(k), preferred_element_type=F32) * scale
                dk = tn(ds, q) * scale
                g[0:length, q_cols] = dq.astype(BF16)
                g[0:length, k_cols] = jnp.where(low_lane, dk[0:length], dk[length : 2 * length]).astype(BF16)
                g[0:length, v_cols] = jnp.where(low_lane, dv[0:length], dv[length : 2 * length]).astype(BF16)

            for n in range(count):
                pair_of_heads(first + n)
            if first + count == width // 128:

                def sums(rows, carry):
                    a, b = carry
                    return (
                        a + fold(g[rows, 0:width].astype(F32)),
                        b + fold(g[rows, 2 * width : 3 * width].astype(F32)),
                    )

                a, b = each(sums, 32, (zeros8, zeros8))
                put_sum(QB, a)
                put_sum(VB, b)
                right_far(0).start()

        return run

    for first in range(0, width // 128, 2):
        tasks.append((3.0, task_attend(first, 2)))
    ends[0] = len(tasks)
    d_first = big.at[pl.ds(U0 + 2 * length, length), :]
    tasks += add_pair(d_first, None, lambda j: slice(j * width, (j + 1) * width), 3, width)

    def task_last():
        def body(rows, carry):
            sg, sb = carry
            da = d_first[rows, :]
            hat, s = normal(x_in[rows, :].astype(F32))
            d = da * w_row(G1)
            dx_out[rows, :] = dmid[rows, :] + s * (d - mean(d) - hat * mean(d * hat))
            return (sg + fold(da * hat), sb + fold(da))

        sg, sb = each(body, 16, (zeros8, zeros8))
        put_sum(G1, sg)
        put_sum(B1, sb)
        vec_in[0, 23:24, :] = jnp.zeros((1, half_w), F32)
        vec_in[1, 23:24, :] = jnp.zeros((1, half_w), F32)
        vec_copy(0).start()

    tasks.append((1.5, task_last))

    vec_steps = (core, to["X"], to["Y"], {"rep": r + 4 * (1 - 2 * (z % 2))}, across)

    def vec_copy(step):
        source = vec_in.at[1 - c] if step == 0 else vec_own.at[step]
        return pltpu.make_async_remote_copy(
            src_ref=source, dst_ref=vec_got.at[step], send_sem=v_send.at[step], recv_sem=v_recv.at[step],
            device_id=vec_steps[step], device_id_type=MESH,
        )

    def vec_task(k):
        vec_copy(k).wait_recv()
        total = (vec_in[c] if k == 0 else vec_own[k]) + vec_got[k]
        if k < 4:
            vec_own[k + 1] = total
            vec_copy(k + 1).start()
        else:
            vec_out[...] = total

    units = unit_table(dims)
    kinds = KINDS
    xy_at, z_at = {}, {}
    for unit, kind in enumerate(kinds):
        (z_at if kind[0] == "Z" else xy_at)[unit] = len(z_at) if kind[0] == "Z" else len(xy_at)

    def copy(unit, name, source, dest, device):
        return functools.partial(
            pltpu.make_async_remote_copy,
            src_ref=source, dst_ref=dest, send_sem=send.at[unit], recv_sem=recv.at[unit, SLOT[name]],
            device_id=device, device_id_type=MESH,
        )

    def rows_of(unit, start, count):
        if not isinstance(start, int):
            start = pl.multiple_of(start, 16)
        return res.at[unit, pl.ds(start, count), :]

    def product(unit, start, count, dest, dest_start, got=None, got_start=0, near_start=None):
        m, row, col = units[unit]
        step = 128 if count % 128 == 0 else min(count, 64)

        def block(index, _):
            part, strip = index // (UNIT_COLS // 256), index % (UNIT_COLS // 256)
            cols = pl.ds(pl.multiple_of(strip * 256, 256), 256)
            value = jnp.dot(
                at[pl.ds(pl.multiple_of(at_base[m] + row + start + part * step, 16), step), :],
                g[:, pl.ds(pl.multiple_of(g_base[m] + col + strip * 256, 256), 256)],
                preferred_element_type=F32,
            )
            if near_start is not None:
                for peer in range(3):
                    rows = peer * (UNIT_ROWS // 4) + near_start + part * step
                    value = value + jnp.dot(
                        near_left[unit, pl.ds(pl.multiple_of(rows, 16), step), :],
                        near_right[peer, :, pl.ds(pl.multiple_of(col + strip * 256, 256), 256)],
                        preferred_element_type=F32,
                    )
            if got is not None:
                value = value + got[pl.ds(pl.multiple_of(got_start + part * step, 16), step), cols].astype(F32)
            dest[pl.ds(pl.multiple_of(dest_start + part * step, 16), step), cols] = value.astype(BF16)
            return 0

        lax.fori_loop(0, (count // step) * (UNIT_COLS // 256), block, 0)

    def accumulate(unit, start, count, got, got_start, dest, dest_start):
        def block(strip, _):
            cols = pl.ds(pl.multiple_of(strip * 256, 256), 256)
            value = res[unit, pl.ds(pl.multiple_of(start, 16), count), cols].astype(F32)
            value = value + got[pl.ds(pl.multiple_of(got_start, 16), count), cols].astype(F32)
            dest[pl.ds(pl.multiple_of(dest_start, 16), count), cols] = value.astype(BF16)
            return 0

        lax.fori_loop(0, UNIT_COLS // 256, block, 0)

    def gather_line(unit, base, size, level):
        up, down = "u%d" % level, "w%d" % level
        low, high = z - (level - 1), z + (level - 1)

        @pl.when((low >= 0) & (z < 3))
        def _():
            part = rows_of(unit, base + low * size, size)
            copy(unit, up, part, part, to["U"])().start()

        @pl.when((high <= 3) & (z > 0))
        def _():
            part = rows_of(unit, base + high * size, size)
            copy(unit, down, part, part, to["D"])().start()

    def gather_arrived(unit, base, size, level):
        def wait(chunks):
            part = give.at[pl.ds(0, chunks * size), :]
            copy(unit, "u%d" % level, part, part, to["U"])().wait_recv()

        if level == 1:
            pl.when(line_mid)(lambda: wait(2))
        if level == 2:
            wait(1)
        else:
            pl.when(line_end)(lambda: wait(1))

    def finish(unit, ends, mids):
        def wait(rows):
            part = give.at[pl.ds(0, rows), :]
            copy(unit, "d1", part, part, to["X"])().wait_send()

        pl.when(line_end)(lambda: wait(ends))
        pl.when(line_mid)(lambda: wait(mids))

    def task_xy(unit, step):
        half, quarter, size = UNIT_ROWS // 2, UNIT_ROWS // 4, UNIT_ROWS // 16
        first, second = ("X", "Y") if kinds[unit][-1] == "X" else ("Y", "X")
        p, q = (x, y) if first == "X" else (y, x)
        by_tokens = kinds[unit][0] == "Q"
        line, block, out, other = line_xy.at[xy_at[unit]], res.at[unit], give.at[pl.ds(unit * GIVE_ROWS, GIVE_ROWS), :], pair.at[unit]
        keep, away_half = p * half, (1 - p) * half
        base = keep + q * quarter
        away = keep + (1 - q) * quarter
        at_z = half + quarter
        d1 = copy(unit, "d1", out.at[pl.ds(0, half), :], rows_of(unit, away_half, half), to[first])

        def left_for(peer):
            m, row, _ = units[unit]
            px, py = ((1 - x, y), (x, 1 - y), (1 - x, 1 - y))[peer]
            at_p, at_q = (px, py) if first == "X" else (py, px)
            rows = pl.ds(pl.multiple_of(at_base[m] + row + at_p * half + at_q * quarter, quarter), quarter)
            dest = near_left.at[unit, pl.ds(peer * quarter, quarter), :]
            return copy(unit, "d1", at.at[rows, :], dest, to[("X", "Y", "XY")[peer]])

        d2 = copy(unit, "d2", out.at[pl.ds(half, quarter), :], other.at[pl.ds(0, quarter), :], to[second])
        z1 = copy(unit, "z1", out.at[pl.ds(at_z, 3 * size), :], line.at[pl.ds(0, 3 * size), :], inward)
        z2 = copy(unit, "z2", out.at[pl.ds(at_z, 2 * size), :], line.at[pl.ds(3 * size, 2 * size), :], across)
        z3 = copy(unit, "z3", out.at[pl.ds(at_z + 2 * size, size), :], line.at[pl.ds(0, size), :], outward)
        own_quarter = rows_of(unit, base, quarter)
        g2 = copy(unit, "g2", own_quarter, own_quarter, to[second])
        own_half = rows_of(unit, keep, half)
        g1 = copy(unit, "g1", own_half, own_half, to[first])
        own = base + z * size
        if step == 0 and by_tokens:
            for peer in range(3):
                left_for(peer)().start()
        elif step == 1 and by_tokens:
            pass
        elif step == 2 and by_tokens:
            arrived = near_left.at[unit]
            copy(unit, "d1", arrived, arrived, to["X"])().wait_recv()

            product(unit, base, quarter, block, base, near_start=0)

            @pl.when(line_end)
            def _():
                from_row = pl.multiple_of(base + (1 - upper) * size, 16)
                for n in range(3):
                    out[at_z + n * size : at_z + (n + 1) * size, :] = block[pl.ds(from_row + n * size, size), :]
                z1().start()

        elif step == 0:
            product(unit, away_half, half, out, 0)
            d1().start()
        elif step == 1:
            d1().wait_recv()
            product(unit, away, quarter, out, half, block, away)
            d2().start()
            product(unit, base, quarter, block, base, block, base)
        elif step == 2:
            d2().wait_recv()

            @pl.when(line_end)
            def _():
                skip = (1 - upper) * size
                accumulate(unit, base + skip, 3 * size, other, skip, out, at_z)
                z1().start()
                accumulate(unit, own, size, other, z * size, block, own)

            @pl.when(line_mid)
            def _():
                accumulate(unit, base, quarter, other, 0, block, base)

        elif step == 3:

            @pl.when(line_mid)
            def _():
                z1().wait_recv()
                accumulate(unit, base + (1 - upper) * 2 * size, 2 * size, line, (1 - upper) * size, out, at_z)
                z2().start()
                accumulate(unit, own, size, line, upper * 2 * size, block, own)

        elif step == 4:

            @pl.when(line_mid)
            def _():
                z2().wait_recv()
                accumulate(unit, base + upper * 3 * size, size, line, (3 + upper) * size, out, at_z + 2 * size)
                z3().start()
                accumulate(unit, own, size, line, (4 - upper) * size, block, own)
                gather_line(unit, base, size, 1)

        elif step == 5:

            @pl.when(line_end)
            def _():
                z3().wait_recv()
                accumulate(unit, own, size, line, 0, block, own)
                gather_line(unit, base, size, 1)

        elif step in (6, 7):
            gather_arrived(unit, base, size, step - 5)
            gather_line(unit, base, size, step - 4)
        elif step == 8:
            gather_arrived(unit, base, size, 3)
            g2().start()
        elif step == 9:
            g2().wait_recv()
            g1().start()
        else:
            g1().wait_recv()
            sent = half + quarter + (3 * size if by_tokens else half + quarter)
            finish(unit, sent + 4 * size, sent + 8 * size)

    def task_z(unit, step):
        size, half, quarter = UNIT_ROWS // 4, UNIT_ROWS // 8, UNIT_ROWS // 16
        first, second = ("X", "Y") if kinds[unit] == "ZX" else ("Y", "X")
        p, q = (x, y) if kinds[unit] == "ZX" else (y, x)
        line, block, out, other = line_z.at[z_at[unit]], res.at[unit], give.at[pl.ds(unit * GIVE_ROWS, GIVE_ROWS), :], pair.at[unit]
        own = z * size
        keep, away_half = own + p * half, own + (1 - p) * half
        base, away = keep + q * quarter, keep + (1 - q) * quarter
        at_d = 3 * size
        z1 = copy(unit, "z1", out.at[pl.ds(0, 3 * size), :], line.at[pl.ds(0, 3 * size), :], inward)
        z2 = copy(unit, "z2", out.at[pl.ds(0, 2 * size), :], line.at[pl.ds(3 * size, 2 * size), :], across)
        z3 = copy(unit, "z3", out.at[pl.ds(2 * size, size), :], line.at[pl.ds(0, size), :], outward)
        d1 = copy(unit, "d1", out.at[pl.ds(at_d, half), :], other.at[pl.ds(0, half), :], to[first])
        d2 = copy(unit, "d2", out.at[pl.ds(at_d + half, quarter), :], other.at[pl.ds(half, quarter), :], to[second])
        own_quarter = rows_of(unit, base, quarter)
        g2 = copy(unit, "g2", own_quarter, own_quarter, to[second])
        own_half = rows_of(unit, keep, half)
        g1 = copy(unit, "g1", own_half, own_half, to[first])
        if step == 0:

            @pl.when(line_end)
            def _():
                product(unit, (1 - upper) * size, 3 * size, out, 0)
                z1().start()

        elif step == 1:

            @pl.when(line_mid)
            def _():
                z1().wait_recv()
                product(unit, (1 - upper) * 2 * size, 2 * size, out, 0, line, (1 - upper) * size)
                z2().start()
                product(unit, own, size, block, own, line, upper * 2 * size)

        elif step == 2:

            @pl.when(line_mid)
            def _():
                z2().wait_recv()
                product(unit, upper * 3 * size, size, out, 2 * size, line, (3 + upper) * size)
                z3().start()
                got = (4 - upper) * size
                accumulate(unit, away_half, half, line, got + (1 - p) * half, out, at_d)
                d1().start()
                accumulate(unit, keep, half, line, got + p * half, block, keep)

        elif step == 3:

            @pl.when(line_end)
            def _():
                z3().wait_recv()
                product(unit, away_half, half, out, at_d, line, (1 - p) * half)
                d1().start()
                product(unit, keep, half, block, keep, line, p * half)

        elif step == 4:
            d1().wait_recv()
            accumulate(unit, away, quarter, other, (1 - q) * quarter, out, at_d + half)
            d2().start()
            accumulate(unit, base, quarter, other, q * quarter, block, base)
        elif step == 5:
            d2().wait_recv()
            accumulate(unit, base, quarter, other, half, block, base)
            g2().start()
        elif step == 6:
            g2().wait_recv()
            g1().start()
        elif step == 7:
            g1().wait_recv()
            gather_line(unit, 0, size, 1)
        elif step in (8, 9):
            gather_arrived(unit, 0, size, step - 7)
            gather_line(unit, 0, size, step - 6)
        else:
            gather_arrived(unit, 0, size, 3)
            finish(unit, 2 * half + 2 * quarter + 4 * size, 2 * half + 2 * quarter + 8 * size)


    for kind, a, b in program_order(units, ends):
        if kind == "task":
            if a == 0:
                fill(len(stream))
            tasks[a][1]()
        elif kind == "wait":
            wait_pair(a)
            if a == 3:
                for k in range(3):
                    cotangent_copy(k, True).wait()
            if a == 1:
                for k in range(parts):
                    given(k)
        elif kind == "vec":
            vec_task(a)
        elif kinds[a][0] == "Z":
            task_z(a, b)
        else:
            task_xy(a, b)
    for step in range(5):
        vec_copy(step).wait_send()


def whole_layer(layer_input, cotangent, weights, params):
    dims = tuple(w.shape for w in weights)
    at_rows = sum(rows for rows, _ in dims)
    g_cols = sum(cols for _, cols in dims)
    at_base = [sum(rows for rows, _ in dims[:m]) for m in range(4)]
    g_base = [sum(cols for _, cols in dims[:m]) for m in range(4)]
    length, width = layer_input.shape
    hidden = dims[2][1]
    blocks = hidden // width
    units = unit_table(dims)
    kinds = KINDS
    n, n_z = len(units), sum(kind[0] == "Z" for kind in kinds)
    tiles = n // 2
    hbm = pl.BlockSpec(memory_space=pl.ANY)
    vmem = pl.BlockSpec(memory_space=pltpu.VMEM)
    dma = pltpu.SemaphoreType.DMA
    small = (24, width // 2)
    got = pl.pallas_call(
        functools.partial(layer_kernel, dims, at_base, g_base),
        out_shape=[
            pltpu.VMEM((length, width), BF16),
            pltpu.VMEM((length, width), F32),
            pltpu.VMEM((n, UNIT_ROWS, UNIT_COLS), BF16),
            pltpu.VMEM(small, F32),
            jax.ShapeDtypeStruct((2, tiles, 512, UNIT_COLS), BF16),
        ],
        in_specs=[vmem, hbm] + [hbm] * 4 + [vmem] * 13,
        out_specs=[vmem] * 4 + [hbm],
        scratch_shapes=[
            pltpu.VMEM((at_rows, 2 * length), BF16),
            pltpu.VMEM((2 * length, g_cols), BF16),
            pltpu.VMEM((n * GIVE_ROWS, UNIT_COLS), BF16),
            pltpu.VMEM((n, UNIT_ROWS // 4, UNIT_COLS), BF16),
            pltpu.VMEM((n - n_z, 5 * UNIT_ROWS // 16, UNIT_COLS), BF16),
            pltpu.VMEM((n_z, 5 * UNIT_ROWS // 4, UNIT_COLS), BF16),
            pltpu.VMEM((4, 512, UNIT_COLS), BF16),
            pltpu.VMEM((3 * blocks * length, width), F32),
            pltpu.VMEM((2 * at_rows, length), BF16),
            pltpu.VMEM((length, width), BF16),
            pltpu.VMEM((blocks * length, width), BF16),
            pltpu.VMEM((length, 3 * width), BF16),
            pltpu.VMEM((width // 128, length, 2 * length), F32),
            pltpu.VMEM((length, width), F32),
            pltpu.VMEM((length, width), F32),
            pltpu.VMEM((length, width), F32),
            pltpu.VMEM((length, width), F32),
            pltpu.VMEM((2 * 256, UNIT_COLS), F32),
            pltpu.VMEM((dims[3][0] // UNIT_ROWS, 3 * UNIT_ROWS // 4, 2 * length), BF16),
            pltpu.VMEM((3, 2 * length, width), BF16),
            pltpu.VMEM((16, width), F32),
            pltpu.VMEM((8, hidden), F32),
            pltpu.VMEM((length, 128), F32),
            pltpu.VMEM((24, hidden), F32),
            pltpu.VMEM((2,) + small, F32),
            pltpu.VMEM((5,) + small, F32),
            pltpu.VMEM((5,) + small, F32),
            dma((n,)),
            dma((n, 9)),
            dma((5,)),
            dma((5,)),
            dma((4, 2)),
            dma((4, 2)),
            dma((4,)),
            dma((10,)),
            dma((16,)),
            dma((16,)),
            dma((2 * tiles,)),
            dma((16,)),
            dma((4,)),
            dma((2, 2)),
            dma((1,)),
            dma((3, 2)),
            dma((3, 2)),
        ],
        compiler_params=pltpu.CompilerParams(
            collective_id=0, has_side_effects=True, vmem_limit_bytes=50 * MIB + 786432
        ),
        name="whole_layer",
    )(layer_input, cotangent, *weights, *params)
    return got[:4]


def finish_kernel(dims, *refs):
    y_in, dx_in, res, vec = refs[0:4]
    y_out, dx_out, outs, smalls = refs[4], refs[5], refs[6:10], refs[10:23]
    wide, lines, o_sem, s_sem = refs[23], refs[24:37], refs[37], refs[38]
    slots = wide.shape[0]
    copies = [pltpu.make_async_copy(y_in, y_out, s_sem.at[13]), pltpu.make_async_copy(dx_in, dx_out, s_sem.at[14])]
    rows_of = [range(0, 2)] + [range(k, k + 1) for k in range(2, 11)] + [range(11 + 4 * k, 15 + 4 * k) for k in range(3)]
    for k, rows in enumerate(rows_of):
        if k == 2:
            head_of = lax.broadcasted_iota(jnp.int32, (1, vec.shape[1]), 1) // 64
            lane = lax.broadcasted_iota(jnp.int32, lines[k].shape, 1)
            total = jnp.zeros(lines[k].shape, F32)
            for h in range(vec.shape[1] // 64):
                one = jnp.sum(jnp.where(head_of == h, vec[3:4, :], 0.0), axis=-1, keepdims=True)
                total = jnp.where(lane == h, one, total)
            lines[k][...] = total
        elif len(rows) == 4:
            for j, row in enumerate(rows):
                lines[k][:, j * vec.shape[1] : (j + 1) * vec.shape[1]] = vec[row : row + 1, :]
        else:
            lines[k][...] = vec[rows.start : rows.stop, :]
        copies.append(pltpu.make_async_copy(lines[k], smalls[k], s_sem.at[k]))
    for piece in copies:
        piece.start()
    units = unit_table(dims)

    def put(unit):
        m, row, col = units[unit]
        return pltpu.make_async_copy(
            wide.at[unit % slots], outs[m].at[pl.ds(row, UNIT_ROWS), pl.ds(col, UNIT_COLS)], o_sem.at[unit % slots]
        )

    for unit in range(len(units)):
        if unit >= slots:
            put(unit - slots).wait()

        def widen(b, _, unit=unit):
            rows = pl.ds(pl.multiple_of(b * 32, 32), 32)
            wide[unit % slots, rows, :] = res[unit, rows, :].astype(F32)
            return 0

        lax.fori_loop(0, UNIT_ROWS // 32, widen, 0)
        put(unit).start()
    for unit in range(len(units) - slots, len(units)):
        put(unit).wait()
    for piece in copies:
        piece.wait()


def write_results(got, dims):
    y, dx, _, vec = got
    half = vec.shape[1]
    small = [(2, half), (1, half), (1, half // 64)] + [(1, half)] * 7 + [(1, 4 * half)] * 3
    hbm = pl.BlockSpec(memory_space=pl.ANY)
    vmem = pl.BlockSpec(memory_space=pltpu.VMEM)
    dma = pltpu.SemaphoreType.DMA
    return pl.pallas_call(
        functools.partial(finish_kernel, dims),
        out_shape=[jax.ShapeDtypeStruct(y.shape, BF16), jax.ShapeDtypeStruct(dx.shape, F32)]
        + [jax.ShapeDtypeStruct(d, F32) for d in dims]
        + [jax.ShapeDtypeStruct(s, F32) for s in small],
        in_specs=[vmem] * 4,
        out_specs=[hbm] * 19,
        scratch_shapes=[pltpu.VMEM((6, UNIT_ROWS, UNIT_COLS), F32)]
        + [pltpu.VMEM(s, F32) for s in small]
        + [dma((6,)), dma((15,))],
        compiler_params=pltpu.CompilerParams(vmem_limit_bytes=30 * MIB),
        name="write_results",
    )(*got)


def on_pair_of_cores(
    layer_input, cotangent, w_qkv, qv_bias, w_out, out_bias, head_scale, ln1_gain, ln1_bias, ln2_gain, ln2_bias,
    ln3_gain, ln3_bias, w_fc1, fc1_bias, ln4_gain, ln4_bias, w_fc2, fc2_bias,
):
    params = (
        qv_bias, out_bias, head_scale, ln1_gain, ln1_bias, ln2_gain, ln2_bias, ln3_gain, ln3_bias,
        fc1_bias, ln4_gain, ln4_bias, fc2_bias,
    )
    params = [p.reshape(-1, p.shape[-1]) for p in params]
    weights = (w_qkv, w_out, w_fc1, w_fc2)
    got = whole_layer(layer_input, cotangent, weights, params)
    output, grad_input, qkv, out, up, down, *smalls = write_results(got, tuple(w.shape for w in weights))
    rows = [s.reshape(-1) for s in smalls]
    return (
        output, grad_input, qkv, smalls[0], out, rows[1], rows[2], rows[3], rows[4], rows[5], rows[6], rows[7], rows[8], up,
        rows[10], rows[11], rows[12], down, rows[9],
    )


def fits_pair(mesh):
    return mesh.shape["shard"] == 2 and mesh.shape["rep"] == 16


def solution(mesh):
    return jax.shard_map(
        on_pair_of_cores if fits_pair(mesh) else on_any_mesh,
        mesh=mesh,
        in_specs=(
            P(("rep", "shard"), None),
            P(("rep", "shard"), None),
            P("shard", None),
            P(None, "shard"),
            P("shard", None),
            P("shard"),
            P("shard"),
            P("shard"),
            P("shard"),
            P("shard"),
            P("shard"),
            P("shard"),
            P("shard"),
            P("shard", None),
            P("shard"),
            P("shard"),
            P("shard"),
            P("shard", None),
            P("shard"),
        ),
        out_specs=(
            P(("rep", "shard"), None),
            P(("rep", "shard"), None),
            P("shard", None),
            P(None, "shard"),
            P("shard", None),
            P("shard"),
            P("shard"),
            P("shard"),
            P("shard"),
            P("shard"),
            P("shard"),
            P("shard"),
            P("shard"),
            P("shard", None),
            P("shard"),
            P("shard"),
            P("shard"),
            P("shard", None),
            P("shard"),
        ),
        check_vma=False,
    )
```
